32 devices in a mesh: dp: 8 (over z, y), tensor: 4 (over x, core).
Axes of the slice: x: 2, y: 2, z: 4, core: 2. Of those that a mesh axis runs over, the one named last changes fastest.
Arguments:
- x_embed: bfloat16 [8, 1024, 768], P('dp', 'tensor'), may hold values from -6 to 6
- thoughts: bfloat16 [8, 6, 768], P('dp'), may hold values from -6 to 6
- thought_pos: int32 [8, 6], P('dp'), may hold values from 0 to 1023, as said below
- img_start: int32 [8, 2], P('dp'), may hold values from 0 to 768, as said below
- pre_attn_gain: bfloat16 [768], P('dp'), may hold values from 0.5 to 1.5
- pre_attn_bias: bfloat16 [768], P('dp'), may hold values from -4 to 4
- w_qkv: bfloat16 [3, 768, 768], P(None, 'dp', 'tensor'), may hold values from -0.21875 to 0.21875
- b_qv: bfloat16 [2, 768], P(None, ('tensor', 'dp')), may hold values from -4 to 4
- w_proj: bfloat16 [768, 768], P('tensor', 'dp'), may hold values from -0.875 to 0.875
- b_proj: bfloat16 [768], P('dp'), may hold values from -4 to 4
- pre_mlp_gain: bfloat16 [768], P('dp'), may hold values from 0.5 to 1.5
- pre_mlp_bias: bfloat16 [768], P('dp'), may hold values from -4 to 4
- w_up: bfloat16 [768, 3072], P('dp', 'tensor'), may hold values from -0.21875 to 0.21875
- b_up: bfloat16 [3072], P(('tensor', 'dp')), may hold values from -4 to 4
- w_down: bfloat16 [3072, 768], P('tensor', 'dp'), may hold values from -0.109375 to 0.109375
- b_down: bfloat16 [768], P('dp'), may hold values from -4 to 4
- grad_out: bfloat16 [8, 1024, 768], P('dp', 'tensor'), may hold values from -6 to 6
Outputs:
- block_out: bfloat16 [8, 1024, 768], P('dp', 'tensor')
- grad_embed: float32 [8, 1024, 768], P('dp', 'tensor')
- grad_thoughts: float32 [8, 6, 768], P('dp', None, 'tensor')
- grad_pre_attn_gain: float32 [768], P('dp')
- grad_pre_attn_bias: float32 [768], P('dp')
- grad_w_qkv: float32 [3, 768, 768], P(None, 'dp', 'tensor')
- grad_b_qv: float32 [2, 768], P(None, ('tensor', 'dp'))
- grad_w_proj: float32 [768, 768], P('tensor', 'dp')
- grad_b_proj: float32 [768], P('dp')
- grad_pre_mlp_gain: float32 [768], P('dp')
- grad_pre_mlp_bias: float32 [768], P('dp')
- grad_w_up: float32 [768, 3072], P('dp', 'tensor')
- grad_b_up: float32 [3072], P(('tensor', 'dp'))
- grad_w_down: float32 [3072, 768], P('tensor', 'dp')
- grad_b_down: float32 [768], P('dp')
The draws below stay inside these ranges and needn't reach their ends.
Inputs may be any that keep to these rules, and one draw needn't show every extreme that they name: `thought_pos`: in each sequence the 6 thought positions are consecutive and ascending. `img_start`: span i of a sequence starts between i * 512 and (i + 1) * 512 - 256, so the spans of a sequence never intersect.
All inputs are finite; a program needn't handle non-finite values.
Results may differ from the reference program's by a relative error of at most 0.017.
Values may be sent and summed in bfloat16 or wider, within the bound.
No kernel may reach another device: no remote copies, remote signals or barrier semaphores. Data moves between devices by JAX's collectives and lax.ppermute only.
A program may use at most 128 MiB of HBM per device.

```python
import math
import jax
import jax.numpy as jnp
from jax import lax

D = 768
HEADS = 12
HD = 64
FF = 3072
LEN = 1024
IMG = 256
NI = 2
NT = 6
SEQS = 8


def draw_thought_pos(key, part):
    first_rows = jax.random.randint(key, (SEQS,), 0, LEN - NT + 1).astype(jnp.int32)
    first_rows = first_rows.at[0].set(0).at[SEQS - 1].set(LEN - NT)
    return (first_rows[:, None] + jnp.arange(NT, dtype=jnp.int32)[None, :]).astype(jnp.int32)


def draw_img_start(key, part):
    offsets = jax.random.randint(key, (SEQS, NI), 0, LEN // NI - IMG + 1).astype(jnp.int32)
    offsets = offsets.at[0, 0].set(0).at[SEQS - 1, NI - 1].set(LEN // NI - IMG)
    return (offsets + (jnp.arange(NI, dtype=jnp.int32) * (LEN // NI))[None, :]).astype(jnp.int32)


def shard_levels(key, shape, shards, least, high):
    gain, own = 1.0, jax.random.fold_in(key, 6)
    for position, blocks in shards:
        draws = jnp.exp(jax.random.uniform(jax.random.fold_in(own, position), (blocks,), jnp.float32, least / len(shards), high / len(shards)))
        gain = gain * jnp.repeat(draws, shape[position] // blocks).reshape([-1 if axis == position else 1 for axis in range(len(shape))])
    return gain


def bell_draw(key, dims, spread, limit, pieces=(), kind=jnp.bfloat16):
    result = jax.random.normal(key, dims, jnp.float32) * spread
    if len(pieces) > 0:
        result = shard_levels(key, dims, pieces, -0.22, 0.18) * result
    return jnp.clip(result, min=-limit, max=limit).astype(kind)


def setup_inputs(seed: int = 0) -> dict:
    key_list = jax.random.split(jax.random.key(seed), 18)
    return {
        "x_embed": bell_draw(key_list[0], (SEQS, LEN, D), 1.0, 6.0, ((0, 8), (1, 4))),
        "thoughts": bell_draw(key_list[1], (SEQS, NT, D), 1.0, 6.0, ((0, 8),)),
        "thought_pos": draw_thought_pos(jax.random.fold_in(key_list[17], 71), 0),
        "img_start": draw_img_start(jax.random.fold_in(key_list[17], 71), 0),
        "pre_attn_gain": jnp.clip(1.0 + 0.1 * jax.random.normal(key_list[4], (D,), jnp.float32), 0.5, 1.5).astype(jnp.bfloat16),
        "pre_attn_bias": bell_draw(key_list[5], (D,), 0.3, 4.0, ((0, 8),)),
        "w_qkv": bell_draw(key_list[6], (3, D, D), D ** -0.5, 0.21875, ((1, 8), (2, 4))),
        "b_qv": bell_draw(key_list[7], (2, D), 0.3, 4.0, ((1, 32),)),
        "w_proj": bell_draw(key_list[8], (D, D), (D // 16) ** -0.5, 0.875, ((0, 4), (1, 8))),
        "b_proj": bell_draw(key_list[9], (D,), 0.3, 4.0, ((0, 8),)),
        "pre_mlp_gain": jnp.clip(1.0 + 0.1 * jax.random.normal(key_list[10], (D,), jnp.float32), 0.5, 1.5).astype(jnp.bfloat16),
        "pre_mlp_bias": bell_draw(key_list[11], (D,), 0.3, 4.0, ((0, 8),)),
        "w_up": bell_draw(key_list[12], (D, FF), D ** -0.5, 0.21875, ((0, 8), (1, 4))),
        "b_up": bell_draw(key_list[13], (FF,), 0.3, 4.0, ((0, 32),)),
        "w_down": bell_draw(key_list[14], (FF, D), FF ** -0.5, 0.109375, ((0, 4), (1, 8))),
        "b_down": bell_draw(key_list[15], (D,), 0.3, 4.0, ((0, 8),)),
        "grad_out": bell_draw(key_list[16], (SEQS, LEN, D), 1.0, 6.0, ((0, 8), (1, 4))),
    }


EPSILON = 1e-05

@jax.custom_vjp
def low(v):
    return lax.optimization_barrier(v.astype(jnp.bfloat16)).astype(jnp.float32)

@jax.custom_vjp
def low_back(v):
    return v

def low_keep(v):
    return (low(v), None)

def low_pass(kept, grad):
    return (grad,)

def back_keep(v):
    return (v, None)

def back_low(kept, grad):
    return (low(grad),)
low.defvjp(low_keep, low_pass)
low_back.defvjp(back_keep, back_low)

def rounded(values):
    return low_back(low(values))

def layer_norm(inputs, scales, shifts):
    row_mean = lax.optimization_barrier(jnp.mean(inputs, axis=-1, keepdims=True))
    centred = inputs - row_mean
    variance = lax.optimization_barrier(jnp.mean(centred * centred, axis=-1, keepdims=True))
    return centred * lax.rsqrt(variance + EPSILON) * scales + shifts

def gelu_tanh(values):
    return 0.5 * values * (1.0 + jnp.tanh(0.7978845608028654 * (values + 0.044715 * values * values * values)))

def span_mask(query_pos, key_pos, starts):
    allowed = (key_pos[None, :] <= query_pos[:, None])[None, :, :]
    for span_index in range(starts.shape[1]):
        span_first = starts[:, span_index][:, None]
        in_query = (query_pos[None, :] >= span_first) & (query_pos[None, :] < span_first + IMG)
        in_key = (key_pos[None, :] >= span_first) & (key_pos[None, :] < span_first + IMG)
        allowed = allowed | in_query[:, :, None] & in_key[:, None, :]
    return allowed

def attend(queries, key_rows, value_rows, starts):
    group_size, seq_length, head_count, head_width = queries.shape
    block_rows = min(512, seq_length)
    block_total = seq_length // block_rows
    stacked = queries.reshape(group_size, block_total, block_rows, head_count, head_width).transpose(1, 0, 2, 3, 4)
    key_pos = jnp.arange(seq_length, dtype=jnp.int32)

    @jax.checkpoint
    def one_block(block_item):
        query_block, block_index = block_item
        query_pos = block_index * block_rows + jnp.arange(block_rows, dtype=jnp.int32)
        scores = jnp.einsum('gqhd,gkhd->ghqk', query_block, key_rows, precision=lax.Precision.HIGHEST) * 0.125
        scores = low_back(scores)
        allowed = span_mask(query_pos, key_pos, starts)
        masked = jnp.where(allowed[:, None, :, :], scores, -1e+30)
        row_top = lax.optimization_barrier(jnp.max(masked, axis=-1, keepdims=True))
        exp_scores = jnp.exp(masked - row_top)
        attn_probs = low(exp_scores / lax.optimization_barrier(jnp.sum(exp_scores, axis=-1, keepdims=True)))
        return jnp.einsum('ghqk,gkhd->gqhd', attn_probs, value_rows, precision=lax.Precision.HIGHEST)
    outputs = lax.map(one_block, (stacked, jnp.arange(block_total, dtype=jnp.int32)))
    return outputs.transpose(1, 0, 2, 3, 4).reshape(group_size, seq_length, head_count, head_width)

def forward(embed_rows, latent, positions_in, starts, params):
    gain_one, bias_one, query_key_value_weight, qv_bias, output_projection_weight, proj_bias, gain_two, bias_two, up_weight, up_bias, down_weight, down_bias = params
    seq_length = embed_rows.shape[1]
    positions = jnp.arange(seq_length, dtype=jnp.int32)
    thought_matches = (positions[None, :, None] == positions_in[:, None, :]).astype(jnp.float32)
    spliced = embed_rows * (1.0 - lax.optimization_barrier(jnp.sum(thought_matches, axis=-1, keepdims=True))) + jnp.einsum('glt,gtd->gld', thought_matches, latent, precision=lax.Precision.HIGHEST)
    normed = low(layer_norm(spliced, gain_one, bias_one))
    mixed_rows = jnp.einsum('gld,cde->cgle', normed, query_key_value_weight, precision=lax.Precision.HIGHEST)
    all_bias = jnp.stack([qv_bias[0], jnp.zeros_like(qv_bias[0]), qv_bias[1]])
    mixed_rows = rounded(mixed_rows + all_bias[:, None, None, :])
    head_shape = (embed_rows.shape[0], seq_length, HEADS, HD)
    attended = attend(mixed_rows[0].reshape(head_shape), mixed_rows[1].reshape(head_shape), mixed_rows[2].reshape(head_shape), starts)
    attended = rounded(attended.reshape(embed_rows.shape))
    branch = jnp.einsum('gle,ed->gld', attended, output_projection_weight, precision=lax.Precision.HIGHEST)
    residual = spliced + low_back(branch) + proj_bias
    normed_two = low(layer_norm(residual, gain_two, bias_two))
    hidden_before_norm = jnp.einsum('gld,df->glf', normed_two, up_weight, precision=lax.Precision.HIGHEST) + up_bias
    hidden = low(gelu_tanh(low_back(hidden_before_norm)))
    perceptron_portion = jnp.einsum('glf,fd->gld', hidden, down_weight, precision=lax.Precision.HIGHEST)
    return residual + low_back(perceptron_portion) + down_bias

def reference(x_embed, thoughts, thought_pos, img_start, pre_attn_gain, pre_attn_bias, w_qkv, b_qv, w_proj, b_proj, pre_mlp_gain, pre_mlp_bias, w_up, b_up, w_down, b_down, grad_out):
    params = (pre_attn_gain.astype(jnp.float32), pre_attn_bias.astype(jnp.float32), w_qkv.astype(jnp.float32), b_qv.astype(jnp.float32), w_proj.astype(jnp.float32), b_proj.astype(jnp.float32), pre_mlp_gain.astype(jnp.float32), pre_mlp_bias.astype(jnp.float32), w_up.astype(jnp.float32), b_up.astype(jnp.float32), w_down.astype(jnp.float32), b_down.astype(jnp.float32))
    seq_total = x_embed.shape[0]
    seq_length = x_embed.shape[1]
    group_size = math.gcd(seq_total, max(1, 4096 // seq_length))
    group_total = seq_total // group_size

    def split_groups(source):
        return source.reshape((group_total, group_size) + source.shape[1:])
    inputs = (split_groups(x_embed.astype(jnp.float32)), split_groups(thoughts.astype(jnp.float32)), split_groups(thought_pos), split_groups(img_start), split_groups(grad_out.astype(jnp.float32)))

    def one_group(totals, block_item):
        embed_rows, latent, positions_in, starts, cotangent = block_item

        def apply_block(embed_arg, latent_arg, param_arg):
            return forward(embed_arg, latent_arg, positions_in, starts, param_arg)
        output, pullback = jax.vjp(apply_block, embed_rows, latent, params)
        grad_rows, grad_latent, grad_params = pullback(cotangent)
        totals = jax.tree.map(jnp.add, totals, grad_params)
        return (totals, (output.astype(jnp.bfloat16), grad_rows, grad_latent))
    zero_grads = jax.tree.map(jnp.zeros_like, params)
    totals, (outputs, grad_rows, grad_latent) = lax.scan(one_group, zero_grads, inputs)
    block_out = outputs.reshape(seq_total, seq_length, x_embed.shape[2])
    grad_embed = grad_rows.reshape(seq_total, seq_length, x_embed.shape[2])
    grad_thoughts = grad_latent.reshape(thoughts.shape)
    return (block_out, grad_embed, grad_thoughts, totals[0], totals[1], totals[2], totals[3], totals[4], totals[5], totals[6], totals[7], totals[8], totals[9], totals[10], totals[11])
```

```python
import math

import jax
import jax.numpy as jnp
from jax import lax
from jax.sharding import PartitionSpec as P

HD = 64
IMG = 256
EPSILON = 1e-05
F32 = jnp.float32
LOW = jnp.bfloat16


def swapped(array, axis, mask):
    return lax.ppermute(array, axis, [(i, i ^ mask) for i in range(lax.axis_size(axis))])


def dp_steps():
    size = lax.axis_size("dp")
    if size == 8:
        return ((6, 4), (2, 6), (1, 1))
    return tuple((1 << b, 1 << b) for b in reversed(range(size.bit_length() - 1)))


def parity(index, mask):
    bit = jnp.int32(0)
    for b in range(mask.bit_length()):
        if mask >> b & 1:
            bit = bit ^ ((index >> b) & 1)
    return bit


def slot_owners(steps):
    owners = [0]
    for mask, _ in steps:
        owners = owners + [o ^ mask for o in owners]
    return owners


def dp_gather(shard):
    steps, me = dp_steps(), lax.axis_index("dp")
    slots = shard[None]
    for mask, kinds in steps:
        other = swapped(slots, "dp", mask)
        first = parity(me, kinds) == 0
        slots = jnp.where(
            first, jnp.concatenate([slots, other]), jnp.concatenate([other, slots])
        )
    owners = slot_owners(steps)
    return jnp.stack([slots[owners.index(s)] for s in range(len(owners))])


def dp_scatter_sum(blocks):
    steps, me = dp_steps(), lax.axis_index("dp")
    slots = jnp.stack([blocks[s] for s in slot_owners(steps)])
    for mask, kinds in reversed(steps):
        half = slots.shape[0] // 2
        first = parity(me, kinds) == 0
        keep = jnp.where(first, slots[:half], slots[half:])
        send = jnp.where(first, slots[half:], slots[:half]).astype(LOW)
        slots = keep.astype(F32) + swapped(send, "dp", mask).astype(F32)
    return slots[0]


def rows_gather(own):
    other = swapped(own, "tensor", 2)
    first = (lax.axis_index("tensor") >> 1) == 0
    both = jnp.stack([jnp.where(first, own, other), jnp.where(first, other, own)])
    return jnp.stack([both, swapped(both, "tensor", 1)], axis=1)


def rows_all_sum(part):
    got = swapped(part[1].astype(LOW), "tensor", 1)
    mine = (part[0] + got.astype(F32)).astype(LOW)
    other = swapped(mine, "tensor", 2)
    total = (mine.astype(F32) + other.astype(F32)).astype(LOW)
    return jnp.stack([total, swapped(total, "tensor", 1)])


def rows_scatter_sum(part):
    mine = part[:, 0] + swapped(part[:, 1].astype(LOW), "tensor", 1).astype(F32)
    first = (lax.axis_index("tensor") >> 1) == 0
    keep = jnp.where(first, mine[0], mine[1])
    send = jnp.where(first, mine[1], mine[0]).astype(LOW)
    return keep + swapped(send, "tensor", 2).astype(F32)


def small_all_sum(part):
    part = part + swapped(part, "tensor", 1)
    return part + swapped(part, "tensor", 2)


def normalised(values):
    centred = values - jnp.mean(values, axis=-1, keepdims=True)
    inverse = lax.rsqrt(jnp.mean(centred * centred, axis=-1, keepdims=True) + EPSILON)
    return centred * inverse, inverse


def norm_back(upstream, xhat, inverse, gain):
    scaled = upstream * gain
    return inverse * (
        scaled
        - jnp.mean(scaled, axis=-1, keepdims=True)
        - xhat * jnp.mean(scaled * xhat, axis=-1, keepdims=True)
    )


def gelu_pair(u):
    k, a = 0.7978845608028654, 0.044715
    t = jnp.tanh(k * (u + a * u * u * u))
    return 0.5 * u * (1.0 + t), 0.5 * (1.0 + t) + 0.5 * u * (1.0 - t * t) * (k * (1.0 + 3.0 * a * u * u))


def dot(a, b, ca, cb):
    return lax.dot_general(a, b, (((ca,), (cb,)), ((), ())), preferred_element_type=F32)


def chunk_scores(queries, keys, limits, key_pos, head):
    cols = slice(head * HD, head * HD + HD)
    scores = dot(queries[:, cols], keys[:, cols], 1, 1) * 0.125
    return jnp.where(key_pos[None, :] <= limits[:, None], scores, -1e30)


def local(
    x_embed,
    thoughts,
    thought_pos,
    img_start,
    pre_attn_gain,
    pre_attn_bias,
    w_qkv,
    b_qv,
    w_proj,
    b_proj,
    pre_mlp_gain,
    pre_mlp_bias,
    w_up,
    b_up,
    w_down,
    b_down,
    grad_out,
):
    dp = lax.axis_size("dp")
    tensor_rank = lax.axis_index("tensor")
    core = tensor_rank & 1
    first_chip = (tensor_rank >> 1) == 0
    _, rows, width = x_embed.shape
    length = 4 * rows
    shard_rows = w_qkv.shape[1]
    head_cols = w_qkv.shape[2]
    hidden_cols = w_up.shape[1]

    vectors = jnp.concatenate(
        [pre_attn_gain, pre_attn_bias, b_proj, pre_mlp_gain, pre_mlp_bias, b_down, b_up, b_qv.reshape(-1)]
    )
    qkv_cols = 3 * head_cols
    vec_rows = -(-vectors.shape[0] // (8 * qkv_cols)) * 8
    vec_pack = jnp.pad(vectors, (0, vec_rows * qkv_cols - vectors.shape[0])).reshape(vec_rows, qkv_cols)
    pack_one = jnp.concatenate([jnp.moveaxis(w_qkv, 0, 1).reshape(shard_rows, qkv_cols), vec_pack])
    pack_two = jnp.concatenate([w_proj.T, w_up, w_down.T], axis=1)
    x_rows = rows_gather(x_embed[0])
    got_one = dp_gather(pack_one)
    got_two = dp_gather(pack_two)
    cot_rows = rows_gather(grad_out[0])

    w_in = got_one[:, :shard_rows].reshape(width, qkv_cols)
    got_vec = got_one[:, shard_rows:].reshape(dp, -1)
    places = [0]
    for v in (pre_attn_gain, pre_attn_bias, b_proj, pre_mlp_gain, pre_mlp_bias, b_down, b_up):
        places.append(places[-1] + v.shape[0])
    gain_one, bias_one, proj_bias, gain_two, bias_two, down_bias, up_bias = (
        got_vec[:, a : a + v.shape[0]].reshape(-1).astype(F32)
        for a, v in zip(places, (pre_attn_gain, pre_attn_bias, b_proj, pre_mlp_gain, pre_mlp_bias, b_down, b_up))
    )
    qv_bias = got_vec[:, places[-1] : places[-1] + b_qv.size].reshape(dp, 2, -1)
    qv_bias = jnp.moveaxis(qv_bias, 0, 1).reshape(2, head_cols).astype(F32)
    w_all = got_two.reshape(width, -1)
    w_proj_t = w_all[:, :head_cols]
    w_up_all = w_all[:, head_cols : head_cols + hidden_cols]
    w_down_t = w_all[:, head_cols + hidden_cols :]

    half = 2 * rows
    positions = (
        jnp.arange(2, dtype=jnp.int32)[:, None, None] * half
        + ((jnp.arange(2, dtype=jnp.int32) ^ core) * rows)[None, :, None]
        + jnp.arange(rows, dtype=jnp.int32)[None, None, :]
    ).reshape(length)
    starts = jnp.repeat(img_start[0], half)
    inside = (positions >= starts) & (positions < starts + IMG)
    limits = jnp.where(inside, starts + (IMG - 1), positions)

    matches = positions[:, None] == thought_pos[0][None, :]
    matches_low = matches.astype(LOW)
    covered = jnp.any(matches, axis=-1, keepdims=True)
    spliced = jnp.where(
        covered, dot(matches_low, thoughts[0], 1, 0), x_rows.reshape(length, width).astype(F32)
    )
    xhat_one, inverse_one = normalised(spliced)
    normed = (xhat_one * gain_one + bias_one).astype(LOW)
    all_bias = jnp.concatenate([qv_bias[0], jnp.zeros_like(qv_bias[0]), qv_bias[1]])
    mixed = (dot(normed, w_in, 1, 0) + all_bias).astype(LOW)
    queries, keys, values = (mixed[:, k * head_cols : (k + 1) * head_cols] for k in range(3))

    heads = head_cols // HD
    attended, logs, residuals = [], [], []
    for chunk in range(2):
        part = slice(chunk * half, chunk * half + half)
        seen = slice(0, chunk * half + half)
        outs, chunk_logs = [], []
        for head in range(heads):
            cols = slice(head * HD, head * HD + HD)
            scores = chunk_scores(queries[part], keys[seen], limits[part], positions[seen], head)
            top = jnp.max(scores, axis=-1, keepdims=True)
            exps = jnp.exp(scores - top)
            total = jnp.sum(exps, axis=-1, keepdims=True)
            outs.append(dot((exps / total).astype(LOW), values[seen, cols], 1, 0))
            chunk_logs.append(top + jnp.log(total))
        attended.append(jnp.concatenate(outs, axis=1).astype(LOW))
        logs.append(chunk_logs)
        branch = rows_all_sum(dot(attended[-1], w_proj_t, 1, 1).reshape(2, rows, width))
        residuals.append(spliced[part] + branch.reshape(half, width).astype(F32) + proj_bias)

    cot = cot_rows.reshape(length, width)
    mlp_parts, grad_twos, xhats, inverses = [], [], [], []
    grad_down_t = grad_up = 0.0
    grad_up_b = 0.0
    for chunk in range(2):
        part = slice(chunk * half, chunk * half + half)
        xhat_two, inverse_two = normalised(residuals[chunk])
        normed_two = (xhat_two * gain_two + bias_two).astype(LOW)
        hidden, slope = gelu_pair(dot(normed_two, w_up_all, 1, 0) + up_bias)
        hidden = hidden.astype(LOW)
        grad_hidden = (dot(cot[part], w_down_t, 1, 0) * slope).astype(LOW)
        grad_twos.append(rows_all_sum(dot(grad_hidden, w_up_all, 1, 1).reshape(2, rows, width)))
        mlp_parts.append(dot(hidden, w_down_t, 1, 1).reshape(2, rows, width))
        grad_down_t = grad_down_t + dot(cot[part], hidden, 0, 0)
        grad_up = grad_up + dot(normed_two, grad_hidden, 0, 0)
        grad_up_b = grad_up_b + jnp.sum(grad_hidden.astype(F32), axis=0)
        xhats.append(xhat_two)
        inverses.append(inverse_two)
    scattered = dp_scatter_sum(
        jnp.concatenate([grad_up, grad_down_t], axis=1).reshape(dp, shard_rows, 2 * hidden_cols)
    )
    out_up, out_down = scattered[:, :hidden_cols], scattered[:, hidden_cols:].T

    own = lambda a: jnp.where(first_chip, a[:rows], a[half : half + rows])
    residual = jnp.concatenate(residuals)
    block_out = own(residual) + rows_scatter_sum(jnp.stack(mlp_parts)) + down_bias

    grad_queries, grad_branches, grad_residuals = [], [], []
    grad_gain_two = grad_bias_two = 0.0
    grad_keys, grad_values = [0.0] * 2, [0.0] * 2
    for chunk in range(2):
        part = slice(chunk * half, chunk * half + half)
        seen = slice(0, chunk * half + half)
        upstream = grad_twos[chunk].reshape(half, width).astype(F32)
        grad_gain_two = grad_gain_two + jnp.sum(upstream * xhats[chunk], axis=0)
        grad_bias_two = grad_bias_two + jnp.sum(upstream, axis=0)
        grad_residual = cot[part].astype(F32) + norm_back(upstream, xhats[chunk], inverses[chunk], gain_two)
        grad_branch = grad_residual.astype(LOW)
        grad_att = dot(grad_branch, w_proj_t, 1, 0).astype(LOW)
        dq, dk, dv = [], [], []
        for head in range(heads):
            cols = slice(head * HD, head * HD + HD)
            scores = chunk_scores(queries[part], keys[seen], limits[part], positions[seen], head)
            probs = jnp.exp(scores - logs[chunk][head])
            grad_probs = dot(grad_att[:, cols], values[seen, cols], 1, 1)
            delta = jnp.sum(probs * grad_probs, axis=-1, keepdims=True)
            grad_scores = (probs * (grad_probs - delta)).astype(LOW)
            dq.append(dot(grad_scores, keys[seen, cols], 1, 0))
            dk.append(dot(grad_scores, queries[part, cols], 0, 0))
            dv.append(dot(probs.astype(LOW), grad_att[:, cols], 0, 0))
        grad_queries.append(jnp.concatenate(dq, axis=1) * 0.125)
        dk, dv = jnp.concatenate(dk, axis=1) * 0.125, jnp.concatenate(dv, axis=1)
        for k in range(chunk + 1):
            grad_keys[k] = grad_keys[k] + dk[k * half : (k + 1) * half]
            grad_values[k] = grad_values[k] + dv[k * half : (k + 1) * half]
        grad_residuals.append(grad_residual)
        grad_branches.append(grad_branch)
    grad_mixed = jnp.concatenate(
        [jnp.concatenate(g) for g in (grad_queries, grad_keys, grad_values)], axis=1
    ).astype(LOW)
    grad_residual = jnp.concatenate(grad_residuals)
    grad_branch = jnp.concatenate(grad_branches)

    grad_one_part = dot(grad_mixed, w_in, 1, 1)
    grad_normed = rows_scatter_sum(grad_one_part.reshape(2, 2, rows, width))
    gain_bias_one = small_all_sum(
        jnp.stack([jnp.sum(grad_one_part * xhat_one, axis=0), jnp.sum(grad_one_part, axis=0)])
    )
    grad_in = dot(normed, grad_mixed, 0, 0)
    grad_proj_t = dot(grad_branch, jnp.concatenate(attended), 0, 0)
    scattered = dp_scatter_sum(
        jnp.concatenate([grad_in, grad_proj_t], axis=1).reshape(dp, shard_rows, qkv_cols + head_cols)
    )
    out_qkv = jnp.moveaxis(scattered[:, :qkv_cols].reshape(shard_rows, 3, head_cols), 1, 0)
    out_proj = scattered[:, qkv_cols:].T
    mixed_sums = jnp.sum(grad_mixed.astype(F32), axis=0)
    vec = jnp.concatenate(
        [
            v.reshape(dp, -1)
            for v in (
                gain_bias_one[0],
                gain_bias_one[1],
                jnp.sum(grad_residual, axis=0),
                grad_gain_two,
                grad_bias_two,
                jnp.sum(cot.astype(F32), axis=0),
                grad_up_b,
                mixed_sums[:head_cols],
                mixed_sums[2 * head_cols :],
            )
        ],
        axis=1,
    )
    vec = dp_scatter_sum(vec[:, None, :])[0]
    outs = []
    place = 0
    for n in (*(v.shape[0] for v in (pre_attn_gain, pre_attn_bias, b_proj, pre_mlp_gain, pre_mlp_bias, b_down, b_up)), b_qv.size):
        outs.append(vec[place : place + n])
        place += n
    out_gain_one, out_bias_one, out_b_proj, out_gain_two, out_bias_two, out_b_down, out_b_up, out_qv = outs

    grad_own = norm_back(grad_normed, own(xhat_one), own(inverse_one), gain_one) + own(grad_residual)
    grad_embed = jnp.where(own(covered), 0.0, grad_own)
    thought_part = lax.dot_general(
        own(matches).astype(F32), grad_own, (((0,), (0,)), ((), ())), precision=lax.Precision.HIGHEST
    )
    quarter = width // 4
    halves = thought_part.reshape(-1, 2, 2 * quarter)
    keep = jnp.where(first_chip, halves[:, 0], halves[:, 1])
    send = jnp.where(first_chip, halves[:, 1], halves[:, 0])
    mine = (keep + swapped(send, "tensor", 2)).reshape(-1, 2, quarter)
    keep = jnp.where(core == 0, mine[:, 0], mine[:, 1])
    send = jnp.where(core == 0, mine[:, 1], mine[:, 0])
    grad_thoughts = keep + swapped(send, "tensor", 1)

    return (
        block_out.astype(LOW)[None],
        grad_embed[None],
        grad_thoughts[None],
        out_gain_one,
        out_bias_one,
        out_qkv,
        out_qv.reshape(2, -1),
        out_proj,
        out_b_proj,
        out_gain_two,
        out_bias_two,
        out_up,
        out_b_up,
        out_down,
        out_b_down,
    )


def solution(mesh):
    in_specs = (
        P("dp", "tensor", None),
        P("dp", None, None),
        P("dp", None),
        P("dp", None),
        P("dp"),
        P("dp"),
        P(None, "dp", "tensor"),
        P(None, ("tensor", "dp")),
        P("tensor", "dp"),
        P("dp"),
        P("dp"),
        P("dp"),
        P("dp", "tensor"),
        P(("tensor", "dp")),
        P("tensor", "dp"),
        P("dp"),
        P("dp", "tensor", None),
    )
    out_specs = (
        P("dp", "tensor", None),
        P("dp", "tensor", None),
        P("dp", None, "tensor"),
        P("dp"),
        P("dp"),
        P(None, "dp", "tensor"),
        P(None, ("tensor", "dp")),
        P("tensor", "dp"),
        P("dp"),
        P("dp"),
        P("dp"),
        P("dp", "tensor"),
        P(("tensor", "dp")),
        P("tensor", "dp"),
        P("dp"),
    )
    return jax.shard_map(local, mesh=mesh, in_specs=in_specs, out_specs=out_specs, check_vma=False)
```

```python
import functools

import jax
import jax.numpy as jnp
from jax import lax
from jax.experimental import pallas as pl
from jax.experimental.pallas import tpu as pltpu
from jax.sharding import PartitionSpec as P

HD = 64
IMG = 256
EPSILON = 1e-05
F32 = jnp.float32
LOW = jnp.bfloat16


def swapped(array, axis, mask):
    return lax.ppermute(array, axis, [(i, i ^ mask) for i in range(lax.axis_size(axis))])


def dp_steps():
    size = lax.axis_size("dp")
    if size == 8:
        return ((6, 4), (2, 6), (1, 1))
    return tuple((1 << b, 1 << b) for b in reversed(range(size.bit_length() - 1)))


def parity(index, mask):
    bit = jnp.int32(0)
    for b in range(mask.bit_length()):
        if mask >> b & 1:
            bit = bit ^ ((index >> b) & 1)
    return bit


def slot_owners(steps):
    owners = [0]
    for mask, _ in steps:
        owners = owners + [o ^ mask for o in owners]
    return owners


def dp_gather(shard):
    steps, me = dp_steps(), lax.axis_index("dp")
    slots = shard[None]
    for mask, kinds in steps:
        other = swapped(slots, "dp", mask)
        first = parity(me, kinds) == 0
        slots = jnp.where(
            first, jnp.concatenate([slots, other]), jnp.concatenate([other, slots])
        )
    owners = slot_owners(steps)
    return jnp.stack([slots[owners.index(s)] for s in range(len(owners))])


def dp_scatter_sum(blocks):
    steps, me = dp_steps(), lax.axis_index("dp")
    slots = jnp.stack([blocks[s] for s in slot_owners(steps)])
    for mask, kinds in reversed(steps):
        half = slots.shape[0] // 2
        first = parity(me, kinds) == 0
        keep = jnp.where(first, slots[:half], slots[half:])
        send = jnp.where(first, slots[half:], slots[:half]).astype(LOW)
        slots = keep.astype(F32) + swapped(send, "dp", mask).astype(F32)
    return slots[0]


def rows_gather(own):
    other = swapped(own, "tensor", 2)
    first = (lax.axis_index("tensor") >> 1) == 0
    both = jnp.stack([jnp.where(first, own, other), jnp.where(first, other, own)])
    return both, swapped(both, "tensor", 1)


def rows_all_sum(keep, send):
    mine = (keep + swapped(send, "tensor", 1).astype(F32)).astype(LOW)
    other = swapped(mine, "tensor", 2)
    total = (mine.astype(F32) + other.astype(F32)).astype(LOW)
    return total, swapped(total, "tensor", 1)


def rows_scatter_sum(keep, send):
    mine = keep.astype(F32) + swapped(send, "tensor", 1).astype(F32)
    first = (lax.axis_index("tensor") >> 1) == 0
    keep = jnp.where(first, mine[0], mine[1])
    send = jnp.where(first, mine[1], mine[0]).astype(LOW)
    return keep + swapped(send, "tensor", 2).astype(F32)


def small_all_sum(part):
    part = part + swapped(part, "tensor", 1)
    return part + swapped(part, "tensor", 2)


def dot(a, b, ca, cb, precision=None):
    return lax.dot_general(
        a, b, (((ca,), (cb,)), ((), ())), precision=precision, preferred_element_type=F32
    )


def normalised(values):
    centred = values - jnp.mean(values, axis=-1, keepdims=True)
    inverse = lax.rsqrt(jnp.mean(centred * centred, axis=-1, keepdims=True) + EPSILON)
    return centred * inverse, inverse


def norm_back(upstream, xhat, inverse, gain):
    scaled = upstream * gain
    return inverse * (
        scaled
        - jnp.mean(scaled, axis=-1, keepdims=True)
        - xhat * jnp.mean(scaled * xhat, axis=-1, keepdims=True)
    )


def gelu_pair(u):
    k, a = 0.7978845608028654, 0.044715
    square = u * u
    t = jnp.tanh(u * (k + (k * a) * square))
    rise = 0.5 * (1.0 + t)
    return u * rise, rise + (0.5 * u) * (1.0 - t * t) * (k + (3.0 * k * a) * square)


def iota(shape, dim):
    return lax.broadcasted_iota(jnp.int32, shape, dim)


def call(kernel, outs, cost, *args, scratch=(), mib=40):
    spec = lambda a: pl.BlockSpec(
        memory_space=pltpu.SMEM if a.ndim == 1 and a.dtype == jnp.int32 else pltpu.VMEM
    )
    return pl.pallas_call(
        kernel,
        out_shape=tuple(jax.ShapeDtypeStruct(s, t) for s, t in outs),
        in_specs=[spec(a) for a in args],
        out_specs=tuple(pl.BlockSpec(memory_space=pltpu.VMEM) for _ in outs),
        scratch_shapes=scratch,
        compiler_params=pltpu.CompilerParams(vmem_limit_bytes=mib << 20),
        cost_estimate=pl.CostEstimate(flops=cost, bytes_accessed=0, transcendentals=0),
    )(*args)


def input_kernel(
    place, x_zero, x_one, thoughts, thought_pos, vecs, w_in, bias,
    spliced_ref, xhat_ref, normed_ref, q_ref, k_ref, v_ref,
):
    core = place[0]
    rows = x_zero.shape[1]
    cols = q_ref.shape[1]
    gain, shift = vecs[0:1, :], vecs[1:2, :]
    for upper in range(2):
        for rel, ref in enumerate((x_zero, x_one)):
            first = upper * 2 * rows + (core ^ rel) * rows
            part = slice((2 * upper + rel) * rows, (2 * upper + rel + 1) * rows)
            match = (first + iota((rows, 1), 0)) == thought_pos[...]
            covered = jnp.sum(match.astype(F32), axis=1, keepdims=True) > 0.0
            picked = dot(match.astype(LOW), thoughts[...], 1, 0)
            spliced = jnp.where(covered, picked, ref[upper].astype(F32))
            xhat, _ = normalised(spliced)
            spliced_ref[part, :] = spliced.astype(LOW)
            xhat_ref[part, :] = xhat.astype(LOW)
            normed = (xhat * gain + shift).astype(LOW)
            normed_ref[part, :] = normed
            mixed = (dot(normed, w_in[...], 1, 0) + bias[...]).astype(LOW)
            q_ref[part, :] = mixed[:, :cols]
            k_ref[part, :] = mixed[:, cols : 2 * cols]
            v_ref[part, :] = mixed[:, 2 * cols :]


def query_limits(place, chunk, rows):
    core, start = place[0], place[1 + chunk]
    col = iota((1, 2 * rows), 1)
    query = 2 * rows * chunk + jnp.where(col < rows, col + core * rows, col - core * rows)
    inside = (query >= start) & (query < start + IMG)
    return jnp.where(inside, start + (IMG - 1), query)


def key_positions(place, block, rows):
    first = (block >> 1) * (2 * rows) + (place[0] ^ (block & 1)) * rows
    return first + iota((rows, 1), 0)


def attend_kernel(
    chunk, place, q_ref, k_ref, v_ref, w_proj,
    att_ref, log_ref, keep_ref, send_ref, acc_ref, top_ref, sum_ref,
):
    half, cols = att_ref.shape
    rows = half // 2
    heads = cols // HD
    head_of = iota((1, cols), 1) // HD
    limits = query_limits(place, chunk, rows)
    queries = q_ref[chunk * half : (chunk + 1) * half, :] * LOW(0.125)
    acc_ref[...] = jnp.zeros_like(acc_ref)
    top_ref[...] = jnp.full_like(top_ref, -1e30)
    sum_ref[...] = jnp.zeros_like(sum_ref)

    @pl.loop(0, 2 * chunk + 2)
    def _(block):
        span = pl.ds(pl.multiple_of(block * rows, rows), rows)
        keys = k_ref[span, :]
        values = v_ref[span, :].T
        allowed = key_positions(place, block, rows) <= limits
        for head in range(heads):
            scores = dot(jnp.where(head_of == head, keys, LOW(0)), queries, 1, 1)
            scores = jnp.where(allowed, scores, -1e30)
            top = top_ref[head : head + 1, :]
            new_top = jnp.maximum(top, jnp.max(scores, axis=0, keepdims=True))
            exps = jnp.exp(scores - new_top)
            fade = jnp.exp(top - new_top)
            top_ref[head : head + 1, :] = new_top
            sum_ref[head : head + 1, :] = sum_ref[head : head + 1, :] * fade + jnp.sum(
                exps, axis=0, keepdims=True
            )
            part = slice(head * HD, (head + 1) * HD)
            acc_ref[part, :] = acc_ref[part, :] * fade + dot(values[part, :], exps.astype(LOW), 1, 0)

    for head in range(heads):
        part = slice(head * HD, (head + 1) * HD)
        acc_ref[part, :] = acc_ref[part, :] / sum_ref[head : head + 1, :]
    log_ref[...] = top_ref[...] + jnp.log(jnp.maximum(sum_ref[...], 1e-30))
    attended = acc_ref[...].T.astype(LOW)
    att_ref[...] = attended
    branch = dot(attended, w_proj[...], 1, 1)
    keep_ref[...] = branch[:rows]
    send_ref[...] = branch[rows:].astype(LOW)


def attend(chunk, place, queries, keys, values, w_proj):
    length, cols = queries.shape
    half, width = length // 2, w_proj.shape[0]
    return call(
        functools.partial(attend_kernel, chunk),
        (
            ((half, cols), LOW),
            ((8, half), F32),
            ((half // 2, width), F32),
            ((half // 2, width), LOW),
        ),
        int(2e9) * (chunk + 1),
        place,
        queries,
        keys,
        values,
        w_proj,
        scratch=(
            pltpu.VMEM((cols, half), F32),
            pltpu.VMEM((8, half), F32),
            pltpu.VMEM((8, half), F32),
        ),
    )


def feed_kernel(
    chunk, spliced, total, other, cot_zero, cot_one, vecs, up_bias, w_up, w_down,
    residual_ref, normed_ref, hidden_ref, grad_ref, sum_ref, keep_ref, send_ref,
):
    half, width = residual_ref.shape
    rows = half // 2
    for rel, ref in enumerate((total, other)):
        part = slice(rel * rows, (rel + 1) * rows)
        residual = (
            spliced[chunk * half + rel * rows : chunk * half + (rel + 1) * rows, :].astype(F32)
            + ref[...].astype(F32)
            + vecs[2:3, :]
        )
        residual_ref[part, :] = residual
        xhat, _ = normalised(residual)
        normed_ref[part, :] = (xhat * vecs[3:4, :] + vecs[4:5, :]).astype(LOW)
    hidden_cols = w_up.shape[1]
    step = 256 if hidden_cols % 256 == 0 else hidden_cols
    for first in range(0, hidden_cols, step):
        cols = slice(first, first + step)
        hidden, slope = gelu_pair(dot(normed_ref[...], w_up[:, cols], 1, 0) + up_bias[:, cols])
        hidden_ref[:, cols] = hidden.astype(LOW)
        back = jnp.concatenate(
            [dot(cot_zero[chunk], w_down[:, cols], 1, 0), dot(cot_one[chunk], w_down[:, cols], 1, 0)]
        )
        grad = (back * slope).astype(LOW)
        grad_ref[:, cols] = grad
        sum_ref[:, cols] = jnp.sum(grad.astype(F32), axis=0, keepdims=True)
    back = dot(grad_ref[...], w_up[...], 1, 1)
    keep_ref[...] = back[:rows]
    send_ref[...] = back[rows:].astype(LOW)


def feed(chunk, spliced, total, other, cots, vecs, up_bias, w_up, w_down):
    length, width = spliced.shape
    half, hidden = length // 2, w_up.shape[1]
    return call(
        functools.partial(feed_kernel, chunk),
        (
            ((half, width), F32),
            ((half, width), LOW),
            ((half, hidden), LOW),
            ((half, hidden), LOW),
            ((1, hidden), F32),
            ((half // 2, width), F32),
            ((half // 2, width), LOW),
        ),
        int(4e9),
        spliced,
        total,
        other,
        *cots,
        vecs,
        up_bias,
        w_up,
        w_down,
    )


def back_kernel(
    chunk, place, total, other, residual, cot_zero, cot_one, vecs, w_proj, q_ref, k_ref, v_ref, att, log, *rest,
):
    keys_in, rest = (rest[:2], rest[2:]) if chunk else ((), rest)
    grad_res_ref, branch_ref, dq_ref, dk_ref, dv_ref, sums_ref, dqt_ref, delta_ref, gatt_ref = rest
    half, width = residual.shape
    rows = half // 2
    cols = q_ref.shape[1]
    heads = cols // HD
    gain = vecs[3:4, :]
    sums = [0.0, 0.0, 0.0]
    for rel, (ref, cot) in enumerate(((total, cot_zero), (other, cot_one))):
        part = slice(rel * rows, (rel + 1) * rows)
        upstream = ref[...].astype(F32)
        xhat, inverse = normalised(residual[part, :])
        grad_res = cot[chunk].astype(F32) + norm_back(upstream, xhat, inverse, gain)
        grad_res_ref[part, :] = grad_res
        branch_ref[part, :] = grad_res.astype(LOW)
        for k, term in enumerate((upstream * xhat, upstream, grad_res)):
            sums[k] = sums[k] + jnp.sum(term, axis=0, keepdims=True)
    for k in range(3):
        sums_ref[k : k + 1, :] = sums[k]
    grad_att = dot(branch_ref[...], w_proj[...], 1, 0).astype(LOW)
    gatt_ref[...] = grad_att
    head_of = iota((1, cols), 1) // HD
    head_rows = (iota((8, cols), 0) == iota((8, cols), 1) // HD).astype(F32)
    delta_ref[...] = dot(
        head_rows, grad_att.astype(F32) * att[...].astype(F32), 1, 1, lax.Precision.HIGHEST
    )
    limits = query_limits(place, chunk, rows)
    dqt_ref[...] = jnp.zeros_like(dqt_ref)

    @pl.loop(0, 2 * chunk + 2)
    def _(block):
        span = pl.ds(pl.multiple_of(block * rows, rows), rows)
        keys, values = k_ref[span, :], v_ref[span, :]
        keys_t = keys.T
        queries = q_ref[chunk * half : (chunk + 1) * half, :] * LOW(0.125)
        grad_att = gatt_ref[...]
        allowed = key_positions(place, block, rows) <= limits
        dk = jnp.zeros((rows, cols), F32)
        dv = jnp.zeros((rows, cols), F32)
        for head in range(heads):
            mine = head_of == head
            scores = dot(jnp.where(mine, keys, LOW(0)), queries, 1, 1)
            probs = jnp.exp(jnp.where(allowed, scores, -1e30) - log[head : head + 1, :])
            grad_probs = dot(jnp.where(mine, values, LOW(0)), grad_att, 1, 1)
            grad_scores = (probs * (grad_probs - delta_ref[head : head + 1, :])).astype(LOW)
            dv = dv + dot(probs.astype(LOW), jnp.where(mine, grad_att, LOW(0)), 1, 0)
            dk = dk + dot(grad_scores, jnp.where(mine, queries, LOW(0)), 1, 0)
            part = slice(head * HD, (head + 1) * HD)
            dqt_ref[part, :] = dqt_ref[part, :] + dot(keys_t[part, :], grad_scores, 1, 0)
        if chunk:
            seen = jnp.where(block < 2, 1.0, 0.0)
            early = pl.ds(pl.multiple_of((block & 1) * rows, rows), rows)
            dk = dk + keys_in[0][early, :] * seen
            dv = dv + keys_in[1][early, :] * seen
        dk_ref[span, :] = dk.astype(dk_ref.dtype)
        dv_ref[span, :] = dv.astype(dv_ref.dtype)

    dq_ref[...] = (dqt_ref[...] * 0.125).T.astype(LOW)


def back(chunk, place, total, other, residual, cots, vecs, w_proj, queries, keys, values, att, log, early):
    length, cols = queries.shape
    half, width = residual.shape
    kind = (((half * (chunk + 1), cols), LOW if chunk else F32),) * 2
    return call(
        functools.partial(back_kernel, chunk),
        (((half, width), F32), ((half, width), LOW), ((half, cols), LOW), *kind, ((8, width), F32)),
        int(5e9) * (chunk + 1),
        place,
        total,
        other,
        residual,
        *cots,
        vecs,
        w_proj,
        queries,
        keys,
        values,
        att,
        log,
        *early,
        scratch=(
            pltpu.VMEM((cols, half), F32),
            pltpu.VMEM((8, half), F32),
            pltpu.VMEM((half, cols), LOW),
        ),
    )


def input_back_kernel(dq_zero, dq_one, dk, dv, w_in, xhat, keep_ref, send_ref, mixed_ref, sums_ref, colsum_ref):
    half, cols = dq_zero.shape
    rows = half // 2
    sums = [0.0, 0.0, 0.0]
    for upper, dq in enumerate((dq_zero, dq_one)):
        for rel in range(2):
            part = slice((2 * upper + rel) * rows, (2 * upper + rel + 1) * rows)
            mixed = jnp.concatenate(
                [dq[rel * rows : (rel + 1) * rows, :], dk[part, :], dv[part, :]], axis=1
            )
            mixed_ref[part, :] = mixed
            grad = dot(mixed, w_in[...], 1, 1)
            if rel:
                send_ref[upper] = grad.astype(LOW)
            else:
                keep_ref[upper] = grad
            terms = (grad * xhat[part, :].astype(F32), grad, mixed.astype(F32))
            sums = [a + jnp.sum(b, axis=0, keepdims=True) for a, b in zip(sums, terms)]
    sums_ref[0:1, :] = sums[0]
    sums_ref[1:2, :] = sums[1]
    colsum_ref[...] = sums[2]


def local(
    x_embed,
    thoughts,
    thought_pos,
    img_start,
    pre_attn_gain,
    pre_attn_bias,
    w_qkv,
    b_qv,
    w_proj,
    b_proj,
    pre_mlp_gain,
    pre_mlp_bias,
    w_up,
    b_up,
    w_down,
    b_down,
    grad_out,
):
    dp = lax.axis_size("dp")
    tensor_rank = lax.axis_index("tensor")
    core = tensor_rank & 1
    first_chip = (tensor_rank >> 1) == 0
    _, rows, width = x_embed.shape
    length = 4 * rows
    half = 2 * rows
    shard_rows = w_qkv.shape[1]
    head_cols = w_qkv.shape[2]
    qkv_cols = 3 * head_cols
    hidden_cols = w_up.shape[1]
    place = jnp.concatenate([core.reshape(1).astype(jnp.int32), img_start[0]])

    vectors = (pre_attn_gain, pre_attn_bias, b_proj, pre_mlp_gain, pre_mlp_bias, b_down, b_up, b_qv.reshape(-1))
    vec_count = sum(v.shape[0] for v in vectors)
    vec_rows = -(-vec_count // (8 * qkv_cols)) * 8
    vec_pack = jnp.pad(jnp.concatenate(vectors), (0, vec_rows * qkv_cols - vec_count))
    pack_one = jnp.concatenate(
        [jnp.moveaxis(w_qkv, 0, 1).reshape(shard_rows, qkv_cols), vec_pack.reshape(vec_rows, qkv_cols)]
    )
    pack_two = jnp.concatenate([w_proj.T, w_up, w_down.T], axis=1)
    x_rows = rows_gather(x_embed[0])
    got_one = dp_gather(pack_one)
    got_two = dp_gather(pack_two)
    cots = rows_gather(grad_out[0])

    w_in = got_one[:, :shard_rows].reshape(width, qkv_cols)
    got_vec = got_one[:, shard_rows:].reshape(dp, -1)
    vecs, first = [], 0
    for v in vectors[:-1]:
        vecs.append(got_vec[:, first : first + v.shape[0]].reshape(1, -1).astype(F32))
        first += v.shape[0]
    up_bias = vecs.pop()
    qv_bias = jnp.moveaxis(got_vec[:, first:vec_count].reshape(dp, 2, -1), 0, 1).reshape(2, head_cols)
    all_bias = jnp.stack([qv_bias[0], jnp.zeros_like(qv_bias[0]), qv_bias[1]]).reshape(1, -1).astype(F32)
    vecs = jnp.concatenate(vecs)
    w_all = got_two.reshape(width, -1)
    w_proj_t = w_all[:, :head_cols]
    w_up_all = w_all[:, head_cols : head_cols + hidden_cols]
    w_down_t = w_all[:, head_cols + hidden_cols :]

    spliced, xhat_one, normed, queries, keys, values = call(
        input_kernel,
        (((length, width), LOW),) * 3 + (((length, head_cols), LOW),) * 3,
        int(1e9),
        place,
        *x_rows,
        thoughts[0],
        thought_pos,
        vecs,
        w_in,
        all_bias,
    )

    attended, logs, branches = [], [], []
    for chunk in range(2):
        att, log, keep, send = attend(chunk, place, queries, keys, values, w_proj_t)
        attended.append(att)
        logs.append(log)
        branches.append(rows_all_sum(keep, send))

    fed, grad_twos = [], []
    for chunk in range(2):
        fed.append(feed(chunk, spliced, *branches[chunk], cots, vecs, up_bias, w_up_all, w_down_t))
        grad_twos.append(rows_all_sum(*fed[chunk][5:]))
    residual, normed_two, hidden, grad_hidden, up_sums = (
        [f[k] for f in fed] for k in range(5)
    )

    cot_rows = [jnp.concatenate([c[k] for c in cots]) for k in range(2)]
    grad_up = sum(dot(n, g, 0, 0) for n, g in zip(normed_two, grad_hidden))
    grad_down_t = sum(dot(c, h, 0, 0) for c, h in zip(cot_rows, hidden))
    scattered = dp_scatter_sum(
        jnp.concatenate([grad_up, grad_down_t], axis=1).astype(LOW).reshape(dp, shard_rows, 2 * hidden_cols)
    )
    out_up, out_down = scattered[:, :hidden_cols], scattered[:, hidden_cols:].T
    mlp = [dot(h, w_down_t, 1, 1) for h in hidden]
    mlp_own = rows_scatter_sum(
        jnp.stack([m[:rows] for m in mlp]), jnp.stack([m[rows:] for m in mlp]).astype(LOW)
    )
    own = lambda a, b: jnp.where(first_chip, a[:rows], b[:rows])
    block_out = own(*residual) + mlp_own + vecs[5]

    early, backs = (), []
    for chunk in range(2):
        backs.append(
            back(
                chunk, place, *grad_twos[chunk], residual[chunk], cots, vecs, w_proj_t,
                queries, keys, values, attended[chunk], logs[chunk], early,
            )
        )
        early = backs[0][3:5]
    grad_residual, grad_branch, grad_queries = ([b[k] for b in backs] for k in range(3))
    grad_keys, grad_values = backs[1][3:5]

    keep, send, grad_mixed, one_sums, mixed_sums = call(
        input_back_kernel,
        (
            ((2, rows, width), F32),
            ((2, rows, width), LOW),
            ((length, qkv_cols), LOW),
            ((2, width), F32),
            ((1, qkv_cols), F32),
        ),
        int(2e9),
        *grad_queries,
        grad_keys,
        grad_values,
        w_in,
        xhat_one,
    )
    grad_normed = rows_scatter_sum(keep, send)
    gain_bias_one = small_all_sum(one_sums)
    grad_in = dot(normed, grad_mixed, 0, 0)
    grad_proj_t = sum(dot(g, a, 0, 0) for g, a in zip(grad_branch, attended))
    scattered = dp_scatter_sum(
        jnp.concatenate([grad_in, grad_proj_t], axis=1).astype(LOW).reshape(dp, shard_rows, qkv_cols + head_cols)
    )
    out_qkv = jnp.moveaxis(scattered[:, :qkv_cols].reshape(shard_rows, 3, head_cols), 1, 0)
    out_proj = scattered[:, qkv_cols:].T
    two_sums = backs[0][5] + backs[1][5]
    vec = jnp.concatenate(
        [
            v.reshape(dp, -1)
            for v in (
                gain_bias_one[0],
                gain_bias_one[1],
                two_sums[2],
                two_sums[0],
                two_sums[1],
                sum(jnp.sum(c.astype(F32), axis=(0, 1)) for c in cots),
                up_sums[0] + up_sums[1],
                mixed_sums[0, :head_cols],
                mixed_sums[0, 2 * head_cols :],
            )
        ],
        axis=1,
    )
    vec = dp_scatter_sum(vec[:, None, :])[0]
    small, first = [], 0
    for v in vectors:
        small.append(vec[first : first + v.shape[0]])
        first += v.shape[0]
    out_gain_one, out_bias_one, out_b_proj, out_gain_two, out_bias_two, out_b_down, out_b_up, out_qv = small

    spliced_own = own(spliced, spliced[half:]).astype(F32)
    xhat_own, inverse_own = normalised(spliced_own)
    grad_own = norm_back(grad_normed, xhat_own, inverse_own, vecs[0]) + own(*grad_residual)
    positions = tensor_rank * rows + jnp.arange(rows, dtype=jnp.int32)
    matches = positions[:, None] == thought_pos[0][None, :]
    grad_embed = jnp.where(jnp.any(matches, axis=-1, keepdims=True), 0.0, grad_own)
    thought_part = lax.dot_general(
        matches.astype(F32), grad_own, (((0,), (0,)), ((), ())), precision=lax.Precision.HIGHEST
    )
    quarter = width // 4
    halves = thought_part.reshape(-1, 2, 2 * quarter)
    keep = jnp.where(first_chip, halves[:, 0], halves[:, 1])
    send = jnp.where(first_chip, halves[:, 1], halves[:, 0])
    mine = (keep + swapped(send, "tensor", 2)).reshape(-1, 2, quarter)
    keep = jnp.where(core == 0, mine[:, 0], mine[:, 1])
    send = jnp.where(core == 0, mine[:, 1], mine[:, 0])
    grad_thoughts = keep + swapped(send, "tensor", 1)

    return (
        block_out.astype(LOW)[None],
        grad_embed[None],
        grad_thoughts[None],
        out_gain_one,
        out_bias_one,
        out_qkv,
        out_qv.reshape(2, -1),
        out_proj,
        out_b_proj,
        out_gain_two,
        out_bias_two,
        out_up,
        out_b_up,
        out_down,
        out_b_down,
    )


def solution(mesh):
    in_specs = (
        P("dp", "tensor", None),
        P("dp", None, None),
        P("dp", None),
        P("dp", None),
        P("dp"),
        P("dp"),
        P(None, "dp", "tensor"),
        P(None, ("tensor", "dp")),
        P("tensor", "dp"),
        P("dp"),
        P("dp"),
        P("dp"),
        P("dp", "tensor"),
        P(("tensor", "dp")),
        P("tensor", "dp"),
        P("dp"),
        P("dp", "tensor", None),
    )
    out_specs = (
        P("dp", "tensor", None),
        P("dp", "tensor", None),
        P("dp", None, "tensor"),
        P("dp"),
        P("dp"),
        P(None, "dp", "tensor"),
        P(None, ("tensor", "dp")),
        P("tensor", "dp"),
        P("dp"),
        P("dp"),
        P("dp"),
        P("dp", "tensor"),
        P(("tensor", "dp")),
        P("tensor", "dp"),
        P("dp"),
    )
    return jax.shard_map(local, mesh=mesh, in_specs=in_specs, out_specs=out_specs, check_vma=False)
```

```python
import functools

import jax
import jax.numpy as jnp
from jax import lax
from jax.experimental import pallas as pl
from jax.experimental.pallas import tpu as pltpu
from jax.sharding import PartitionSpec as P

HD = 64
IMG = 256
EPSILON = 1e-05
F32 = jnp.float32
LOW = jnp.bfloat16
COST = 1000


def swapped(array, axis, mask):
    return lax.ppermute(array, axis, [(i, i ^ mask) for i in range(lax.axis_size(axis))])


def dp_steps():
    size = lax.axis_size("dp")
    if size == 8:
        return ((6, 4), (2, 6), (1, 1))
    return tuple((1 << b, 1 << b) for b in reversed(range(size.bit_length() - 1)))


def parity(index, mask):
    bit = jnp.int32(0)
    for b in range(mask.bit_length()):
        if mask >> b & 1:
            bit = bit ^ ((index >> b) & 1)
    return bit


def slot_owners(steps):
    owners = [0]
    for mask, _ in steps:
        owners = owners + [o ^ mask for o in owners]
    return owners


def dp_gather(shard):
    steps, me = dp_steps(), lax.axis_index("dp")
    slots = shard[None]
    for mask, kinds in steps:
        other = swapped(slots, "dp", mask)
        first = parity(me, kinds) == 0
        slots = jnp.where(
            first, jnp.concatenate([slots, other]), jnp.concatenate([other, slots])
        )
    owners = slot_owners(steps)
    return jnp.stack([slots[owners.index(s)] for s in range(len(owners))])


MASKS = ((0,), (1,), (6,), (2, 4), (7,), (3, 5))


def rows_pick(own, other):
    first = (lax.axis_index("tensor") >> 1) == 0
    return jnp.stack([jnp.where(first, own, other), jnp.where(first, other, own)])


def dp_scatter_sum(blocks, place):
    steps, me = dp_steps(), lax.axis_index("dp")
    slots = jnp.stack([blocks[s] for s in slot_owners(steps)])
    for mask, kinds in reversed(steps):
        half = slots.shape[0] // 2
        first = parity(me, kinds) == 0
        keep = jnp.where(first, slots[:half], slots[half:])
        send = jnp.where(first, slots[half:], slots[:half])
        slots = keep.astype(F32) + swapped(send, "dp", mask).astype(F32)
    return slots[0]


def rows_gather(own):
    both = rows_pick(own, swapped(own, "tensor", 2))
    return both, swapped(both, "tensor", 1)


def after(value, *others):
    return lax.optimization_barrier((value, *others))[0]


def together(*values):
    return lax.optimization_barrier(values)


def dot(a, b, ca, cb, precision=None):
    return lax.dot_general(
        a, b, (((ca,), (cb,)), ((), ())), precision=precision, preferred_element_type=F32
    )


def normalised(values):
    centred = values - jnp.mean(values, axis=-1, keepdims=True)
    inverse = lax.rsqrt(jnp.mean(centred * centred, axis=-1, keepdims=True) + EPSILON)
    return centred * inverse, inverse


def norm_back(upstream, xhat, inverse, gain):
    scaled = upstream * gain
    return inverse * (
        scaled
        - jnp.mean(scaled, axis=-1, keepdims=True)
        - xhat * jnp.mean(scaled * xhat, axis=-1, keepdims=True)
    )


def gelu_pair(u):
    k, a = 0.7978845608028654, 0.044715
    square = u * u
    t = jnp.tanh(u * (k + (k * a) * square))
    rise = 0.5 * (1.0 + t)
    return u * rise, rise + (0.5 * u) * (1.0 - t * t) * (k + (3.0 * k * a) * square)


def cots_rows(cots, chunk):
    return jnp.concatenate([c[chunk] for c in cots])


def iota(shape, dim):
    return lax.broadcasted_iota(jnp.int32, shape, dim)


def call(kernel, outs, *args, scratch=(), mib=8, piped=False):
    if piped:
        whole = lambda shape: pl.BlockSpec(shape, lambda i: (0,) * len(shape))
        return pl.pallas_call(
            kernel,
            out_shape=tuple(jax.ShapeDtypeStruct(s, t) for s, t in outs),
            grid=(1,),
            in_specs=[whole(a.shape) for a in args],
            out_specs=tuple(pl.BlockSpec(memory_space=pltpu.VMEM) for _ in outs),
            compiler_params=pltpu.CompilerParams(vmem_limit_bytes=mib << 20),
            cost_estimate=pl.CostEstimate(flops=COST, bytes_accessed=0, transcendentals=0),
        )(*args)
    spec = lambda a: pl.BlockSpec(
        memory_space=pltpu.SMEM if a.ndim == 1 and a.dtype == jnp.int32 else pltpu.VMEM
    )
    return pl.pallas_call(
        kernel,
        out_shape=tuple(jax.ShapeDtypeStruct(s, t) for s, t in outs),
        in_specs=[spec(a) for a in args],
        out_specs=tuple(pl.BlockSpec(memory_space=pltpu.VMEM) for _ in outs),
        scratch_shapes=scratch,
        compiler_params=pltpu.CompilerParams(vmem_limit_bytes=mib << 20),
        cost_estimate=pl.CostEstimate(flops=COST, bytes_accessed=0, transcendentals=0),
    )(*args)


def input_kernel(
    place, x_zero, x_one, thoughts, thought_pos, vecs, w_in, bias,
    spliced_ref, xhat_ref, normed_ref, q_ref, k_ref, v_ref,
):
    core = place[0]
    rows = x_zero.shape[1]
    cols = q_ref.shape[1]
    gain, shift = vecs[0:1, :], vecs[1:2, :]
    for upper in range(2):
        for rel, ref in enumerate((x_zero, x_one)):
            first = upper * 2 * rows + (core ^ rel) * rows
            part = slice((2 * upper + rel) * rows, (2 * upper + rel + 1) * rows)
            match = (first + iota((rows, 1), 0)) == thought_pos[...]
            covered = jnp.sum(match.astype(F32), axis=1, keepdims=True) > 0.0
            picked = dot(match.astype(LOW), thoughts[...], 1, 0)
            spliced = jnp.where(covered, picked, ref[upper].astype(F32))
            xhat, _ = normalised(spliced)
            spliced_ref[part, :] = spliced.astype(LOW)
            xhat_ref[part, :] = xhat.astype(LOW)
            normed = (xhat * gain + shift).astype(LOW)
            normed_ref[part, :] = normed
            mixed = (dot(normed, w_in[...], 1, 0) + bias[...]).astype(LOW)
            q_ref[part, :] = mixed[:, :cols]
            k_ref[part, :] = mixed[:, cols : 2 * cols]
            v_ref[part, :] = mixed[:, 2 * cols :]


def query_limits(place, starts, chunk, rows):
    core, start = place[0], starts[chunk]
    col = iota((1, 2 * rows), 1)
    query = 2 * rows * chunk + jnp.where(col < rows, col + core * rows, col - core * rows)
    inside = (query >= start) & (query < start + IMG)
    return jnp.where(inside, start + (IMG - 1), query)


def key_positions(place, block, rows):
    first = (block >> 1) * (2 * rows) + (place[0] ^ (block & 1)) * rows
    return first + iota((rows, 1), 0)


def attend_kernel(
    chunk, place, starts, q_ref, k_ref, v_ref, w_proj,
    att_ref, log_ref, keep_ref, send_ref, acc_ref, top_ref, sum_ref,
):
    half, cols = att_ref.shape
    rows = half // 2
    heads = cols // HD
    head_of = iota((1, cols), 1) // HD
    limits = query_limits(place, starts, chunk, rows)
    queries = q_ref[chunk * half : (chunk + 1) * half, :] * LOW(0.125)
    acc_ref[...] = jnp.zeros_like(acc_ref)
    top_ref[...] = jnp.full_like(top_ref, -1e30)
    sum_ref[...] = jnp.zeros_like(sum_ref)

    @pl.loop(0, 2 * chunk + 2)
    def _(block):
        span = pl.ds(pl.multiple_of(block * rows, rows), rows)
        keys = k_ref[span, :]
        values = v_ref[span, :].T
        allowed = key_positions(place, block, rows) <= limits
        for head in range(heads):
            scores = dot(jnp.where(head_of == head, keys, LOW(0)), queries, 1, 1)
            scores = jnp.where(allowed, scores, -1e30)
            top = top_ref[head : head + 1, :]
            new_top = jnp.maximum(top, jnp.max(scores, axis=0, keepdims=True))
            exps = jnp.exp(scores - new_top)
            fade = jnp.exp(top - new_top)
            top_ref[head : head + 1, :] = new_top
            sum_ref[head : head + 1, :] = sum_ref[head : head + 1, :] * fade + jnp.sum(
                exps, axis=0, keepdims=True
            )
            part = slice(head * HD, (head + 1) * HD)
            acc_ref[part, :] = acc_ref[part, :] * fade + dot(values[part, :], exps.astype(LOW), 1, 0)

    for head in range(heads):
        part = slice(head * HD, (head + 1) * HD)
        acc_ref[part, :] = acc_ref[part, :] / sum_ref[head : head + 1, :]
    log_ref[...] = top_ref[...] + jnp.log(jnp.maximum(sum_ref[...], 1e-30))
    attended = acc_ref[...].T.astype(LOW)
    att_ref[...] = attended
    branch = dot(attended, w_proj[...], 1, 1)
    keep_ref[...] = branch[:rows]
    send_ref[...] = branch[rows:].astype(LOW)


def attend(chunk, place, starts, queries, keys, values, w_proj):
    length, cols = queries.shape
    half, width = length // 2, w_proj.shape[0]
    return call(
        functools.partial(attend_kernel, chunk),
        (
            ((half, cols), LOW),
            ((8, half), F32),
            ((half // 2, width), F32),
            ((half // 2, width), LOW),
        ),
        place,
        starts,
        queries,
        keys,
        values,
        w_proj,
        scratch=(
            pltpu.VMEM((cols, half), F32),
            pltpu.VMEM((8, half), F32),
            pltpu.VMEM((8, half), F32),
        ),
    )


def feed_kernel(
    chunk, spliced, total, other, cot_zero, cot_one, vecs, up_bias, w_up, w_down,
    residual_ref, normed_ref, hidden_ref, grad_ref, sum_ref, keep_ref, send_ref,
):
    half, width = residual_ref.shape
    rows = half // 2
    for rel, ref in enumerate((total, other)):
        part = slice(rel * rows, (rel + 1) * rows)
        residual = (
            spliced[chunk * half + rel * rows : chunk * half + (rel + 1) * rows, :].astype(F32)
            + ref[...].astype(F32)
            + vecs[2:3, :]
        )
        residual_ref[part, :] = residual
        xhat, _ = normalised(residual)
        normed_ref[part, :] = (xhat * vecs[3:4, :] + vecs[4:5, :]).astype(LOW)
    hidden_cols = w_up.shape[1]
    step = 256 if hidden_cols % 256 == 0 else hidden_cols
    for first in range(0, hidden_cols, step):
        cols = slice(first, first + step)
        hidden, slope = gelu_pair(dot(normed_ref[...], w_up[:, cols], 1, 0) + up_bias[:, cols])
        hidden_ref[:, cols] = hidden.astype(LOW)
        back = jnp.concatenate(
            [dot(cot_zero[chunk], w_down[:, cols], 1, 0), dot(cot_one[chunk], w_down[:, cols], 1, 0)]
        )
        grad = (back * slope).astype(LOW)
        grad_ref[:, cols] = grad
        sum_ref[:, cols] = jnp.sum(grad.astype(F32), axis=0, keepdims=True)
    back = dot(grad_ref[...], w_up[...], 1, 1)
    keep_ref[...] = back[:rows]
    send_ref[...] = back[rows:].astype(LOW)


def feed(chunk, spliced, total, other, cots, vecs, up_bias, w_up, w_down):
    length, width = spliced.shape
    half, hidden = length // 2, w_up.shape[1]
    return call(
        functools.partial(feed_kernel, chunk),
        (
            ((half, width), F32),
            ((half, width), LOW),
            ((half, hidden), LOW),
            ((half, hidden), LOW),
            ((1, hidden), F32),
            ((half // 2, width), F32),
            ((half // 2, width), LOW),
        ),
        spliced,
        total,
        other,
        *cots,
        vecs,
        up_bias,
        w_up,
        w_down,
    )


def back_kernel(
    chunk, place, starts, total, other, residual, cot_zero, cot_one, vecs, w_proj, q_ref, k_ref, v_ref, att, log, *rest,
):
    keys_in, rest = (rest[:2], rest[2:]) if chunk else ((), rest)
    grad_res_ref, branch_ref, dq_ref, dk_ref, dv_ref, sums_ref, dqt_ref, delta_ref, gatt_ref = rest
    half, width = residual.shape
    rows = half // 2
    cols = q_ref.shape[1]
    heads = cols // HD
    gain = vecs[3:4, :]
    sums = [0.0, 0.0, 0.0, 0.0]
    for rel, (ref, cot) in enumerate(((total, cot_zero), (other, cot_one))):
        part = slice(rel * rows, (rel + 1) * rows)
        upstream = ref[...].astype(F32)
        xhat, inverse = normalised(residual[part, :])
        out_grad = cot[chunk].astype(F32)
        grad_res = out_grad + norm_back(upstream, xhat, inverse, gain)
        grad_res_ref[part, :] = grad_res
        branch_ref[part, :] = grad_res.astype(LOW)
        for k, term in enumerate((upstream * xhat, upstream, grad_res, out_grad)):
            sums[k] = sums[k] + jnp.sum(term, axis=0, keepdims=True)
    for k in range(4):
        sums_ref[k : k + 1, :] = sums[k]
    grad_att = dot(branch_ref[...], w_proj[...], 1, 0).astype(LOW)
    gatt_ref[...] = grad_att
    head_of = iota((1, cols), 1) // HD
    head_rows = (iota((8, cols), 0) == iota((8, cols), 1) // HD).astype(F32)
    delta_ref[...] = dot(
        head_rows, grad_att.astype(F32) * att[...].astype(F32), 1, 1, lax.Precision.HIGHEST
    )
    limits = query_limits(place, starts, chunk, rows)
    dqt_ref[...] = jnp.zeros_like(dqt_ref)

    @pl.loop(0, 2 * chunk + 2)
    def _(block):
        span = pl.ds(pl.multiple_of(block * rows, rows), rows)
        keys, values = k_ref[span, :], v_ref[span, :]
        keys_t = keys.T
        queries = q_ref[chunk * half : (chunk + 1) * half, :] * LOW(0.125)
        grad_att = gatt_ref[...]
        allowed = key_positions(place, block, rows) <= limits
        dk = jnp.zeros((rows, cols), F32)
        dv = jnp.zeros((rows, cols), F32)
        for head in range(heads):
            mine = head_of == head
            scores = dot(jnp.where(mine, keys, LOW(0)), queries, 1, 1)
            probs = jnp.exp(jnp.where(allowed, scores, -1e30) - log[head : head + 1, :])
            grad_probs = dot(jnp.where(mine, values, LOW(0)), grad_att, 1, 1)
            grad_scores = (probs * (grad_probs - delta_ref[head : head + 1, :])).astype(LOW)
            dv = dv + dot(probs.astype(LOW), jnp.where(mine, grad_att, LOW(0)), 1, 0)
            dk = dk + dot(grad_scores, jnp.where(mine, queries, LOW(0)), 1, 0)
            part = slice(head * HD, (head + 1) * HD)
            dqt_ref[part, :] = dqt_ref[part, :] + dot(keys_t[part, :], grad_scores, 1, 0)
        if chunk:
            seen = jnp.where(block < 2, 1.0, 0.0)
            early = pl.ds(pl.multiple_of((block & 1) * rows, rows), rows)
            dk = dk + keys_in[0][early, :] * seen
            dv = dv + keys_in[1][early, :] * seen
        dk_ref[span, :] = dk.astype(dk_ref.dtype)
        dv_ref[span, :] = dv.astype(dv_ref.dtype)

    dq_ref[...] = (dqt_ref[...] * 0.125).T.astype(LOW)


def back(chunk, place, starts, total, other, residual, cots, vecs, w_proj, queries, keys, values, att, log, early):
    length, cols = queries.shape
    half, width = residual.shape
    kind = (((half * (chunk + 1), cols), LOW if chunk else F32),) * 2
    return call(
        functools.partial(back_kernel, chunk),
        (((half, width), F32), ((half, width), LOW), ((half, cols), LOW), *kind, ((8, width), F32)),
        place,
        starts,
        total,
        other,
        residual,
        *cots,
        vecs,
        w_proj,
        queries,
        keys,
        values,
        att,
        log,
        *early,
        scratch=(
            pltpu.VMEM((cols, half), F32),
            pltpu.VMEM((8, half), F32),
            pltpu.VMEM((half, cols), LOW),
        ),
    )


def input_back_kernel(
    place, thought_pos, dq_zero, dq_one, dk, dv, w_in, xhat, res_zero, res_one,
    keep_ref, send_ref, mixed_ref, small_ref, colsum_ref, picked_ref, grad_ref,
):
    half, cols = dq_zero.shape
    rows = half // 2
    sums = [0.0, 0.0, 0.0]
    for upper, dq in enumerate((dq_zero, dq_one)):
        for rel in range(2):
            part = slice((2 * upper + rel) * rows, (2 * upper + rel + 1) * rows)
            mixed = jnp.concatenate(
                [dq[rel * rows : (rel + 1) * rows, :], dk[part, :], dv[part, :]], axis=1
            )
            mixed_ref[part, :] = mixed
            grad = dot(mixed, w_in[...], 1, 1)
            grad_ref[part, :] = grad
            if rel:
                send_ref[upper] = grad.astype(LOW)
            else:
                keep_ref[upper] = grad
            terms = (grad * xhat[part, :].astype(F32), grad, mixed.astype(F32))
            sums = [a + jnp.sum(b, axis=0, keepdims=True) for a, b in zip(sums, terms)]
    small_ref[...] = jnp.zeros_like(small_ref)
    picked_ref[...] = jnp.zeros_like(picked_ref)
    count = thought_pos.shape[0]
    for k in range(count):
        at = thought_pos[k]
        row = (at // half) * half + (((at // rows) & 1) ^ place[0]) * rows + at % rows
        small_ref[k : k + 1, :] = grad_ref[pl.ds(row, 1), :]
        low = res_zero[pl.ds(jnp.minimum(row, half - 1), 1), :]
        high = res_one[pl.ds(jnp.maximum(row - half, 0), 1), :]
        picked_ref[k : k + 1, :] = jnp.where(row < half, low, high)
    small_ref[count : count + 1, :] = sums[0]
    small_ref[count + 1 : count + 2, :] = sums[1]
    colsum_ref[...] = sums[2]


def output_kernel(place, keep, got, spliced, res_zero, res_one, vecs, thought_pos, thoughts, small, picked, embed_ref, rows_ref):
    rows = keep.shape[0]
    gain = vecs[0:1, :]
    own = pl.ds(pl.multiple_of(place[3] * (2 * rows), 2 * rows), rows)
    xhat, inverse = normalised(spliced[own, :].astype(F32))
    residual = jnp.where(place[3] == 0, res_zero[:rows, :], res_one[:rows, :])
    grad = norm_back(keep[...] + got[...].astype(F32), xhat, inverse, gain) + residual
    at = (2 * place[3] + place[0]) * rows + iota((rows, 1), 0)
    covered = jnp.sum((at == thought_pos[...]).astype(F32), axis=1, keepdims=True) > 0.0
    embed_ref[...] = jnp.where(covered, 0.0, grad)
    count = thoughts.shape[0]
    xhat, inverse = normalised(thoughts[...].astype(F32))
    grad = norm_back(small[:count, :], xhat, inverse, gain) + picked[:count, :]
    cols = rows_ref.shape[1]
    rank = 2 * place[3] + place[0]
    rows_ref[...] = sum(
        jnp.where(rank == k, 1.0, 0.0) * grad[:, k * cols : (k + 1) * cols] for k in range(4)
    )


def fold_kernel(bit, place, keep, got, keep_ref, send_ref):
    half = keep_ref.shape[0]
    mine = place[bit] * half
    rest = half - mine
    for k in range(half):
        keep_ref[k] = keep[mine + k] + got[mine + k].astype(F32)
        send_ref[k] = (keep[rest + k] + got[rest + k].astype(F32)).astype(LOW)


def fold(bit, place, keep, got):
    shape = (keep.shape[0] // 2, *keep.shape[1:])
    return call(functools.partial(fold_kernel, bit), ((shape, F32), (shape, LOW)), place, keep, got)


def add_kernel(a, b, out):
    out[...] = (a[...].astype(F32) + b[...].astype(F32)).astype(LOW)


def add_full_kernel(a, b, out):
    out[...] = a[...] + b[...]


def add_full(a, b):
    return call(add_full_kernel, ((a.shape, F32),), a, b)[0]


def add_low(a, b):
    return call(add_kernel, ((a.shape, LOW),), a, b)[0]


def to_slots(place, sum_ref, keep_ref, send_ref, rows):
    for slot, owner in enumerate((0, 6, 2, 4)):
        mine = pl.multiple_of((owner ^ place[7]) * rows, rows)
        rest = pl.multiple_of((owner ^ 1 ^ place[7]) * rows, rows)
        keep_ref[slot, :rows, :] = sum_ref[pl.ds(mine, rows), :]
        send_ref[slot, :rows, :] = sum_ref[pl.ds(rest, rows), :].astype(LOW)


def product(left, right):
    return sum(dot(a[...], b[...], 0, 0) for a, b in zip(left, right))


def grad_kernel(place, *refs):
    *sides, keep_ref, send_ref, sum_ref = refs
    half = len(sides) // 2
    sum_ref[...] = product(sides[:half], sides[half:])
    to_slots(place, sum_ref, keep_ref, send_ref, keep_ref.shape[1])


def cot_grad_kernel(place, cot_zero, cot_one, hidden_zero, hidden_one, keep_ref, send_ref, sum_ref):
    rows = cot_zero.shape[1]
    left = [c[upper] for upper in range(2) for c in (cot_zero, cot_one)]
    right = [h[k * rows : (k + 1) * rows, :] for h in (hidden_zero, hidden_one) for k in range(2)]
    sum_ref[...] = sum(dot(a, b, 0, 0) for a, b in zip(left, right))
    to_slots(place, sum_ref, keep_ref, send_ref, keep_ref.shape[1])


def last_kernel(normed, mixed, branch_zero, branch_one, att_zero, att_one, out_ref):
    cols = mixed.shape[1]
    out_ref[:, :cols] = dot(normed[...], mixed[...], 0, 0)
    out_ref[:, cols:] = product((branch_zero, branch_one), (att_zero, att_one))


def slot_kernel(place, sums, small, back_zero, back_one, up_zero, up_one, mixed_sums, keep_ref, send_ref, flat_ref):
    rows = keep_ref.shape[1] - 8
    to_slots(place, sums, keep_ref, send_ref, rows)
    cols = (mixed_sums.shape[1]) // 3
    count = small.shape[0] - 2
    back = back_zero[...] + back_one[...]
    wide = [small[count : count + 1, :], small[count + 1 :, :], back[2:3], back[0:1], back[1:2], back[3:4]]
    wide += [up_zero[...] + up_one[...], mixed_sums[:, :cols], mixed_sums[:, 2 * cols :]]
    for owner in range(8):
        parts = []
        for v in wide:
            n = v.shape[1] // 8
            parts.append(v[:, owner * n : (owner + 1) * n])
        parts.append(jnp.zeros((1, keep_ref.shape[2] - sum(p.shape[1] for p in parts)), F32))
        flat_ref[owner : owner + 1, :] = jnp.concatenate(parts, axis=1)
    for slot, owner in enumerate((0, 6, 2, 4)):
        space = (8, keep_ref.shape[2])
        keep_ref[slot, rows:, :] = jnp.broadcast_to(flat_ref[pl.ds(owner ^ place[7], 1), :], space)
        send_ref[slot, rows:, :] = jnp.broadcast_to(flat_ref[pl.ds(owner ^ 1 ^ place[7], 1), :], space).astype(LOW)


def finish_kernel(keep, got, in_ref, proj_ref, flat_ref):
    rows, cols = in_ref.shape[1:]
    total = keep[0] + got[0].astype(F32)
    for k in range(3):
        in_ref[k] = total[:rows, k * cols : (k + 1) * cols]
    proj_ref[...] = total[:rows, 3 * cols :].T
    flat_ref[...] = total[rows : rows + 1, :]


def pair_kernel(up_keep, up_got, down_keep, down_got, up_ref, down_ref):
    up_ref[...] = up_keep[0] + up_got[0].astype(F32)
    down_ref[...] = (down_keep[0] + down_got[0].astype(F32)).T


def result_kernel(place, keep, got, res_zero, res_one, vecs, out_ref):
    rows = out_ref.shape[0]
    residual = jnp.where(place[3] == 0, res_zero[:rows, :], res_one[:rows, :])
    out_ref[...] = (residual + (keep[...] + got[...].astype(F32)) + vecs[5:6, :]).astype(LOW)


def pick_kernel(place, own, other, out_ref):
    out_ref[place[3]] = own[...]
    out_ref[1 - place[3]] = other[...]


def pick(place, own, other):
    return call(pick_kernel, (((2, *own.shape), own.dtype),), place, own, other)[0]


def stack_kernel(a, b, out_ref):
    out_ref[0] = a[...]
    out_ref[1] = b[...]


def stacked(a, b):
    return call(stack_kernel, (((2, *a.shape), a.dtype),), a, b)[0]


def grad_blocks(kernel, place, shard_rows, *sides):
    width, cols = 8 * shard_rows, sides[-1].shape[1]
    shape = (4, shard_rows, cols)
    scratch = (pltpu.VMEM((width, cols), F32),)
    return call(kernel, ((shape, F32), (shape, LOW)), place, *sides, scratch=scratch, mib=12)


def plain_grad(shard_rows, *sides):
    half = len(sides) // 2
    total = sum(dot(a, b, 0, 0) for a, b in zip(sides[:half], sides[half:])).astype(LOW)
    return dp_scatter_sum(total.reshape(-1, shard_rows, total.shape[1]), None)


def fast(shard_rows):
    return lax.axis_size("dp") == 8 and shard_rows % 16 == 0


def place_pieces(masks, place, pieces, write):
    for piece, owners in zip(pieces, masks):
        for k, mask in enumerate(owners):
            write(place[4] ^ mask, piece, k)


def first_kernel(masks, spans, hidden_cols, place, *refs):
    pieces, (w_in_ref, w_proj_ref, vecs_ref, up_ref, bias_ref, flat_ref) = refs[: len(masks)], refs[len(masks) :]
    width, qkv_cols = w_in_ref.shape
    shard_rows = width // 8

    def write(owner, piece, k):
        at = pl.ds(pl.multiple_of(owner * shard_rows, shard_rows), shard_rows)
        w_in_ref[at, :] = piece[k, :shard_rows, :qkv_cols]
        w_proj_ref[at, :] = piece[k, :shard_rows, qkv_cols:]
        flat_ref[pl.ds(owner, 1), :] = piece[k, shard_rows : shard_rows + 1, :].astype(F32)

    place_pieces(masks, place, pieces, write)
    flat = flat_ref[...]
    joined = [
        jnp.concatenate([flat[s : s + 1, a:b] for s in range(8)], axis=1) for a, b in zip(spans, spans[1:])
    ]
    for k in range(6):
        vecs_ref[k : k + 1, :] = joined[k]
    up_ref[...] = joined[6]
    bias_ref[...] = jnp.concatenate([joined[7], jnp.zeros_like(joined[7]), joined[8]], axis=1)


def plain_kernel(masks, place, *refs):
    out_ref = refs[-1]
    rows = out_ref.shape[0] // 8

    def write(owner, piece, k):
        out_ref[pl.ds(pl.multiple_of(owner * rows, rows), rows), :] = piece[k]

    place_pieces(masks, place, refs[:-1], write)


def pack_kernel(w_qkv, w_proj, w_down, *refs):
    *vectors, first_ref, down_ref = refs
    rows = w_qkv.shape[1]
    parts = [w_qkv[0], w_qkv[1], w_qkv[2], w_proj[...].T]
    first_ref[:rows, :] = jnp.concatenate(parts, axis=1)
    rows_of = [v[...].astype(F32) for v in vectors]
    rows_of = rows_of[:-1] + [rows_of[-1][0:1], rows_of[-1][1:2]]
    flat = jnp.concatenate(rows_of, axis=1)
    flat = jnp.concatenate([flat, jnp.zeros((1, first_ref.shape[1] - flat.shape[1]), F32)], axis=1)
    first_ref[rows:, :] = jnp.broadcast_to(flat, (8, flat.shape[1])).astype(LOW)
    down_ref[...] = w_down[...].T


def spans_of(vectors):
    spans = [0]
    for n in (*(v.shape[1] for v in vectors), vectors[-1].shape[1]):
        spans.append(spans[-1] + n)
    return spans


def first_unpacked(place, pieces, vectors, qkv_cols, head_cols, width):
    shapes = (
        ((width, qkv_cols), LOW),
        ((width, head_cols), LOW),
        ((6, width), F32),
        ((1, 8 * vectors[6].shape[1]), F32),
        ((1, qkv_cols), F32),
    )
    return call(
        functools.partial(first_kernel, MASKS, spans_of(vectors), 0),
        shapes,
        place,
        *pieces,
        scratch=(pltpu.VMEM((8, qkv_cols + head_cols), F32),),
    )


def unpacked(place, pieces):
    rows, cols = pieces[0].shape[1:]
    return call(functools.partial(plain_kernel, MASKS), (((8 * rows, cols), LOW),), place, *pieces)[0]


def plain_first(shard, vectors, qkv_cols, width):
    flat = dp_gather(jnp.concatenate([*vectors[:-1], vectors[-1][0:1], vectors[-1][1:2]], axis=1))[:, 0].astype(F32)
    whole = dp_gather(shard).reshape(width, -1)
    spans = spans_of(vectors)
    joined = [flat[:, a:b].reshape(1, -1) for a, b in zip(spans, spans[1:])]
    return (
        whole[:, :qkv_cols],
        whole[:, qkv_cols:],
        jnp.concatenate(joined[:6]),
        joined[6],
        jnp.concatenate([joined[7], jnp.zeros_like(joined[7]), joined[8]], axis=1),
    )


def down_kernel(hidden_zero, hidden_one, w_down, keep_ref, send_ref):
    rows = keep_ref.shape[1]
    for upper, hidden in enumerate((hidden_zero, hidden_one)):
        part = dot(hidden[...], w_down[...], 1, 1)
        keep_ref[upper] = part[:rows]
        send_ref[upper] = part[rows:].astype(LOW)


def local(
    x_embed,
    thoughts,
    thought_pos,
    img_start,
    pre_attn_gain,
    pre_attn_bias,
    w_qkv,
    b_qv,
    w_proj,
    b_proj,
    pre_mlp_gain,
    pre_mlp_bias,
    w_up,
    b_up,
    w_down,
    b_down,
    grad_out,
):
    dp = lax.axis_size("dp")
    tensor_rank = lax.axis_index("tensor")
    dp_rank = lax.axis_index("dp")
    _, rows, width = x_embed.shape
    length, half = 4 * rows, 2 * rows
    shard_rows = w_qkv.shape[1]
    head_cols = w_qkv.shape[2]
    qkv_cols = 3 * head_cols
    hidden_cols = w_up.shape[1]
    table = []
    for d in range(dp):
        for t in range(4):
            table.append((t & 1, 0, 0, t >> 1, d, (d >> 1 ^ d >> 2) & 1, d >> 2 & 1, d & 1))
    place = jnp.asarray(table, jnp.int32)[dp_rank * 4 + tensor_rank]
    starts = img_start[0]

    flat = [v.reshape(1, -1) for v in (pre_attn_gain, pre_attn_bias, b_proj, pre_mlp_gain, pre_mlp_bias, b_down, b_up)]
    flat.append(b_qv)
    sizes = (qkv_cols, head_cols, width)
    quick = fast(shard_rows)

    if quick:
        pack_one, pack_three = call(
            pack_kernel,
            (((shard_rows + 8, qkv_cols + head_cols), LOW), ((shard_rows, hidden_cols), LOW)),
            w_qkv,
            w_proj,
            w_down,
            *flat,
            piped=True,
        )
        x_far = swapped(x_embed[0], "tensor", 2)
        far_one = swapped(pack_one, "dp", 6)
        across_one = swapped(pack_one, "dp", 1)
        across_two = swapped(w_up, "dp", 1)
        x_far, far_one, across_one, across_two = together(x_far, far_one, across_one, across_two)

        x_both = pick(place, x_embed[0], x_far)
        cot_far = swapped(after(grad_out[0], x_far), "tensor", 2)
        near_one = swapped(stacked(pack_one, far_one), "dp", 2)
        far_across_one = swapped(far_one, "dp", 1)
        across_three = swapped(after(pack_three, across_two), "dp", 1)
        x_other = swapped(x_both, "tensor", 1)
        near_one, far_across_one, across_three, x_other, cot_far = together(
            near_one, far_across_one, across_three, x_other, cot_far
        )

        near_across_one = swapped(near_one, "dp", 1)
        far_two = swapped(after(w_up, near_one), "dp", 6)
        cot_both = pick(place, grad_out[0], cot_far)
        cot_other = swapped(cot_both, "tensor", 1)
        near_across_one, far_two, cot_other = together(near_across_one, far_two, cot_other)

        pieces = (pack_one[None], across_one[None], far_one[None], near_one, far_across_one[None], near_across_one)
        w_in, w_proj_t, vecs, up_bias, all_bias = first_unpacked(place, pieces, flat, *sizes)
        near_two = swapped(stacked(w_up, far_two), "dp", 2)
        far_across_two = swapped(far_two, "dp", 1)
        x_rows, cots = (x_both, x_other), (cot_both, cot_other)
    else:
        x_rows, cots = rows_gather(x_embed[0]), rows_gather(grad_out[0])
        first_pack = jnp.concatenate([w_qkv[0], w_qkv[1], w_qkv[2], w_proj.T], axis=1)
        w_in, w_proj_t, vecs, up_bias, all_bias = plain_first(first_pack, flat, qkv_cols, width)
        w_up_all = dp_gather(w_up).reshape(width, hidden_cols)
        w_down_t = dp_gather(w_down.T).reshape(width, hidden_cols)

    spliced, xhat_one, normed, queries, keys, values = call(
        input_kernel,
        (((length, width), LOW),) * 3 + (((length, head_cols), LOW),) * 3,
        place,
        *x_rows,
        thoughts[0],
        thought_pos,
        vecs,
        w_in,
        all_bias,
    )

    def core_sum(keep, send):
        return add_low(keep, swapped(send, "tensor", 1))

    att_zero, log_zero, *part = attend(0, place, starts, queries, keys, values, w_proj_t)
    if quick:
        near_two, far_across_two, part[1] = together(near_two, far_across_two, part[1])
    branch_zero = core_sum(*part)
    far_zero = swapped(branch_zero, "tensor", 2)
    if quick:
        near_across_two = swapped(near_two, "dp", 1)
        far_three = swapped(after(pack_three, near_two), "dp", 6)
    att_one, log_one, *part = attend(1, after(place, branch_zero), starts, queries, keys, values, w_proj_t)
    if quick:
        near_across_two, far_three, part[1] = together(near_across_two, far_three, part[1])
        near_three = swapped(stacked(pack_three, far_three), "dp", 2)
        far_across_three = swapped(far_three, "dp", 1)
    branch_one = core_sum(*part)
    far_zero, branch_one = together(far_zero, branch_one)
    far_one = swapped(branch_one, "tensor", 2)
    total_zero = add_low(branch_zero, far_zero)
    other_zero = swapped(total_zero, "tensor", 1)
    if quick:
        pieces = (w_up[None], across_two[None], far_two[None], near_two, far_across_two[None], near_across_two)
        w_up_all = unpacked(after(place, other_zero), pieces)
        near_three, far_across_three, w_up_all = together(near_three, far_across_three, w_up_all)
        near_across_three = swapped(near_three, "dp", 1)
        pieces = (pack_three[None], across_three[None], far_three[None], near_three, far_across_three[None], near_across_three)
        w_down_t = unpacked(place, pieces)
    total_one = add_low(branch_one, far_one)
    other_one = swapped(total_one, "tensor", 1)
    attended, logs = (att_zero, att_one), (log_zero, log_one)

    weights = (vecs, up_bias, w_up_all, w_down_t)
    fed_zero = feed(0, spliced, total_zero, other_zero, cots, *weights)
    grad_zero = core_sum(*fed_zero[5:])
    far_zero = swapped(grad_zero, "tensor", 2)
    fed_one = feed(1, after(spliced, grad_zero), total_one, other_one, cots, *weights)
    grad_one = core_sum(*fed_one[5:])
    residual, normed_two, hidden, grad_hidden, up_sums = zip(fed_zero[:5], fed_one[:5])
    ups = (*normed_two, *grad_hidden)
    if quick:
        up_keep, up_send = grad_blocks(grad_kernel, after(place, grad_one), shard_rows, *ups)
        up_got = swapped(up_send, "dp", 1)
        down_keep, down_send = grad_blocks(cot_grad_kernel, after(place, up_keep), shard_rows, *cots, *hidden)
        far_zero, down_send = together(far_zero, down_send)
    else:
        downs = (cots_rows(cots, 0), cots_rows(cots, 1), *hidden)
        out_up, out_down = plain_grad(shard_rows, *ups), plain_grad(shard_rows, *downs)
    far_one = swapped(after(grad_one, far_zero), "tensor", 2)
    total_zero = add_low(grad_zero, far_zero)
    other_zero = swapped(total_zero, "tensor", 1)
    mlp_keep, mlp_send = call(
        down_kernel,
        (((2, rows, width), F32), ((2, rows, width), LOW)),
        after(hidden[0], total_zero),
        hidden[1],
        w_down_t,
    )
    mlp_got = swapped(mlp_send, "tensor", 1)

    back_zero = back(
        0, after(place, mlp_keep), starts, total_zero, other_zero, residual[0], cots, vecs, w_proj_t,
        queries, keys, values, attended[0], logs[0], (),
    )
    if quick:
        up_got, far_one, back_dk = together(up_got, far_one, back_zero[3])
        back_zero = (*back_zero[:3], back_dk, *back_zero[4:])
        up_keep, up_send = fold(5, place, up_keep, up_got)
        up_got = swapped(up_send, "dp", 2)
        down_got = swapped(after(down_send, up_got), "dp", 1)
    total_one = add_low(grad_one, far_one)
    other_one = swapped(total_one, "tensor", 1)
    mlp_keep, mlp_send = fold(3, place, mlp_keep, mlp_got)
    mlp_got = swapped(after(mlp_send, far_one), "tensor", 2)
    back_one = back(
        1, after(place, mlp_keep), starts, total_one, other_one, residual[1], cots, vecs, w_proj_t,
        queries, keys, values, attended[1], logs[1], back_zero[3:5],
    )
    grad_residual, grad_branch, grad_queries = zip(back_zero[:3], back_one[:3])
    grad_keys, grad_values = back_one[3:5]
    if quick:
        grad_keys, mlp_got, up_got = together(grad_keys, mlp_got, up_got)
        up_keep, up_send = fold(6, place, up_keep, up_got)
        up_got = swapped(up_send, "dp", 6)

    count = thoughts.shape[1]
    keep, send, grad_mixed, small, mixed_sums, picked = call(
        input_back_kernel,
        (
            ((2, rows, width), F32),
            ((2, rows, width), LOW),
            ((length, qkv_cols), LOW),
            ((-(-(count + 2) // 8) * 8, width), F32),
            ((1, qkv_cols), F32),
            ((-(-count // 8) * 8, width), F32),
        ),
        place,
        thought_pos[0],
        *grad_queries,
        grad_keys,
        grad_values,
        w_in,
        xhat_one,
        *grad_residual,
        scratch=(pltpu.VMEM((length, width), F32),),
    )
    got = swapped(send, "tensor", 1)
    small_got = swapped(small, "tensor", 1)
    lasts = (normed, grad_mixed, *grad_branch, *attended)
    if quick:
        got, small_got = together(got, small_got)
    keep, send = fold(3, place, keep, got)
    got = swapped(send, "tensor", 2)
    small = add_full(small, small_got)
    small_got = swapped(small, "tensor", 2)
    if quick:
        last = call(last_kernel, (((width, qkv_cols + head_cols), F32),), after(normed, send, small), *lasts[1:])[0]
        last, small_got = together(last, small_got)
    small = add_full(small, small_got)
    rest = (small, back_zero[5], back_one[5], *up_sums, mixed_sums)
    if quick:
        shape = (4, shard_rows + 8, qkv_cols + head_cols)
        scratch = (pltpu.VMEM((8, qkv_cols + head_cols), F32),)
        last_keep, last_send = call(slot_kernel, ((shape, F32), (shape, LOW)), place, last, *rest, scratch=scratch)
        last_got = swapped(last_send, "dp", 1)
        down_keep, down_send = fold(5, place, down_keep, after(down_got, last_send))
        down_got = swapped(down_send, "dp", 2)
        last_got, up_got = together(last_got, up_got)
        last_keep, last_send = fold(5, place, last_keep, last_got)
        last_got = swapped(last_send, "dp", 2)
        down_keep, down_send = fold(6, place, down_keep, down_got)
        down_got = swapped(down_send, "dp", 6)
    mlp = (mlp_keep[0], mlp_got[0], *residual, vecs)
    block_out = call(result_kernel, (((rows, width), LOW),), place, *mlp)[0]
    grad_embed, grad_thoughts = call(
        output_kernel,
        (((rows, width), F32), ((count, width // 4), F32)),
        place,
        keep[0],
        got[0],
        spliced,
        *grad_residual,
        vecs,
        thought_pos,
        thoughts[0],
        small,
        picked,
    )
    if quick:
        last_keep, last_send = fold(6, place, last_keep, last_got)
        last_got = swapped(last_send, "dp", 6)
        out_up, out_down = call(
            pair_kernel,
            (((shard_rows, hidden_cols), F32), ((hidden_cols, shard_rows), F32)),
            up_keep,
            up_got,
            down_keep,
            down_got,
        )
        out_in, out_proj, vec = call(
            finish_kernel,
            (((3, shard_rows, head_cols), F32), ((head_cols, shard_rows), F32), ((1, qkv_cols + head_cols), F32)),
            last_keep,
            last_got,
        )
        vec = vec[0]
    else:
        out_in = plain_grad(shard_rows, *lasts[:2])
        out_in = jnp.moveaxis(out_in.reshape(shard_rows, 3, head_cols), 1, 0)
        out_proj = plain_grad(shard_rows, *lasts[2:]).T
        out_down = out_down.T
        two = back_zero[5] + back_one[5]
        vec = (small[count], small[count + 1], two[2], two[0], two[1], two[3], up_sums[0] + up_sums[1])
        vec += (mixed_sums[0, :head_cols], mixed_sums[0, 2 * head_cols :])
        vec = jnp.concatenate([v.reshape(dp, -1) for v in vec], axis=1)
        vec = dp_scatter_sum(vec[:, None, :], None)[0]
    outs, first = [], 0
    for n in (*(v.shape[1] for v in flat[:7]), b_qv.size):
        outs.append(vec[first : first + n])
        first += n
    out_gain_one, out_bias_one, out_b_proj, out_gain_two, out_bias_two, out_b_down, out_b_up, out_qv = outs

    return (
        block_out[None],
        grad_embed[None],
        grad_thoughts[None],
        out_gain_one,
        out_bias_one,
        out_in,
        out_qv.reshape(2, -1),
        out_proj,
        out_b_proj,
        out_gain_two,
        out_bias_two,
        out_up,
        out_b_up,
        out_down,
        out_b_down,
    )


def solution(mesh):
    in_specs = (
        P("dp", "tensor", None),
        P("dp", None, None),
        P("dp", None),
        P("dp", None),
        P("dp"),
        P("dp"),
        P(None, "dp", "tensor"),
        P(None, ("tensor", "dp")),
        P("tensor", "dp"),
        P("dp"),
        P("dp"),
        P("dp"),
        P("dp", "tensor"),
        P(("tensor", "dp")),
        P("tensor", "dp"),
        P("dp"),
        P("dp", "tensor", None),
    )
    out_specs = (
        P("dp", "tensor", None),
        P("dp", "tensor", None),
        P("dp", None, "tensor"),
        P("dp"),
        P("dp"),
        P(None, "dp", "tensor"),
        P(None, ("tensor", "dp")),
        P("tensor", "dp"),
        P("dp"),
        P("dp"),
        P("dp"),
        P("dp", "tensor"),
        P(("tensor", "dp")),
        P("tensor", "dp"),
        P("dp"),
    )
    return jax.shard_map(local, mesh=mesh, in_specs=in_specs, out_specs=out_specs, check_vma=False)
```

```python
import functools

import jax
import jax.numpy as jnp
from jax import lax
from jax.experimental import pallas as pl
from jax.experimental.pallas import tpu as pltpu
from jax.sharding import PartitionSpec as P

HD = 64
IMG = 256
EPSILON = 1e-05
F32 = jnp.float32
LOW = jnp.bfloat16
COST = 1000


def swapped(array, axis, mask):
    return lax.ppermute(array, axis, [(i, i ^ mask) for i in range(lax.axis_size(axis))])


def dp_steps():
    size = lax.axis_size("dp")
    if size == 8:
        return ((6, 4), (2, 6), (1, 1))
    return tuple((1 << b, 1 << b) for b in reversed(range(size.bit_length() - 1)))


def parity(index, mask):
    bit = jnp.int32(0)
    for b in range(mask.bit_length()):
        if mask >> b & 1:
            bit = bit ^ ((index >> b) & 1)
    return bit


def slot_owners(steps):
    owners = [0]
    for mask, _ in steps:
        owners = owners + [o ^ mask for o in owners]
    return owners


def dp_gather(shard):
    steps, me = dp_steps(), lax.axis_index("dp")
    slots = shard[None]
    for mask, kinds in steps:
        other = swapped(slots, "dp", mask)
        first = parity(me, kinds) == 0
        slots = jnp.where(
            first, jnp.concatenate([slots, other]), jnp.concatenate([other, slots])
        )
    owners = slot_owners(steps)
    return jnp.stack([slots[owners.index(s)] for s in range(len(owners))])


MASKS = ((0,), (1,), (6,), (2, 4), (7,), (3, 5))


def rows_pick(own, other):
    first = (lax.axis_index("tensor") >> 1) == 0
    return jnp.stack([jnp.where(first, own, other), jnp.where(first, other, own)])


def dp_scatter_sum(blocks):
    steps, me = dp_steps(), lax.axis_index("dp")
    slots = jnp.stack([blocks[s] for s in slot_owners(steps)])
    for mask, kinds in reversed(steps):
        half = slots.shape[0] // 2
        first = parity(me, kinds) == 0
        keep = jnp.where(first, slots[:half], slots[half:])
        send = jnp.where(first, slots[half:], slots[:half])
        slots = keep.astype(F32) + swapped(send, "dp", mask).astype(F32)
    return slots[0]


def rows_gather(own):
    both = rows_pick(own, swapped(own, "tensor", 2))
    return both, swapped(both, "tensor", 1)


def after(value, *others):
    return lax.optimization_barrier((value, *others))[0]


def together(*values):
    return lax.optimization_barrier(values)


def dot(a, b, ca, cb, precision=None):
    return lax.dot_general(
        a, b, (((ca,), (cb,)), ((), ())), precision=precision, preferred_element_type=F32
    )


def normalised(values):
    centred = values - jnp.mean(values, axis=-1, keepdims=True)
    inverse = lax.rsqrt(jnp.mean(centred * centred, axis=-1, keepdims=True) + EPSILON)
    return centred * inverse, inverse


def norm_back(upstream, xhat, inverse, gain):
    scaled = upstream * gain
    return inverse * (
        scaled
        - jnp.mean(scaled, axis=-1, keepdims=True)
        - xhat * jnp.mean(scaled * xhat, axis=-1, keepdims=True)
    )


def gelu_pair(u):
    k, a = 0.7978845608028654, 0.044715
    square = u * u
    t = jnp.tanh(u * (k + (k * a) * square))
    rise = 0.5 * (1.0 + t)
    return u * rise, rise + (0.5 * u) * (1.0 - t * t) * (k + (3.0 * k * a) * square)


def cots_rows(cots, chunk):
    return jnp.concatenate([c[chunk] for c in cots])


def iota(shape, dim):
    return lax.broadcasted_iota(jnp.int32, shape, dim)


def call(kernel, outs, *args, scratch=(), mib=8):
    spec = lambda a: pl.BlockSpec(
        memory_space=pltpu.SMEM if a.ndim == 1 and a.dtype == jnp.int32 else pltpu.VMEM
    )
    return pl.pallas_call(
        kernel,
        out_shape=tuple(jax.ShapeDtypeStruct(s, t) for s, t in outs),
        in_specs=[spec(a) for a in args],
        out_specs=tuple(pl.BlockSpec(memory_space=pltpu.VMEM) for _ in outs),
        scratch_shapes=scratch,
        compiler_params=pltpu.CompilerParams(vmem_limit_bytes=mib << 20),
        cost_estimate=pl.CostEstimate(flops=COST, bytes_accessed=0, transcendentals=0),
    )(*args)


def input_kernel(
    place, x_zero, x_one, thoughts, thought_pos, vecs, w_in, bias,
    spliced_ref, xhat_ref, normed_ref, q_ref, k_ref, v_ref,
):
    core = place[0]
    rows = x_zero.shape[1]
    cols = q_ref.shape[1]
    gain, shift = vecs[0:1, :], vecs[1:2, :]
    for upper in range(2):
        for rel, ref in enumerate((x_zero, x_one)):
            first = upper * 2 * rows + (core ^ rel) * rows
            part = slice((2 * upper + rel) * rows, (2 * upper + rel + 1) * rows)
            match = (first + iota((rows, 1), 0)) == thought_pos[...]
            covered = jnp.sum(match.astype(F32), axis=1, keepdims=True) > 0.0
            picked = dot(match.astype(LOW), thoughts[...], 1, 0)
            spliced = jnp.where(covered, picked, ref[upper].astype(F32))
            xhat, _ = normalised(spliced)
            spliced_ref[part, :] = spliced.astype(LOW)
            xhat_ref[part, :] = xhat.astype(LOW)
            normed = (xhat * gain + shift).astype(LOW)
            normed_ref[part, :] = normed
            mixed = (dot(normed, w_in[...], 1, 0) + bias[...]).astype(LOW)
            q_ref[part, :] = mixed[:, :cols]
            k_ref[part, :] = mixed[:, cols : 2 * cols]
            v_ref[part, :] = mixed[:, 2 * cols :]


def query_limits(place, starts, chunk, rows):
    core, start = place[0], starts[chunk]
    col = iota((1, 2 * rows), 1)
    query = 2 * rows * chunk + jnp.where(col < rows, col + core * rows, col - core * rows)
    inside = (query >= start) & (query < start + IMG)
    return jnp.where(inside, start + (IMG - 1), query)


def key_positions(place, block, rows):
    first = (block >> 1) * (2 * rows) + (place[0] ^ (block & 1)) * rows
    return first + iota((rows, 1), 0)


def attend_kernel(
    chunk, place, starts, q_ref, k_ref, v_ref, w_proj,
    att_ref, log_ref, keep_ref, send_ref, acc_ref, top_ref, sum_ref,
):
    half, cols = att_ref.shape
    rows = half // 2
    heads = cols // HD
    head_of = iota((1, cols), 1) // HD
    limits = query_limits(place, starts, chunk, rows)
    queries = q_ref[chunk * half : (chunk + 1) * half, :] * LOW(0.125)
    acc_ref[...] = jnp.zeros_like(acc_ref)
    top_ref[...] = jnp.full_like(top_ref, -1e30)
    sum_ref[...] = jnp.zeros_like(sum_ref)

    @pl.loop(0, 2 * chunk + 2)
    def _(block):
        span = pl.ds(pl.multiple_of(block * rows, rows), rows)
        keys = k_ref[span, :]
        values = v_ref[span, :].T
        allowed = key_positions(place, block, rows) <= limits
        for head in range(heads):
            scores = dot(jnp.where(head_of == head, keys, LOW(0)), queries, 1, 1)
            scores = jnp.where(allowed, scores, -1e30)
            top = top_ref[head : head + 1, :]
            new_top = jnp.maximum(top, jnp.max(scores, axis=0, keepdims=True))
            exps = jnp.exp(scores - new_top)
            fade = jnp.exp(top - new_top)
            top_ref[head : head + 1, :] = new_top
            sum_ref[head : head + 1, :] = sum_ref[head : head + 1, :] * fade + jnp.sum(
                exps, axis=0, keepdims=True
            )
            part = slice(head * HD, (head + 1) * HD)
            acc_ref[part, :] = acc_ref[part, :] * fade + dot(values[part, :], exps.astype(LOW), 1, 0)

    for head in range(heads):
        part = slice(head * HD, (head + 1) * HD)
        acc_ref[part, :] = acc_ref[part, :] / sum_ref[head : head + 1, :]
    log_ref[...] = top_ref[...] + jnp.log(jnp.maximum(sum_ref[...], 1e-30))
    attended = acc_ref[...].T.astype(LOW)
    att_ref[...] = attended
    branch = dot(attended, w_proj[...], 1, 1)
    keep_ref[...] = branch[:rows]
    send_ref[...] = branch[rows:].astype(LOW)


def attend(chunk, place, starts, queries, keys, values, w_proj):
    length, cols = queries.shape
    half, width = length // 2, w_proj.shape[0]
    return call(
        functools.partial(attend_kernel, chunk),
        (
            ((half, cols), LOW),
            ((8, half), F32),
            ((half // 2, width), F32),
            ((half // 2, width), LOW),
        ),
        place,
        starts,
        queries,
        keys,
        values,
        w_proj,
        scratch=(
            pltpu.VMEM((cols, half), F32),
            pltpu.VMEM((8, half), F32),
            pltpu.VMEM((8, half), F32),
        ),
    )


def feed_kernel(
    chunk, spliced, total, other, cot_zero, cot_one, vecs, up_bias, w_up, w_down,
    residual_ref, normed_ref, hidden_ref, grad_ref, sum_ref, keep_ref, send_ref,
):
    half, width = residual_ref.shape
    rows = half // 2
    for rel, ref in enumerate((total, other)):
        part = slice(rel * rows, (rel + 1) * rows)
        residual = (
            spliced[chunk * half + rel * rows : chunk * half + (rel + 1) * rows, :].astype(F32)
            + ref[...].astype(F32)
            + vecs[2:3, :]
        )
        residual_ref[part, :] = residual
        xhat, _ = normalised(residual)
        normed_ref[part, :] = (xhat * vecs[3:4, :] + vecs[4:5, :]).astype(LOW)
    hidden_cols = w_up.shape[1]
    step = 256 if hidden_cols % 256 == 0 else hidden_cols
    for first in range(0, hidden_cols, step):
        cols = slice(first, first + step)
        hidden, slope = gelu_pair(dot(normed_ref[...], w_up[:, cols], 1, 0) + up_bias[:, cols])
        hidden_ref[:, cols] = hidden.astype(LOW)
        back = jnp.concatenate(
            [dot(cot_zero[chunk], w_down[:, cols], 1, 0), dot(cot_one[chunk], w_down[:, cols], 1, 0)]
        )
        grad = (back * slope).astype(LOW)
        grad_ref[:, cols] = grad
        sum_ref[:, cols] = jnp.sum(grad.astype(F32), axis=0, keepdims=True)
    back = dot(grad_ref[...], w_up[...], 1, 1)
    keep_ref[...] = back[:rows]
    send_ref[...] = back[rows:].astype(LOW)


def feed(chunk, spliced, total, other, cots, vecs, up_bias, w_up, w_down):
    length, width = spliced.shape
    half, hidden = length // 2, w_up.shape[1]
    return call(
        functools.partial(feed_kernel, chunk),
        (
            ((half, width), F32),
            ((half, width), LOW),
            ((half, hidden), LOW),
            ((half, hidden), LOW),
            ((1, hidden), F32),
            ((half // 2, width), F32),
            ((half // 2, width), LOW),
        ),
        spliced,
        total,
        other,
        *cots,
        vecs,
        up_bias,
        w_up,
        w_down,
    )


def norm_back_kernel(
    chunk, total, other, residual, cot_zero, cot_one, vecs, w_proj, att,
    grad_res_ref, branch_ref, gatt_ref, delta_ref, sums_ref,
):
    half, width = residual.shape
    rows = half // 2
    gain = vecs[3:4, :]
    sums = [0.0, 0.0, 0.0, 0.0]
    for rel, (ref, cot) in enumerate(((total, cot_zero), (other, cot_one))):
        part = slice(rel * rows, (rel + 1) * rows)
        upstream = ref[...].astype(F32)
        xhat, inverse = normalised(residual[part, :])
        out_grad = cot[chunk].astype(F32)
        grad_res = out_grad + norm_back(upstream, xhat, inverse, gain)
        grad_res_ref[part, :] = grad_res
        branch_ref[part, :] = grad_res.astype(LOW)
        for k, term in enumerate((upstream * xhat, upstream, grad_res, out_grad)):
            sums[k] = sums[k] + jnp.sum(term, axis=0, keepdims=True)
    for k in range(4):
        sums_ref[k : k + 1, :] = sums[k]
    grad_att = dot(branch_ref[...], w_proj[...], 1, 0).astype(LOW)
    gatt_ref[...] = grad_att
    cols = att.shape[1]
    head_rows = (iota((8, cols), 0) == iota((8, cols), 1) // HD).astype(F32)
    delta_ref[...] = dot(
        head_rows, grad_att.astype(F32) * att[...].astype(F32), 1, 1, lax.Precision.HIGHEST
    )


def branch_back(chunk, total, other, residual, cots, vecs, w_proj, att):
    half, width = residual.shape
    cols = att.shape[1]
    return call(
        functools.partial(norm_back_kernel, chunk),
        (((half, width), F32), ((half, width), LOW), ((half, cols), LOW), ((8, half), F32), ((8, width), F32)),
        total,
        other,
        residual,
        *cots,
        vecs,
        w_proj,
        att,
    )


def back_kernel(chunk, place, starts, q_ref, k_ref, v_ref, log, gatt_ref, delta_ref, *rest):
    keys_in, rest = (rest[:2], rest[2:]) if chunk else ((), rest)
    dq_ref, dk_ref, dv_ref, dqt_ref = rest
    half, cols = gatt_ref.shape
    rows = half // 2
    heads = cols // HD
    head_of = iota((1, cols), 1) // HD
    limits = query_limits(place, starts, chunk, rows)
    dqt_ref[...] = jnp.zeros_like(dqt_ref)

    @pl.loop(0, 2 * chunk + 2)
    def _(block):
        span = pl.ds(pl.multiple_of(block * rows, rows), rows)
        keys, values = k_ref[span, :], v_ref[span, :]
        keys_t = keys.T
        queries = q_ref[chunk * half : (chunk + 1) * half, :] * LOW(0.125)
        grad_att = gatt_ref[...]
        allowed = key_positions(place, block, rows) <= limits
        dk = jnp.zeros((rows, cols), F32)
        dv = jnp.zeros((rows, cols), F32)
        for head in range(heads):
            mine = head_of == head
            scores = dot(jnp.where(mine, keys, LOW(0)), queries, 1, 1)
            probs = jnp.exp(jnp.where(allowed, scores, -1e30) - log[head : head + 1, :])
            grad_probs = dot(jnp.where(mine, values, LOW(0)), grad_att, 1, 1)
            grad_scores = (probs * (grad_probs - delta_ref[head : head + 1, :])).astype(LOW)
            dv = dv + dot(probs.astype(LOW), jnp.where(mine, grad_att, LOW(0)), 1, 0)
            dk = dk + dot(grad_scores, jnp.where(mine, queries, LOW(0)), 1, 0)
            part = slice(head * HD, (head + 1) * HD)
            dqt_ref[part, :] = dqt_ref[part, :] + dot(keys_t[part, :], grad_scores, 1, 0)
        if chunk:
            seen = jnp.where(block < 2, 1.0, 0.0)
            early = pl.ds(pl.multiple_of((block & 1) * rows, rows), rows)
            dk = dk + keys_in[0][early, :] * seen
            dv = dv + keys_in[1][early, :] * seen
        dk_ref[span, :] = dk.astype(dk_ref.dtype)
        dv_ref[span, :] = dv.astype(dv_ref.dtype)

    dq_ref[...] = (dqt_ref[...] * 0.125).T.astype(LOW)


def back(chunk, place, starts, queries, keys, values, log, grad_att, delta, early):
    half, cols = grad_att.shape
    kind = (((half * (chunk + 1), cols), LOW if chunk else F32),) * 2
    return call(
        functools.partial(back_kernel, chunk),
        (((half, cols), LOW), *kind),
        place,
        starts,
        queries,
        keys,
        values,
        log,
        grad_att,
        delta,
        *early,
        scratch=(pltpu.VMEM((cols, half), F32),),
    )


def input_back_kernel(
    place, thought_pos, dq_zero, dq_one, dk, dv, w_in, xhat, res_zero, res_one,
    keep_ref, send_ref, mixed_ref, small_ref, colsum_ref, picked_ref, grad_ref,
):
    half, cols = dq_zero.shape
    rows = half // 2
    sums = [0.0, 0.0, 0.0]
    for upper, dq in enumerate((dq_zero, dq_one)):
        for rel in range(2):
            part = slice((2 * upper + rel) * rows, (2 * upper + rel + 1) * rows)
            mixed = jnp.concatenate(
                [dq[rel * rows : (rel + 1) * rows, :], dk[part, :], dv[part, :]], axis=1
            )
            mixed_ref[part, :] = mixed
            grad = dot(mixed, w_in[...], 1, 1)
            grad_ref[part, :] = grad
            if rel:
                send_ref[upper] = grad.astype(LOW)
            else:
                keep_ref[upper] = grad
            terms = (grad * xhat[part, :].astype(F32), grad, mixed.astype(F32))
            sums = [a + jnp.sum(b, axis=0, keepdims=True) for a, b in zip(sums, terms)]
    small_ref[...] = jnp.zeros_like(small_ref)
    picked_ref[...] = jnp.zeros_like(picked_ref)
    count = thought_pos.shape[0]
    for k in range(count):
        at = thought_pos[k]
        row = (at // half) * half + (((at // rows) & 1) ^ place[0]) * rows + at % rows
        small_ref[k : k + 1, :] = grad_ref[pl.ds(row, 1), :]
        low = res_zero[pl.ds(jnp.minimum(row, half - 1), 1), :]
        high = res_one[pl.ds(jnp.maximum(row - half, 0), 1), :]
        picked_ref[k : k + 1, :] = jnp.where(row < half, low, high)
    small_ref[count : count + 1, :] = sums[0]
    small_ref[count + 1 : count + 2, :] = sums[1]
    colsum_ref[...] = sums[2]


def output_kernel(place, keep, got, spliced, res_zero, res_one, vecs, thought_pos, thoughts, small, picked, embed_ref, rows_ref):
    rows = keep.shape[0]
    gain = vecs[0:1, :]
    own = pl.ds(pl.multiple_of(place[3] * (2 * rows), 2 * rows), rows)
    xhat, inverse = normalised(spliced[own, :].astype(F32))
    residual = jnp.where(place[3] == 0, res_zero[:rows, :], res_one[:rows, :])
    grad = norm_back(keep[...] + got[...].astype(F32), xhat, inverse, gain) + residual
    at = (2 * place[3] + place[0]) * rows + iota((rows, 1), 0)
    covered = jnp.sum((at == thought_pos[...]).astype(F32), axis=1, keepdims=True) > 0.0
    embed_ref[...] = jnp.where(covered, 0.0, grad)
    count = thoughts.shape[0]
    xhat, inverse = normalised(thoughts[...].astype(F32))
    grad = norm_back(small[:count, :], xhat, inverse, gain) + picked[:count, :]
    cols = rows_ref.shape[1]
    rank = 2 * place[3] + place[0]
    rows_ref[...] = sum(
        jnp.where(rank == k, 1.0, 0.0) * grad[:, k * cols : (k + 1) * cols] for k in range(4)
    )


def fold_kernel(bit, place, keep, got, keep_ref, send_ref):
    half = keep_ref.shape[0]
    mine = place[bit] * half
    rest = half - mine
    for k in range(half):
        keep_ref[k] = keep[mine + k] + got[mine + k].astype(F32)
        send_ref[k] = (keep[rest + k] + got[rest + k].astype(F32)).astype(LOW)


def fold(bit, place, keep, got):
    shape = (keep.shape[0] // 2, *keep.shape[1:])
    return call(functools.partial(fold_kernel, bit), ((shape, F32), (shape, LOW)), place, keep, got)


def add_kernel(a, b, out):
    out[...] = (a[...].astype(F32) + b[...].astype(F32)).astype(LOW)


def add_full_kernel(a, b, out):
    out[...] = a[...] + b[...]


def add_full(a, b):
    return call(add_full_kernel, ((a.shape, F32),), a, b)[0]


def add_low(a, b):
    return call(add_kernel, ((a.shape, LOW),), a, b)[0]


def to_slots(place, sum_ref, first, keep_ref, send_ref):
    rows, cols = sum_ref.shape[0] // 8, keep_ref.shape[2]
    for slot, owner in enumerate((0, 6, 2, 4)):
        mine = pl.ds(pl.multiple_of((owner ^ place[7]) * rows, rows), rows)
        rest = pl.ds(pl.multiple_of((owner ^ 1 ^ place[7]) * rows, rows), rows)
        keep_ref[slot, :rows, :] = sum_ref[mine, first : first + cols]
        send_ref[slot, :rows, :] = sum_ref[rest, first : first + cols].astype(LOW)


def all_slots(place, sum_ref, blocks):
    first = 0
    for keep_ref, send_ref in zip(blocks[::2], blocks[1::2]):
        to_slots(place, sum_ref, first, keep_ref, send_ref)
        first += keep_ref.shape[2]


def product(left, right):
    return sum(dot(a[...], b[...], 0, 0) for a, b in zip(left, right))


def grad_kernel(count, place, *refs):
    sides, blocks, sum_ref = refs[:count], refs[count:-1], refs[-1]
    half = count // 2
    sum_ref[...] = product(sides[:half], sides[half:])
    all_slots(place, sum_ref, blocks)


def cot_grad_kernel(count, place, cot_zero, cot_one, hidden_zero, hidden_one, *refs):
    blocks, sum_ref = refs[:-1], refs[-1]
    rows = cot_zero.shape[1]
    left = [c[upper] for upper in range(2) for c in (cot_zero, cot_one)]
    right = [h[k * rows : (k + 1) * rows, :] for h in (hidden_zero, hidden_one) for k in range(2)]
    sum_ref[...] = sum(dot(a, b, 0, 0) for a, b in zip(left, right))
    all_slots(place, sum_ref, blocks)


def last_kernel(place, normed, mixed, branch_zero, branch_one, att_zero, att_one, keep_ref, send_ref, rest_ref, sum_ref):
    cols = att_zero.shape[1]
    sum_ref[:, :cols] = product((branch_zero, branch_one), (att_zero, att_one))
    sum_ref[:, cols:] = dot(normed[...], mixed[...], 0, 0)
    to_slots(place, sum_ref, 0, keep_ref, send_ref)
    rest_ref[...] = sum_ref[:, keep_ref.shape[2] :]


def slot_kernel(place, rest, small, back_zero, back_one, up_zero, up_one, mixed_sums, keep_ref, send_ref, flat_ref):
    to_slots(place, rest, 0, keep_ref, send_ref)
    cols, wide_cols = mixed_sums.shape[1] // 3, keep_ref.shape[2]
    rows = keep_ref.shape[1] - 8
    count = small.shape[0] - 2
    back = back_zero[...] + back_one[...]
    wide = [small[count : count + 1, :], small[count + 1 :, :], back[2:3], back[0:1], back[1:2], back[3:4]]
    wide += [up_zero[...] + up_one[...], mixed_sums[:, :cols], mixed_sums[:, 2 * cols :]]
    for owner in range(8):
        parts = []
        for v in wide:
            n = v.shape[1] // 8
            parts.append(v[:, owner * n : (owner + 1) * n])
        parts.append(jnp.zeros((1, 2 * wide_cols - sum(p.shape[1] for p in parts)), F32))
        flat_ref[owner : owner + 1, :] = jnp.concatenate(parts, axis=1)
    first = iota((8, wide_cols), 0) == 0
    for slot, owner in enumerate((0, 6, 2, 4)):
        mine, other = (flat_ref[pl.ds(owner ^ k ^ place[7], 1), :] for k in range(2))
        keep_ref[slot, rows:, :] = jnp.where(first, mine[:, :wide_cols], mine[:, wide_cols:])
        send_ref[slot, rows:, :] = jnp.where(first, other[:, :wide_cols], other[:, wide_cols:]).astype(LOW)


def finish_kernel(one_keep, one_got, two_keep, two_got, in_ref, proj_ref, flat_ref):
    rows, cols = in_ref.shape[1:]
    one = one_keep[0] + one_got[0].astype(F32)
    two = two_keep[0] + two_got[0].astype(F32)
    proj_ref[...] = one[:, :cols].T
    in_ref[0] = one[:, cols:]
    in_ref[1] = two[:rows, :cols]
    in_ref[2] = two[:rows, cols:]
    flat_ref[...] = jnp.concatenate([two[rows : rows + 1, :], two[rows + 1 : rows + 2, :]], axis=1)


def pair_kernel(*refs):
    *parts, out_ref = refs
    out_ref[...] = jnp.concatenate(
        [keep[0] + got[0].astype(F32) for keep, got in zip(parts[::2], parts[1::2])], axis=1
    )


def joined(*parts):
    shape = (parts[0].shape[1], sum(p.shape[2] for p in parts[::2]))
    return call(pair_kernel, ((shape, F32),), *parts)[0]


def result_kernel(place, keep, got, res_zero, res_one, vecs, out_ref):
    rows = out_ref.shape[0]
    residual = jnp.where(place[3] == 0, res_zero[:rows, :], res_one[:rows, :])
    out_ref[...] = (residual + (keep[...] + got[...].astype(F32)) + vecs[5:6, :]).astype(LOW)


def pick_kernel(place, own, other, out_ref):
    out_ref[place[3]] = own[...]
    out_ref[1 - place[3]] = other[...]


def pick(place, own, other):
    return call(pick_kernel, (((2, *own.shape), own.dtype),), place, own, other)[0]


def stack_kernel(a, b, out_ref):
    out_ref[0] = a[...]
    out_ref[1] = b[...]


def stacked(a, b):
    return call(stack_kernel, (((2, *a.shape), a.dtype),), a, b)[0]


def grad_blocks(kernel, place, splits, *sides):
    width, cols = sides[0].shape[-1], sides[-1].shape[1]
    shapes = []
    for n in splits:
        shapes += [((4, width // 8, n), F32), ((4, width // 8, n), LOW)]
    scratch = (pltpu.VMEM((width, cols), F32),)
    return call(functools.partial(kernel, len(sides)), shapes, place, *sides, scratch=scratch, mib=12)


def plain_grad(shard_rows, *sides):
    half = len(sides) // 2
    total = sum(dot(a, b, 0, 0) for a, b in zip(sides[:half], sides[half:])).astype(LOW)
    return dp_scatter_sum(total.reshape(-1, shard_rows, total.shape[1]))


def fast(shard_rows):
    return lax.axis_size("dp") == 8 and shard_rows % 16 == 0


def place_pieces(masks, place, pieces, write):
    for piece, owners in zip(pieces, masks):
        for k, mask in enumerate(owners):
            write(place[4] ^ mask, piece, k)


def first_kernel(masks, spans, hidden_cols, place, *refs):
    pieces, (w_in_ref, w_proj_ref, vecs_ref, up_ref, bias_ref, flat_ref) = refs[: len(masks)], refs[len(masks) :]
    width, qkv_cols = w_in_ref.shape
    shard_rows = width // 8

    def write(owner, piece, k):
        at = pl.ds(pl.multiple_of(owner * shard_rows, shard_rows), shard_rows)
        w_in_ref[at, :] = piece[k, :shard_rows, :qkv_cols]
        w_proj_ref[at, :] = piece[k, :shard_rows, qkv_cols:]
        flat_ref[pl.ds(owner, 1), :] = piece[k, shard_rows : shard_rows + 1, :].astype(F32)

    place_pieces(masks, place, pieces, write)
    flat = flat_ref[...]
    joined = [
        jnp.concatenate([flat[s : s + 1, a:b] for s in range(8)], axis=1) for a, b in zip(spans, spans[1:])
    ]
    for k in range(6):
        vecs_ref[k : k + 1, :] = joined[k]
    up_ref[...] = joined[6]
    bias_ref[...] = jnp.concatenate([joined[7], jnp.zeros_like(joined[7]), joined[8]], axis=1)


def plain_kernel(masks, place, *refs):
    out_ref = refs[-1]
    rows = out_ref.shape[0] // 8

    def write(owner, piece, k):
        out_ref[pl.ds(pl.multiple_of(owner * rows, rows), rows), :] = piece[k]

    place_pieces(masks, place, refs[:-1], write)


def pack_kernel(count, *refs):
    sources, out_ref, held, sems = refs[:count], refs[count], refs[count + 1 : -1], refs[-1]
    copies = [pltpu.make_async_copy(a, b, sems.at[k]) for k, (a, b) in enumerate(zip(sources, held))]
    for c in copies:
        c.start()
    for c in copies:
        c.wait()
    w_qkv, w_proj, *vectors = held
    rows = w_qkv.shape[1]
    out_ref[:rows, :] = jnp.concatenate([w_qkv[0], w_qkv[1], w_qkv[2], w_proj[...].T], axis=1)
    rows_of = [v[...].astype(F32) for v in vectors]
    rows_of = rows_of[:-1] + [rows_of[-1][0:1], rows_of[-1][1:2]]
    flat = jnp.concatenate(rows_of, axis=1)
    flat = jnp.concatenate([flat, jnp.zeros((1, out_ref.shape[1] - flat.shape[1]), F32)], axis=1)
    out_ref[rows:, :] = jnp.broadcast_to(flat, (8, flat.shape[1])).astype(LOW)


def first_pack(*args):
    w_qkv, w_proj = args[:2]
    return pl.pallas_call(
        functools.partial(pack_kernel, len(args)),
        out_shape=jax.ShapeDtypeStruct((w_qkv.shape[1] + 8, 3 * w_qkv.shape[2] + w_proj.shape[0]), LOW),
        in_specs=[pl.BlockSpec(memory_space=pl.ANY) for _ in args],
        out_specs=pl.BlockSpec(memory_space=pltpu.VMEM),
        scratch_shapes=[
            *(pltpu.VMEM(a.shape, a.dtype) for a in args),
            pltpu.SemaphoreType.DMA((len(args),)),
        ],
        compiler_params=pltpu.CompilerParams(vmem_limit_bytes=63 << 20),
        cost_estimate=pl.CostEstimate(flops=COST, bytes_accessed=0, transcendentals=0),
    )(*args)


def spans_of(vectors):
    spans = [0]
    for n in (*(v.shape[1] for v in vectors), vectors[-1].shape[1]):
        spans.append(spans[-1] + n)
    return spans


def first_unpacked(place, pieces, vectors, qkv_cols, head_cols, width):
    shapes = (
        ((width, qkv_cols), LOW),
        ((width, head_cols), LOW),
        ((6, width), F32),
        ((1, 8 * vectors[6].shape[1]), F32),
        ((1, qkv_cols), F32),
    )
    return call(
        functools.partial(first_kernel, MASKS, spans_of(vectors), 0),
        shapes,
        place,
        *pieces,
        scratch=(pltpu.VMEM((8, qkv_cols + head_cols), F32),),
    )


def unpacked(place, pieces):
    rows, cols = pieces[0].shape[1:]
    return call(functools.partial(plain_kernel, MASKS), (((8 * rows, cols), LOW),), place, *pieces)[0]


def plain_first(shard, vectors, qkv_cols, width):
    flat = dp_gather(jnp.concatenate([*vectors[:-1], vectors[-1][0:1], vectors[-1][1:2]], axis=1))[:, 0].astype(F32)
    whole = dp_gather(shard).reshape(width, -1)
    spans = spans_of(vectors)
    joined = [flat[:, a:b].reshape(1, -1) for a, b in zip(spans, spans[1:])]
    return (
        whole[:, :qkv_cols],
        whole[:, qkv_cols:],
        jnp.concatenate(joined[:6]),
        joined[6],
        jnp.concatenate([joined[7], jnp.zeros_like(joined[7]), joined[8]], axis=1),
    )


def down_kernel(hidden_zero, hidden_one, w_down, keep_ref, send_ref):
    rows = keep_ref.shape[1]
    for upper, hidden in enumerate((hidden_zero, hidden_one)):
        part = dot(hidden[...], w_down[...], 1, 1)
        keep_ref[upper] = part[:rows]
        send_ref[upper] = part[rows:].astype(LOW)


def local(x_embed, thoughts, thought_pos, img_start, *rest):
    *params, grad_out = rest
    dp = lax.axis_size("dp")
    table = []
    for d in range(dp):
        for t in range(4):
            table.append((t & 1, 0, 0, t >> 1, d, (d >> 1 ^ d >> 2) & 1, d >> 2 & 1, d & 1))
    place = jnp.asarray(table, jnp.int32)[lax.axis_index("dp") * 4 + lax.axis_index("tensor")]
    block = quick_block if fast(params[2].shape[1]) else plain_block
    outs = block(place, img_start[0], x_embed[0], thoughts[0], thought_pos, params, grad_out[0])
    vec, outs = outs[-1], outs[:-1]
    sizes = [params[k].size for k in (0, 1, 5, 6, 7, 11, 9, 3)]
    small, first = [], 0
    for n in sizes:
        small.append(vec[first : first + n])
        first += n
    gain_one, bias_one, proj_b, gain_two, bias_two, down_b, up_b, qv_b = small
    block_out, grad_embed, grad_thoughts, grad_in, grad_proj, grad_up, grad_down = outs
    return (
        block_out[None],
        grad_embed[None],
        grad_thoughts[None],
        gain_one,
        bias_one,
        grad_in,
        qv_b.reshape(2, -1),
        grad_proj,
        proj_b,
        gain_two,
        bias_two,
        grad_up,
        up_b,
        grad_down,
        down_b,
    )


def vectors_of(params):
    return [params[k].reshape(1, -1) for k in (0, 1, 5, 6, 7, 11, 9)] + [params[3]]


def input_side(place, x_rows, thoughts, thought_pos, vecs, w_in, bias):
    length, width = 4 * x_rows[0].shape[1], x_rows[0].shape[2]
    return call(
        input_kernel,
        (((length, width), LOW),) * 3 + (((length, w_in.shape[1] // 3), LOW),) * 3,
        place,
        *x_rows,
        thoughts,
        thought_pos,
        vecs,
        w_in,
        bias,
    )


def input_back(place, thought_pos, grad_queries, grad_keys, grad_values, w_in, xhat, grad_residual):
    length, width = xhat.shape
    count = thought_pos.shape[1]
    return call(
        input_back_kernel,
        (
            ((2, length // 4, width), F32),
            ((2, length // 4, width), LOW),
            ((length, w_in.shape[1]), LOW),
            ((-(-(count + 2) // 8) * 8, width), F32),
            ((1, w_in.shape[1]), F32),
            ((-(-count // 8) * 8, width), F32),
        ),
        place,
        thought_pos[0],
        *grad_queries,
        grad_keys,
        grad_values,
        w_in,
        xhat,
        *grad_residual,
        scratch=(pltpu.VMEM((length, width), F32),),
    )


def output_side(place, keep, got, spliced, grad_residual, vecs, thought_pos, thoughts, small, picked):
    rows, width = keep.shape
    return call(
        output_kernel,
        (((rows, width), F32), ((thoughts.shape[0], width // 4), F32)),
        place,
        keep,
        got,
        spliced,
        *grad_residual,
        vecs,
        thought_pos,
        thoughts,
        small,
        picked,
    )


def result(place, keep, got, residual, vecs):
    return call(result_kernel, ((keep.shape, LOW),), place, keep, got, *residual, vecs)[0]


def down_part(hidden, w_down_t):
    shape = (2, hidden[0].shape[0] // 2, w_down_t.shape[0])
    return call(down_kernel, ((shape, F32), (shape, LOW)), *hidden, w_down_t)


def quick_block(place, starts, x_own, thoughts, thought_pos, params, cot_own):
    across = lambda a: swapped(a, "dp", 1)
    near = lambda a: swapped(a, "dp", 2)
    far = lambda a: swapped(a, "dp", 6)
    core = lambda a: swapped(a, "tensor", 1)
    over = lambda a: swapped(a, "tensor", 2)
    w_qkv, w_proj, w_up, w_down_own = params[2], params[4], params[8], params[10].T
    shard_rows, head_cols = w_qkv.shape[1:]
    width = x_own.shape[1]
    vectors = vectors_of(params)

    x_far = over(x_own)
    pack = first_pack(w_qkv, w_proj, *vectors)
    pack_far, pack_across, up_across = far(pack), across(pack), across(w_up)
    x_far, pack_far, pack_across, up_across = together(x_far, pack_far, pack_across, up_across)

    x_both = pick(place, x_own, x_far)
    x_other = core(x_both)
    pack_near, pack_far_across = near(stacked(pack, pack_far)), across(pack_far)
    up_far = far(after(w_up, pack_far))
    down_across = across(after(w_down_own, up_across))
    cot_far = over(after(cot_own, x_far))
    x_other, pack_near, pack_far_across, down_across, up_far, cot_far = together(
        x_other, pack_near, pack_far_across, down_across, up_far, cot_far
    )

    pack_near_across = across(pack_near)
    up_near = near(stacked(w_up, up_far))
    down_far = far(after(w_down_own, up_far))
    cot_both = pick(place, cot_own, cot_far)
    cot_other = core(cot_both)
    pieces = (pack[None], pack_across[None], pack_far[None], pack_near, pack_far_across[None], pack_near_across)
    w_in, w_proj_t, vecs, up_bias, all_bias = first_unpacked(place, pieces, vectors, 3 * head_cols, head_cols, width)
    spliced, xhat, normed, queries, keys, values = input_side(
        place, (x_both, x_other), thoughts, thought_pos, vecs, w_in, all_bias
    )
    att_zero, log_zero, keep_zero, send_zero = attend(0, place, starts, queries, keys, values, w_proj_t)
    send_zero, up_near, down_far, cot_other = together(send_zero, up_near, down_far, cot_other)
    cots = (cot_both, cot_other)

    mine_zero = add_low(keep_zero, core(send_zero))
    far_zero = over(mine_zero)
    up_far_across, up_near_across = across(after(up_far, send_zero)), across(up_near)
    down_near = near(stacked(w_down_own, down_far))
    att_one, log_one, keep_one, send_one = attend(1, after(place, mine_zero), starts, queries, keys, values, w_proj_t)
    send_one, far_zero, up_far_across, up_near_across, down_near = together(
        send_one, far_zero, up_far_across, up_near_across, down_near
    )

    mine_one = add_low(keep_one, core(send_one))
    far_one = over(mine_one)
    total_zero = add_low(mine_zero, far_zero)
    other_zero = core(total_zero)
    down_far_across, down_near_across = across(after(down_far, send_one)), across(down_near)
    pieces = (w_up[None], up_across[None], up_far[None], up_near, up_far_across[None], up_near_across)
    w_up_all = unpacked(place, pieces)
    other_zero, down_far_across, down_near_across, w_up_all = together(
        other_zero, down_far_across, down_near_across, w_up_all
    )
    pieces = (w_down_own[None], down_across[None], down_far[None], down_near, down_far_across[None], down_near_across)
    w_down_t = unpacked(place, pieces)

    weights = (vecs, up_bias, w_up_all, w_down_t)
    residual_zero, normed_zero, hidden_zero, grad_zero, up_sum_zero, keep_zero, send_zero = feed(
        0, spliced, total_zero, other_zero, cots, *weights
    )
    send_zero, far_one = together(send_zero, far_one)
    total_one = add_low(mine_one, far_one)
    other_one = core(total_one)
    mine_zero = add_low(keep_zero, core(send_zero))
    far_zero = over(mine_zero)
    residual_one, normed_one, hidden_one, grad_one, up_sum_one, keep_one, send_one = feed(
        1, after(spliced, mine_zero), total_one, other_one, cots, *weights
    )
    quarter = hidden_one.shape[1] // 3
    a_keep, a_send, b_keep, b_send = grad_blocks(
        grad_kernel, place, (quarter, 2 * quarter), normed_zero, normed_one, grad_zero, grad_one
    )
    a_got = across(a_send)
    mine_one = add_low(keep_one, core(send_one))
    c_keep, c_send = grad_blocks(
        cot_grad_kernel, after(place, a_send), (3 * quarter,), *cots, hidden_zero, hidden_one
    )
    mlp_keep, mlp_send = down_part((hidden_zero, after(hidden_one, a_send)), w_down_t)
    far_zero, mine_one, c_send, mlp_send, a_got = together(far_zero, mine_one, c_send, mlp_send, a_got)
    residual = (residual_zero, residual_one)

    far_one = over(mine_one)
    b_got = across(after(b_send, a_got))
    a_keep, a_send = fold(5, place, a_keep, a_got)
    a_got = near(a_send)
    mlp_got = core(mlp_send)
    total_zero = add_low(mine_zero, far_zero)
    res_zero, branch_zero, gatt_zero, delta_zero, sums_zero = branch_back(
        0, total_zero, core(total_zero), residual_zero, cots, vecs, w_proj_t, att_zero
    )
    dq_zero, *early = back(0, place, starts, queries, keys, values, log_zero, gatt_zero, delta_zero, ())
    early[0], far_one, mlp_got, a_got, b_got = together(early[0], far_one, mlp_got, a_got, b_got)

    total_one = add_low(mine_one, far_one)
    other_one = core(total_one)
    c_got = across(after(c_send, b_got))
    mlp_keep, mlp_send = fold(3, place, mlp_keep, mlp_got)
    mlp_got = over(mlp_send)
    a_keep, a_send = fold(6, place, a_keep, a_got)
    a_got = far(a_send)
    b_keep, b_send = fold(5, place, b_keep, b_got)
    b_got = near(b_send)
    res_one, branch_one, gatt_one, delta_one, sums_one = branch_back(
        1, total_one, other_one, residual_one, cots, vecs, w_proj_t, att_one
    )
    dq_one, dk, dv = back(1, place, starts, queries, keys, values, log_one, gatt_one, delta_one, early)
    dk, mlp_got, a_got, b_got, c_got = together(dk, mlp_got, a_got, b_got, c_got)

    grad_residual = (res_zero, res_one)
    c_keep, c_send = fold(5, place, c_keep, c_got)
    c_got = near(c_send)
    b_keep, b_send = fold(6, place, b_keep, b_got)
    b_got = far(b_send)
    keep, send, grad_mixed, small, mixed_sums, picked = input_back(
        place, thought_pos, (dq_zero, dq_one), dk, dv, w_in, xhat, grad_residual
    )
    got, small_got = core(send), core(small)
    shape = (4, shard_rows, 2 * head_cols)
    d_keep, d_send, rest = call(
        last_kernel,
        ((shape, F32), (shape, LOW), ((width, 2 * head_cols), F32)),
        place,
        normed,
        grad_mixed,
        branch_zero,
        branch_one,
        att_zero,
        att_one,
        scratch=(pltpu.VMEM((width, 4 * head_cols), F32),),
        mib=12,
    )
    got, small_got, d_send = together(got, small_got, d_send)
    d_got = across(d_send)
    keep, send = fold(3, place, keep, got)
    got = over(send)
    small = add_full(small, small_got)
    small_got = over(small)
    block_out = result(place, mlp_keep[0], mlp_got[0], residual, vecs)
    small_got, b_got, c_got, block_out = together(small_got, b_got, c_got, block_out)
    small = add_full(small, small_got)
    c_keep, c_send = fold(6, place, c_keep, c_got)
    c_got = far(c_send)
    grad_up = joined(a_keep, a_got, b_keep, b_got)
    shape = (4, shard_rows + 8, 2 * head_cols)
    e_keep, e_send = call(
        slot_kernel,
        ((shape, F32), (shape, LOW)),
        place,
        rest,
        small,
        sums_zero,
        sums_one,
        up_sum_zero,
        up_sum_one,
        mixed_sums,
        scratch=(pltpu.VMEM((8, 4 * head_cols), F32),),
    )
    e_send, d_got, grad_up = together(e_send, d_got, grad_up)
    e_got = across(e_send)
    d_keep, d_send = fold(5, place, d_keep, d_got)
    d_got = near(d_send)
    got, e_got, d_got, c_got = together(got, e_got, d_got, c_got)
    e_keep, e_send = fold(5, place, e_keep, e_got)
    e_got = near(e_send)
    d_keep, d_send = fold(6, place, d_keep, d_got)
    d_got = far(d_send)
    grad_embed, grad_thoughts = output_side(
        place, keep[0], got[0], spliced, grad_residual, vecs, thought_pos, thoughts, small, picked
    )
    grad_embed, d_got, e_got = together(grad_embed, d_got, e_got)
    e_keep, e_send = fold(6, place, e_keep, e_got)
    e_got = far(e_send)
    grad_down = joined(c_keep, c_got)
    grad_down, e_got = together(grad_down, e_got)
    grad_in, grad_proj, vec = call(
        finish_kernel,
        (((3, shard_rows, head_cols), F32), ((head_cols, shard_rows), F32), ((1, 4 * head_cols), F32)),
        d_keep,
        d_got,
        e_keep,
        e_got,
    )
    return block_out, grad_embed, grad_thoughts, grad_in, grad_proj, grad_up, grad_down.T, vec[0]


def plain_block(place, starts, x_own, thoughts, thought_pos, params, cot_own):
    dp = lax.axis_size("dp")
    w_qkv, w_proj, w_up, w_down_own = params[2], params[4], params[8], params[10].T
    shard_rows, head_cols = w_qkv.shape[1:]
    width = x_own.shape[1]
    x_rows, cots = rows_gather(x_own), rows_gather(cot_own)
    shard = jnp.concatenate([w_qkv[0], w_qkv[1], w_qkv[2], w_proj.T], axis=1)
    w_in, w_proj_t, vecs, up_bias, all_bias = plain_first(shard, vectors_of(params), 3 * head_cols, width)
    w_up_all = dp_gather(w_up).reshape(width, -1)
    w_down_t = dp_gather(w_down_own).reshape(width, -1)
    spliced, xhat, normed, queries, keys, values = input_side(
        place, x_rows, thoughts, thought_pos, vecs, w_in, all_bias
    )

    def all_sum(keep, send):
        mine = add_low(keep, swapped(send, "tensor", 1))
        total = add_low(mine, swapped(mine, "tensor", 2))
        return total, swapped(total, "tensor", 1)

    def own_sum(keep, send):
        keep, send = fold(3, place, keep, swapped(send, "tensor", 1))
        return keep[0], swapped(send, "tensor", 2)[0]

    atts, logs, feds, grad_twos = [], [], [], []
    for chunk in range(2):
        att, log, *part = attend(chunk, place, starts, queries, keys, values, w_proj_t)
        feds.append(feed(chunk, spliced, *all_sum(*part), cots, vecs, up_bias, w_up_all, w_down_t))
        grad_twos.append(all_sum(*feds[-1][5:]))
        atts.append(att)
        logs.append(log)
    residual, normed_two, hidden, grad_hidden, up_sums = zip(feds[0][:5], feds[1][:5])
    block_out = result(place, *own_sum(*down_part(hidden, w_down_t)), residual, vecs)
    grad_up = plain_grad(shard_rows, *normed_two, *grad_hidden)
    grad_down = plain_grad(shard_rows, cots_rows(cots, 0), cots_rows(cots, 1), *hidden)
    branches, dqs, early = [], [], ()
    for chunk in range(2):
        branches.append(
            branch_back(chunk, *grad_twos[chunk], residual[chunk], cots, vecs, w_proj_t, atts[chunk])
        )
        dq, *early = back(
            chunk, place, starts, queries, keys, values, logs[chunk], *branches[-1][2:4], early
        )
        dqs.append(dq)
    grad_residual, grad_branch = zip(branches[0][:2], branches[1][:2])
    keep, send, grad_mixed, small, mixed_sums, picked = input_back(
        place, thought_pos, dqs, *early, w_in, xhat, grad_residual
    )
    small = small + swapped(small, "tensor", 1)
    small = small + swapped(small, "tensor", 2)
    grad_embed, grad_thoughts = output_side(
        place, *own_sum(keep, send), spliced, grad_residual, vecs, thought_pos, thoughts, small, picked
    )
    grad_in = plain_grad(shard_rows, normed, grad_mixed).reshape(shard_rows, 3, head_cols)
    grad_proj = plain_grad(shard_rows, *grad_branch, *atts)
    two = branches[0][4] + branches[1][4]
    count = small.shape[0] - 2
    vec = (small[count], small[count + 1], two[2], two[0], two[1], two[3], up_sums[0] + up_sums[1])
    vec += (mixed_sums[0, :head_cols], mixed_sums[0, 2 * head_cols :])
    vec = jnp.concatenate([v.reshape(dp, -1) for v in vec], axis=1)
    vec = dp_scatter_sum(vec[:, None, :])[0]
    return (
        block_out,
        grad_embed,
        grad_thoughts,
        jnp.moveaxis(grad_in, 1, 0),
        grad_proj.T,
        grad_up,
        grad_down.T,
        vec,
    )


def solution(mesh):
    in_specs = (
        P("dp", "tensor", None),
        P("dp", None, None),
        P("dp", None),
        P("dp", None),
        P("dp"),
        P("dp"),
        P(None, "dp", "tensor"),
        P(None, ("tensor", "dp")),
        P("tensor", "dp"),
        P("dp"),
        P("dp"),
        P("dp"),
        P("dp", "tensor"),
        P(("tensor", "dp")),
        P("tensor", "dp"),
        P("dp"),
        P("dp", "tensor", None),
    )
    out_specs = (
        P("dp", "tensor", None),
        P("dp", "tensor", None),
        P("dp", None, "tensor"),
        P("dp"),
        P("dp"),
        P(None, "dp", "tensor"),
        P(None, ("tensor", "dp")),
        P("tensor", "dp"),
        P("dp"),
        P("dp"),
        P("dp"),
        P("dp", "tensor"),
        P(("tensor", "dp")),
        P("tensor", "dp"),
        P("dp"),
    )
    return jax.shard_map(local, mesh=mesh, in_specs=in_specs, out_specs=out_specs, check_vma=False)
```

```python
import functools

import jax
import jax.numpy as jnp
from jax import lax
from jax.experimental import pallas as pl
from jax.experimental.pallas import tpu as pltpu
from jax.sharding import PartitionSpec as P

HD = 64
IMG = 256
EPSILON = 1e-05
F32 = jnp.float32
LOW = jnp.bfloat16
COST = 1000


def swapped(array, axis, mask):
    return lax.ppermute(array, axis, [(i, i ^ mask) for i in range(lax.axis_size(axis))])


def dp_masks():
    return [1 << b for b in reversed(range(lax.axis_size("dp").bit_length() - 1))]


def slot_owners(masks):
    owners = [0]
    for mask in masks:
        owners = owners + [o ^ mask for o in owners]
    return owners


def dp_gather(shard):
    masks, me = dp_masks(), lax.axis_index("dp")
    slots = shard[None]
    for mask in masks:
        other = swapped(slots, "dp", mask)
        first = (me & mask) == 0
        slots = jnp.where(
            first, jnp.concatenate([slots, other]), jnp.concatenate([other, slots])
        )
    owners = slot_owners(masks)
    return jnp.stack([slots[owners.index(s)] for s in range(len(owners))])


MASKS = ((0,), (1,), (4,), (2, 6), (5,), (3, 7))


def rows_pick(own, other):
    first = (lax.axis_index("tensor") >> 1) == 0
    return jnp.stack([jnp.where(first, own, other), jnp.where(first, other, own)])


def dp_scatter_sum(blocks):
    masks, me = dp_masks(), lax.axis_index("dp")
    slots = jnp.stack([blocks[s] for s in slot_owners(masks)])
    for mask in reversed(masks):
        half = slots.shape[0] // 2
        first = (me & mask) == 0
        keep = jnp.where(first, slots[:half], slots[half:])
        send = jnp.where(first, slots[half:], slots[:half])
        slots = keep.astype(F32) + swapped(send, "dp", mask).astype(F32)
    return slots[0]


def rows_gather(own):
    both = rows_pick(own, swapped(own, "tensor", 2))
    return both, swapped(both, "tensor", 1)


def after(value, *others):
    return lax.optimization_barrier((value, *others))[0]


def together(*values):
    return lax.optimization_barrier(values)


def dot(a, b, ca, cb, precision=None):
    return lax.dot_general(
        a, b, (((ca,), (cb,)), ((), ())), precision=precision, preferred_element_type=F32
    )


def normalised(values):
    centred = values - jnp.mean(values, axis=-1, keepdims=True)
    inverse = lax.rsqrt(jnp.mean(centred * centred, axis=-1, keepdims=True) + EPSILON)
    return centred * inverse, inverse


def norm_back(upstream, xhat, inverse, gain):
    scaled = upstream * gain
    return inverse * (
        scaled
        - jnp.mean(scaled, axis=-1, keepdims=True)
        - xhat * jnp.mean(scaled * xhat, axis=-1, keepdims=True)
    )


def gelu_pair(u):
    k, a = 0.7978845608028654, 0.044715
    square = u * u
    t = jnp.tanh(u * (k + (k * a) * square))
    rise = 0.5 * (1.0 + t)
    return u * rise, rise + (0.5 * u) * (1.0 - t * t) * (k + (3.0 * k * a) * square)


def cots_rows(cots, chunk):
    return jnp.concatenate([c[chunk] for c in cots])


def iota(shape, dim):
    return lax.broadcasted_iota(jnp.int32, shape, dim)


def call(kernel, outs, *args, scratch=(), mib=8):
    spec = lambda a: pl.BlockSpec(
        memory_space=pltpu.SMEM if a.ndim == 1 and a.dtype == jnp.int32 else pltpu.VMEM
    )
    return pl.pallas_call(
        kernel,
        out_shape=tuple(jax.ShapeDtypeStruct(s, t) for s, t in outs),
        in_specs=[spec(a) for a in args],
        out_specs=tuple(pl.BlockSpec(memory_space=pltpu.VMEM) for _ in outs),
        scratch_shapes=scratch,
        compiler_params=pltpu.CompilerParams(vmem_limit_bytes=mib << 20),
        cost_estimate=pl.CostEstimate(flops=COST, bytes_accessed=0, transcendentals=0),
    )(*args)


def splice_kernel(place, x_zero, x_one, thoughts, thought_pos, spliced_ref, xhat_ref):
    core = place[0]
    rows = x_zero.shape[1]
    for upper in range(2):
        for rel, ref in enumerate((x_zero, x_one)):
            first = upper * 2 * rows + (core ^ rel) * rows
            part = slice((2 * upper + rel) * rows, (2 * upper + rel + 1) * rows)
            match = (first + iota((rows, 1), 0)) == thought_pos[...]
            covered = jnp.sum(match.astype(F32), axis=1, keepdims=True) > 0.0
            picked = dot(match.astype(LOW), thoughts[...], 1, 0)
            spliced = jnp.where(covered, picked, ref[upper].astype(F32))
            spliced_ref[part, :] = spliced.astype(LOW)
            xhat_ref[part, :] = normalised(spliced)[0]


def input_kernel(xhat, vecs, w_in, bias, normed_ref, q_ref, k_ref, v_ref):
    rows = xhat.shape[0] // 4
    cols = q_ref.shape[1]
    for k in range(4):
        part = slice(k * rows, (k + 1) * rows)
        normed = (xhat[part, :] * vecs[0:1, :] + vecs[1:2, :]).astype(LOW)
        normed_ref[part, :] = normed
        mixed = (dot(normed, w_in[...], 1, 0) + bias[...]).astype(LOW)
        q_ref[part, :] = mixed[:, :cols]
        k_ref[part, :] = mixed[:, cols : 2 * cols]
        v_ref[part, :] = mixed[:, 2 * cols :]


def query_limits(place, starts, chunk, rows):
    core, start = place[0], starts[chunk]
    col = iota((1, 2 * rows), 1)
    query = 2 * rows * chunk + jnp.where(col < rows, col + core * rows, col - core * rows)
    inside = (query >= start) & (query < start + IMG)
    return jnp.where(inside, start + (IMG - 1), query)


def key_positions(place, block, rows):
    first = (block >> 1) * (2 * rows) + (place[0] ^ (block & 1)) * rows
    return first + iota((rows, 1), 0)


def attend_kernel(
    chunk, place, starts, q_ref, k_ref, v_ref, w_proj,
    att_ref, log_ref, keep_ref, send_ref, acc_ref, top_ref, sum_ref,
):
    half, cols = att_ref.shape
    rows = half // 2
    heads = cols // HD
    head_of = iota((1, cols), 1) // HD
    limits = query_limits(place, starts, chunk, rows)
    queries = q_ref[chunk * half : (chunk + 1) * half, :] * LOW(0.125)
    acc_ref[...] = jnp.zeros_like(acc_ref)
    top_ref[...] = jnp.full_like(top_ref, -1e30)
    sum_ref[...] = jnp.zeros_like(sum_ref)

    @pl.loop(0, 2 * chunk + 2)
    def _(block):
        span = pl.ds(pl.multiple_of(block * rows, rows), rows)
        keys = k_ref[span, :]
        values = v_ref[span, :].T
        allowed = key_positions(place, block, rows) <= limits
        for head in range(heads):
            scores = dot(jnp.where(head_of == head, keys, LOW(0)), queries, 1, 1)
            scores = jnp.where(allowed, scores, -1e30)
            top = top_ref[head : head + 1, :]
            new_top = jnp.maximum(top, jnp.max(scores, axis=0, keepdims=True))
            exps = jnp.exp(scores - new_top)
            fade = jnp.exp(top - new_top)
            top_ref[head : head + 1, :] = new_top
            sum_ref[head : head + 1, :] = sum_ref[head : head + 1, :] * fade + jnp.sum(
                exps, axis=0, keepdims=True
            )
            part = slice(head * HD, (head + 1) * HD)
            acc_ref[part, :] = acc_ref[part, :] * fade + dot(values[part, :], exps.astype(LOW), 1, 0)

    for head in range(heads):
        part = slice(head * HD, (head + 1) * HD)
        acc_ref[part, :] = acc_ref[part, :] / sum_ref[head : head + 1, :]
    log_ref[...] = top_ref[...] + jnp.log(jnp.maximum(sum_ref[...], 1e-30))
    attended = acc_ref[...].T.astype(LOW)
    att_ref[...] = attended
    branch = dot(attended, w_proj[...], 1, 1)
    keep_ref[...] = branch[:rows]
    send_ref[...] = branch[rows:].astype(LOW)


def attend(chunk, place, starts, queries, keys, values, w_proj):
    length, cols = queries.shape
    half, width = length // 2, w_proj.shape[0]
    return call(
        functools.partial(attend_kernel, chunk),
        (
            ((half, cols), LOW),
            ((8, half), F32),
            ((half // 2, width), F32),
            ((half // 2, width), LOW),
        ),
        place,
        starts,
        queries,
        keys,
        values,
        w_proj,
        scratch=(
            pltpu.VMEM((cols, half), F32),
            pltpu.VMEM((8, half), F32),
            pltpu.VMEM((8, half), F32),
        ),
    )


def feed_kernel(
    chunk, spliced, total, other, cot_zero, cot_one, vecs, up_bias, w_up, w_down,
    residual_ref, normed_ref, hidden_ref, grad_ref, sum_ref, keep_ref, send_ref,
):
    half, width = residual_ref.shape
    rows = half // 2
    for rel, ref in enumerate((total, other)):
        part = slice(rel * rows, (rel + 1) * rows)
        residual = (
            spliced[chunk * half + rel * rows : chunk * half + (rel + 1) * rows, :].astype(F32)
            + ref[...].astype(F32)
            + vecs[2:3, :]
        )
        residual_ref[part, :] = residual
        xhat, _ = normalised(residual)
        normed_ref[part, :] = (xhat * vecs[3:4, :] + vecs[4:5, :]).astype(LOW)
    hidden_cols = w_up.shape[1]
    step = 256 if hidden_cols % 256 == 0 else hidden_cols
    for first in range(0, hidden_cols, step):
        cols = slice(first, first + step)
        hidden, slope = gelu_pair(dot(normed_ref[...], w_up[:, cols], 1, 0) + up_bias[:, cols])
        hidden_ref[:, cols] = hidden.astype(LOW)
        back = jnp.concatenate(
            [dot(cot_zero[chunk], w_down[:, cols], 1, 0), dot(cot_one[chunk], w_down[:, cols], 1, 0)]
        )
        grad = (back * slope).astype(LOW)
        grad_ref[:, cols] = grad
        sum_ref[:, cols] = jnp.sum(grad.astype(F32), axis=0, keepdims=True)
    back = dot(grad_ref[...], w_up[...], 1, 1)
    keep_ref[...] = back[:rows]
    send_ref[...] = back[rows:].astype(LOW)


def feed(chunk, spliced, total, other, cots, vecs, up_bias, w_up, w_down):
    length, width = spliced.shape
    half, hidden = length // 2, w_up.shape[1]
    return call(
        functools.partial(feed_kernel, chunk),
        (
            ((half, width), F32),
            ((half, width), LOW),
            ((half, hidden), LOW),
            ((half, hidden), LOW),
            ((1, hidden), F32),
            ((half // 2, width), F32),
            ((half // 2, width), LOW),
        ),
        spliced,
        total,
        other,
        *cots,
        vecs,
        up_bias,
        w_up,
        w_down,
    )


def norm_back_kernel(
    chunk, total, other, residual, cot_zero, cot_one, vecs, w_proj, att,
    grad_res_ref, branch_ref, gatt_ref, delta_ref, sums_ref,
):
    half, width = residual.shape
    rows = half // 2
    gain = vecs[3:4, :]
    sums = [0.0, 0.0, 0.0, 0.0]
    for rel, (ref, cot) in enumerate(((total, cot_zero), (other, cot_one))):
        part = slice(rel * rows, (rel + 1) * rows)
        upstream = ref[...].astype(F32)
        xhat, inverse = normalised(residual[part, :])
        out_grad = cot[chunk].astype(F32)
        grad_res = out_grad + norm_back(upstream, xhat, inverse, gain)
        grad_res_ref[part, :] = grad_res
        branch_ref[part, :] = grad_res.astype(LOW)
        for k, term in enumerate((upstream * xhat, upstream, grad_res, out_grad)):
            sums[k] = sums[k] + jnp.sum(term, axis=0, keepdims=True)
    for k in range(4):
        sums_ref[k : k + 1, :] = sums[k]
    grad_att = dot(branch_ref[...], w_proj[...], 1, 0).astype(LOW)
    gatt_ref[...] = grad_att
    cols = att.shape[1]
    head_rows = (iota((8, cols), 0) == iota((8, cols), 1) // HD).astype(F32)
    delta_ref[...] = dot(
        head_rows, grad_att.astype(F32) * att[...].astype(F32), 1, 1, lax.Precision.HIGHEST
    )


def branch_back(chunk, total, other, residual, cots, vecs, w_proj, att):
    half, width = residual.shape
    cols = att.shape[1]
    return call(
        functools.partial(norm_back_kernel, chunk),
        (((half, width), F32), ((half, width), LOW), ((half, cols), LOW), ((8, half), F32), ((8, width), F32)),
        total,
        other,
        residual,
        *cots,
        vecs,
        w_proj,
        att,
    )


def back_kernel(chunk, place, starts, q_ref, k_ref, v_ref, log, gatt_ref, delta_ref, *rest):
    keys_in, rest = (rest[:2], rest[2:]) if chunk else ((), rest)
    dq_ref, dk_ref, dv_ref, dqt_ref = rest
    half, cols = gatt_ref.shape
    rows = half // 2
    heads = cols // HD
    head_of = iota((1, cols), 1) // HD
    limits = query_limits(place, starts, chunk, rows)
    dqt_ref[...] = jnp.zeros_like(dqt_ref)

    @pl.loop(0, 2 * chunk + 2)
    def _(block):
        span = pl.ds(pl.multiple_of(block * rows, rows), rows)
        keys, values = k_ref[span, :], v_ref[span, :]
        keys_t = keys.T
        queries = q_ref[chunk * half : (chunk + 1) * half, :] * LOW(0.125)
        grad_att = gatt_ref[...]
        allowed = key_positions(place, block, rows) <= limits
        dk = jnp.zeros((rows, cols), F32)
        dv = jnp.zeros((rows, cols), F32)
        for head in range(heads):
            mine = head_of == head
            scores = dot(jnp.where(mine, keys, LOW(0)), queries, 1, 1)
            probs = jnp.exp(jnp.where(allowed, scores, -1e30) - log[head : head + 1, :])
            grad_probs = dot(jnp.where(mine, values, LOW(0)), grad_att, 1, 1)
            grad_scores = (probs * (grad_probs - delta_ref[head : head + 1, :])).astype(LOW)
            dv = dv + dot(probs.astype(LOW), jnp.where(mine, grad_att, LOW(0)), 1, 0)
            dk = dk + dot(grad_scores, jnp.where(mine, queries, LOW(0)), 1, 0)
            part = slice(head * HD, (head + 1) * HD)
            dqt_ref[part, :] = dqt_ref[part, :] + dot(keys_t[part, :], grad_scores, 1, 0)
        if chunk:
            seen = jnp.where(block < 2, 1.0, 0.0)
            early = pl.ds(pl.multiple_of((block & 1) * rows, rows), rows)
            dk = dk + keys_in[0][early, :] * seen
            dv = dv + keys_in[1][early, :] * seen
        dk_ref[span, :] = dk.astype(dk_ref.dtype)
        dv_ref[span, :] = dv.astype(dv_ref.dtype)

    dq_ref[...] = (dqt_ref[...] * 0.125).T.astype(LOW)


def back(chunk, place, starts, queries, keys, values, log, grad_att, delta, early):
    half, cols = grad_att.shape
    kind = (((half * (chunk + 1), cols), LOW if chunk else F32),) * 2
    return call(
        functools.partial(back_kernel, chunk),
        (((half, cols), LOW), *kind),
        place,
        starts,
        queries,
        keys,
        values,
        log,
        grad_att,
        delta,
        *early,
        scratch=(pltpu.VMEM((cols, half), F32),),
    )


def input_back_kernel(
    place, thought_pos, dq_zero, dq_one, dk, dv, w_in, xhat, res_zero, res_one,
    keep_ref, send_ref, small_ref, colsum_ref, picked_ref, grad_ref,
):
    half, cols = dq_zero.shape
    rows = half // 2
    sums = [0.0, 0.0, 0.0]
    for upper, dq in enumerate((dq_zero, dq_one)):
        for rel in range(2):
            part = slice((2 * upper + rel) * rows, (2 * upper + rel + 1) * rows)
            mixed = jnp.concatenate(
                [dq[rel * rows : (rel + 1) * rows, :], dk[part, :], dv[part, :]], axis=1
            )
            grad = dot(mixed, w_in[...], 1, 1)
            grad_ref[part, :] = grad
            if rel:
                send_ref[upper] = grad.astype(LOW)
            else:
                keep_ref[upper] = grad
            terms = (grad * xhat[part, :], grad, mixed.astype(F32))
            sums = [a + jnp.sum(b, axis=0, keepdims=True) for a, b in zip(sums, terms)]
    small_ref[...] = jnp.zeros_like(small_ref)
    picked_ref[...] = jnp.zeros_like(picked_ref)
    count = thought_pos.shape[0]
    for k in range(count):
        at = thought_pos[k]
        row = (at // half) * half + (((at // rows) & 1) ^ place[0]) * rows + at % rows
        small_ref[k : k + 1, :] = grad_ref[pl.ds(row, 1), :]
        low = res_zero[pl.ds(jnp.minimum(row, half - 1), 1), :]
        high = res_one[pl.ds(jnp.maximum(row - half, 0), 1), :]
        picked_ref[k : k + 1, :] = jnp.where(row < half, low, high)
    small_ref[count : count + 1, :] = sums[0]
    small_ref[count + 1 : count + 2, :] = sums[1]
    colsum_ref[...] = sums[2]


def output_kernel(place, keep, got, spliced, res_zero, res_one, vecs, thought_pos, thoughts, small, picked, *rest):
    pairs, (embed_ref, rows_ref, *more) = rest[: 2 * ((len(rest) - 2) // 3)], rest[2 * ((len(rest) - 2) // 3) :]
    rows = keep.shape[0]
    gain = vecs[0:1, :]
    own = pl.ds(pl.multiple_of(place[3] * (2 * rows), 2 * rows), rows)
    xhat, inverse = normalised(spliced[own, :].astype(F32))
    residual = jnp.where(place[3] == 0, res_zero[:rows, :], res_one[:rows, :])
    grad = norm_back(keep[...] + got[...].astype(F32), xhat, inverse, gain) + residual
    at = (2 * place[3] + place[0]) * rows + iota((rows, 1), 0)
    covered = jnp.sum((at == thought_pos[...]).astype(F32), axis=1, keepdims=True) > 0.0
    embed_ref[...] = jnp.where(covered, 0.0, grad)
    count = thoughts.shape[0]
    xhat, inverse = normalised(thoughts[...].astype(F32))
    grad = norm_back(small[:count, :], xhat, inverse, gain) + picked[:count, :]
    cols = rows_ref.shape[2]
    rank = 2 * place[3] + place[0]
    grad = sum(jnp.where(rank == k, 1.0, 0.0) * grad[:, k * cols : (k + 1) * cols] for k in range(4))
    for k in range(count):
        rows_ref[k] = grad[k : k + 1, :]
    for ref, keep, got in zip(more, pairs[::2], pairs[1::2]):
        ref[...] = keep[0] + got[0].astype(F32)


def fold_kernel(bit, place, *refs):
    *parts, keep_ref, send_ref = refs
    half = keep_ref.shape[0]
    mine = place[bit] * half
    rest = half - mine
    first = 0
    for keep, got in zip(parts[::2], parts[1::2]):
        rows, cols = keep.shape[1:]
        below = rows < 16 and first > 0
        if below:
            at = (slice(keep_ref.shape[1] - rows, None), slice(0, cols))
        else:
            at = (slice(0, rows), slice(first, first + cols))
            first += cols
        for k in range(half):
            keep_ref[(k, *at)] = keep[mine + k] + got[mine + k].astype(F32)
            send_ref[(k, *at)] = (keep[rest + k] + got[rest + k].astype(F32)).astype(LOW)


def fold(bit, place, *parts):
    under = [p.shape[1] for p in parts[2::2] if p.shape[1] < 16]
    cols = sum(p.shape[2] for k, p in enumerate(parts[::2]) if k == 0 or p.shape[1] >= 16)
    shape = (parts[0].shape[0] // 2, parts[0].shape[1] + sum(under), cols)
    return call(functools.partial(fold_kernel, bit), ((shape, F32), (shape, LOW)), place, *parts)


def add_kernel(a, b, out):
    out[...] = (a[...].astype(F32) + b[...].astype(F32)).astype(LOW)


def add_full_kernel(a, b, out):
    out[...] = a[...] + b[...]


def add_full(a, b):
    return call(add_full_kernel, ((a.shape, F32),), a, b)[0]


def add_low(a, b):
    return call(add_kernel, ((a.shape, LOW),), a, b)[0]


def to_slots(place, sum_ref, first, keep_ref, send_ref, bit=0):
    rows, cols = sum_ref.shape[0] // 8, keep_ref.shape[2]
    here = place[(7, 5, 6)[bit]] << bit
    for slot, owner in enumerate(((0, 4, 2, 6), (0, 1, 4, 5))[bit]):
        mine = pl.ds(pl.multiple_of((owner ^ here) * rows, rows), rows)
        rest = pl.ds(pl.multiple_of((owner ^ here ^ (1 << bit)) * rows, rows), rows)
        keep_ref[slot, :rows, :] = sum_ref[mine, first : first + cols]
        send_ref[slot, :rows, :] = sum_ref[rest, first : first + cols].astype(LOW)


def all_slots(place, sum_ref, blocks):
    first = 0
    for keep_ref, send_ref in zip(blocks[::2], blocks[1::2]):
        to_slots(place, sum_ref, first, keep_ref, send_ref)
        first += keep_ref.shape[2]


def product(left, right):
    return sum(dot(a[...], b[...], 0, 0) for a, b in zip(left, right))


def grad_kernel(count, place, *refs):
    sides, blocks, sum_ref = refs[:count], refs[count:-1], refs[-1]
    half = count // 2
    sum_ref[...] = product(sides[:half], sides[half:])
    all_slots(place, sum_ref, blocks)


def cot_grad_kernel(count, place, cot_zero, cot_one, hidden_zero, hidden_one, *refs):
    blocks, sum_ref = refs[:-1], refs[-1]
    rows = cot_zero.shape[1]
    left = [c[upper] for upper in range(2) for c in (cot_zero, cot_one)]
    right = [h[k * rows : (k + 1) * rows, :] for h in (hidden_zero, hidden_one) for k in range(2)]
    sum_ref[...] = sum(dot(a, b, 0, 0) for a, b in zip(left, right))
    all_slots(place, sum_ref, blocks)


def last_kernel(place, normed, dq_zero, dq_one, dk, dv, branch_zero, branch_one, att_zero, att_one, *refs):
    *blocks, sum_ref = refs
    half, cols = att_zero.shape
    sum_ref[:, :cols] = product((branch_zero, branch_one), (att_zero, att_one))
    sum_ref[:, cols : 2 * cols] = dot(normed[:half, :], dq_zero[...], 0, 0) + dot(normed[half:, :], dq_one[...], 0, 0)
    sum_ref[:, 2 * cols : 3 * cols] = dot(normed[...], dk[...], 0, 0)
    sum_ref[:, 3 * cols :] = dot(normed[...], dv[...], 0, 0)
    all_slots(place, sum_ref, blocks)


def slot_kernel(place, small, back_zero, back_one, up_zero, up_one, mixed_sums, keep_ref, send_ref, flat_ref):
    cols, wide_cols = mixed_sums.shape[1] // 3, keep_ref.shape[2]
    count = small.shape[0] - 2
    back = back_zero[...] + back_one[...]
    wide = [small[count : count + 1, :], small[count + 1 :, :], back[2:3], back[0:1], back[1:2], back[3:4]]
    wide += [up_zero[...] + up_one[...], mixed_sums[:, :cols], mixed_sums[:, 2 * cols :]]
    for owner in range(8):
        parts = []
        for v in wide:
            n = v.shape[1] // 8
            parts.append(v[:, owner * n : (owner + 1) * n])
        parts.append(jnp.zeros((1, 2 * wide_cols - sum(p.shape[1] for p in parts)), F32))
        flat_ref[owner : owner + 1, :] = jnp.concatenate(parts, axis=1)
    first = iota((8, wide_cols), 0) == 0
    for slot, owner in enumerate((0, 4, 2, 6)):
        mine, other = (flat_ref[pl.ds(owner ^ k ^ place[7], 1), :] for k in range(2))
        keep_ref[slot] = jnp.where(first, mine[:, :wide_cols], mine[:, wide_cols:])
        send_ref[slot] = jnp.where(first, other[:, :wide_cols], other[:, wide_cols:]).astype(LOW)


def finish_kernel(
    d_keep, d_got, e_keep, e_got, in_ref, proj_ref, gain_one, bias_one, proj_b, gain_two, bias_two, down_b, up_b, qv_b
):
    rows, cols = in_ref.shape[1:]
    one = d_keep[0] + d_got[0].astype(F32)
    two = e_keep[0] + e_got[0].astype(F32)
    proj_ref[...] = one[:, :cols].T
    in_ref[0] = one[:, cols:]
    in_ref[1] = two[:rows, :cols]
    in_ref[2] = two[:rows, cols:]
    flat = jnp.concatenate([two[rows : rows + 1, :], two[rows + 1 : rows + 2, :]], axis=1)
    first = 0
    for ref in (gain_one, bias_one, proj_b, gain_two, bias_two, down_b, up_b):
        ref[...] = flat[:, first : first + ref.shape[1]]
        first += ref.shape[1]
    count = qv_b.shape[1]
    qv_b[...] = jnp.concatenate([flat[:, first : first + count], flat[:, first + count : first + 2 * count]])


def parts_kernel(keep, got, one_ref, two_ref):
    cols = one_ref.shape[1]
    one_ref[...] = keep[0, :, :cols] + got[0, :, :cols].astype(F32)
    two_ref[...] = keep[0, :, cols:] + got[0, :, cols:].astype(F32)


def parted(keep, got):
    shape = (keep.shape[1], keep.shape[2] // 2)
    return call(parts_kernel, ((shape, F32),) * 2, keep, got)


def result_of(place, keep, got, res_zero, res_one, vecs):
    rows = keep.shape[0]
    residual = jnp.where(place[3] == 0, res_zero[:rows, :], res_one[:rows, :])
    return (residual + (keep[...] + got[...].astype(F32)) + vecs[5:6, :]).astype(LOW)


def result_kernel(place, keep, got, res_zero, res_one, vecs, out_ref):
    out_ref[...] = result_of(place, keep, got, res_zero, res_one, vecs)


def pick_kernel(place, own, other, out_ref):
    out_ref[place[3]] = own[...]
    out_ref[1 - place[3]] = other[...]


def pick(place, own, other):
    return call(pick_kernel, (((2, *own.shape), own.dtype),), place, own, other)[0]


def copy_kernel(*refs):
    half = len(refs) // 2
    for a, b in zip(refs[:half], refs[half:]):
        b[...] = a[...]


def brought(*arrays):
    return call(copy_kernel, tuple((a.shape, a.dtype) for a in arrays), *arrays)


def stack_kernel(a, b, out_ref):
    out_ref[0] = a[...]
    out_ref[1] = b[...]


def stacked(a, b):
    return call(stack_kernel, (((2, *a.shape), a.dtype),), a, b)[0]


def grad_blocks(kernel, place, splits, *sides):
    width, cols = sides[0].shape[-1], sides[-1].shape[1]
    shapes = []
    for n in splits:
        shapes += [((4, width // 8, n), F32), ((4, width // 8, n), LOW)]
    scratch = (pltpu.VMEM((width, cols), F32),)
    return call(functools.partial(kernel, len(sides)), shapes, place, *sides, scratch=scratch, mib=12)


def plain_grad(shard_rows, *sides):
    half = len(sides) // 2
    total = sum(dot(a, b, 0, 0) for a, b in zip(sides[:half], sides[half:])).astype(LOW)
    return dp_scatter_sum(total.reshape(-1, shard_rows, total.shape[1]))


def fast(shard_rows):
    return lax.axis_size("dp") == 8 and shard_rows % 16 == 0


def place_pieces(masks, place, pieces, write):
    for piece, owners in zip(pieces, masks):
        for k, mask in enumerate(owners):
            write(place[4] ^ mask, piece, k)


def first_kernel(masks, spans, hidden_cols, place, *refs):
    pieces, (w_in_ref, w_proj_ref, vecs_ref, up_ref, bias_ref, flat_ref) = refs[: len(masks)], refs[len(masks) :]
    width, qkv_cols = w_in_ref.shape
    shard_rows = width // 8

    def write(owner, piece, k):
        at = pl.ds(pl.multiple_of(owner * shard_rows, shard_rows), shard_rows)
        w_in_ref[at, :] = piece[k, :shard_rows, :qkv_cols]
        w_proj_ref[at, :] = piece[k, :shard_rows, qkv_cols:]
        flat_ref[pl.ds(owner, 1), :] = piece[k, shard_rows : shard_rows + 1, :].astype(F32)

    place_pieces(masks, place, pieces, write)
    flat = flat_ref[...]
    joined = [
        jnp.concatenate([flat[s : s + 1, a:b] for s in range(8)], axis=1) for a, b in zip(spans, spans[1:])
    ]
    for k in range(6):
        vecs_ref[k : k + 1, :] = joined[k]
    up_ref[...] = joined[6]
    bias_ref[...] = jnp.concatenate([joined[7], jnp.zeros_like(joined[7]), joined[8]], axis=1)


def plain_kernel(masks, place, *refs):
    out_ref = refs[-1]
    rows = out_ref.shape[0] // 8

    def write(owner, piece, k):
        out_ref[pl.ds(pl.multiple_of(owner * rows, rows), rows), :] = piece[k]

    place_pieces(masks, place, refs[:-1], write)


def pack_kernel(count, *refs):
    sources, out_ref, held, sems = refs[:count], refs[count], refs[count + 1 : -1], refs[-1]
    copies = [pltpu.make_async_copy(a, b, sems.at[k]) for k, (a, b) in enumerate(zip(sources, held))]
    for c in copies:
        c.start()
    for c in copies:
        c.wait()
    w_qkv, w_proj, *vectors = held
    rows = w_qkv.shape[1]
    out_ref[:rows, :] = jnp.concatenate([w_qkv[0], w_qkv[1], w_qkv[2], w_proj[...].T], axis=1)
    rows_of = [v[...].astype(F32) for v in vectors]
    rows_of = rows_of[:-1] + [rows_of[-1][0:1], rows_of[-1][1:2]]
    flat = jnp.concatenate(rows_of, axis=1)
    flat = jnp.concatenate([flat, jnp.zeros((1, out_ref.shape[1] - flat.shape[1]), F32)], axis=1)
    out_ref[rows:, :] = jnp.broadcast_to(flat, (8, flat.shape[1])).astype(LOW)


def first_pack(*args):
    w_qkv, w_proj = args[:2]
    return pl.pallas_call(
        functools.partial(pack_kernel, len(args)),
        out_shape=jax.ShapeDtypeStruct((w_qkv.shape[1] + 8, 3 * w_qkv.shape[2] + w_proj.shape[0]), LOW),
        in_specs=[pl.BlockSpec(memory_space=pl.ANY) for _ in args],
        out_specs=pl.BlockSpec(memory_space=pltpu.VMEM),
        scratch_shapes=[
            *(pltpu.VMEM(a.shape, a.dtype) for a in args),
            pltpu.SemaphoreType.DMA((len(args),)),
        ],
        compiler_params=pltpu.CompilerParams(vmem_limit_bytes=63 << 20),
        cost_estimate=pl.CostEstimate(flops=COST, bytes_accessed=0, transcendentals=0),
    )(*args)


def spans_of(vectors):
    spans = [0]
    for n in (*(v.shape[1] for v in vectors), vectors[-1].shape[1]):
        spans.append(spans[-1] + n)
    return spans


def first_unpacked(place, pieces, vectors, qkv_cols, head_cols, width):
    shapes = (
        ((width, qkv_cols), LOW),
        ((width, head_cols), LOW),
        ((6, width), F32),
        ((1, 8 * vectors[6].shape[1]), F32),
        ((1, qkv_cols), F32),
    )
    return call(
        functools.partial(first_kernel, MASKS, spans_of(vectors), 0),
        shapes,
        place,
        *pieces,
        scratch=(pltpu.VMEM((8, qkv_cols + head_cols), F32),),
    )


def unpacked(place, pieces):
    rows, cols = pieces[0].shape[1:]
    return call(functools.partial(plain_kernel, MASKS), (((8 * rows, cols), LOW),), place, *pieces)[0]


def plain_first(shard, vectors, qkv_cols, width):
    flat = dp_gather(jnp.concatenate([*vectors[:-1], vectors[-1][0:1], vectors[-1][1:2]], axis=1))[:, 0].astype(F32)
    whole = dp_gather(shard).reshape(width, -1)
    spans = spans_of(vectors)
    joined = [flat[:, a:b].reshape(1, -1) for a, b in zip(spans, spans[1:])]
    return (
        whole[:, :qkv_cols],
        whole[:, qkv_cols:],
        jnp.concatenate(joined[:6]),
        joined[6],
        jnp.concatenate([joined[7], jnp.zeros_like(joined[7]), joined[8]], axis=1),
    )


def down_kernel(hidden_zero, hidden_one, w_down, keep_ref, send_ref):
    rows = keep_ref.shape[1]
    for upper, hidden in enumerate((hidden_zero, hidden_one)):
        part = dot(hidden[...], w_down[...], 1, 1)
        keep_ref[upper] = part[:rows]
        send_ref[upper] = part[rows:].astype(LOW)


def local(x_embed, thoughts, thought_pos, img_start, *rest):
    *params, grad_out = rest
    dp = lax.axis_size("dp")
    table = []
    for d in range(dp):
        for t in range(4):
            table.append((t & 1, 0, 0, t >> 1, d, d >> 1 & 1, d >> 2 & 1, d & 1))
    place = jnp.asarray(table, jnp.int32)[lax.axis_index("dp") * 4 + lax.axis_index("tensor")]
    block = quick_block if fast(params[2].shape[1]) else plain_block
    block_out, grad_embed, grad_thoughts, grad_in, grad_proj, grad_up, grad_down, small = block(
        place, img_start[0], x_embed[0], thoughts[0], thought_pos, params, grad_out[0]
    )
    gain_one, bias_one, proj_b, gain_two, bias_two, down_b, up_b, qv_b = small
    flat = lambda a: a.reshape(-1)
    return (
        block_out[None],
        grad_embed[None],
        grad_thoughts,
        flat(gain_one),
        flat(bias_one),
        grad_in,
        qv_b.reshape(2, -1),
        grad_proj,
        flat(proj_b),
        flat(gain_two),
        flat(bias_two),
        grad_up,
        flat(up_b),
        grad_down,
        flat(down_b),
    )


def vectors_of(params):
    return [params[k].reshape(1, -1) for k in (0, 1, 5, 6, 7, 11, 9)] + [params[3]]


def splice_side(place, x_rows, thoughts, thought_pos):
    shape = (4 * x_rows[0].shape[1], x_rows[0].shape[2])
    return call(splice_kernel, ((shape, LOW), (shape, F32)), place, *x_rows, thoughts, thought_pos)


def input_side(xhat, vecs, w_in, bias):
    length, width = xhat.shape
    kinds = (((length, width), LOW),) + (((length, w_in.shape[1] // 3), LOW),) * 3
    return call(input_kernel, kinds, xhat, vecs, w_in, bias)


def input_back(place, thought_pos, grad_queries, grad_keys, grad_values, w_in, xhat, grad_residual):
    length, width = xhat.shape
    count = thought_pos.shape[1]
    return call(
        input_back_kernel,
        (
            ((2, length // 4, width), F32),
            ((2, length // 4, width), LOW),
            ((-(-(count + 2) // 8) * 8, width), F32),
            ((1, w_in.shape[1]), F32),
            ((-(-count // 8) * 8, width), F32),
        ),
        place,
        thought_pos[0],
        *grad_queries,
        grad_keys,
        grad_values,
        w_in,
        xhat,
        *grad_residual,
        scratch=(pltpu.VMEM((length, width), F32),),
    )


def output_side(place, keep, got, spliced, grad_residual, vecs, thought_pos, thoughts, small, picked, *pairs):
    rows, width = keep.shape
    embed, own, *more = call(
        output_kernel,
        (
            ((rows, width), F32),
            ((thoughts.shape[0], 1, width // 4), F32),
            *((p.shape[1:], F32) for p in pairs[::2]),
        ),
        place,
        keep,
        got,
        spliced,
        *grad_residual,
        vecs,
        thought_pos,
        thoughts,
        small,
        picked,
        *pairs,
    )
    return embed, jnp.moveaxis(own, 1, 0), *more


def result(place, keep, got, residual, vecs):
    return call(result_kernel, ((keep.shape, LOW),), place, keep, got, *residual, vecs)[0]


def down_part(hidden, w_down_t):
    shape = (2, hidden[0].shape[0] // 2, w_down_t.shape[0])
    return call(down_kernel, ((shape, F32), (shape, LOW)), *hidden, w_down_t)


def quick_block(place, starts, x_own, thoughts, thought_pos, params, cot_own):
    across = lambda a: swapped(a, "dp", 1)
    near = lambda a: swapped(a, "dp", 2)
    far = lambda a: swapped(a, "dp", 4)
    core = lambda a: swapped(a, "tensor", 1)
    over = lambda a: swapped(a, "tensor", 2)
    w_qkv, w_proj, w_up, w_down_own = params[2], params[4], params[8], params[10].T
    shard_rows, head_cols = w_qkv.shape[1:]
    width = x_own.shape[1]
    vectors = vectors_of(params)

    pack = first_pack(w_qkv, w_proj, *vectors)
    pack_far, pack_across = far(pack), across(pack)
    x_far = over(after(x_own, pack))
    pack_here, x_here = brought(pack, after(x_own, pack))
    x_far, pack_far, pack_across, pack_here, x_here = together(x_far, pack_far, pack_across, pack_here, x_here)

    pack_near, pack_far_across = near(stacked(pack_here, pack_far)), across(pack_far)
    up_far, up_across = far(after(w_up, pack_far)), across(after(w_up, pack_far))
    cot_far = over(after(cot_own, x_far))
    pack_near, pack_far_across, up_far, up_across, cot_far = together(
        pack_near, pack_far_across, up_far, up_across, cot_far
    )

    pack_near_across = across(pack_near)
    up_near = near(stacked(w_up, up_far))
    down_far = far(after(w_down_own, up_far))
    x_both = pick(place, x_here, after(x_far, up_far))
    x_other = core(x_both)
    spliced, xhat = splice_side(place, (x_both, x_other), thoughts, thought_pos)
    pack_near_across, xhat = together(pack_near_across, xhat)
    up_far_across, down_across = across(after(up_far, pack_near_across)), across(after(w_down_own, pack_near_across))
    pieces = (pack_here[None], pack_across[None], pack_far[None], pack_near, pack_far_across[None], pack_near_across)
    w_in, w_proj_t, vecs, up_bias, all_bias = first_unpacked(place, pieces, vectors, 3 * head_cols, head_cols, width)
    normed, queries, keys, values = input_side(xhat, vecs, w_in, all_bias)
    att_zero, log_zero, keep_zero, send_zero = attend(0, place, starts, queries, keys, values, w_proj_t)
    send_zero, up_near, down_far, up_far_across, down_across = together(
        send_zero, up_near, down_far, up_far_across, down_across
    )

    mine_zero = add_low(keep_zero, core(send_zero))
    far_zero = over(mine_zero)
    up_near_across, down_far_across = across(up_near), across(down_far)
    down_near = near(stacked(w_down_own, down_far))
    att_one, log_one, keep_one, send_one = attend(1, after(place, mine_zero), starts, queries, keys, values, w_proj_t)
    send_one, far_zero, up_near_across, down_far_across, down_near = together(
        send_one, far_zero, up_near_across, down_far_across, down_near
    )

    mine_one = add_low(keep_one, core(send_one))
    far_one = over(mine_one)
    total_zero = add_low(mine_zero, far_zero)
    other_zero = core(total_zero)
    down_near_across = across(down_near)
    pieces = (w_up[None], up_across[None], up_far[None], up_near, up_far_across[None], up_near_across)
    w_up_all = unpacked(place, pieces)
    cot_both = pick(place, cot_own, cot_far)
    cot_other = core(cot_both)
    other_zero, down_near_across, w_up_all, cot_other = together(other_zero, down_near_across, w_up_all, cot_other)
    cots = (cot_both, cot_other)
    pieces = (w_down_own[None], down_across[None], down_far[None], down_near, down_far_across[None], down_near_across)
    w_down_t = unpacked(place, pieces)

    weights = (vecs, up_bias, w_up_all, w_down_t)
    residual_zero, normed_zero, hidden_zero, grad_zero, up_sum_zero, keep_zero, send_zero = feed(
        0, spliced, total_zero, other_zero, cots, *weights
    )
    send_zero, far_one = together(send_zero, far_one)
    total_one = add_low(mine_one, far_one)
    other_one = core(total_one)
    mine_zero = add_low(keep_zero, core(send_zero))
    far_zero = over(mine_zero)
    residual_one, normed_one, hidden_one, grad_one, up_sum_one, keep_one, send_one = feed(
        1, after(spliced, mine_zero), total_one, other_one, cots, *weights
    )
    quarter = hidden_one.shape[1] // 3
    a_keep, a_send, b_keep, b_send = grad_blocks(
        grad_kernel, place, (quarter, 2 * quarter), normed_zero, normed_one, grad_zero, grad_one
    )
    a_got = across(a_send)
    mine_one = add_low(keep_one, core(send_one))
    c_keep, c_send = grad_blocks(
        cot_grad_kernel, after(place, a_send), (3 * quarter,), *cots, hidden_zero, hidden_one
    )
    mlp_keep, mlp_send = down_part((hidden_zero, after(hidden_one, a_send)), w_down_t)
    total_zero = add_low(after(mine_zero, a_got, c_send, mlp_send), far_zero)
    other_zero = core(total_zero)
    other_zero, mine_one = together(other_zero, mine_one)
    residual = (residual_zero, residual_one)

    far_one = over(mine_one)
    b_got = across(after(b_send, other_zero))
    mlp_got = core(after(mlp_send, other_zero))
    res_zero, branch_zero, gatt_zero, delta_zero, sums_zero = branch_back(
        0, total_zero, other_zero, residual_zero, cots, vecs, w_proj_t, att_zero
    )
    dq_zero, *early = back(0, place, starts, queries, keys, values, log_zero, gatt_zero, delta_zero, ())
    early[0], far_one, b_got, mlp_got = together(early[0], far_one, b_got, mlp_got)

    total_one = add_low(mine_one, far_one)
    other_one = core(total_one)
    c_got = across(after(c_send, b_got))
    mlp_keep, mlp_send = fold(3, place, mlp_keep, mlp_got)
    mlp_got = over(mlp_send)
    b_keep, b_send = fold(5, place, a_keep, a_got, b_keep, b_got)
    b_got = near(b_send)
    res_one, branch_one, gatt_one, delta_one, sums_one = branch_back(
        1, total_one, other_one, residual_one, cots, vecs, w_proj_t, att_one
    )
    dq_one, dk, dv = back(1, place, starts, queries, keys, values, log_one, gatt_one, delta_one, early)
    dk, b_got, c_got, mlp_got = together(dk, b_got, c_got, mlp_got)

    grad_residual = (res_zero, res_one)
    shapes = (((4, shard_rows, 2 * head_cols), F32), ((4, shard_rows, 2 * head_cols), LOW)) * 2
    d_keep, d_send, e_keep, e_send = call(
        last_kernel,
        shapes,
        place,
        normed,
        dq_zero,
        dq_one,
        dk,
        dv,
        branch_zero,
        branch_one,
        att_zero,
        att_one,
        scratch=(pltpu.VMEM((width, 4 * head_cols), F32),),
        mib=12,
    )
    d_got = across(d_send)
    c_keep, c_send = fold(5, place, c_keep, after(c_got, d_send))
    c_got = near(c_send)
    keep, send, small, mixed_sums, picked = input_back(
        place, thought_pos, (dq_zero, dq_one), after(dk, d_send), dv, w_in, xhat, grad_residual
    )
    small = add_full(small, core(small))
    small_got = over(small)
    small_got, d_got, c_got = together(small_got, d_got, c_got)

    e_got = across(after(e_send, d_got))
    got = core(after(send, d_got))
    keep, send = fold(3, place, keep, got)
    got = over(send)
    small = add_full(small, small_got)
    d_keep, d_send = fold(5, place, d_keep, d_got)
    d_got = near(d_send)
    b_keep, b_send = fold(6, place, b_keep, after(b_got, c_got), c_keep, c_got)
    b_got = far(b_send)
    shape = (4, 8, 2 * head_cols)
    vec_keep, vec_send = call(
        slot_kernel,
        ((shape, F32), (shape, LOW)),
        place,
        small,
        sums_zero,
        sums_one,
        up_sum_zero,
        up_sum_one,
        mixed_sums,
        scratch=(pltpu.VMEM((8, 4 * head_cols), F32),),
    )
    vec_got = across(vec_send)
    block_out = result(place, mlp_keep[0], mlp_got[0], residual, vecs)
    e_got, d_got, vec_got, block_out = together(e_got, d_got, vec_got, block_out)

    e_keep, e_send = fold(5, place, e_keep, e_got, vec_keep, vec_got)
    e_got = near(e_send)
    d_keep, d_send = fold(6, place, d_keep, d_got)
    d_got = far(d_send)
    grad_embed, grad_thoughts = output_side(
        place, keep[0], got[0], spliced, grad_residual, vecs, thought_pos, thoughts, small, picked
    )
    grad_embed, e_got, d_got, b_got = together(grad_embed, e_got, d_got, b_got)

    e_keep, e_send = fold(6, place, e_keep, e_got)
    e_got = far(e_send)
    grad_up, grad_down = parted(b_keep, b_got)
    grad_down, e_got = together(grad_down, e_got)
    grad_in, grad_proj, *small = call(
        finish_kernel,
        (
            ((3, shard_rows, head_cols), F32),
            ((head_cols, shard_rows), F32),
            *((v.shape, F32) for v in vectors),
        ),
        d_keep,
        d_got,
        e_keep,
        e_got,
    )
    return block_out, grad_embed, grad_thoughts, grad_in, grad_proj, grad_up, grad_down.T, small


def plain_block(place, starts, x_own, thoughts, thought_pos, params, cot_own):
    dp = lax.axis_size("dp")
    w_qkv, w_proj, w_up, w_down_own = params[2], params[4], params[8], params[10].T
    shard_rows, head_cols = w_qkv.shape[1:]
    width = x_own.shape[1]
    x_rows, cots = rows_gather(x_own), rows_gather(cot_own)
    shard = jnp.concatenate([w_qkv[0], w_qkv[1], w_qkv[2], w_proj.T], axis=1)
    w_in, w_proj_t, vecs, up_bias, all_bias = plain_first(shard, vectors_of(params), 3 * head_cols, width)
    w_up_all = dp_gather(w_up).reshape(width, -1)
    w_down_t = dp_gather(w_down_own).reshape(width, -1)
    spliced, xhat = splice_side(place, x_rows, thoughts, thought_pos)
    normed, queries, keys, values = input_side(xhat, vecs, w_in, all_bias)

    def all_sum(keep, send):
        mine = add_low(keep, swapped(send, "tensor", 1))
        total = add_low(mine, swapped(mine, "tensor", 2))
        return total, swapped(total, "tensor", 1)

    def own_sum(keep, send):
        keep, send = fold(3, place, keep, swapped(send, "tensor", 1))
        return keep[0], swapped(send, "tensor", 2)[0]

    atts, logs, feds, grad_twos = [], [], [], []
    for chunk in range(2):
        att, log, *part = attend(chunk, place, starts, queries, keys, values, w_proj_t)
        feds.append(feed(chunk, spliced, *all_sum(*part), cots, vecs, up_bias, w_up_all, w_down_t))
        grad_twos.append(all_sum(*feds[-1][5:]))
        atts.append(att)
        logs.append(log)
    residual, normed_two, hidden, grad_hidden, up_sums = zip(feds[0][:5], feds[1][:5])
    block_out = result(place, *own_sum(*down_part(hidden, w_down_t)), residual, vecs)
    grad_up = plain_grad(shard_rows, *normed_two, *grad_hidden)
    grad_down = plain_grad(shard_rows, cots_rows(cots, 0), cots_rows(cots, 1), *hidden)
    branches, dqs, early = [], [], ()
    for chunk in range(2):
        branches.append(
            branch_back(chunk, *grad_twos[chunk], residual[chunk], cots, vecs, w_proj_t, atts[chunk])
        )
        dq, *early = back(
            chunk, place, starts, queries, keys, values, logs[chunk], *branches[-1][2:4], early
        )
        dqs.append(dq)
    grad_residual, grad_branch = zip(branches[0][:2], branches[1][:2])
    keep, send, small, mixed_sums, picked = input_back(
        place, thought_pos, dqs, *early, w_in, xhat, grad_residual
    )
    grad_mixed = jnp.concatenate([jnp.concatenate(dqs), *early], axis=1)
    small = small + swapped(small, "tensor", 1)
    small = small + swapped(small, "tensor", 2)
    grad_embed, grad_thoughts = output_side(
        place, *own_sum(keep, send), spliced, grad_residual, vecs, thought_pos, thoughts, small, picked
    )
    grad_in = plain_grad(shard_rows, normed, grad_mixed).reshape(shard_rows, 3, head_cols)
    grad_proj = plain_grad(shard_rows, *grad_branch, *atts)
    two = branches[0][4] + branches[1][4]
    count = small.shape[0] - 2
    vec = (small[count], small[count + 1], two[2], two[0], two[1], two[3], up_sums[0] + up_sums[1])
    vec += (mixed_sums[0, :head_cols], mixed_sums[0, 2 * head_cols :])
    vec = jnp.concatenate([v.reshape(dp, -1) for v in vec], axis=1)
    vec = dp_scatter_sum(vec[:, None, :])[0]
    small, first = [], 0
    for n in (params[k].size for k in (0, 1, 5, 6, 7, 11, 9, 3)):
        small.append(vec[first : first + n])
        first += n
    return (
        block_out,
        grad_embed,
        grad_thoughts,
        jnp.moveaxis(grad_in, 1, 0),
        grad_proj.T,
        grad_up,
        grad_down.T,
        small,
    )


def solution(mesh):
    in_specs = (
        P("dp", "tensor", None),
        P("dp", None, None),
        P("dp", None),
        P("dp", None),
        P("dp"),
        P("dp"),
        P(None, "dp", "tensor"),
        P(None, ("tensor", "dp")),
        P("tensor", "dp"),
        P("dp"),
        P("dp"),
        P("dp"),
        P("dp", "tensor"),
        P(("tensor", "dp")),
        P("tensor", "dp"),
        P("dp"),
        P("dp", "tensor", None),
    )
    out_specs = (
        P("dp", "tensor", None),
        P("dp", "tensor", None),
        P("dp", None, "tensor"),
        P("dp"),
        P("dp"),
        P(None, "dp", "tensor"),
        P(None, ("tensor", "dp")),
        P("tensor", "dp"),
        P("dp"),
        P("dp"),
        P("dp"),
        P("dp", "tensor"),
        P(("tensor", "dp")),
        P("tensor", "dp"),
        P("dp"),
    )
    return jax.shard_map(local, mesh=mesh, in_specs=in_specs, out_specs=out_specs, check_vma=False)
```

```python
import functools

import jax
import jax.numpy as jnp
from jax import lax
from jax.experimental import pallas as pl
from jax.experimental.pallas import tpu as pltpu
from jax.sharding import PartitionSpec as P

HD = 64
IMG = 256
EPSILON = 1e-05
F32 = jnp.float32
LOW = jnp.bfloat16
COST = 1000


def swapped(array, axis, mask):
    return lax.ppermute(array, axis, [(i, i ^ mask) for i in range(lax.axis_size(axis))])


def dp_masks():
    return [1 << b for b in reversed(range(lax.axis_size("dp").bit_length() - 1))]


def slot_owners(masks):
    owners = [0]
    for mask in masks:
        owners = owners + [o ^ mask for o in owners]
    return owners


def dp_gather(shard):
    masks, me = dp_masks(), lax.axis_index("dp")
    slots = shard[None]
    for mask in masks:
        other = swapped(slots, "dp", mask)
        first = (me & mask) == 0
        slots = jnp.where(
            first, jnp.concatenate([slots, other]), jnp.concatenate([other, slots])
        )
    owners = slot_owners(masks)
    return jnp.stack([slots[owners.index(s)] for s in range(len(owners))])


MASKS = ((0,), (1,), (4,), (2, 6), (5,), (3, 7))


def rows_pick(own, other):
    first = (lax.axis_index("tensor") >> 1) == 0
    return jnp.stack([jnp.where(first, own, other), jnp.where(first, other, own)])


def dp_scatter_sum(blocks):
    masks, me = dp_masks(), lax.axis_index("dp")
    slots = jnp.stack([blocks[s] for s in slot_owners(masks)])
    for mask in reversed(masks):
        half = slots.shape[0] // 2
        first = (me & mask) == 0
        keep = jnp.where(first, slots[:half], slots[half:])
        send = jnp.where(first, slots[half:], slots[:half])
        slots = keep.astype(F32) + swapped(send, "dp", mask).astype(F32)
    return slots[0]


def rows_gather(own):
    both = rows_pick(own, swapped(own, "tensor", 2))
    return both, swapped(both, "tensor", 1)


def after(value, *others):
    return lax.optimization_barrier((value, *others))[0]


def together(*values):
    return lax.optimization_barrier(values)


def dot(a, b, ca, cb, precision=None):
    return lax.dot_general(
        a, b, (((ca,), (cb,)), ((), ())), precision=precision, preferred_element_type=F32
    )


def normalised(values):
    centred = values - jnp.mean(values, axis=-1, keepdims=True)
    inverse = lax.rsqrt(jnp.mean(centred * centred, axis=-1, keepdims=True) + EPSILON)
    return centred * inverse, inverse


def norm_back(upstream, xhat, inverse, gain):
    scaled = upstream * gain
    return inverse * (
        scaled
        - jnp.mean(scaled, axis=-1, keepdims=True)
        - xhat * jnp.mean(scaled * xhat, axis=-1, keepdims=True)
    )


def gelu_pair(u):
    k, a = 0.7978845608028654, 0.044715
    square = u * u
    t = jnp.tanh(u * (k + (k * a) * square))
    rise = 0.5 * (1.0 + t)
    return u * rise, rise + (0.5 * u) * (1.0 - t * t) * (k + (3.0 * k * a) * square)


def cots_rows(cots, chunk):
    return jnp.concatenate([c[chunk] for c in cots])


def iota(shape, dim):
    return lax.broadcasted_iota(jnp.int32, shape, dim)


def call(kernel, outs, *args, scratch=(), mib=8, cost=0):
    spec = lambda a: pl.BlockSpec(
        memory_space=pltpu.SMEM if a.ndim == 1 and a.dtype == jnp.int32 else pltpu.VMEM
    )
    return pl.pallas_call(
        kernel,
        out_shape=tuple(jax.ShapeDtypeStruct(s, t) for s, t in outs),
        in_specs=[spec(a) for a in args],
        out_specs=tuple(pl.BlockSpec(memory_space=pltpu.VMEM) for _ in outs),
        scratch_shapes=scratch,
        compiler_params=pltpu.CompilerParams(vmem_limit_bytes=mib << 20),
        cost_estimate=pl.CostEstimate(flops=COST + cost, bytes_accessed=0, transcendentals=0),
    )(*args)


def splice_kernel(place, x_zero, x_one, thoughts, thought_pos, spliced_ref, xhat_ref):
    core = place[0]
    rows = x_zero.shape[1]
    for upper in range(2):
        for rel, ref in enumerate((x_zero, x_one)):
            first = upper * 2 * rows + (core ^ rel) * rows
            part = slice((2 * upper + rel) * rows, (2 * upper + rel + 1) * rows)
            match = (first + iota((rows, 1), 0)) == thought_pos[...]
            covered = jnp.sum(match.astype(F32), axis=1, keepdims=True) > 0.0
            picked = dot(match.astype(LOW), thoughts[...], 1, 0)
            spliced = jnp.where(covered, picked, ref[upper].astype(F32))
            spliced_ref[part, :] = spliced.astype(LOW)
            xhat_ref[part, :] = normalised(spliced)[0]


def input_kernel(xhat, vecs, w_in, bias, normed_ref, q_ref, k_ref, v_ref):
    rows = xhat.shape[0] // 4
    cols = q_ref.shape[1]
    for k in range(4):
        part = slice(k * rows, (k + 1) * rows)
        normed = (xhat[part, :] * vecs[0:1, :] + vecs[1:2, :]).astype(LOW)
        normed_ref[part, :] = normed
        mixed = (dot(normed, w_in[...], 1, 0) + bias[...]).astype(LOW)
        q_ref[part, :] = mixed[:, :cols]
        k_ref[part, :] = mixed[:, cols : 2 * cols]
        v_ref[part, :] = mixed[:, 2 * cols :]


def query_limits(place, starts, chunk, rows):
    core, start = place[0], starts[chunk]
    col = iota((1, 2 * rows), 1)
    query = 2 * rows * chunk + jnp.where(col < rows, col + core * rows, col - core * rows)
    inside = (query >= start) & (query < start + IMG)
    return jnp.where(inside, start + (IMG - 1), query)


def key_positions(place, block, rows):
    first = (block >> 1) * (2 * rows) + (place[0] ^ (block & 1)) * rows
    return first + iota((rows, 1), 0)


def attend_kernel(
    chunk, place, starts, q_ref, k_ref, v_ref, w_proj,
    att_ref, log_ref, keep_ref, send_ref, acc_ref, top_ref, sum_ref,
):
    half, cols = att_ref.shape
    rows = half // 2
    heads = cols // HD
    head_of = iota((1, cols), 1) // HD
    limits = query_limits(place, starts, chunk, rows)
    queries = q_ref[chunk * half : (chunk + 1) * half, :] * LOW(0.125)
    acc_ref[...] = jnp.zeros_like(acc_ref)
    top_ref[...] = jnp.full_like(top_ref, -1e30)
    sum_ref[...] = jnp.zeros_like(sum_ref)

    @pl.loop(0, 2 * chunk + 2)
    def _(block):
        span = pl.ds(pl.multiple_of(block * rows, rows), rows)
        keys = k_ref[span, :]
        values = v_ref[span, :].T
        allowed = key_positions(place, block, rows) <= limits
        for head in range(heads):
            scores = dot(jnp.where(head_of == head, keys, LOW(0)), queries, 1, 1)
            scores = jnp.where(allowed, scores, -1e30)
            top = top_ref[head : head + 1, :]
            new_top = jnp.maximum(top, jnp.max(scores, axis=0, keepdims=True))
            exps = jnp.exp(scores - new_top)
            fade = jnp.exp(top - new_top)
            top_ref[head : head + 1, :] = new_top
            sum_ref[head : head + 1, :] = sum_ref[head : head + 1, :] * fade + jnp.sum(
                exps, axis=0, keepdims=True
            )
            part = slice(head * HD, (head + 1) * HD)
            acc_ref[part, :] = acc_ref[part, :] * fade + dot(values[part, :], exps.astype(LOW), 1, 0)

    for head in range(heads):
        part = slice(head * HD, (head + 1) * HD)
        acc_ref[part, :] = acc_ref[part, :] / sum_ref[head : head + 1, :]
    log_ref[...] = top_ref[...] + jnp.log(jnp.maximum(sum_ref[...], 1e-30))
    attended = acc_ref[...].T.astype(LOW)
    att_ref[...] = attended
    branch = dot(attended, w_proj[...], 1, 1)
    keep_ref[...] = branch[:rows]
    send_ref[...] = branch[rows:].astype(LOW)


def attend(chunk, place, starts, queries, keys, values, w_proj):
    length, cols = queries.shape
    half, width = length // 2, w_proj.shape[0]
    return call(
        functools.partial(attend_kernel, chunk),
        (
            ((half, cols), LOW),
            ((8, half), F32),
            ((half // 2, width), F32),
            ((half // 2, width), LOW),
        ),
        place,
        starts,
        queries,
        keys,
        values,
        w_proj,
        scratch=(
            pltpu.VMEM((cols, half), F32),
            pltpu.VMEM((8, half), F32),
            pltpu.VMEM((8, half), F32),
        ),
    )


def feed_kernel(
    chunk, spliced, total, other, cot_zero, cot_one, vecs, up_bias, w_up, w_down,
    residual_ref, normed_ref, hidden_ref, grad_ref, sum_ref, keep_ref, send_ref,
):
    half, width = residual_ref.shape
    rows = half // 2
    for rel, ref in enumerate((total, other)):
        part = slice(rel * rows, (rel + 1) * rows)
        residual = (
            spliced[chunk * half + rel * rows : chunk * half + (rel + 1) * rows, :].astype(F32)
            + ref[...].astype(F32)
            + vecs[2:3, :]
        )
        residual_ref[part, :] = residual
        xhat, _ = normalised(residual)
        normed_ref[part, :] = (xhat * vecs[3:4, :] + vecs[4:5, :]).astype(LOW)
    hidden_cols = w_up.shape[1]
    step = 256 if hidden_cols % 256 == 0 else hidden_cols
    for first in range(0, hidden_cols, step):
        cols = slice(first, first + step)
        hidden, slope = gelu_pair(dot(normed_ref[...], w_up[:, cols], 1, 0) + up_bias[:, cols])
        hidden_ref[:, cols] = hidden.astype(LOW)
        back = jnp.concatenate(
            [dot(cot_zero[chunk], w_down[:, cols], 1, 0), dot(cot_one[chunk], w_down[:, cols], 1, 0)]
        )
        grad = (back * slope).astype(LOW)
        grad_ref[:, cols] = grad
        sum_ref[:, cols] = jnp.sum(grad.astype(F32), axis=0, keepdims=True)
    back = dot(grad_ref[...], w_up[...], 1, 1)
    keep_ref[...] = back[:rows]
    send_ref[...] = back[rows:].astype(LOW)


def feed(chunk, spliced, total, other, cots, vecs, up_bias, w_up, w_down):
    length, width = spliced.shape
    half, hidden = length // 2, w_up.shape[1]
    return call(
        functools.partial(feed_kernel, chunk),
        (
            ((half, width), F32),
            ((half, width), LOW),
            ((half, hidden), LOW),
            ((half, hidden), LOW),
            ((1, hidden), F32),
            ((half // 2, width), F32),
            ((half // 2, width), LOW),
        ),
        spliced,
        total,
        other,
        *cots,
        vecs,
        up_bias,
        w_up,
        w_down,
    )


def norm_back_kernel(
    chunk, total, other, residual, cot_zero, cot_one, vecs, w_proj, att,
    grad_res_ref, branch_ref, gatt_ref, delta_ref, sums_ref,
):
    half, width = residual.shape
    rows = half // 2
    gain = vecs[3:4, :]
    sums = [0.0, 0.0, 0.0, 0.0]
    for rel, (ref, cot) in enumerate(((total, cot_zero), (other, cot_one))):
        part = slice(rel * rows, (rel + 1) * rows)
        upstream = ref[...].astype(F32)
        xhat, inverse = normalised(residual[part, :])
        out_grad = cot[chunk].astype(F32)
        grad_res = out_grad + norm_back(upstream, xhat, inverse, gain)
        grad_res_ref[part, :] = grad_res
        branch_ref[part, :] = grad_res.astype(LOW)
        for k, term in enumerate((upstream * xhat, upstream, grad_res, out_grad)):
            sums[k] = sums[k] + jnp.sum(term, axis=0, keepdims=True)
    for k in range(4):
        sums_ref[k : k + 1, :] = sums[k]
    grad_att = dot(branch_ref[...], w_proj[...], 1, 0).astype(LOW)
    gatt_ref[...] = grad_att
    cols = att.shape[1]
    head_rows = (iota((8, cols), 0) == iota((8, cols), 1) // HD).astype(F32)
    delta_ref[...] = dot(
        head_rows, grad_att.astype(F32) * att[...].astype(F32), 1, 1, lax.Precision.HIGHEST
    )


def branch_back(chunk, total, other, residual, cots, vecs, w_proj, att):
    half, width = residual.shape
    cols = att.shape[1]
    return call(
        functools.partial(norm_back_kernel, chunk),
        (((half, width), F32), ((half, width), LOW), ((half, cols), LOW), ((8, half), F32), ((8, width), F32)),
        total,
        other,
        residual,
        *cots,
        vecs,
        w_proj,
        att,
    )


def back_kernel(chunk, place, starts, q_ref, k_ref, v_ref, log, gatt_ref, delta_ref, *rest):
    keys_in, rest = (rest[:2], rest[2:]) if chunk else ((), rest)
    dq_ref, dk_ref, dv_ref, dqt_ref = rest
    half, cols = gatt_ref.shape
    rows = half // 2
    heads = cols // HD
    head_of = iota((1, cols), 1) // HD
    limits = query_limits(place, starts, chunk, rows)
    dqt_ref[...] = jnp.zeros_like(dqt_ref)

    @pl.loop(0, 2 * chunk + 2)
    def _(block):
        span = pl.ds(pl.multiple_of(block * rows, rows), rows)
        keys, values = k_ref[span, :], v_ref[span, :]
        keys_t = keys.T
        queries = q_ref[chunk * half : (chunk + 1) * half, :] * LOW(0.125)
        grad_att = gatt_ref[...]
        allowed = key_positions(place, block, rows) <= limits
        dk = jnp.zeros((rows, cols), F32)
        dv = jnp.zeros((rows, cols), F32)
        for head in range(heads):
            mine = head_of == head
            scores = dot(jnp.where(mine, keys, LOW(0)), queries, 1, 1)
            probs = jnp.exp(jnp.where(allowed, scores, -1e30) - log[head : head + 1, :])
            grad_probs = dot(jnp.where(mine, values, LOW(0)), grad_att, 1, 1)
            grad_scores = (probs * (grad_probs - delta_ref[head : head + 1, :])).astype(LOW)
            dv = dv + dot(probs.astype(LOW), jnp.where(mine, grad_att, LOW(0)), 1, 0)
            dk = dk + dot(grad_scores, jnp.where(mine, queries, LOW(0)), 1, 0)
            part = slice(head * HD, (head + 1) * HD)
            dqt_ref[part, :] = dqt_ref[part, :] + dot(keys_t[part, :], grad_scores, 1, 0)
        if chunk:
            seen = jnp.where(block < 2, 1.0, 0.0)
            early = pl.ds(pl.multiple_of((block & 1) * rows, rows), rows)
            dk = dk + keys_in[0][early, :] * seen
            dv = dv + keys_in[1][early, :] * seen
        dk_ref[span, :] = dk.astype(dk_ref.dtype)
        dv_ref[span, :] = dv.astype(dv_ref.dtype)

    dq_ref[...] = (dqt_ref[...] * 0.125).T.astype(LOW)


def back(chunk, place, starts, queries, keys, values, log, grad_att, delta, early):
    half, cols = grad_att.shape
    kind = (((half * (chunk + 1), cols), LOW if chunk else F32),) * 2
    return call(
        functools.partial(back_kernel, chunk),
        (((half, cols), LOW), *kind),
        place,
        starts,
        queries,
        keys,
        values,
        log,
        grad_att,
        delta,
        *early,
        scratch=(pltpu.VMEM((cols, half), F32),),
    )


def input_back_kernel(
    place, thought_pos, dq_zero, dq_one, dk, dv, w_in, xhat, res_zero, res_one,
    keep_ref, low_ref, high_ref, small_ref, colsum_ref, picked_ref, grad_ref,
):
    half, cols = dq_zero.shape
    rows = half // 2
    sums = [0.0, 0.0, 0.0]
    for upper, dq in enumerate((dq_zero, dq_one)):
        for rel in range(2):
            part = slice((2 * upper + rel) * rows, (2 * upper + rel + 1) * rows)
            mixed = jnp.concatenate(
                [dq[rel * rows : (rel + 1) * rows, :], dk[part, :], dv[part, :]], axis=1
            )
            grad = dot(mixed, w_in[...], 1, 1)
            grad_ref[part, :] = grad
            if rel:
                (low_ref, high_ref)[upper][...] = grad.astype(LOW)
            else:
                keep_ref[upper] = grad
            terms = (grad * xhat[part, :], grad, mixed.astype(F32))
            sums = [a + jnp.sum(b, axis=0, keepdims=True) for a, b in zip(sums, terms)]
    small_ref[...] = jnp.zeros_like(small_ref)
    picked_ref[...] = jnp.zeros_like(picked_ref)
    count = thought_pos.shape[0]
    for k in range(count):
        at = thought_pos[k]
        row = (at // half) * half + (((at // rows) & 1) ^ place[0]) * rows + at % rows
        small_ref[k : k + 1, :] = grad_ref[pl.ds(row, 1), :]
        low = res_zero[pl.ds(jnp.minimum(row, half - 1), 1), :]
        high = res_one[pl.ds(jnp.maximum(row - half, 0), 1), :]
        picked_ref[k : k + 1, :] = jnp.where(row < half, low, high)
    small_ref[count : count + 1, :] = sums[0]
    small_ref[count + 1 : count + 2, :] = sums[1]
    colsum_ref[...] = sums[2]


def output_kernel(place, keep, got, spliced, res_zero, res_one, vecs, thought_pos, thoughts, small, picked, *rest):
    pairs, (embed_ref, rows_ref, *more) = rest[: 2 * ((len(rest) - 2) // 3)], rest[2 * ((len(rest) - 2) // 3) :]
    rows = keep.shape[0]
    gain = vecs[0:1, :]
    own = pl.ds(pl.multiple_of(place[3] * (2 * rows), 2 * rows), rows)
    xhat, inverse = normalised(spliced[own, :].astype(F32))
    residual = jnp.where(place[3] == 0, res_zero[:rows, :], res_one[:rows, :])
    grad = norm_back(keep[...] + got[...].astype(F32), xhat, inverse, gain) + residual
    at = (2 * place[3] + place[0]) * rows + iota((rows, 1), 0)
    covered = jnp.sum((at == thought_pos[...]).astype(F32), axis=1, keepdims=True) > 0.0
    embed_ref[...] = jnp.where(covered, 0.0, grad)
    count = thoughts.shape[0]
    xhat, inverse = normalised(thoughts[...].astype(F32))
    grad = norm_back(small[:count, :], xhat, inverse, gain) + picked[:count, :]
    cols = rows_ref.shape[2]
    rank = 2 * place[3] + place[0]
    grad = sum(jnp.where(rank == k, 1.0, 0.0) * grad[:, k * cols : (k + 1) * cols] for k in range(4))
    for k in range(count):
        rows_ref[k] = grad[k : k + 1, :]
    for ref, keep, got in zip(more, pairs[::2], pairs[1::2]):
        ref[...] = keep[0] + got[0].astype(F32)


def fold_kernel(bit, place, *refs):
    *parts, keep_ref, send_ref = refs
    half = keep_ref.shape[0]
    mine = place[bit] * half
    rest = half - mine
    first = 0
    for keep, got in zip(parts[::2], parts[1::2]):
        rows, cols = keep.shape[1:]
        below = rows < 16 and first > 0
        if below:
            at = (slice(keep_ref.shape[1] - rows, None), slice(0, cols))
        else:
            at = (slice(0, rows), slice(first, first + cols))
            first += cols
        for k in range(half):
            keep_ref[(k, *at)] = keep[mine + k] + got[mine + k].astype(F32)
            send_ref[(k, *at)] = (keep[rest + k] + got[rest + k].astype(F32)).astype(LOW)


def fold(bit, place, *parts):
    under = [p.shape[1] for p in parts[2::2] if p.shape[1] < 16]
    cols = sum(p.shape[2] for k, p in enumerate(parts[::2]) if k == 0 or p.shape[1] >= 16)
    shape = (parts[0].shape[0] // 2, parts[0].shape[1] + sum(under), cols)
    return call(functools.partial(fold_kernel, bit), ((shape, F32), (shape, LOW)), place, *parts)


def fold_two_kernel(bit, place, keep, low, high, keep_ref, send_ref):
    first = place[bit] == 0
    low, high = keep[0] + low[...].astype(F32), keep[1] + high[...].astype(F32)
    keep_ref[...] = jnp.where(first, low, high)
    send_ref[...] = jnp.where(first, high, low).astype(LOW)


def fold_two(bit, place, keep, low, high):
    kinds = ((low.shape, F32), (low.shape, LOW))
    return call(functools.partial(fold_two_kernel, bit), kinds, place, keep, low, high)


def add_kernel(a, b, out):
    out[...] = (a[...].astype(F32) + b[...].astype(F32)).astype(LOW)


def add_full_kernel(a, b, out):
    out[...] = a[...] + b[...]


def add_full(a, b):
    return call(add_full_kernel, ((a.shape, F32),), a, b)[0]


def add_low(a, b, cost=0):
    return call(add_kernel, ((a.shape, LOW),), a, b, cost=cost)[0]


def to_slots(place, sum_ref, first, keep_ref, send_ref, bit=0):
    rows, cols = sum_ref.shape[0] // 8, keep_ref.shape[2]
    here = place[(7, 5, 6)[bit]] << bit
    for slot, owner in enumerate(((0, 4, 2, 6), (0, 1, 4, 5))[bit]):
        mine = pl.ds(pl.multiple_of((owner ^ here) * rows, rows), rows)
        rest = pl.ds(pl.multiple_of((owner ^ here ^ (1 << bit)) * rows, rows), rows)
        keep_ref[slot, :rows, :] = sum_ref[mine, first : first + cols]
        send_ref[slot, :rows, :] = sum_ref[rest, first : first + cols].astype(LOW)


def all_slots(place, sum_ref, blocks):
    first = 0
    for keep_ref, send_ref in zip(blocks[::2], blocks[1::2]):
        to_slots(place, sum_ref, first, keep_ref, send_ref)
        first += keep_ref.shape[2]


def product(left, right):
    return sum(dot(a[...], b[...], 0, 0) for a, b in zip(left, right))


def grad_kernel(count, place, *refs):
    sides, blocks, sum_ref = refs[:count], refs[count:-1], refs[-1]
    half = count // 2
    sum_ref[...] = product(sides[:half], sides[half:])
    all_slots(place, sum_ref, blocks)


def cot_grad_kernel(count, place, cot_zero, cot_one, hidden_zero, hidden_one, *refs):
    blocks, sum_ref = refs[:-1], refs[-1]
    rows = cot_zero.shape[1]
    left = [c[upper] for upper in range(2) for c in (cot_zero, cot_one)]
    right = [h[k * rows : (k + 1) * rows, :] for h in (hidden_zero, hidden_one) for k in range(2)]
    sum_ref[...] = sum(dot(a, b, 0, 0) for a, b in zip(left, right))
    all_slots(place, sum_ref, blocks)


def last_kernel_one(place, normed, dq_zero, dq_one, branch_zero, branch_one, att_zero, att_one, *refs):
    *blocks, sum_ref = refs
    half, cols = att_zero.shape
    sum_ref[:, :cols] = product((branch_zero, branch_one), (att_zero, att_one))
    sum_ref[:, cols:] = dot(normed[:half, :], dq_zero[...], 0, 0) + dot(normed[half:, :], dq_one[...], 0, 0)
    all_slots(place, sum_ref, blocks)


def last_kernel_two(
    place, normed, dk, dv, small, back_zero, back_one, up_zero, up_one, mixed_sums, keep_ref, send_ref, sum_ref, flat_ref
):
    cols = dk.shape[1]
    sum_ref[:, :cols] = dot(normed[...], dk[...], 0, 0)
    sum_ref[:, cols:] = dot(normed[...], dv[...], 0, 0)
    to_slots(place, sum_ref, 0, keep_ref, send_ref)
    rows, wide_cols = keep_ref.shape[1] - 8, keep_ref.shape[2]
    count = small.shape[0] - 2
    back = back_zero[...] + back_one[...]
    wide = [small[count : count + 1, :], small[count + 1 :, :], back[2:3], back[0:1], back[1:2], back[3:4]]
    wide += [up_zero[...] + up_one[...], mixed_sums[:, :cols], mixed_sums[:, 2 * cols :]]
    for owner in range(8):
        parts = []
        for v in wide:
            n = v.shape[1] // 8
            parts.append(v[:, owner * n : (owner + 1) * n])
        parts.append(jnp.zeros((1, 2 * wide_cols - sum(p.shape[1] for p in parts)), F32))
        flat_ref[owner : owner + 1, :] = jnp.concatenate(parts, axis=1)
    first = iota((8, wide_cols), 0) == 0
    for slot, owner in enumerate((0, 4, 2, 6)):
        mine, other = (flat_ref[pl.ds(owner ^ k ^ place[7], 1), :] for k in range(2))
        keep_ref[slot, rows:, :] = jnp.where(first, mine[:, :wide_cols], mine[:, wide_cols:])
        send_ref[slot, rows:, :] = jnp.where(first, other[:, :wide_cols], other[:, wide_cols:]).astype(LOW)


def finish_kernel(
    d_keep, d_got, e_keep, e_got, in_ref, proj_ref, gain_one, bias_one, proj_b, gain_two, bias_two, down_b, up_b, qv_b
):
    rows, cols = in_ref.shape[1:]
    one = d_keep[0] + d_got[0].astype(F32)
    two = e_keep[0] + e_got[0].astype(F32)
    proj_ref[...] = one[:, :cols].T
    in_ref[0] = one[:, cols:]
    in_ref[1] = two[:rows, :cols]
    in_ref[2] = two[:rows, cols:]
    flat = jnp.concatenate([two[rows : rows + 1, :], two[rows + 1 : rows + 2, :]], axis=1)
    first = 0
    for ref in (gain_one, bias_one, proj_b, gain_two, bias_two, down_b, up_b):
        ref[...] = flat[:, first : first + ref.shape[1]]
        first += ref.shape[1]
    count = qv_b.shape[1]
    qv_b[...] = jnp.concatenate([flat[:, first : first + count], flat[:, first + count : first + 2 * count]])


def result_of(place, keep, got, res_zero, res_one, vecs):
    rows = keep.shape[0]
    residual = jnp.where(place[3] == 0, res_zero[:rows, :], res_one[:rows, :])
    return (residual + (keep[...] + got[...].astype(F32)) + vecs[5:6, :]).astype(LOW)


def result_kernel(place, keep, got, res_zero, res_one, vecs, out_ref):
    out_ref[...] = result_of(place, keep, got, res_zero, res_one, vecs)


def pick_kernel(place, own, other, out_ref):
    out_ref[place[3]] = own[...]
    out_ref[1 - place[3]] = other[...]


def pick(place, own, other):
    return call(pick_kernel, (((2, *own.shape), own.dtype),), place, own, other)[0]


def copy_kernel(*refs):
    half = len(refs) // 2
    for a, b in zip(refs[:half], refs[half:]):
        b[...] = a[...]


def brought(*arrays, cost=0):
    return call(copy_kernel, tuple((a.shape, a.dtype) for a in arrays), *arrays, cost=cost)


def stack_kernel(a, b, out_ref):
    out_ref[0] = a[...]
    out_ref[1] = b[...]


def stacked(a, b):
    return call(stack_kernel, (((2, *a.shape), a.dtype),), a, b)[0]


def grad_blocks(kernel, place, splits, *sides):
    width, cols = sides[0].shape[-1], sides[-1].shape[1]
    shapes = []
    for n in splits:
        shapes += [((4, width // 8, n), F32), ((4, width // 8, n), LOW)]
    scratch = (pltpu.VMEM((width, cols), F32),)
    return call(functools.partial(kernel, len(sides)), shapes, place, *sides, scratch=scratch, mib=12)


def plain_grad(shard_rows, *sides):
    half = len(sides) // 2
    total = sum(dot(a, b, 0, 0) for a, b in zip(sides[:half], sides[half:])).astype(LOW)
    return dp_scatter_sum(total.reshape(-1, shard_rows, total.shape[1]))


def fast(shard_rows):
    return lax.axis_size("dp") == 8 and shard_rows % 16 == 0


def place_pieces(masks, place, pieces, write):
    for piece, owners in zip(pieces, masks):
        for k, mask in enumerate(owners):
            write(place[4] ^ mask, piece, k)


def first_kernel(masks, spans, hidden_cols, place, *refs):
    pieces, (w_in_ref, w_proj_ref, vecs_ref, up_ref, bias_ref, flat_ref) = refs[: len(masks)], refs[len(masks) :]
    width, qkv_cols = w_in_ref.shape
    shard_rows = width // 8

    def write(owner, piece, k):
        at = pl.ds(pl.multiple_of(owner * shard_rows, shard_rows), shard_rows)
        w_in_ref[at, :] = piece[k, :shard_rows, :qkv_cols]
        w_proj_ref[at, :] = piece[k, :shard_rows, qkv_cols:]
        flat_ref[pl.ds(owner, 1), :] = piece[k, shard_rows : shard_rows + 1, :].astype(F32)

    place_pieces(masks, place, pieces, write)
    flat = flat_ref[...]
    joined = [
        jnp.concatenate([flat[s : s + 1, a:b] for s in range(8)], axis=1) for a, b in zip(spans, spans[1:])
    ]
    for k in range(6):
        vecs_ref[k : k + 1, :] = joined[k]
    up_ref[...] = joined[6]
    bias_ref[...] = jnp.concatenate([joined[7], jnp.zeros_like(joined[7]), joined[8]], axis=1)


def plain_kernel(masks, second, place, *refs):
    *pieces, out_ref = refs
    rows = out_ref.shape[0] // 8
    for number, (piece, owners) in enumerate(zip(pieces, masks)):
        for k, mask in enumerate(owners):
            at = pl.ds(pl.multiple_of((place[4] ^ mask) * rows, rows), rows)
            out_ref[at, :] = piece[second if number == 1 else k]


def pack_kernel(count, *refs):
    sources, out_ref, held, sems = refs[:count], refs[count], refs[count + 1 : -1], refs[-1]
    copies = [pltpu.make_async_copy(a, b, sems.at[k]) for k, (a, b) in enumerate(zip(sources, held))]
    for c in copies:
        c.start()
    for c in copies:
        c.wait()
    w_qkv, w_proj, *vectors = held
    rows = w_qkv.shape[1]
    out_ref[:rows, :] = jnp.concatenate([w_qkv[0], w_qkv[1], w_qkv[2], w_proj[...].T], axis=1)
    rows_of = [v[...].astype(F32) for v in vectors]
    rows_of = rows_of[:-1] + [rows_of[-1][0:1], rows_of[-1][1:2]]
    flat = jnp.concatenate(rows_of, axis=1)
    flat = jnp.concatenate([flat, jnp.zeros((1, out_ref.shape[1] - flat.shape[1]), F32)], axis=1)
    out_ref[rows:, :] = jnp.broadcast_to(flat, (8, flat.shape[1])).astype(LOW)


def first_pack(*args):
    w_qkv, w_proj = args[:2]
    return pl.pallas_call(
        functools.partial(pack_kernel, len(args)),
        out_shape=jax.ShapeDtypeStruct((w_qkv.shape[1] + 8, 3 * w_qkv.shape[2] + w_proj.shape[0]), LOW),
        in_specs=[pl.BlockSpec(memory_space=pl.ANY) for _ in args],
        out_specs=pl.BlockSpec(memory_space=pltpu.VMEM),
        scratch_shapes=[
            *(pltpu.VMEM(a.shape, a.dtype) for a in args),
            pltpu.SemaphoreType.DMA((len(args),)),
        ],
        compiler_params=pltpu.CompilerParams(vmem_limit_bytes=63 << 20),
        cost_estimate=pl.CostEstimate(flops=COST, bytes_accessed=0, transcendentals=0),
    )(*args)


def spans_of(vectors):
    spans = [0]
    for n in (*(v.shape[1] for v in vectors), vectors[-1].shape[1]):
        spans.append(spans[-1] + n)
    return spans


def first_unpacked(place, pieces, vectors, qkv_cols, head_cols, width):
    shapes = (
        ((width, qkv_cols), LOW),
        ((width, head_cols), LOW),
        ((6, width), F32),
        ((1, 8 * vectors[6].shape[1]), F32),
        ((1, qkv_cols), F32),
    )
    return call(
        functools.partial(first_kernel, MASKS, spans_of(vectors), 0),
        shapes,
        place,
        *pieces,
        scratch=(pltpu.VMEM((8, qkv_cols + head_cols), F32),),
    )


def unpacked(place, pieces, second):
    rows, cols = pieces[0].shape[1:]
    return call(functools.partial(plain_kernel, MASKS, second), (((8 * rows, cols), LOW),), place, *pieces)[0]


def plain_first(shard, vectors, qkv_cols, width):
    flat = dp_gather(jnp.concatenate([*vectors[:-1], vectors[-1][0:1], vectors[-1][1:2]], axis=1))[:, 0].astype(F32)
    whole = dp_gather(shard).reshape(width, -1)
    spans = spans_of(vectors)
    joined = [flat[:, a:b].reshape(1, -1) for a, b in zip(spans, spans[1:])]
    return (
        whole[:, :qkv_cols],
        whole[:, qkv_cols:],
        jnp.concatenate(joined[:6]),
        joined[6],
        jnp.concatenate([joined[7], jnp.zeros_like(joined[7]), joined[8]], axis=1),
    )


def down_kernel(hidden_zero, hidden_one, w_down, keep_ref, send_ref):
    rows = keep_ref.shape[1]
    for upper, hidden in enumerate((hidden_zero, hidden_one)):
        part = dot(hidden[...], w_down[...], 1, 1)
        keep_ref[upper] = part[:rows]
        send_ref[upper] = part[rows:].astype(LOW)


def local(x_embed, thoughts, thought_pos, img_start, *rest):
    *params, grad_out = rest
    dp = lax.axis_size("dp")
    table = []
    for d in range(dp):
        for t in range(4):
            table.append((t & 1, 0, 0, t >> 1, d, d >> 1 & 1, d >> 2 & 1, d & 1))
    place = jnp.asarray(table, jnp.int32)[lax.axis_index("dp") * 4 + lax.axis_index("tensor")]
    block = quick_block if fast(params[2].shape[1]) else plain_block
    block_out, grad_embed, grad_thoughts, grad_in, grad_proj, grad_up, grad_down, small = block(
        place, img_start[0], x_embed[0], thoughts[0], thought_pos, params, grad_out[0]
    )
    gain_one, bias_one, proj_b, gain_two, bias_two, down_b, up_b, qv_b = small
    flat = lambda a: a.reshape(-1)
    return (
        block_out[None],
        grad_embed[None],
        grad_thoughts,
        flat(gain_one),
        flat(bias_one),
        grad_in,
        qv_b.reshape(2, -1),
        grad_proj,
        flat(proj_b),
        flat(gain_two),
        flat(bias_two),
        grad_up,
        flat(up_b),
        grad_down,
        flat(down_b),
    )


def vectors_of(params):
    return [params[k].reshape(1, -1) for k in (0, 1, 5, 6, 7, 11, 9)] + [params[3]]


def splice_side(place, x_rows, thoughts, thought_pos):
    shape = (4 * x_rows[0].shape[1], x_rows[0].shape[2])
    return call(splice_kernel, ((shape, LOW), (shape, F32)), place, *x_rows, thoughts, thought_pos)


def input_side(xhat, vecs, w_in, bias):
    length, width = xhat.shape
    kinds = (((length, width), LOW),) + (((length, w_in.shape[1] // 3), LOW),) * 3
    return call(input_kernel, kinds, xhat, vecs, w_in, bias)


def input_back(place, thought_pos, grad_queries, grad_keys, grad_values, w_in, xhat, grad_residual):
    length, width = xhat.shape
    count = thought_pos.shape[1]
    return call(
        input_back_kernel,
        (
            ((2, length // 4, width), F32),
            ((length // 4, width), LOW),
            ((length // 4, width), LOW),
            ((-(-(count + 2) // 8) * 8, width), F32),
            ((1, w_in.shape[1]), F32),
            ((-(-count // 8) * 8, width), F32),
        ),
        place,
        thought_pos[0],
        *grad_queries,
        grad_keys,
        grad_values,
        w_in,
        xhat,
        *grad_residual,
        scratch=(pltpu.VMEM((length, width), F32),),
    )


def output_side(place, keep, got, spliced, grad_residual, vecs, thought_pos, thoughts, small, picked, *pairs):
    rows, width = keep.shape
    embed, own, *more = call(
        output_kernel,
        (
            ((rows, width), F32),
            ((thoughts.shape[0], 1, width // 4), F32),
            *((p.shape[1:], F32) for p in pairs[::2]),
        ),
        place,
        keep,
        got,
        spliced,
        *grad_residual,
        vecs,
        thought_pos,
        thoughts,
        small,
        picked,
        *pairs,
    )
    return embed, jnp.moveaxis(own, 1, 0), *more


def result(place, keep, got, residual, vecs):
    return call(result_kernel, ((keep.shape, LOW),), place, keep, got, *residual, vecs)[0]


def down_part(hidden, w_down_t):
    shape = (2, hidden[0].shape[0] // 2, w_down_t.shape[0])
    return call(down_kernel, ((shape, F32), (shape, LOW)), *hidden, w_down_t)


def quick_block(place, starts, x_own, thoughts, thought_pos, params, cot_own):
    across = lambda a: swapped(a, "dp", 1)
    near = lambda a: swapped(a, "dp", 2)
    far = lambda a: swapped(a, "dp", 4)
    core = lambda a: swapped(a, "tensor", 1)
    over = lambda a: swapped(a, "tensor", 2)
    w_qkv, w_proj, w_up, w_down_own = params[2], params[4], params[8], params[10].T
    shard_rows, head_cols = w_qkv.shape[1:]
    width = x_own.shape[1]
    vectors = vectors_of(params)

    pack = first_pack(w_qkv, w_proj, *vectors)
    pack_across = across(pack)
    pack_far = far(pack)
    x_far = over(after(x_own, pack))
    pack_here, x_here = brought(pack, after(x_own, pack))
    both = stacked(after(w_up, pack), w_down_own)
    x_far, pack_far, pack_across, pack_here, x_here, both = together(
        x_far, pack_far, pack_across, pack_here, x_here, both
    )

    pack_near, pack_far_across = near(stacked(pack_here, pack_far)), across(pack_far)
    up_far = far(after(w_up, pack_far))
    both_across = across(both)
    cot_far = over(after(cot_own, x_far))
    pack_near, pack_far_across, up_far, both_across, cot_far = together(
        pack_near, pack_far_across, up_far, both_across, cot_far
    )

    pack_near_across = across(pack_near)
    up_near = near(stacked(w_up, up_far))
    down_far = far(after(w_down_own, up_far))
    x_both = pick(place, x_here, after(x_far, up_far))
    x_other = core(x_both)
    spliced, xhat = splice_side(place, (x_both, x_other), thoughts, thought_pos)
    pack_near_across, xhat = together(pack_near_across, xhat)
    up_far_across = across(after(up_far, pack_near_across))
    pieces = (pack_here[None], pack_across[None], pack_far[None], pack_near, pack_far_across[None], pack_near_across)
    w_in, w_proj_t, vecs, up_bias, all_bias = first_unpacked(place, pieces, vectors, 3 * head_cols, head_cols, width)
    normed, queries, keys, values = input_side(xhat, vecs, w_in, all_bias)
    att_zero, log_zero, keep_zero, send_zero = attend(0, place, starts, queries, keys, values, w_proj_t)
    send_zero, up_near, down_far, up_far_across = together(send_zero, up_near, down_far, up_far_across)

    mine_zero = add_low(keep_zero, core(send_zero))
    far_zero = over(mine_zero)
    down_near = near(stacked(w_down_own, down_far))
    down_far_across = across(down_far)
    up_near_across = across(up_near)
    att_one, log_one, keep_one, send_one = attend(1, after(place, mine_zero), starts, queries, keys, values, w_proj_t)
    send_one, far_zero, up_near_across, down_far_across, down_near = together(
        send_one, far_zero, up_near_across, down_far_across, down_near
    )

    mine_one = add_low(keep_one, core(send_one))
    far_one = over(mine_one)
    total_zero = add_low(mine_zero, far_zero)
    other_zero = core(total_zero)
    down_near_across = across(down_near)
    pieces = (w_up[None], both_across, up_far[None], up_near, up_far_across[None], up_near_across)
    w_up_all = unpacked(place, pieces, 0)
    cot_both = pick(place, cot_own, cot_far)
    cot_other = core(cot_both)
    other_zero, down_near_across, w_up_all, cot_other = together(other_zero, down_near_across, w_up_all, cot_other)
    cots = (cot_both, cot_other)
    pieces = (w_down_own[None], both_across, down_far[None], down_near, down_far_across[None], down_near_across)
    w_down_t = unpacked(place, pieces, 1)

    weights = (vecs, up_bias, w_up_all, w_down_t)
    residual_zero, normed_zero, hidden_zero, grad_zero, up_sum_zero, keep_zero, send_zero = feed(
        0, spliced, total_zero, other_zero, cots, *weights
    )
    send_zero, far_one = together(send_zero, far_one)
    total_one = add_low(mine_one, far_one)
    other_one = core(total_one)
    mine_zero = add_low(keep_zero, core(send_zero))
    far_zero = over(mine_zero)
    residual_one, normed_one, hidden_one, grad_one, up_sum_one, keep_one, send_one = feed(
        1, after(spliced, mine_zero), total_one, other_one, cots, *weights
    )
    hidden_cols = hidden_one.shape[1]
    mine_one = add_low(keep_one, core(send_one))
    far_one = over(mine_one)
    b_keep, b_send = grad_blocks(
        grad_kernel, place, (hidden_cols,), normed_zero, normed_one, grad_zero, grad_one
    )
    b_got = across(b_send)
    c_keep, c_send = grad_blocks(
        cot_grad_kernel, after(place, b_send), (hidden_cols,), *cots, hidden_zero, hidden_one
    )
    mlp_keep, mlp_send = down_part((hidden_zero, after(hidden_one, b_send)), w_down_t)
    total_zero = add_low(after(mine_zero, c_send, mlp_send), far_zero, cost=0)
    other_zero = core(total_zero)
    residual = (residual_zero, residual_one)

    res_zero, branch_zero, gatt_zero, delta_zero, sums_zero = branch_back(
        0, total_zero, other_zero, residual_zero, cots, vecs, w_proj_t, att_zero
    )
    dq_zero, *early = back(0, place, starts, queries, keys, values, log_zero, gatt_zero, delta_zero, ())
    c_got = across(after(c_send, other_zero))
    total_one = add_low(after(mine_one, early[0], b_got), far_one)
    other_one = core(total_one)
    b_keep, b_send = fold(5, place, b_keep, after(b_got, total_one))
    b_got = near(b_send)
    mlp_keep, mlp_send = fold(3, place, mlp_keep, core(after(mlp_send, other_zero)))
    mlp_got = over(after(mlp_send, total_one))
    res_one, branch_one, gatt_one, delta_one, sums_one = branch_back(
        1, total_one, other_one, residual_one, cots, vecs, w_proj_t, att_one
    )
    dq_one, dk, dv = back(1, place, starts, queries, keys, values, log_one, gatt_one, delta_one, early)
    dk, b_got = together(dk, b_got)

    grad_residual = (res_zero, res_one)
    kinds = (((4, shard_rows, 2 * head_cols), F32), ((4, shard_rows, 2 * head_cols), LOW))
    scratch = (pltpu.VMEM((width, 2 * head_cols), F32),)
    d_keep, d_send = call(
        last_kernel_one, kinds, place, normed, dq_zero, dq_one, branch_zero, branch_one, att_zero, att_one, scratch=scratch
    )
    d_got = across(after(d_send, dk))
    c_keep, c_send = fold(5, place, c_keep, c_got)
    c_got = near(c_send)
    b_keep, b_send = fold(6, place, b_keep, b_got)
    b_got = far(b_send)
    keep, send_low, send_high, small, mixed_sums, picked = input_back(
        place, thought_pos, (dq_zero, dq_one), dk, dv, w_in, xhat, grad_residual
    )
    got_low, got_high = core(send_low), core(send_high)
    small = add_full(small, core(small))
    small = add_full(small, over(small))
    shape = (4, shard_rows + 8, 2 * head_cols)
    e_keep, e_send = call(
        last_kernel_two,
        ((shape, F32), (shape, LOW)),
        place,
        after(normed, b_got),
        dk,
        dv,
        small,
        sums_zero,
        sums_one,
        up_sum_zero,
        up_sum_one,
        mixed_sums,
        scratch=(*scratch, pltpu.VMEM((8, 4 * head_cols), F32)),
    )
    e_got = across(e_send)
    keep, send = fold_two(3, place, keep, got_low, got_high)
    got = over(after(send, small))
    d_keep, d_send = fold(5, place, d_keep, after(d_got, c_got))
    d_got = near(d_send)
    c_keep, c_send = fold(6, place, c_keep, after(c_got, d_send))
    c_got = far(c_send)
    e_got, d_got = together(e_got, d_got)

    e_keep, e_send = fold(5, place, e_keep, e_got)
    e_got = near(e_send)
    d_keep, d_send = fold(6, place, d_keep, after(d_got, c_got))
    d_got = far(d_send)

    e_keep, e_send = fold(6, place, e_keep, after(e_got, d_got))
    e_got = far(e_send)
    block_out = result(place, mlp_keep[0], mlp_got[0], residual, vecs)
    grad_embed, grad_thoughts, grad_up, grad_down = output_side(
        place, keep, got, spliced, grad_residual, vecs, thought_pos, thoughts, small, picked,
        b_keep, b_got, c_keep, c_got,
    )
    grad_embed, block_out, e_got, d_got = together(grad_embed, block_out, e_got, d_got)
    grad_in, grad_proj, *small = call(
        finish_kernel,
        (
            ((3, shard_rows, head_cols), F32),
            ((head_cols, shard_rows), F32),
            *((v.shape, F32) for v in vectors),
        ),
        d_keep,
        d_got,
        e_keep,
        e_got,
    )
    return block_out, grad_embed, grad_thoughts, grad_in, grad_proj, grad_up, grad_down.T, small


def plain_block(place, starts, x_own, thoughts, thought_pos, params, cot_own):
    dp = lax.axis_size("dp")
    w_qkv, w_proj, w_up, w_down_own = params[2], params[4], params[8], params[10].T
    shard_rows, head_cols = w_qkv.shape[1:]
    width = x_own.shape[1]
    x_rows, cots = rows_gather(x_own), rows_gather(cot_own)
    shard = jnp.concatenate([w_qkv[0], w_qkv[1], w_qkv[2], w_proj.T], axis=1)
    w_in, w_proj_t, vecs, up_bias, all_bias = plain_first(shard, vectors_of(params), 3 * head_cols, width)
    w_up_all = dp_gather(w_up).reshape(width, -1)
    w_down_t = dp_gather(w_down_own).reshape(width, -1)
    spliced, xhat = splice_side(place, x_rows, thoughts, thought_pos)
    normed, queries, keys, values = input_side(xhat, vecs, w_in, all_bias)

    def all_sum(keep, send):
        mine = add_low(keep, swapped(send, "tensor", 1))
        total = add_low(mine, swapped(mine, "tensor", 2))
        return total, swapped(total, "tensor", 1)

    def own_sum(keep, send):
        keep, send = fold(3, place, keep, swapped(send, "tensor", 1))
        return keep[0], swapped(send, "tensor", 2)[0]

    atts, logs, feds, grad_twos = [], [], [], []
    for chunk in range(2):
        att, log, *part = attend(chunk, place, starts, queries, keys, values, w_proj_t)
        feds.append(feed(chunk, spliced, *all_sum(*part), cots, vecs, up_bias, w_up_all, w_down_t))
        grad_twos.append(all_sum(*feds[-1][5:]))
        atts.append(att)
        logs.append(log)
    residual, normed_two, hidden, grad_hidden, up_sums = zip(feds[0][:5], feds[1][:5])
    block_out = result(place, *own_sum(*down_part(hidden, w_down_t)), residual, vecs)
    grad_up = plain_grad(shard_rows, *normed_two, *grad_hidden)
    grad_down = plain_grad(shard_rows, cots_rows(cots, 0), cots_rows(cots, 1), *hidden)
    branches, dqs, early = [], [], ()
    for chunk in range(2):
        branches.append(
            branch_back(chunk, *grad_twos[chunk], residual[chunk], cots, vecs, w_proj_t, atts[chunk])
        )
        dq, *early = back(
            chunk, place, starts, queries, keys, values, logs[chunk], *branches[-1][2:4], early
        )
        dqs.append(dq)
    grad_residual, grad_branch = zip(branches[0][:2], branches[1][:2])
    keep, *send, small, mixed_sums, picked = input_back(
        place, thought_pos, dqs, *early, w_in, xhat, grad_residual
    )
    grad_mixed = jnp.concatenate([jnp.concatenate(dqs), *early], axis=1)
    small = small + swapped(small, "tensor", 1)
    small = small + swapped(small, "tensor", 2)
    grad_embed, grad_thoughts = output_side(
        place, *own_sum(keep, jnp.stack(send)), spliced, grad_residual, vecs, thought_pos, thoughts, small, picked
    )
    grad_in = plain_grad(shard_rows, normed, grad_mixed).reshape(shard_rows, 3, head_cols)
    grad_proj = plain_grad(shard_rows, *grad_branch, *atts)
    two = branches[0][4] + branches[1][4]
    count = small.shape[0] - 2
    vec = (small[count], small[count + 1], two[2], two[0], two[1], two[3], up_sums[0] + up_sums[1])
    vec += (mixed_sums[0, :head_cols], mixed_sums[0, 2 * head_cols :])
    vec = jnp.concatenate([v.reshape(dp, -1) for v in vec], axis=1)
    vec = dp_scatter_sum(vec[:, None, :])[0]
    small, first = [], 0
    for n in (params[k].size for k in (0, 1, 5, 6, 7, 11, 9, 3)):
        small.append(vec[first : first + n])
        first += n
    return (
        block_out,
        grad_embed,
        grad_thoughts,
        jnp.moveaxis(grad_in, 1, 0),
        grad_proj.T,
        grad_up,
        grad_down.T,
        small,
    )


def solution(mesh):
    in_specs = (
        P("dp", "tensor", None),
        P("dp", None, None),
        P("dp", None),
        P("dp", None),
        P("dp"),
        P("dp"),
        P(None, "dp", "tensor"),
        P(None, ("tensor", "dp")),
        P("tensor", "dp"),
        P("dp"),
        P("dp"),
        P("dp"),
        P("dp", "tensor"),
        P(("tensor", "dp")),
        P("tensor", "dp"),
        P("dp"),
        P("dp", "tensor", None),
    )
    out_specs = (
        P("dp", "tensor", None),
        P("dp", "tensor", None),
        P("dp", None, "tensor"),
        P("dp"),
        P("dp"),
        P(None, "dp", "tensor"),
        P(None, ("tensor", "dp")),
        P("tensor", "dp"),
        P("dp"),
        P("dp"),
        P("dp"),
        P("dp", "tensor"),
        P(("tensor", "dp")),
        P("tensor", "dp"),
        P("dp"),
    )
    return jax.shard_map(local, mesh=mesh, in_specs=in_specs, out_specs=out_specs, check_vma=False)
```

```python
import functools

import jax
import jax.numpy as jnp
from jax import lax
from jax.experimental import pallas as pl
from jax.experimental.pallas import tpu as pltpu
from jax.sharding import PartitionSpec as P

HD = 64
IMG = 256
EPSILON = 1e-05
F32 = jnp.float32
LOW = jnp.bfloat16
COST = 1000


def swapped(array, axis, mask):
    return lax.ppermute(array, axis, [(i, i ^ mask) for i in range(lax.axis_size(axis))])


def dp_masks():
    return [1 << b for b in reversed(range(lax.axis_size("dp").bit_length() - 1))]


def slot_owners(masks):
    owners = [0]
    for mask in masks:
        owners = owners + [o ^ mask for o in owners]
    return owners


def dp_gather(shard):
    masks, me = dp_masks(), lax.axis_index("dp")
    slots = shard[None]
    for mask in masks:
        other = swapped(slots, "dp", mask)
        first = (me & mask) == 0
        slots = jnp.where(
            first, jnp.concatenate([slots, other]), jnp.concatenate([other, slots])
        )
    owners = slot_owners(masks)
    return jnp.stack([slots[owners.index(s)] for s in range(len(owners))])


MASKS = ((0,), (1,), (4,), (2, 6), (5,), (3, 7))


def rows_pick(own, other):
    first = (lax.axis_index("tensor") >> 1) == 0
    return jnp.stack([jnp.where(first, own, other), jnp.where(first, other, own)])


def dp_scatter_sum(blocks):
    masks, me = dp_masks(), lax.axis_index("dp")
    slots = jnp.stack([blocks[s] for s in slot_owners(masks)])
    for mask in reversed(masks):
        half = slots.shape[0] // 2
        first = (me & mask) == 0
        keep = jnp.where(first, slots[:half], slots[half:])
        send = jnp.where(first, slots[half:], slots[:half])
        slots = keep.astype(F32) + swapped(send, "dp", mask).astype(F32)
    return slots[0]


def rows_gather(own):
    both = rows_pick(own, swapped(own, "tensor", 2))
    return both, swapped(both, "tensor", 1)


def after(value, *others):
    return lax.optimization_barrier((value, *others))[0]


def together(*values):
    return lax.optimization_barrier(values)


def dot(a, b, ca, cb, precision=None):
    return lax.dot_general(
        a, b, (((ca,), (cb,)), ((), ())), precision=precision, preferred_element_type=F32
    )


def normalised(values):
    centred = values - jnp.mean(values, axis=-1, keepdims=True)
    inverse = lax.rsqrt(jnp.mean(centred * centred, axis=-1, keepdims=True) + EPSILON)
    return centred * inverse, inverse


def norm_back(upstream, xhat, inverse, gain):
    scaled = upstream * gain
    return inverse * (
        scaled
        - jnp.mean(scaled, axis=-1, keepdims=True)
        - xhat * jnp.mean(scaled * xhat, axis=-1, keepdims=True)
    )


def gelu_pair(u):
    k, a = 0.7978845608028654, 0.044715
    square = u * u
    t = jnp.tanh(u * (k + (k * a) * square))
    rise = 0.5 * (1.0 + t)
    return u * rise, rise + (0.5 * u) * (1.0 - t * t) * (k + (3.0 * k * a) * square)


def cots_rows(cots, chunk):
    return jnp.concatenate([c[chunk] for c in cots])


def iota(shape, dim):
    return lax.broadcasted_iota(jnp.int32, shape, dim)


def call(kernel, outs, *args, scratch=(), mib=8, cost=0):
    spec = lambda a: pl.BlockSpec(
        memory_space=pltpu.SMEM if a.ndim == 1 and a.dtype == jnp.int32 else pltpu.VMEM
    )
    return pl.pallas_call(
        kernel,
        out_shape=tuple(jax.ShapeDtypeStruct(s, t) for s, t in outs),
        in_specs=[spec(a) for a in args],
        out_specs=tuple(pl.BlockSpec(memory_space=pltpu.VMEM) for _ in outs),
        scratch_shapes=scratch,
        compiler_params=pltpu.CompilerParams(vmem_limit_bytes=mib << 20),
        cost_estimate=pl.CostEstimate(flops=COST + cost, bytes_accessed=0, transcendentals=0),
    )(*args)


def splice_kernel(place, x_zero, x_one, thoughts, thought_pos, spliced_ref, xhat_ref):
    core = place[0]
    rows = x_zero.shape[1]
    for upper in range(2):
        for rel, ref in enumerate((x_zero, x_one)):
            first = upper * 2 * rows + (core ^ rel) * rows
            part = slice((2 * upper + rel) * rows, (2 * upper + rel + 1) * rows)
            match = (first + iota((rows, 1), 0)) == thought_pos[...]
            covered = jnp.sum(match.astype(F32), axis=1, keepdims=True) > 0.0
            picked = dot(match.astype(LOW), thoughts[...], 1, 0)
            spliced = jnp.where(covered, picked, ref[upper].astype(F32))
            spliced_ref[part, :] = spliced.astype(LOW)
            xhat_ref[part, :] = normalised(spliced)[0]


def input_kernel(xhat, vecs, w_in, bias, normed_ref, q_ref, k_ref, v_ref):
    rows = xhat.shape[0] // 4
    cols = q_ref.shape[1]
    for k in range(4):
        part = slice(k * rows, (k + 1) * rows)
        normed = (xhat[part, :] * vecs[0:1, :] + vecs[1:2, :]).astype(LOW)
        normed_ref[part, :] = normed
        mixed = (dot(normed, w_in[...], 1, 0) + bias[...]).astype(LOW)
        q_ref[part, :] = mixed[:, :cols]
        k_ref[part, :] = mixed[:, cols : 2 * cols]
        v_ref[part, :] = mixed[:, 2 * cols :]


def query_limits(place, starts, chunk, rows):
    core, start = place[0], starts[chunk]
    col = iota((1, 2 * rows), 1)
    query = 2 * rows * chunk + jnp.where(col < rows, col + core * rows, col - core * rows)
    inside = (query >= start) & (query < start + IMG)
    return jnp.where(inside, start + (IMG - 1), query)


def key_positions(place, block, rows):
    first = (block >> 1) * (2 * rows) + (place[0] ^ (block & 1)) * rows
    return first + iota((rows, 1), 0)


def attend_kernel(
    chunk, place, starts, q_ref, k_ref, v_ref, w_proj,
    att_ref, log_ref, keep_ref, send_ref, acc_ref, top_ref, sum_ref,
):
    half, cols = att_ref.shape
    rows = half // 2
    heads = cols // HD
    head_of = iota((1, cols), 1) // HD
    limits = query_limits(place, starts, chunk, rows)
    queries = q_ref[chunk * half : (chunk + 1) * half, :] * LOW(0.125)
    acc_ref[...] = jnp.zeros_like(acc_ref)
    top_ref[...] = jnp.full_like(top_ref, -1e30)
    sum_ref[...] = jnp.zeros_like(sum_ref)

    @pl.loop(0, 2 * chunk + 2)
    def _(block):
        span = pl.ds(pl.multiple_of(block * rows, rows), rows)
        keys = k_ref[span, :]
        values = v_ref[span, :].T
        allowed = key_positions(place, block, rows) <= limits
        for head in range(heads):
            scores = dot(jnp.where(head_of == head, keys, LOW(0)), queries, 1, 1)
            scores = jnp.where(allowed, scores, -1e30)
            top = top_ref[head : head + 1, :]
            new_top = jnp.maximum(top, jnp.max(scores, axis=0, keepdims=True))
            exps = jnp.exp(scores - new_top)
            fade = jnp.exp(top - new_top)
            top_ref[head : head + 1, :] = new_top
            sum_ref[head : head + 1, :] = sum_ref[head : head + 1, :] * fade + jnp.sum(
                exps, axis=0, keepdims=True
            )
            part = slice(head * HD, (head + 1) * HD)
            acc_ref[part, :] = acc_ref[part, :] * fade + dot(values[part, :], exps.astype(LOW), 1, 0)

    for head in range(heads):
        part = slice(head * HD, (head + 1) * HD)
        acc_ref[part, :] = acc_ref[part, :] / sum_ref[head : head + 1, :]
    log_ref[...] = top_ref[...] + jnp.log(jnp.maximum(sum_ref[...], 1e-30))
    attended = acc_ref[...].T.astype(LOW)
    att_ref[...] = attended
    branch = dot(attended, w_proj[...], 1, 1)
    keep_ref[...] = branch[:rows]
    send_ref[...] = branch[rows:].astype(LOW)


def attend(chunk, place, starts, queries, keys, values, w_proj):
    length, cols = queries.shape
    half, width = length // 2, w_proj.shape[0]
    return call(
        functools.partial(attend_kernel, chunk),
        (
            ((half, cols), LOW),
            ((8, half), F32),
            ((half // 2, width), F32),
            ((half // 2, width), LOW),
        ),
        place,
        starts,
        queries,
        keys,
        values,
        w_proj,
        scratch=(
            pltpu.VMEM((cols, half), F32),
            pltpu.VMEM((8, half), F32),
            pltpu.VMEM((8, half), F32),
        ),
    )


def feed_kernel(
    chunk, spliced, total, other, cot_zero, cot_one, vecs, up_bias, w_up, w_down,
    residual_ref, normed_ref, hidden_ref, grad_ref, sum_ref, keep_ref, send_ref,
):
    half, width = residual_ref.shape
    rows = half // 2
    for rel, ref in enumerate((total, other)):
        part = slice(rel * rows, (rel + 1) * rows)
        residual = (
            spliced[chunk * half + rel * rows : chunk * half + (rel + 1) * rows, :].astype(F32)
            + ref[...].astype(F32)
            + vecs[2:3, :]
        )
        residual_ref[part, :] = residual
        xhat, _ = normalised(residual)
        normed_ref[part, :] = (xhat * vecs[3:4, :] + vecs[4:5, :]).astype(LOW)
    hidden_cols = w_up.shape[1]
    step = 256 if hidden_cols % 256 == 0 else hidden_cols
    for first in range(0, hidden_cols, step):
        cols = slice(first, first + step)
        hidden, slope = gelu_pair(dot(normed_ref[...], w_up[:, cols], 1, 0) + up_bias[:, cols])
        hidden_ref[:, cols] = hidden.astype(LOW)
        back = jnp.concatenate(
            [dot(cot_zero[chunk], w_down[:, cols], 1, 0), dot(cot_one[chunk], w_down[:, cols], 1, 0)]
        )
        grad = (back * slope).astype(LOW)
        grad_ref[:, cols] = grad
        sum_ref[:, cols] = jnp.sum(grad.astype(F32), axis=0, keepdims=True)
    back = dot(grad_ref[...], w_up[...], 1, 1)
    keep_ref[...] = back[:rows]
    send_ref[...] = back[rows:].astype(LOW)


def feed(chunk, spliced, total, other, cots, vecs, up_bias, w_up, w_down):
    length, width = spliced.shape
    half, hidden = length // 2, w_up.shape[1]
    return call(
        functools.partial(feed_kernel, chunk),
        (
            ((half, width), F32),
            ((half, width), LOW),
            ((half, hidden), LOW),
            ((half, hidden), LOW),
            ((1, hidden), F32),
            ((half // 2, width), F32),
            ((half // 2, width), LOW),
        ),
        spliced,
        total,
        other,
        *cots,
        vecs,
        up_bias,
        w_up,
        w_down,
    )


def norm_back_kernel(
    chunk, total, other, residual, cot_zero, cot_one, vecs, w_proj, att,
    grad_res_ref, branch_ref, gatt_ref, delta_ref, sums_ref,
):
    half, width = residual.shape
    rows = half // 2
    gain = vecs[3:4, :]
    sums = [0.0, 0.0, 0.0, 0.0]
    for rel, (ref, cot) in enumerate(((total, cot_zero), (other, cot_one))):
        part = slice(rel * rows, (rel + 1) * rows)
        upstream = ref[...].astype(F32)
        xhat, inverse = normalised(residual[part, :])
        out_grad = cot[chunk].astype(F32)
        grad_res = out_grad + norm_back(upstream, xhat, inverse, gain)
        grad_res_ref[part, :] = grad_res
        branch_ref[part, :] = grad_res.astype(LOW)
        for k, term in enumerate((upstream * xhat, upstream, grad_res, out_grad)):
            sums[k] = sums[k] + jnp.sum(term, axis=0, keepdims=True)
    for k in range(4):
        sums_ref[k : k + 1, :] = sums[k]
    grad_att = dot(branch_ref[...], w_proj[...], 1, 0).astype(LOW)
    gatt_ref[...] = grad_att
    cols = att.shape[1]
    head_rows = (iota((8, cols), 0) == iota((8, cols), 1) // HD).astype(F32)
    delta_ref[...] = dot(
        head_rows, grad_att.astype(F32) * att[...].astype(F32), 1, 1, lax.Precision.HIGHEST
    )


def branch_back(chunk, total, other, residual, cots, vecs, w_proj, att):
    half, width = residual.shape
    cols = att.shape[1]
    return call(
        functools.partial(norm_back_kernel, chunk),
        (((half, width), F32), ((half, width), LOW), ((half, cols), LOW), ((8, half), F32), ((8, width), F32)),
        total,
        other,
        residual,
        *cots,
        vecs,
        w_proj,
        att,
    )


def probs_kernel(chunk, place, starts, q_ref, k_ref, log, out_ref):
    heads, _, half = out_ref.shape
    cols = q_ref.shape[1]
    rows = half // 2
    head_of = iota((1, cols), 1) // HD
    limits = query_limits(place, starts, chunk, rows)

    @pl.loop(0, 2 * chunk + 2)
    def _(block):
        span = pl.ds(pl.multiple_of(block * rows, rows), rows)
        keys = k_ref[span, :]
        queries = q_ref[chunk * half : (chunk + 1) * half, :] * LOW(0.125)
        allowed = key_positions(place, block, rows) <= limits
        for head in range(heads):
            scores = dot(jnp.where(head_of == head, keys, LOW(0)), queries, 1, 1)
            probs = jnp.exp(jnp.where(allowed, scores, -1e30) - log[head : head + 1, :])
            out_ref[head, span, :] = probs.astype(LOW)


def probs_of(chunk, place, starts, queries, keys, log):
    length, cols = queries.shape
    half = length // 2
    shape = (cols // HD, half * (chunk + 1), half)
    return call(functools.partial(probs_kernel, chunk), ((shape, LOW),), place, starts, queries, keys, log)[0]


def back_kernel(chunk, place, q_ref, k_ref, v_ref, probs_ref, gatt_ref, delta_ref, *rest):
    keys_in, rest = (rest[:2], rest[2:]) if chunk else ((), rest)
    dq_ref, dk_ref, dv_ref, dqt_ref = rest
    half, cols = gatt_ref.shape
    rows = half // 2
    heads = cols // HD
    head_of = iota((1, cols), 1) // HD
    dqt_ref[...] = jnp.zeros_like(dqt_ref)

    @pl.loop(0, 2 * chunk + 2)
    def _(block):
        span = pl.ds(pl.multiple_of(block * rows, rows), rows)
        values = v_ref[span, :]
        keys_t = k_ref[span, :].T
        queries = q_ref[chunk * half : (chunk + 1) * half, :] * LOW(0.125)
        grad_att = gatt_ref[...]
        dk = jnp.zeros((rows, cols), F32)
        dv = jnp.zeros((rows, cols), F32)
        for head in range(heads):
            mine = head_of == head
            probs = probs_ref[head, span, :]
            grad_probs = dot(jnp.where(mine, values, LOW(0)), grad_att, 1, 1)
            grad_scores = (probs.astype(F32) * (grad_probs - delta_ref[head : head + 1, :])).astype(LOW)
            dv = dv + dot(probs, jnp.where(mine, grad_att, LOW(0)), 1, 0)
            dk = dk + dot(grad_scores, jnp.where(mine, queries, LOW(0)), 1, 0)
            part = slice(head * HD, (head + 1) * HD)
            dqt_ref[part, :] = dqt_ref[part, :] + dot(keys_t[part, :], grad_scores, 1, 0)
        if chunk:
            seen = jnp.where(block < 2, 1.0, 0.0)
            early = pl.ds(pl.multiple_of((block & 1) * rows, rows), rows)
            dk = dk + keys_in[0][early, :] * seen
            dv = dv + keys_in[1][early, :] * seen
        dk_ref[span, :] = dk.astype(dk_ref.dtype)
        dv_ref[span, :] = dv.astype(dv_ref.dtype)

    dq_ref[...] = (dqt_ref[...] * 0.125).T.astype(LOW)


def back(chunk, place, queries, keys, values, probs, grad_att, delta, early):
    half, cols = grad_att.shape
    kind = (((half * (chunk + 1), cols), LOW if chunk else F32),) * 2
    return call(
        functools.partial(back_kernel, chunk),
        (((half, cols), LOW), *kind),
        place,
        queries,
        keys,
        values,
        probs,
        grad_att,
        delta,
        *early,
        scratch=(pltpu.VMEM((cols, half), F32),),
    )


def input_back_kernel(
    place, thought_pos, dq_zero, dq_one, dk, dv, w_in, xhat, res_zero, res_one,
    keep_ref, low_ref, high_ref, small_ref, colsum_ref, picked_ref, grad_ref,
):
    half, cols = dq_zero.shape
    rows = half // 2
    sums = [0.0, 0.0, 0.0]
    for upper, dq in enumerate((dq_zero, dq_one)):
        for rel in range(2):
            part = slice((2 * upper + rel) * rows, (2 * upper + rel + 1) * rows)
            mixed = jnp.concatenate(
                [dq[rel * rows : (rel + 1) * rows, :], dk[part, :], dv[part, :]], axis=1
            )
            grad = dot(mixed, w_in[...], 1, 1)
            grad_ref[part, :] = grad
            if rel:
                (low_ref, high_ref)[upper][...] = grad.astype(LOW)
            else:
                keep_ref[upper] = grad
            terms = (grad * xhat[part, :], grad, mixed.astype(F32))
            sums = [a + jnp.sum(b, axis=0, keepdims=True) for a, b in zip(sums, terms)]
    small_ref[...] = jnp.zeros_like(small_ref)
    picked_ref[...] = jnp.zeros_like(picked_ref)
    count = thought_pos.shape[0]
    for k in range(count):
        at = thought_pos[k]
        row = (at // half) * half + (((at // rows) & 1) ^ place[0]) * rows + at % rows
        small_ref[k : k + 1, :] = grad_ref[pl.ds(row, 1), :]
        low = res_zero[pl.ds(jnp.minimum(row, half - 1), 1), :]
        high = res_one[pl.ds(jnp.maximum(row - half, 0), 1), :]
        picked_ref[k : k + 1, :] = jnp.where(row < half, low, high)
    small_ref[count : count + 1, :] = sums[0]
    small_ref[count + 1 : count + 2, :] = sums[1]
    colsum_ref[...] = sums[2]


def output_kernel(place, keep, got, spliced, res_zero, res_one, vecs, thought_pos, thoughts, small, picked, *rest):
    pairs, (embed_ref, rows_ref, *more) = rest[: 2 * ((len(rest) - 2) // 3)], rest[2 * ((len(rest) - 2) // 3) :]
    rows = keep.shape[0]
    gain = vecs[0:1, :]
    own = pl.ds(pl.multiple_of(place[3] * (2 * rows), 2 * rows), rows)
    xhat, inverse = normalised(spliced[own, :].astype(F32))
    residual = jnp.where(place[3] == 0, res_zero[:rows, :], res_one[:rows, :])
    grad = norm_back(keep[...] + got[...].astype(F32), xhat, inverse, gain) + residual
    at = (2 * place[3] + place[0]) * rows + iota((rows, 1), 0)
    covered = jnp.sum((at == thought_pos[...]).astype(F32), axis=1, keepdims=True) > 0.0
    embed_ref[...] = jnp.where(covered, 0.0, grad)
    count = thoughts.shape[0]
    xhat, inverse = normalised(thoughts[...].astype(F32))
    grad = norm_back(small[:count, :], xhat, inverse, gain) + picked[:count, :]
    cols = rows_ref.shape[2]
    rank = 2 * place[3] + place[0]
    grad = sum(jnp.where(rank == k, 1.0, 0.0) * grad[:, k * cols : (k + 1) * cols] for k in range(4))
    for k in range(count):
        rows_ref[k] = grad[k : k + 1, :]
    for ref, keep, got in zip(more, pairs[::2], pairs[1::2]):
        ref[...] = keep[0] + got[0].astype(F32)


def fold_kernel(bit, place, *refs):
    *parts, keep_ref, send_ref = refs
    half = keep_ref.shape[0]
    mine = place[bit] * half
    rest = half - mine
    first = 0
    for keep, got in zip(parts[::2], parts[1::2]):
        rows, cols = keep.shape[1:]
        below = rows < 16 and first > 0
        if below:
            at = (slice(keep_ref.shape[1] - rows, None), slice(0, cols))
        else:
            at = (slice(0, rows), slice(first, first + cols))
            first += cols
        for k in range(half):
            keep_ref[(k, *at)] = keep[mine + k] + got[mine + k].astype(F32)
            send_ref[(k, *at)] = (keep[rest + k] + got[rest + k].astype(F32)).astype(LOW)


def fold(bit, place, *parts):
    under = [p.shape[1] for p in parts[2::2] if p.shape[1] < 16]
    cols = sum(p.shape[2] for k, p in enumerate(parts[::2]) if k == 0 or p.shape[1] >= 16)
    shape = (parts[0].shape[0] // 2, parts[0].shape[1] + sum(under), cols)
    return call(functools.partial(fold_kernel, bit), ((shape, F32), (shape, LOW)), place, *parts)


def fold_two_kernel(bit, place, keep, low, high, keep_ref, send_ref):
    first = place[bit] == 0
    low, high = keep[0] + low[...].astype(F32), keep[1] + high[...].astype(F32)
    keep_ref[...] = jnp.where(first, low, high)
    send_ref[...] = jnp.where(first, high, low).astype(LOW)


def fold_two(bit, place, keep, low, high):
    kinds = ((low.shape, F32), (low.shape, LOW))
    return call(functools.partial(fold_two_kernel, bit), kinds, place, keep, low, high)


def add_kernel(a, b, out):
    out[...] = (a[...].astype(F32) + b[...].astype(F32)).astype(LOW)


def add_full_kernel(a, b, out):
    out[...] = a[...] + b[...]


def add_full(a, b):
    return call(add_full_kernel, ((a.shape, F32),), a, b)[0]


def add_low(a, b, cost=0):
    return call(add_kernel, ((a.shape, LOW),), a, b, cost=cost)[0]


def to_slots(place, sum_ref, first, keep_ref, send_ref, bit=0):
    rows, cols = sum_ref.shape[0] // 8, keep_ref.shape[2]
    here = place[(7, 5, 6)[bit]] << bit
    for slot, owner in enumerate(((0, 4, 2, 6), (0, 1, 4, 5))[bit]):
        mine = pl.ds(pl.multiple_of((owner ^ here) * rows, rows), rows)
        rest = pl.ds(pl.multiple_of((owner ^ here ^ (1 << bit)) * rows, rows), rows)
        keep_ref[slot, :rows, :] = sum_ref[mine, first : first + cols]
        send_ref[slot, :rows, :] = sum_ref[rest, first : first + cols].astype(LOW)


def all_slots(place, sum_ref, blocks):
    first = 0
    for keep_ref, send_ref in zip(blocks[::2], blocks[1::2]):
        to_slots(place, sum_ref, first, keep_ref, send_ref)
        first += keep_ref.shape[2]


def product(left, right):
    return sum(dot(a[...], b[...], 0, 0) for a, b in zip(left, right))


def grad_kernel(count, place, *refs):
    sides, blocks, sum_ref = refs[:count], refs[count:-1], refs[-1]
    half = count // 2
    sum_ref[...] = product(sides[:half], sides[half:])
    all_slots(place, sum_ref, blocks)


def cot_grad_kernel(count, place, cot_zero, cot_one, hidden_zero, hidden_one, *refs):
    blocks, sum_ref = refs[:-1], refs[-1]
    rows = cot_zero.shape[1]
    left = [c[upper] for upper in range(2) for c in (cot_zero, cot_one)]
    right = [h[k * rows : (k + 1) * rows, :] for h in (hidden_zero, hidden_one) for k in range(2)]
    sum_ref[...] = sum(dot(a, b, 0, 0) for a, b in zip(left, right))
    all_slots(place, sum_ref, blocks)


def last_kernel_one(place, normed, dq_zero, dq_one, branch_zero, branch_one, att_zero, att_one, *refs):
    *blocks, sum_ref = refs
    half, cols = att_zero.shape
    sum_ref[:, :cols] = product((branch_zero, branch_one), (att_zero, att_one))
    sum_ref[:, cols:] = dot(normed[:half, :], dq_zero[...], 0, 0) + dot(normed[half:, :], dq_one[...], 0, 0)
    all_slots(place, sum_ref, blocks)


def last_kernel_two(
    place, normed, dk, dv, small, back_zero, back_one, up_zero, up_one, mixed_sums, keep_ref, send_ref, sum_ref, flat_ref
):
    cols = dk.shape[1]
    sum_ref[:, :cols] = dot(normed[...], dk[...], 0, 0)
    sum_ref[:, cols:] = dot(normed[...], dv[...], 0, 0)
    to_slots(place, sum_ref, 0, keep_ref, send_ref)
    rows, wide_cols = keep_ref.shape[1] - 8, keep_ref.shape[2]
    count = small.shape[0] - 2
    back = back_zero[...] + back_one[...]
    wide = [small[count : count + 1, :], small[count + 1 :, :], back[2:3], back[0:1], back[1:2], back[3:4]]
    wide += [up_zero[...] + up_one[...], mixed_sums[:, :cols], mixed_sums[:, 2 * cols :]]
    for owner in range(8):
        parts = []
        for v in wide:
            n = v.shape[1] // 8
            parts.append(v[:, owner * n : (owner + 1) * n])
        parts.append(jnp.zeros((1, 2 * wide_cols - sum(p.shape[1] for p in parts)), F32))
        flat_ref[owner : owner + 1, :] = jnp.concatenate(parts, axis=1)
    first = iota((8, wide_cols), 0) == 0
    for slot, owner in enumerate((0, 4, 2, 6)):
        mine, other = (flat_ref[pl.ds(owner ^ k ^ place[7], 1), :] for k in range(2))
        keep_ref[slot, rows:, :] = jnp.where(first, mine[:, :wide_cols], mine[:, wide_cols:])
        send_ref[slot, rows:, :] = jnp.where(first, other[:, :wide_cols], other[:, wide_cols:]).astype(LOW)


def finish_kernel(
    d_keep, d_got, e_keep, e_got, in_ref, proj_ref, gain_one, bias_one, proj_b, gain_two, bias_two, down_b, up_b, qv_b
):
    rows, cols = in_ref.shape[1:]
    one = d_keep[0] + d_got[0].astype(F32)
    two = e_keep[0] + e_got[0].astype(F32)
    proj_ref[...] = one[:, :cols].T
    in_ref[0] = one[:, cols:]
    in_ref[1] = two[:rows, :cols]
    in_ref[2] = two[:rows, cols:]
    flat = jnp.concatenate([two[rows : rows + 1, :], two[rows + 1 : rows + 2, :]], axis=1)
    first = 0
    for ref in (gain_one, bias_one, proj_b, gain_two, bias_two, down_b, up_b):
        ref[...] = flat[:, first : first + ref.shape[1]]
        first += ref.shape[1]
    count = qv_b.shape[1]
    qv_b[...] = jnp.concatenate([flat[:, first : first + count], flat[:, first + count : first + 2 * count]])


def result_of(place, keep, got, res_zero, res_one, vecs):
    rows = keep.shape[0]
    residual = jnp.where(place[3] == 0, res_zero[:rows, :], res_one[:rows, :])
    return (residual + (keep[...] + got[...].astype(F32)) + vecs[5:6, :]).astype(LOW)


def result_kernel(place, keep, got, res_zero, res_one, vecs, out_ref):
    out_ref[...] = result_of(place, keep, got, res_zero, res_one, vecs)


def stack_three_kernel(pair, one, out_ref):
    out_ref[0] = pair[0]
    out_ref[1] = pair[1]
    out_ref[2] = one[...]


def stacked_three(pair, one):
    return call(stack_three_kernel, (((3, *one.shape), one.dtype),), pair, one)[0]


def pick_kernel(place, own, other, out_ref):
    out_ref[place[3]] = own[...]
    out_ref[1 - place[3]] = other[...]


def pick(place, own, other):
    return call(pick_kernel, (((2, *own.shape), own.dtype),), place, own, other)[0]


def copy_kernel(*refs):
    half = len(refs) // 2
    for a, b in zip(refs[:half], refs[half:]):
        b[...] = a[...]


def brought(*arrays, cost=0):
    return call(copy_kernel, tuple((a.shape, a.dtype) for a in arrays), *arrays, cost=cost)


def stack_kernel(a, b, out_ref):
    out_ref[0] = a[...]
    out_ref[1] = b[...]


def stacked(a, b):
    return call(stack_kernel, (((2, *a.shape), a.dtype),), a, b)[0]


def grad_blocks(kernel, place, splits, *sides):
    width, cols = sides[0].shape[-1], sides[-1].shape[1]
    shapes = []
    for n in splits:
        shapes += [((4, width // 8, n), F32), ((4, width // 8, n), LOW)]
    scratch = (pltpu.VMEM((width, cols), F32),)
    return call(functools.partial(kernel, len(sides)), shapes, place, *sides, scratch=scratch, mib=12)


def plain_grad(shard_rows, *sides):
    half = len(sides) // 2
    total = sum(dot(a, b, 0, 0) for a, b in zip(sides[:half], sides[half:])).astype(LOW)
    return dp_scatter_sum(total.reshape(-1, shard_rows, total.shape[1]))


def fast(shard_rows):
    return lax.axis_size("dp") == 8 and shard_rows % 16 == 0


def place_pieces(masks, place, pieces, write):
    for piece, owners in zip(pieces, masks):
        for k, mask in enumerate(owners):
            write(place[4] ^ mask, piece, k)


def first_kernel(masks, spans, hidden_cols, place, *refs):
    pieces, (w_in_ref, w_proj_ref, vecs_ref, up_ref, bias_ref, flat_ref) = refs[: len(masks)], refs[len(masks) :]
    width, qkv_cols = w_in_ref.shape
    shard_rows = width // 8

    def write(owner, piece, k):
        at = pl.ds(pl.multiple_of(owner * shard_rows, shard_rows), shard_rows)
        w_in_ref[at, :] = piece[k, :shard_rows, :qkv_cols]
        w_proj_ref[at, :] = piece[k, :shard_rows, qkv_cols:]
        flat_ref[pl.ds(owner, 1), :] = piece[k, shard_rows : shard_rows + 1, :].astype(F32)

    place_pieces(masks, place, pieces, write)
    flat = flat_ref[...]
    joined = [
        jnp.concatenate([flat[s : s + 1, a:b] for s in range(8)], axis=1) for a, b in zip(spans, spans[1:])
    ]
    for k in range(6):
        vecs_ref[k : k + 1, :] = joined[k]
    up_ref[...] = joined[6]
    bias_ref[...] = jnp.concatenate([joined[7], jnp.zeros_like(joined[7]), joined[8]], axis=1)


def plain_kernel(masks, firsts, place, *refs):
    *pieces, out_ref = refs
    rows = out_ref.shape[0] // 8
    for number, (piece, owners) in enumerate(zip(pieces, masks)):
        for k, mask in enumerate(owners):
            at = pl.ds(pl.multiple_of((place[4] ^ mask) * rows, rows), rows)
            out_ref[at, :] = piece[firsts[number] + k]


def pack_kernel(count, *refs):
    sources, out_ref, held, sems = refs[:count], refs[count], refs[count + 1 : -1], refs[-1]
    copies = [pltpu.make_async_copy(a, b, sems.at[k]) for k, (a, b) in enumerate(zip(sources, held))]
    for c in copies:
        c.start()
    for c in copies:
        c.wait()
    w_qkv, w_proj, *vectors = held
    rows = w_qkv.shape[1]
    out_ref[:rows, :] = jnp.concatenate([w_qkv[0], w_qkv[1], w_qkv[2], w_proj[...].T], axis=1)
    rows_of = [v[...].astype(F32) for v in vectors]
    rows_of = rows_of[:-1] + [rows_of[-1][0:1], rows_of[-1][1:2]]
    flat = jnp.concatenate(rows_of, axis=1)
    flat = jnp.concatenate([flat, jnp.zeros((1, out_ref.shape[1] - flat.shape[1]), F32)], axis=1)
    out_ref[rows:, :] = jnp.broadcast_to(flat, (8, flat.shape[1])).astype(LOW)


def first_pack(*args):
    w_qkv, w_proj = args[:2]
    return pl.pallas_call(
        functools.partial(pack_kernel, len(args)),
        out_shape=jax.ShapeDtypeStruct((w_qkv.shape[1] + 8, 3 * w_qkv.shape[2] + w_proj.shape[0]), LOW),
        in_specs=[pl.BlockSpec(memory_space=pl.ANY) for _ in args],
        out_specs=pl.BlockSpec(memory_space=pltpu.VMEM),
        scratch_shapes=[
            *(pltpu.VMEM(a.shape, a.dtype) for a in args),
            pltpu.SemaphoreType.DMA((len(args),)),
        ],
        compiler_params=pltpu.CompilerParams(vmem_limit_bytes=63 << 20),
        cost_estimate=pl.CostEstimate(flops=COST, bytes_accessed=0, transcendentals=0),
    )(*args)


def spans_of(vectors):
    spans = [0]
    for n in (*(v.shape[1] for v in vectors), vectors[-1].shape[1]):
        spans.append(spans[-1] + n)
    return spans


def first_unpacked(place, pieces, vectors, qkv_cols, head_cols, width):
    shapes = (
        ((width, qkv_cols), LOW),
        ((width, head_cols), LOW),
        ((6, width), F32),
        ((1, 8 * vectors[6].shape[1]), F32),
        ((1, qkv_cols), F32),
    )
    return call(
        functools.partial(first_kernel, MASKS, spans_of(vectors), 0),
        shapes,
        place,
        *pieces,
        scratch=(pltpu.VMEM((8, qkv_cols + head_cols), F32),),
    )


def unpacked(place, pieces, firsts):
    rows, cols = pieces[0].shape[1:]
    return call(functools.partial(plain_kernel, MASKS, firsts), (((8 * rows, cols), LOW),), place, *pieces)[0]


def plain_first(shard, vectors, qkv_cols, width):
    flat = dp_gather(jnp.concatenate([*vectors[:-1], vectors[-1][0:1], vectors[-1][1:2]], axis=1))[:, 0].astype(F32)
    whole = dp_gather(shard).reshape(width, -1)
    spans = spans_of(vectors)
    joined = [flat[:, a:b].reshape(1, -1) for a, b in zip(spans, spans[1:])]
    return (
        whole[:, :qkv_cols],
        whole[:, qkv_cols:],
        jnp.concatenate(joined[:6]),
        joined[6],
        jnp.concatenate([joined[7], jnp.zeros_like(joined[7]), joined[8]], axis=1),
    )


def down_kernel(hidden_zero, hidden_one, w_down, keep_ref, send_ref):
    rows = keep_ref.shape[1]
    for upper, hidden in enumerate((hidden_zero, hidden_one)):
        part = dot(hidden[...], w_down[...], 1, 1)
        keep_ref[upper] = part[:rows]
        send_ref[upper] = part[rows:].astype(LOW)


def local(x_embed, thoughts, thought_pos, img_start, *rest):
    *params, grad_out = rest
    dp = lax.axis_size("dp")
    table = []
    for d in range(dp):
        for t in range(4):
            table.append((t & 1, 0, 0, t >> 1, d, d >> 1 & 1, d >> 2 & 1, d & 1))
    place = jnp.asarray(table, jnp.int32)[lax.axis_index("dp") * 4 + lax.axis_index("tensor")]
    block = quick_block if fast(params[2].shape[1]) else plain_block
    block_out, grad_embed, grad_thoughts, grad_in, grad_proj, grad_up, grad_down, small = block(
        place, img_start[0], x_embed[0], thoughts[0], thought_pos, params, grad_out[0]
    )
    gain_one, bias_one, proj_b, gain_two, bias_two, down_b, up_b, qv_b = small
    flat = lambda a: a.reshape(-1)
    return (
        block_out[None],
        grad_embed[None],
        grad_thoughts,
        flat(gain_one),
        flat(bias_one),
        grad_in,
        qv_b.reshape(2, -1),
        grad_proj,
        flat(proj_b),
        flat(gain_two),
        flat(bias_two),
        grad_up,
        flat(up_b),
        grad_down,
        flat(down_b),
    )


def vectors_of(params):
    return [params[k].reshape(1, -1) for k in (0, 1, 5, 6, 7, 11, 9)] + [params[3]]


def splice_side(place, x_rows, thoughts, thought_pos):
    shape = (4 * x_rows[0].shape[1], x_rows[0].shape[2])
    return call(splice_kernel, ((shape, LOW), (shape, F32)), place, *x_rows, thoughts, thought_pos)


def input_side(xhat, vecs, w_in, bias):
    length, width = xhat.shape
    kinds = (((length, width), LOW),) + (((length, w_in.shape[1] // 3), LOW),) * 3
    return call(input_kernel, kinds, xhat, vecs, w_in, bias)


def input_back(place, thought_pos, grad_queries, grad_keys, grad_values, w_in, xhat, grad_residual):
    length, width = xhat.shape
    count = thought_pos.shape[1]
    return call(
        input_back_kernel,
        (
            ((2, length // 4, width), F32),
            ((length // 4, width), LOW),
            ((length // 4, width), LOW),
            ((-(-(count + 2) // 8) * 8, width), F32),
            ((1, w_in.shape[1]), F32),
            ((-(-count // 8) * 8, width), F32),
        ),
        place,
        thought_pos[0],
        *grad_queries,
        grad_keys,
        grad_values,
        w_in,
        xhat,
        *grad_residual,
        scratch=(pltpu.VMEM((length, width), F32),),
    )


def output_side(place, keep, got, spliced, grad_residual, vecs, thought_pos, thoughts, small, picked, *pairs):
    rows, width = keep.shape
    embed, own, *more = call(
        output_kernel,
        (
            ((rows, width), F32),
            ((thoughts.shape[0], 1, width // 4), F32),
            *((p.shape[1:], F32) for p in pairs[::2]),
        ),
        place,
        keep,
        got,
        spliced,
        *grad_residual,
        vecs,
        thought_pos,
        thoughts,
        small,
        picked,
        *pairs,
    )
    return embed, jnp.moveaxis(own, 1, 0), *more


def result(place, keep, got, residual, vecs):
    return call(result_kernel, ((keep.shape, LOW),), place, keep, got, *residual, vecs)[0]


def down_part(hidden, w_down_t):
    shape = (2, hidden[0].shape[0] // 2, w_down_t.shape[0])
    return call(down_kernel, ((shape, F32), (shape, LOW)), *hidden, w_down_t)


def quick_block(place, starts, x_own, thoughts, thought_pos, params, cot_own):
    across = lambda a: swapped(a, "dp", 1)
    near = lambda a: swapped(a, "dp", 2)
    far = lambda a: swapped(a, "dp", 4)
    core = lambda a: swapped(a, "tensor", 1)
    over = lambda a: swapped(a, "tensor", 2)
    w_qkv, w_proj, w_up, w_down_own = params[2], params[4], params[8], params[10].T
    shard_rows, head_cols = w_qkv.shape[1:]
    width = x_own.shape[1]
    vectors = vectors_of(params)

    pack = first_pack(w_qkv, w_proj, *vectors)
    pack_across = across(pack)
    pack_far = far(pack)
    x_far = over(after(x_own, pack))
    pack_here, x_here = brought(pack, after(x_own, pack))
    both = stacked(after(w_up, pack), w_down_own)
    x_far, pack_far, pack_across, pack_here, x_here, both = together(
        x_far, pack_far, pack_across, pack_here, x_here, both
    )

    pack_near, pack_far_across = near(stacked(pack_here, pack_far)), across(pack_far)
    up_far = far(after(w_up, pack_far))
    both_across = across(both)
    cot_far = over(after(cot_own, x_far))
    pack_near, pack_far_across, up_far, both_across, cot_far = together(
        pack_near, pack_far_across, up_far, both_across, cot_far
    )

    pack_near_across = across(pack_near)
    up_near = near(stacked(w_up, up_far))
    down_far = far(after(w_down_own, up_far))
    x_both = pick(place, x_here, after(x_far, up_far))
    x_other = core(x_both)
    spliced, xhat = splice_side(place, (x_both, x_other), thoughts, thought_pos)
    pack_near_across, xhat = together(pack_near_across, xhat)
    up_far_across = across(after(up_far, pack_near_across))
    pieces = (pack_here[None], pack_across[None], pack_far[None], pack_near, pack_far_across[None], pack_near_across)
    w_in, w_proj_t, vecs, up_bias, all_bias = first_unpacked(place, pieces, vectors, 3 * head_cols, head_cols, width)
    normed, queries, keys, values = input_side(xhat, vecs, w_in, all_bias)
    att_zero, log_zero, keep_zero, send_zero = attend(0, place, starts, queries, keys, values, w_proj_t)
    send_zero, up_near, down_far, up_far_across = together(send_zero, up_near, down_far, up_far_across)
    near_and_far = stacked_three(up_near, down_far)

    mine_zero = add_low(keep_zero, core(send_zero))
    far_zero = over(mine_zero)
    down_near = near(stacked(w_down_own, down_far))
    three_across = across(near_and_far)
    att_one, log_one, keep_one, send_one = attend(1, after(place, mine_zero), starts, queries, keys, values, w_proj_t)
    send_one, far_zero, three_across, down_near = together(send_one, far_zero, three_across, down_near)
    down_near_across = across(down_near)

    mine_one = add_low(keep_one, core(send_one))
    far_one = over(mine_one)
    total_zero = add_low(mine_zero, far_zero)
    other_zero = core(total_zero)
    pieces = (w_up[None], both_across, up_far[None], up_near, up_far_across[None], three_across)
    w_up_all = unpacked(place, pieces, (0, 0, 0, 0, 0, 0))
    cot_both = pick(place, cot_own, cot_far)
    cot_other = core(cot_both)
    other_zero, cot_other, w_up_all, down_near_across = together(other_zero, cot_other, w_up_all, down_near_across)
    cots = (cot_both, cot_other)
    pieces = (w_down_own[None], both_across, down_far[None], down_near, three_across, down_near_across)
    probs_one = probs_of(1, after(place, mine_one), starts, queries, keys, log_one)
    probs_zero = probs_of(0, after(place, mine_one), starts, queries, keys, log_zero)
    probs_one, probs_zero, w_pieces = together(probs_one, probs_zero, pieces[0])
    pieces = (w_pieces, *pieces[1:])
    w_down_t = unpacked(place, pieces, (0, 1, 0, 0, 2, 0))

    weights = (vecs, up_bias, w_up_all, w_down_t)
    residual_zero, normed_zero, hidden_zero, grad_zero, up_sum_zero, keep_zero, send_zero = feed(
        0, spliced, total_zero, other_zero, cots, *weights
    )
    total_one = add_low(mine_one, far_one)
    other_one = core(total_one)
    mine_zero = add_low(keep_zero, core(send_zero))
    far_zero = over(mine_zero)
    residual_one, normed_one, hidden_one, grad_one, up_sum_one, keep_one, send_one = feed(
        1, after(spliced, mine_zero), total_one, other_one, cots, *weights
    )
    hidden_cols = hidden_one.shape[1]
    mine_one = add_low(keep_one, core(send_one))
    far_one = over(mine_one)
    b_keep, b_send = grad_blocks(
        grad_kernel, place, (hidden_cols,), normed_zero, normed_one, grad_zero, grad_one
    )
    b_got = across(b_send)
    c_keep, c_send = grad_blocks(
        cot_grad_kernel, after(place, b_send), (hidden_cols,), *cots, hidden_zero, hidden_one
    )
    mlp_keep, mlp_send = down_part((hidden_zero, after(hidden_one, b_send)), w_down_t)
    total_zero = add_low(after(mine_zero, c_send, mlp_send), far_zero, cost=0)
    other_zero = core(total_zero)
    residual = (residual_zero, residual_one)

    res_zero, branch_zero, gatt_zero, delta_zero, sums_zero = branch_back(
        0, total_zero, other_zero, residual_zero, cots, vecs, w_proj_t, att_zero
    )
    dq_zero, *early = back(0, place, queries, keys, values, probs_zero, gatt_zero, delta_zero, ())
    c_got = across(after(c_send, other_zero))
    total_one = add_low(after(mine_one, early[0], b_got), far_one)
    other_one = core(total_one)
    b_keep, b_send = fold(5, place, b_keep, after(b_got, total_one))
    b_got = near(b_send)
    mlp_keep, mlp_send = fold(3, place, mlp_keep, core(after(mlp_send, other_zero)))
    mlp_got = over(after(mlp_send, total_one))
    res_one, branch_one, gatt_one, delta_one, sums_one = branch_back(
        1, total_one, other_one, residual_one, cots, vecs, w_proj_t, att_one
    )
    dq_one, dk, dv = back(1, place, queries, keys, values, probs_one, gatt_one, delta_one, early)
    dk, b_got, c_got = together(dk, b_got, c_got)

    grad_residual = (res_zero, res_one)
    kinds = (((4, shard_rows, 2 * head_cols), F32), ((4, shard_rows, 2 * head_cols), LOW))
    scratch = (pltpu.VMEM((width, 2 * head_cols), F32),)
    d_keep, d_send = call(
        last_kernel_one, kinds, place, normed, dq_zero, dq_one, branch_zero, branch_one, att_zero, att_one, scratch=scratch
    )
    d_got = across(after(d_send, dk))
    c_keep, c_send = fold(5, place, c_keep, c_got)
    c_got = near(c_send)
    b_keep, b_send = fold(6, place, b_keep, b_got)
    b_got = far(b_send)
    keep, send_low, send_high, small, mixed_sums, picked = input_back(
        place, thought_pos, (dq_zero, dq_one), dk, dv, w_in, xhat, grad_residual
    )
    got_low, got_high = core(send_low), core(send_high)
    small = add_full(small, core(small))
    small = add_full(small, over(small))
    shape = (4, shard_rows + 8, 2 * head_cols)
    e_keep, e_send = call(
        last_kernel_two,
        ((shape, F32), (shape, LOW)),
        place,
        normed,
        dk,
        dv,
        small,
        sums_zero,
        sums_one,
        up_sum_zero,
        up_sum_one,
        mixed_sums,
        scratch=(*scratch, pltpu.VMEM((8, 4 * head_cols), F32)),
    )
    e_got = across(e_send)
    keep, send = fold_two(3, place, keep, got_low, got_high)
    got = over(after(send, small))
    d_keep, d_send = fold(5, place, d_keep, after(d_got, c_got))
    d_got = near(d_send)
    c_keep, c_send = fold(6, place, c_keep, after(c_got, d_send))
    c_got = far(c_send)
    e_got, d_got, b_got = together(e_got, d_got, b_got)

    e_keep, e_send = fold(5, place, e_keep, e_got)
    e_got = near(e_send)
    d_keep, d_send = fold(6, place, d_keep, d_got)
    d_got = far(d_send)

    e_keep, e_send = fold(6, place, e_keep, e_got)
    e_got = far(e_send)
    block_out = result(place, mlp_keep[0], mlp_got[0], residual, vecs)
    grad_embed, grad_thoughts, grad_up, grad_down = output_side(
        place, keep, got, spliced, grad_residual, vecs, thought_pos, thoughts, small, picked,
        b_keep, b_got, c_keep, c_got,
    )
    grad_embed, block_out, e_got, d_got = together(grad_embed, block_out, e_got, d_got)
    grad_in, grad_proj, *small = call(
        finish_kernel,
        (
            ((3, shard_rows, head_cols), F32),
            ((head_cols, shard_rows), F32),
            *((v.shape, F32) for v in vectors),
        ),
        d_keep,
        d_got,
        e_keep,
        e_got,
    )
    return block_out, grad_embed, grad_thoughts, grad_in, grad_proj, grad_up, grad_down.T, small


def plain_block(place, starts, x_own, thoughts, thought_pos, params, cot_own):
    dp = lax.axis_size("dp")
    w_qkv, w_proj, w_up, w_down_own = params[2], params[4], params[8], params[10].T
    shard_rows, head_cols = w_qkv.shape[1:]
    width = x_own.shape[1]
    x_rows, cots = rows_gather(x_own), rows_gather(cot_own)
    shard = jnp.concatenate([w_qkv[0], w_qkv[1], w_qkv[2], w_proj.T], axis=1)
    w_in, w_proj_t, vecs, up_bias, all_bias = plain_first(shard, vectors_of(params), 3 * head_cols, width)
    w_up_all = dp_gather(w_up).reshape(width, -1)
    w_down_t = dp_gather(w_down_own).reshape(width, -1)
    spliced, xhat = splice_side(place, x_rows, thoughts, thought_pos)
    normed, queries, keys, values = input_side(xhat, vecs, w_in, all_bias)

    def all_sum(keep, send):
        mine = add_low(keep, swapped(send, "tensor", 1))
        total = add_low(mine, swapped(mine, "tensor", 2))
        return total, swapped(total, "tensor", 1)

    def own_sum(keep, send):
        keep, send = fold(3, place, keep, swapped(send, "tensor", 1))
        return keep[0], swapped(send, "tensor", 2)[0]

    atts, logs, feds, grad_twos = [], [], [], []
    for chunk in range(2):
        att, log, *part = attend(chunk, place, starts, queries, keys, values, w_proj_t)
        feds.append(feed(chunk, spliced, *all_sum(*part), cots, vecs, up_bias, w_up_all, w_down_t))
        grad_twos.append(all_sum(*feds[-1][5:]))
        atts.append(att)
        logs.append(log)
    residual, normed_two, hidden, grad_hidden, up_sums = zip(feds[0][:5], feds[1][:5])
    block_out = result(place, *own_sum(*down_part(hidden, w_down_t)), residual, vecs)
    grad_up = plain_grad(shard_rows, *normed_two, *grad_hidden)
    grad_down = plain_grad(shard_rows, cots_rows(cots, 0), cots_rows(cots, 1), *hidden)
    branches, dqs, early = [], [], ()
    for chunk in range(2):
        branches.append(
            branch_back(chunk, *grad_twos[chunk], residual[chunk], cots, vecs, w_proj_t, atts[chunk])
        )
        probs = probs_of(chunk, place, starts, queries, keys, logs[chunk])
        dq, *early = back(
            chunk, place, queries, keys, values, probs, *branches[-1][2:4], early
        )
        dqs.append(dq)
    grad_residual, grad_branch = zip(branches[0][:2], branches[1][:2])
    keep, *send, small, mixed_sums, picked = input_back(
        place, thought_pos, dqs, *early, w_in, xhat, grad_residual
    )
    grad_mixed = jnp.concatenate([jnp.concatenate(dqs), *early], axis=1)
    small = small + swapped(small, "tensor", 1)
    small = small + swapped(small, "tensor", 2)
    grad_embed, grad_thoughts = output_side(
        place, *own_sum(keep, jnp.stack(send)), spliced, grad_residual, vecs, thought_pos, thoughts, small, picked
    )
    grad_in = plain_grad(shard_rows, normed, grad_mixed).reshape(shard_rows, 3, head_cols)
    grad_proj = plain_grad(shard_rows, *grad_branch, *atts)
    two = branches[0][4] + branches[1][4]
    count = small.shape[0] - 2
    vec = (small[count], small[count + 1], two[2], two[0], two[1], two[3], up_sums[0] + up_sums[1])
    vec += (mixed_sums[0, :head_cols], mixed_sums[0, 2 * head_cols :])
    vec = jnp.concatenate([v.reshape(dp, -1) for v in vec], axis=1)
    vec = dp_scatter_sum(vec[:, None, :])[0]
    small, first = [], 0
    for n in (params[k].size for k in (0, 1, 5, 6, 7, 11, 9, 3)):
        small.append(vec[first : first + n])
        first += n
    return (
        block_out,
        grad_embed,
        grad_thoughts,
        jnp.moveaxis(grad_in, 1, 0),
        grad_proj.T,
        grad_up,
        grad_down.T,
        small,
    )


def solution(mesh):
    in_specs = (
        P("dp", "tensor", None),
        P("dp", None, None),
        P("dp", None),
        P("dp", None),
        P("dp"),
        P("dp"),
        P(None, "dp", "tensor"),
        P(None, ("tensor", "dp")),
        P("tensor", "dp"),
        P("dp"),
        P("dp"),
        P("dp"),
        P("dp", "tensor"),
        P(("tensor", "dp")),
        P("tensor", "dp"),
        P("dp"),
        P("dp", "tensor", None),
    )
    out_specs = (
        P("dp", "tensor", None),
        P("dp", "tensor", None),
        P("dp", None, "tensor"),
        P("dp"),
        P("dp"),
        P(None, "dp", "tensor"),
        P(None, ("tensor", "dp")),
        P("tensor", "dp"),
        P("dp"),
        P("dp"),
        P("dp"),
        P("dp", "tensor"),
        P(("tensor", "dp")),
        P("tensor", "dp"),
        P("dp"),
    )
    return jax.shard_map(local, mesh=mesh, in_specs=in_specs, out_specs=out_specs, check_vma=False)
```

```python
import functools

import jax
import jax.numpy as jnp
from jax import lax
from jax.experimental import pallas as pl
from jax.experimental.pallas import tpu as pltpu
from jax.sharding import PartitionSpec as P

HD = 64
IMG = 256
EPSILON = 1e-05
F32 = jnp.float32
LOW = jnp.bfloat16
COST = 1000


def swapped(array, axis, mask):
    return lax.ppermute(array, axis, [(i, i ^ mask) for i in range(lax.axis_size(axis))])


def dp_masks():
    return [1 << b for b in reversed(range(lax.axis_size("dp").bit_length() - 1))]


def slot_owners(masks):
    owners = [0]
    for mask in masks:
        owners = owners + [o ^ mask for o in owners]
    return owners


def dp_gather(shard):
    masks, me = dp_masks(), lax.axis_index("dp")
    slots = shard[None]
    for mask in masks:
        other = swapped(slots, "dp", mask)
        first = (me & mask) == 0
        slots = jnp.where(
            first, jnp.concatenate([slots, other]), jnp.concatenate([other, slots])
        )
    owners = slot_owners(masks)
    return jnp.stack([slots[owners.index(s)] for s in range(len(owners))])


MASKS = ((0,), (1,), (4,), (2, 6), (5,), (3, 7))


def rows_pick(own, other):
    first = (lax.axis_index("tensor") >> 1) == 0
    return jnp.stack([jnp.where(first, own, other), jnp.where(first, other, own)])


def dp_scatter_sum(blocks):
    masks, me = dp_masks(), lax.axis_index("dp")
    slots = jnp.stack([blocks[s] for s in slot_owners(masks)])
    for mask in reversed(masks):
        half = slots.shape[0] // 2
        first = (me & mask) == 0
        keep = jnp.where(first, slots[:half], slots[half:])
        send = jnp.where(first, slots[half:], slots[:half])
        slots = keep.astype(F32) + swapped(send, "dp", mask).astype(F32)
    return slots[0]


def rows_gather(own):
    both = rows_pick(own, swapped(own, "tensor", 2))
    return both, swapped(both, "tensor", 1)


def after(value, *others):
    return lax.optimization_barrier((value, *others))[0]


def together(*values):
    return lax.optimization_barrier(values)


def dot(a, b, ca, cb, precision=None):
    return lax.dot_general(
        a, b, (((ca,), (cb,)), ((), ())), precision=precision, preferred_element_type=F32
    )


def normalised(values):
    centred = values - jnp.mean(values, axis=-1, keepdims=True)
    inverse = lax.rsqrt(jnp.mean(centred * centred, axis=-1, keepdims=True) + EPSILON)
    return centred * inverse, inverse


def norm_back(upstream, xhat, inverse, gain):
    scaled = upstream * gain
    return inverse * (
        scaled
        - jnp.mean(scaled, axis=-1, keepdims=True)
        - xhat * jnp.mean(scaled * xhat, axis=-1, keepdims=True)
    )


def gelu_pair(u):
    k, a = 0.7978845608028654, 0.044715
    square = u * u
    t = jnp.tanh(u * (k + (k * a) * square))
    rise = 0.5 * (1.0 + t)
    return u * rise, rise + (0.5 * u) * (1.0 - t * t) * (k + (3.0 * k * a) * square)


def cots_rows(cots, chunk):
    return jnp.concatenate([c[chunk] for c in cots])


def iota(shape, dim):
    return lax.broadcasted_iota(jnp.int32, shape, dim)


def call(kernel, outs, *args, scratch=(), mib=8, cost=0):
    spec = lambda a: pl.BlockSpec(
        memory_space=pltpu.SMEM if a.ndim == 1 and a.dtype == jnp.int32 else pltpu.VMEM
    )
    return pl.pallas_call(
        kernel,
        out_shape=tuple(jax.ShapeDtypeStruct(s, t) for s, t in outs),
        in_specs=[spec(a) for a in args],
        out_specs=tuple(pl.BlockSpec(memory_space=pltpu.VMEM) for _ in outs),
        scratch_shapes=scratch,
        compiler_params=pltpu.CompilerParams(vmem_limit_bytes=mib << 20),
        cost_estimate=pl.CostEstimate(flops=COST + cost, bytes_accessed=0, transcendentals=0),
    )(*args)


def splice_kernel(place, x_zero, x_one, thoughts, thought_pos, spliced_ref, xhat_ref):
    core = place[0]
    rows = x_zero.shape[1]
    for upper in range(2):
        for rel, ref in enumerate((x_zero, x_one)):
            first = upper * 2 * rows + (core ^ rel) * rows
            part = slice((2 * upper + rel) * rows, (2 * upper + rel + 1) * rows)
            match = (first + iota((rows, 1), 0)) == thought_pos[...]
            covered = jnp.sum(match.astype(F32), axis=1, keepdims=True) > 0.0
            picked = dot(match.astype(LOW), thoughts[...], 1, 0)
            spliced = jnp.where(covered, picked, ref[upper].astype(F32))
            spliced_ref[part, :] = spliced.astype(LOW)
            xhat_ref[part, :] = normalised(spliced)[0]


def input_kernel(xhat, vecs, w_in, bias, normed_ref, q_ref, k_ref, v_ref):
    rows = xhat.shape[0] // 4
    cols = q_ref.shape[1]
    for k in range(4):
        part = slice(k * rows, (k + 1) * rows)
        normed = (xhat[part, :] * vecs[0:1, :] + vecs[1:2, :]).astype(LOW)
        normed_ref[part, :] = normed
        mixed = (dot(normed, w_in[...], 1, 0) + bias[...]).astype(LOW)
        q_ref[part, :] = mixed[:, :cols]
        k_ref[part, :] = mixed[:, cols : 2 * cols]
        v_ref[part, :] = mixed[:, 2 * cols :]


def query_limits(place, starts, chunk, rows):
    core, start = place[0], starts[chunk]
    col = iota((1, 2 * rows), 1)
    query = 2 * rows * chunk + jnp.where(col < rows, col + core * rows, col - core * rows)
    inside = (query >= start) & (query < start + IMG)
    return jnp.where(inside, start + (IMG - 1), query)


def key_positions(place, block, rows):
    first = (block >> 1) * (2 * rows) + (place[0] ^ (block & 1)) * rows
    return first + iota((rows, 1), 0)


def attend_kernel(
    chunk, place, starts, q_ref, k_ref, v_ref, w_proj,
    att_ref, log_ref, keep_ref, send_ref, acc_ref, top_ref, sum_ref,
):
    half, cols = att_ref.shape
    rows = half // 2
    heads = cols // HD
    head_of = iota((1, cols), 1) // HD
    limits = query_limits(place, starts, chunk, rows)
    queries = q_ref[chunk * half : (chunk + 1) * half, :] * LOW(0.125)
    acc_ref[...] = jnp.zeros_like(acc_ref)
    top_ref[...] = jnp.full_like(top_ref, -1e30)
    sum_ref[...] = jnp.zeros_like(sum_ref)

    @pl.loop(0, 2 * chunk + 2)
    def _(block):
        span = pl.ds(pl.multiple_of(block * rows, rows), rows)
        keys = k_ref[span, :]
        values = v_ref[span, :].T
        allowed = key_positions(place, block, rows) <= limits
        for head in range(heads):
            scores = dot(jnp.where(head_of == head, keys, LOW(0)), queries, 1, 1)
            scores = jnp.where(allowed, scores, -1e30)
            top = top_ref[head : head + 1, :]
            new_top = jnp.maximum(top, jnp.max(scores, axis=0, keepdims=True))
            exps = jnp.exp(scores - new_top)
            fade = jnp.exp(top - new_top)
            top_ref[head : head + 1, :] = new_top
            sum_ref[head : head + 1, :] = sum_ref[head : head + 1, :] * fade + jnp.sum(
                exps, axis=0, keepdims=True
            )
            part = slice(head * HD, (head + 1) * HD)
            acc_ref[part, :] = acc_ref[part, :] * fade + dot(values[part, :], exps.astype(LOW), 1, 0)

    for head in range(heads):
        part = slice(head * HD, (head + 1) * HD)
        acc_ref[part, :] = acc_ref[part, :] / sum_ref[head : head + 1, :]
    log_ref[...] = top_ref[...] + jnp.log(jnp.maximum(sum_ref[...], 1e-30))
    attended = acc_ref[...].T.astype(LOW)
    att_ref[...] = attended
    branch = dot(attended, w_proj[...], 1, 1)
    keep_ref[...] = branch[:rows]
    send_ref[...] = branch[rows:].astype(LOW)


def attend(chunk, place, starts, queries, keys, values, w_proj):
    length, cols = queries.shape
    half, width = length // 2, w_proj.shape[0]
    return call(
        functools.partial(attend_kernel, chunk),
        (
            ((half, cols), LOW),
            ((8, half), F32),
            ((half // 2, width), F32),
            ((half // 2, width), LOW),
        ),
        place,
        starts,
        queries,
        keys,
        values,
        w_proj,
        scratch=(
            pltpu.VMEM((cols, half), F32),
            pltpu.VMEM((8, half), F32),
            pltpu.VMEM((8, half), F32),
        ),
    )


def feed_kernel(
    chunk, spliced, total, other, cot_zero, cot_one, vecs, up_bias, w_up, w_down,
    residual_ref, normed_ref, hidden_ref, grad_ref, sum_ref, keep_ref, send_ref,
):
    half, width = residual_ref.shape
    rows = half // 2
    for rel, ref in enumerate((total, other)):
        part = slice(rel * rows, (rel + 1) * rows)
        residual = (
            spliced[chunk * half + rel * rows : chunk * half + (rel + 1) * rows, :].astype(F32)
            + ref[...].astype(F32)
            + vecs[2:3, :]
        )
        residual_ref[part, :] = residual
        xhat, _ = normalised(residual)
        normed_ref[part, :] = (xhat * vecs[3:4, :] + vecs[4:5, :]).astype(LOW)
    hidden_cols = w_up.shape[1]
    step = 256 if hidden_cols % 256 == 0 else hidden_cols
    for first in range(0, hidden_cols, step):
        cols = slice(first, first + step)
        hidden, slope = gelu_pair(dot(normed_ref[...], w_up[:, cols], 1, 0) + up_bias[:, cols])
        hidden_ref[:, cols] = hidden.astype(LOW)
        back = jnp.concatenate(
            [dot(cot_zero[chunk], w_down[:, cols], 1, 0), dot(cot_one[chunk], w_down[:, cols], 1, 0)]
        )
        grad = (back * slope).astype(LOW)
        grad_ref[:, cols] = grad
        sum_ref[:, cols] = jnp.sum(grad.astype(F32), axis=0, keepdims=True)
    back = dot(grad_ref[...], w_up[...], 1, 1)
    keep_ref[...] = back[:rows]
    send_ref[...] = back[rows:].astype(LOW)


def feed(chunk, spliced, total, other, cots, vecs, up_bias, w_up, w_down):
    length, width = spliced.shape
    half, hidden = length // 2, w_up.shape[1]
    return call(
        functools.partial(feed_kernel, chunk),
        (
            ((half, width), F32),
            ((half, width), LOW),
            ((half, hidden), LOW),
            ((half, hidden), LOW),
            ((1, hidden), F32),
            ((half // 2, width), F32),
            ((half // 2, width), LOW),
        ),
        spliced,
        total,
        other,
        *cots,
        vecs,
        up_bias,
        w_up,
        w_down,
    )


def norm_back_kernel(
    chunk, total, other, residual, cot_zero, cot_one, vecs, w_proj, att,
    grad_res_ref, branch_ref, gatt_ref, delta_ref, sums_ref,
):
    half, width = residual.shape
    rows = half // 2
    gain = vecs[3:4, :]
    sums = [0.0, 0.0, 0.0, 0.0]
    for rel, (ref, cot) in enumerate(((total, cot_zero), (other, cot_one))):
        part = slice(rel * rows, (rel + 1) * rows)
        upstream = ref[...].astype(F32)
        xhat, inverse = normalised(residual[part, :])
        out_grad = cot[chunk].astype(F32)
        grad_res = out_grad + norm_back(upstream, xhat, inverse, gain)
        grad_res_ref[part, :] = grad_res
        branch_ref[part, :] = grad_res.astype(LOW)
        for k, term in enumerate((upstream * xhat, upstream, grad_res, out_grad)):
            sums[k] = sums[k] + jnp.sum(term, axis=0, keepdims=True)
    for k in range(4):
        sums_ref[k : k + 1, :] = sums[k]
    grad_att = dot(branch_ref[...], w_proj[...], 1, 0).astype(LOW)
    gatt_ref[...] = grad_att
    cols = att.shape[1]
    head_rows = (iota((8, cols), 0) == iota((8, cols), 1) // HD).astype(F32)
    delta_ref[...] = dot(
        head_rows, grad_att.astype(F32) * att[...].astype(F32), 1, 1, lax.Precision.HIGHEST
    )


def branch_back(chunk, total, other, residual, cots, vecs, w_proj, att):
    half, width = residual.shape
    cols = att.shape[1]
    return call(
        functools.partial(norm_back_kernel, chunk),
        (((half, width), F32), ((half, width), LOW), ((half, cols), LOW), ((8, half), F32), ((8, width), F32)),
        total,
        other,
        residual,
        *cots,
        vecs,
        w_proj,
        att,
    )


def probs_kernel(chunk, place, starts, q_ref, k_ref, log, out_ref):
    heads, _, half = out_ref.shape
    cols = q_ref.shape[1]
    rows = half // 2
    head_of = iota((1, cols), 1) // HD
    limits = query_limits(place, starts, chunk, rows)

    @pl.loop(0, 2 * chunk + 2)
    def _(block):
        span = pl.ds(pl.multiple_of(block * rows, rows), rows)
        keys = k_ref[span, :]
        queries = q_ref[chunk * half : (chunk + 1) * half, :] * LOW(0.125)
        allowed = key_positions(place, block, rows) <= limits
        for head in range(heads):
            scores = dot(jnp.where(head_of == head, keys, LOW(0)), queries, 1, 1)
            probs = jnp.exp(jnp.where(allowed, scores, -1e30) - log[head : head + 1, :])
            out_ref[head, span, :] = probs.astype(LOW)


def probs_of(chunk, place, starts, queries, keys, log):
    length, cols = queries.shape
    half = length // 2
    shape = (cols // HD, half * (chunk + 1), half)
    return call(functools.partial(probs_kernel, chunk), ((shape, LOW),), place, starts, queries, keys, log)[0]


def back_kernel(chunk, place, q_ref, k_ref, v_ref, probs_ref, gatt_ref, delta_ref, *rest):
    keys_in, rest = (rest[:2], rest[2:]) if chunk else ((), rest)
    dq_ref, dk_ref, dv_ref, dqt_ref = rest
    half, cols = gatt_ref.shape
    rows = half // 2
    heads = cols // HD
    head_of = iota((1, cols), 1) // HD
    dqt_ref[...] = jnp.zeros_like(dqt_ref)

    @pl.loop(0, 2 * chunk + 2)
    def _(block):
        span = pl.ds(pl.multiple_of(block * rows, rows), rows)
        values = v_ref[span, :]
        keys_t = k_ref[span, :].T
        queries = q_ref[chunk * half : (chunk + 1) * half, :] * LOW(0.125)
        grad_att = gatt_ref[...]
        dk = jnp.zeros((rows, cols), F32)
        dv = jnp.zeros((rows, cols), F32)
        for head in range(heads):
            mine = head_of == head
            probs = probs_ref[head, span, :]
            grad_probs = dot(jnp.where(mine, values, LOW(0)), grad_att, 1, 1)
            grad_scores = (probs.astype(F32) * (grad_probs - delta_ref[head : head + 1, :])).astype(LOW)
            dv = dv + dot(probs, jnp.where(mine, grad_att, LOW(0)), 1, 0)
            dk = dk + dot(grad_scores, jnp.where(mine, queries, LOW(0)), 1, 0)
            part = slice(head * HD, (head + 1) * HD)
            dqt_ref[part, :] = dqt_ref[part, :] + dot(keys_t[part, :], grad_scores, 1, 0)
        if chunk:
            seen = jnp.where(block < 2, 1.0, 0.0)
            early = pl.ds(pl.multiple_of((block & 1) * rows, rows), rows)
            dk = dk + keys_in[0][early, :] * seen
            dv = dv + keys_in[1][early, :] * seen
        dk_ref[span, :] = dk.astype(dk_ref.dtype)
        dv_ref[span, :] = dv.astype(dv_ref.dtype)

    dq_ref[...] = (dqt_ref[...] * 0.125).T.astype(LOW)


def back(chunk, place, queries, keys, values, probs, grad_att, delta, early):
    half, cols = grad_att.shape
    kind = (((half * (chunk + 1), cols), LOW if chunk else F32),) * 2
    return call(
        functools.partial(back_kernel, chunk),
        (((half, cols), LOW), *kind),
        place,
        queries,
        keys,
        values,
        probs,
        grad_att,
        delta,
        *early,
        scratch=(pltpu.VMEM((cols, half), F32),),
    )


def input_back_kernel(
    place, thought_pos, dq_zero, dq_one, dk, dv, w_in, xhat, res_zero, res_one,
    keep_ref, low_ref, high_ref, small_ref, colsum_ref, picked_ref, grad_ref,
):
    half, cols = dq_zero.shape
    rows = half // 2
    sums = [0.0, 0.0, 0.0]
    for upper, dq in enumerate((dq_zero, dq_one)):
        for rel in range(2):
            part = slice((2 * upper + rel) * rows, (2 * upper + rel + 1) * rows)
            mixed = jnp.concatenate(
                [dq[rel * rows : (rel + 1) * rows, :], dk[part, :], dv[part, :]], axis=1
            )
            grad = dot(mixed, w_in[...], 1, 1)
            grad_ref[part, :] = grad
            if rel:
                (low_ref, high_ref)[upper][...] = grad.astype(LOW)
            else:
                keep_ref[upper] = grad
            terms = (grad * xhat[part, :], grad, mixed.astype(F32))
            sums = [a + jnp.sum(b, axis=0, keepdims=True) for a, b in zip(sums, terms)]
    small_ref[...] = jnp.zeros_like(small_ref)
    picked_ref[...] = jnp.zeros_like(picked_ref)
    count = thought_pos.shape[0]
    for k in range(count):
        at = thought_pos[k]
        row = (at // half) * half + (((at // rows) & 1) ^ place[0]) * rows + at % rows
        small_ref[k : k + 1, :] = grad_ref[pl.ds(row, 1), :]
        low = res_zero[pl.ds(jnp.minimum(row, half - 1), 1), :]
        high = res_one[pl.ds(jnp.maximum(row - half, 0), 1), :]
        picked_ref[k : k + 1, :] = jnp.where(row < half, low, high)
    small_ref[count : count + 1, :] = sums[0]
    small_ref[count + 1 : count + 2, :] = sums[1]
    colsum_ref[...] = sums[2]


def output_kernel(place, keep, got, spliced, res_zero, res_one, vecs, thought_pos, thoughts, small, picked, *rest):
    pairs, (embed_ref, rows_ref, *more) = rest[: 2 * ((len(rest) - 2) // 3)], rest[2 * ((len(rest) - 2) // 3) :]
    rows = keep.shape[0]
    gain = vecs[0:1, :]
    own = pl.ds(pl.multiple_of(place[3] * (2 * rows), 2 * rows), rows)
    xhat, inverse = normalised(spliced[own, :].astype(F32))
    residual = jnp.where(place[3] == 0, res_zero[:rows, :], res_one[:rows, :])
    grad = norm_back(keep[...] + got[...].astype(F32), xhat, inverse, gain) + residual
    at = (2 * place[3] + place[0]) * rows + iota((rows, 1), 0)
    covered = jnp.sum((at == thought_pos[...]).astype(F32), axis=1, keepdims=True) > 0.0
    embed_ref[...] = jnp.where(covered, 0.0, grad)
    count = thoughts.shape[0]
    xhat, inverse = normalised(thoughts[...].astype(F32))
    grad = norm_back(small[:count, :], xhat, inverse, gain) + picked[:count, :]
    cols = rows_ref.shape[2]
    rank = 2 * place[3] + place[0]
    grad = sum(jnp.where(rank == k, 1.0, 0.0) * grad[:, k * cols : (k + 1) * cols] for k in range(4))
    for k in range(count):
        rows_ref[k] = grad[k : k + 1, :]
    for ref, keep, got in zip(more, pairs[::2], pairs[1::2]):
        ref[...] = keep[0] + got[0].astype(F32)


def end_kernel(place, keep, got, mlp_got, pre_zero, pre_one, *rest):
    *rest, result_ref = rest
    width = result_ref.shape[1]
    result_ref[...] = result_of(place, keep[:, width:], mlp_got, pre_zero, pre_one, rest[3])
    output_kernel(place, keep[:, :width], got, *rest)


def fold_kernel(bit, place, *refs):
    *parts, keep_ref, send_ref = refs
    half = keep_ref.shape[0]
    mine = place[bit] * half
    rest = half - mine
    first = 0
    for keep, got in zip(parts[::2], parts[1::2]):
        rows, cols = keep.shape[1:]
        below = rows < 16 and first > 0
        if below:
            at = (slice(keep_ref.shape[1] - rows, None), slice(0, cols))
        else:
            at = (slice(0, rows), slice(first, first + cols))
            first += cols
        for k in range(half):
            keep_ref[(k, *at)] = keep[mine + k] + got[mine + k].astype(F32)
            send_ref[(k, *at)] = (keep[rest + k] + got[rest + k].astype(F32)).astype(LOW)


def fold(bit, place, *parts):
    under = [p.shape[1] for p in parts[2::2] if p.shape[1] < 16]
    cols = sum(p.shape[2] for k, p in enumerate(parts[::2]) if k == 0 or p.shape[1] >= 16)
    shape = (parts[0].shape[0] // 2, parts[0].shape[1] + sum(under), cols)
    return call(functools.partial(fold_kernel, bit), ((shape, F32), (shape, LOW)), place, *parts)


def fold_rows_kernel(bit, place, keep, low, high, mlp_keep, mlp_got, keep_ref, send_ref, mlp_ref):
    first, cols = place[bit] == 0, low.shape[1]
    low, high = keep[0] + low[...].astype(F32), keep[1] + high[...].astype(F32)
    keep_ref[:, :cols] = jnp.where(first, low, high)
    send_ref[...] = jnp.where(first, high, low).astype(LOW)
    low, high = (mlp_keep[k] + mlp_got[k].astype(F32) for k in range(2))
    keep_ref[:, cols:] = jnp.where(first, low, high)
    mlp_ref[...] = jnp.where(first, high, low).astype(LOW)


def fold_rows(bit, place, keep, low, high, mlp_keep, mlp_got):
    shape = (low.shape[0], 2 * low.shape[1])
    args = (keep, low, high, mlp_keep, mlp_got)
    kinds = ((shape, F32), (low.shape, LOW), (low.shape, LOW))
    return call(functools.partial(fold_rows_kernel, bit), kinds, place, *args)


def add_kernel(a, b, out):
    out[...] = (a[...].astype(F32) + b[...].astype(F32)).astype(LOW)


def add_full_kernel(a, b, out):
    out[...] = a[...] + b[...]


def add_full(a, b):
    return call(add_full_kernel, ((a.shape, F32),), a, b)[0]


def add_low(a, b, cost=0):
    return call(add_kernel, ((a.shape, LOW),), a, b, cost=cost)[0]


def to_slots(place, sum_ref, first, keep_ref, send_ref, bit=0):
    rows, cols = sum_ref.shape[0] // 8, keep_ref.shape[2]
    here = place[(7, 5, 6)[bit]] << bit
    for slot, owner in enumerate(((0, 4, 2, 6), (0, 1, 4, 5))[bit]):
        mine = pl.ds(pl.multiple_of((owner ^ here) * rows, rows), rows)
        rest = pl.ds(pl.multiple_of((owner ^ here ^ (1 << bit)) * rows, rows), rows)
        keep_ref[slot, :rows, :] = sum_ref[mine, first : first + cols]
        send_ref[slot, :rows, :] = sum_ref[rest, first : first + cols].astype(LOW)


def all_slots(place, sum_ref, blocks):
    first = 0
    for keep_ref, send_ref in zip(blocks[::2], blocks[1::2]):
        to_slots(place, sum_ref, first, keep_ref, send_ref)
        first += keep_ref.shape[2]


def product(left, right):
    return sum(dot(a[...], b[...], 0, 0) for a, b in zip(left, right))


def grad_kernel(count, place, *refs):
    sides, blocks, sum_ref = refs[:count], refs[count:-1], refs[-1]
    half = count // 2
    sum_ref[...] = product(sides[:half], sides[half:])
    all_slots(place, sum_ref, blocks)


def cot_grad_kernel(count, place, cot_zero, cot_one, hidden_zero, hidden_one, *refs):
    blocks, sum_ref = refs[:-1], refs[-1]
    rows = cot_zero.shape[1]
    left = [c[upper] for upper in range(2) for c in (cot_zero, cot_one)]
    right = [h[k * rows : (k + 1) * rows, :] for h in (hidden_zero, hidden_one) for k in range(2)]
    sum_ref[...] = sum(dot(a, b, 0, 0) for a, b in zip(left, right))
    all_slots(place, sum_ref, blocks)


def last_kernel_one(place, normed, dq_zero, dq_one, branch_zero, branch_one, att_zero, att_one, *refs):
    *blocks, sum_ref = refs
    half, cols = att_zero.shape
    sum_ref[:, :cols] = product((branch_zero, branch_one), (att_zero, att_one))
    sum_ref[:, cols:] = dot(normed[:half, :], dq_zero[...], 0, 0) + dot(normed[half:, :], dq_one[...], 0, 0)
    all_slots(place, sum_ref, blocks)


def last_kernel_two(
    place, normed, dk, dv, small, back_zero, back_one, up_zero, up_one, mixed_sums, keep_ref, send_ref, sum_ref, flat_ref
):
    cols = dk.shape[1]
    sum_ref[:, :cols] = dot(normed[...], dk[...], 0, 0)
    sum_ref[:, cols:] = dot(normed[...], dv[...], 0, 0)
    to_slots(place, sum_ref, 0, keep_ref, send_ref)
    rows, wide_cols = keep_ref.shape[1] - 8, keep_ref.shape[2]
    count = small.shape[0] - 2
    back = back_zero[...] + back_one[...]
    wide = [small[count : count + 1, :], small[count + 1 :, :], back[2:3], back[0:1], back[1:2], back[3:4]]
    wide += [up_zero[...] + up_one[...], mixed_sums[:, :cols], mixed_sums[:, 2 * cols :]]
    for owner in range(8):
        parts = []
        for v in wide:
            n = v.shape[1] // 8
            parts.append(v[:, owner * n : (owner + 1) * n])
        parts.append(jnp.zeros((1, 2 * wide_cols - sum(p.shape[1] for p in parts)), F32))
        flat_ref[owner : owner + 1, :] = jnp.concatenate(parts, axis=1)
    first = iota((8, wide_cols), 0) == 0
    for slot, owner in enumerate((0, 4, 2, 6)):
        mine, other = (flat_ref[pl.ds(owner ^ k ^ place[7], 1), :] for k in range(2))
        keep_ref[slot, rows:, :] = jnp.where(first, mine[:, :wide_cols], mine[:, wide_cols:])
        send_ref[slot, rows:, :] = jnp.where(first, other[:, :wide_cols], other[:, wide_cols:]).astype(LOW)


def finish_kernel(
    d_keep, d_got, e_keep, e_got, in_ref, proj_ref, gain_one, bias_one, proj_b, gain_two, bias_two, down_b, up_b, qv_b
):
    rows, cols = in_ref.shape[1:]
    one = d_keep[0] + d_got[0].astype(F32)
    two = e_keep[0] + e_got[0].astype(F32)
    proj_ref[...] = one[:, :cols].T
    in_ref[0] = one[:, cols:]
    in_ref[1] = two[:rows, :cols]
    in_ref[2] = two[:rows, cols:]
    flat = jnp.concatenate([two[rows : rows + 1, :], two[rows + 1 : rows + 2, :]], axis=1)
    first = 0
    for ref in (gain_one, bias_one, proj_b, gain_two, bias_two, down_b, up_b):
        ref[...] = flat[:, first : first + ref.shape[1]]
        first += ref.shape[1]
    count = qv_b.shape[1]
    qv_b[...] = jnp.concatenate([flat[:, first : first + count], flat[:, first + count : first + 2 * count]])


def result_of(place, keep, got, res_zero, res_one, vecs):
    rows = keep.shape[0]
    residual = jnp.where(place[3] == 0, res_zero[:rows, :], res_one[:rows, :])
    return (residual + (keep[...] + got[...].astype(F32)) + vecs[5:6, :]).astype(LOW)


def result_kernel(place, keep, got, res_zero, res_one, vecs, out_ref):
    out_ref[...] = result_of(place, keep, got, res_zero, res_one, vecs)


def stack_three_kernel(pair, one, out_ref):
    out_ref[0] = pair[0]
    out_ref[1] = pair[1]
    out_ref[2] = one[...]


def stacked_three(pair, one):
    return call(stack_three_kernel, (((3, *one.shape), one.dtype),), pair, one)[0]


def pick_kernel(place, own, other, out_ref):
    out_ref[place[3]] = own[...]
    out_ref[1 - place[3]] = other[...]


def pick(place, own, other):
    return call(pick_kernel, (((2, *own.shape), own.dtype),), place, own, other)[0]


def copy_kernel(*refs):
    half = len(refs) // 2
    for a, b in zip(refs[:half], refs[half:]):
        b[...] = a[...]


def brought(*arrays, cost=0):
    return call(copy_kernel, tuple((a.shape, a.dtype) for a in arrays), *arrays, cost=cost)


def stack_kernel(a, b, out_ref):
    out_ref[0] = a[...]
    out_ref[1] = b[...]


def stacked(a, b):
    return call(stack_kernel, (((2, *a.shape), a.dtype),), a, b)[0]


def grad_blocks(kernel, place, splits, *sides):
    width, cols = sides[0].shape[-1], sides[-1].shape[1]
    shapes = []
    for n in splits:
        shapes += [((4, width // 8, n), F32), ((4, width // 8, n), LOW)]
    scratch = (pltpu.VMEM((width, cols), F32),)
    return call(functools.partial(kernel, len(sides)), shapes, place, *sides, scratch=scratch, mib=12)


def plain_grad(shard_rows, *sides):
    half = len(sides) // 2
    total = sum(dot(a, b, 0, 0) for a, b in zip(sides[:half], sides[half:])).astype(LOW)
    return dp_scatter_sum(total.reshape(-1, shard_rows, total.shape[1]))


def fast(shard_rows):
    return lax.axis_size("dp") == 8 and shard_rows % 16 == 0


def place_pieces(masks, place, pieces, write):
    for piece, owners in zip(pieces, masks):
        for k, mask in enumerate(owners):
            write(place[4] ^ mask, piece, k)


def first_kernel(masks, spans, hidden_cols, place, *refs):
    pieces, (w_in_ref, w_proj_ref, vecs_ref, up_ref, bias_ref, flat_ref) = refs[: len(masks)], refs[len(masks) :]
    width, qkv_cols = w_in_ref.shape
    shard_rows = width // 8

    def write(owner, piece, k):
        at = pl.ds(pl.multiple_of(owner * shard_rows, shard_rows), shard_rows)
        w_in_ref[at, :] = piece[k, :shard_rows, :qkv_cols]
        w_proj_ref[at, :] = piece[k, :shard_rows, qkv_cols:]
        flat_ref[pl.ds(owner, 1), :] = piece[k, shard_rows : shard_rows + 1, :].astype(F32)

    place_pieces(masks, place, pieces, write)
    flat = flat_ref[...]
    joined = [
        jnp.concatenate([flat[s : s + 1, a:b] for s in range(8)], axis=1) for a, b in zip(spans, spans[1:])
    ]
    for k in range(6):
        vecs_ref[k : k + 1, :] = joined[k]
    up_ref[...] = joined[6]
    bias_ref[...] = jnp.concatenate([joined[7], jnp.zeros_like(joined[7]), joined[8]], axis=1)


def plain_kernel(masks, firsts, place, *refs):
    *pieces, out_ref = refs
    rows = out_ref.shape[0] // 8
    for number, (piece, owners) in enumerate(zip(pieces, masks)):
        for k, mask in enumerate(owners):
            at = pl.ds(pl.multiple_of((place[4] ^ mask) * rows, rows), rows)
            out_ref[at, :] = piece[firsts[number] + k]


def pack_kernel(count, *refs):
    sources, out_ref, held, sems = refs[:count], refs[count], refs[count + 1 : -1], refs[-1]
    copies = [pltpu.make_async_copy(a, b, sems.at[k]) for k, (a, b) in enumerate(zip(sources, held))]
    for c in copies:
        c.start()
    for c in copies:
        c.wait()
    w_qkv, w_proj, *vectors = held
    rows = w_qkv.shape[1]
    out_ref[:rows, :] = jnp.concatenate([w_qkv[0], w_qkv[1], w_qkv[2], w_proj[...].T], axis=1)
    rows_of = [v[...].astype(F32) for v in vectors]
    rows_of = rows_of[:-1] + [rows_of[-1][0:1], rows_of[-1][1:2]]
    flat = jnp.concatenate(rows_of, axis=1)
    flat = jnp.concatenate([flat, jnp.zeros((1, out_ref.shape[1] - flat.shape[1]), F32)], axis=1)
    out_ref[rows:, :] = jnp.broadcast_to(flat, (8, flat.shape[1])).astype(LOW)


def first_pack(*args):
    w_qkv, w_proj = args[:2]
    return pl.pallas_call(
        functools.partial(pack_kernel, len(args)),
        out_shape=jax.ShapeDtypeStruct((w_qkv.shape[1] + 8, 3 * w_qkv.shape[2] + w_proj.shape[0]), LOW),
        in_specs=[pl.BlockSpec(memory_space=pl.ANY) for _ in args],
        out_specs=pl.BlockSpec(memory_space=pltpu.VMEM),
        scratch_shapes=[
            *(pltpu.VMEM(a.shape, a.dtype) for a in args),
            pltpu.SemaphoreType.DMA((len(args),)),
        ],
        compiler_params=pltpu.CompilerParams(vmem_limit_bytes=63 << 20),
        cost_estimate=pl.CostEstimate(flops=COST, bytes_accessed=0, transcendentals=0),
    )(*args)


def spans_of(vectors):
    spans = [0]
    for n in (*(v.shape[1] for v in vectors), vectors[-1].shape[1]):
        spans.append(spans[-1] + n)
    return spans


def first_unpacked(place, pieces, vectors, qkv_cols, head_cols, width):
    shapes = (
        ((width, qkv_cols), LOW),
        ((width, head_cols), LOW),
        ((6, width), F32),
        ((1, 8 * vectors[6].shape[1]), F32),
        ((1, qkv_cols), F32),
    )
    return call(
        functools.partial(first_kernel, MASKS, spans_of(vectors), 0),
        shapes,
        place,
        *pieces,
        scratch=(pltpu.VMEM((8, qkv_cols + head_cols), F32),),
    )


def unpacked(place, pieces, firsts):
    rows, cols = pieces[0].shape[1:]
    return call(functools.partial(plain_kernel, MASKS, firsts), (((8 * rows, cols), LOW),), place, *pieces)[0]


def plain_first(shard, vectors, qkv_cols, width):
    flat = dp_gather(jnp.concatenate([*vectors[:-1], vectors[-1][0:1], vectors[-1][1:2]], axis=1))[:, 0].astype(F32)
    whole = dp_gather(shard).reshape(width, -1)
    spans = spans_of(vectors)
    joined = [flat[:, a:b].reshape(1, -1) for a, b in zip(spans, spans[1:])]
    return (
        whole[:, :qkv_cols],
        whole[:, qkv_cols:],
        jnp.concatenate(joined[:6]),
        joined[6],
        jnp.concatenate([joined[7], jnp.zeros_like(joined[7]), joined[8]], axis=1),
    )


def down_kernel(hidden_zero, hidden_one, w_down, keep_ref, send_ref):
    rows = keep_ref.shape[1]
    for upper, hidden in enumerate((hidden_zero, hidden_one)):
        part = dot(hidden[...], w_down[...], 1, 1)
        keep_ref[upper] = part[:rows]
        send_ref[upper] = part[rows:].astype(LOW)


def local(x_embed, thoughts, thought_pos, img_start, *rest):
    *params, grad_out = rest
    dp = lax.axis_size("dp")
    table = []
    for d in range(dp):
        for t in range(4):
            table.append((t & 1, 0, 0, t >> 1, d, d >> 1 & 1, d >> 2 & 1, d & 1))
    place = jnp.asarray(table, jnp.int32)[lax.axis_index("dp") * 4 + lax.axis_index("tensor")]
    block = quick_block if fast(params[2].shape[1]) else plain_block
    block_out, grad_embed, grad_thoughts, grad_in, grad_proj, grad_up, grad_down, small = block(
        place, img_start[0], x_embed[0], thoughts[0], thought_pos, params, grad_out[0]
    )
    gain_one, bias_one, proj_b, gain_two, bias_two, down_b, up_b, qv_b = small
    flat = lambda a: a.reshape(-1)
    return (
        block_out[None],
        grad_embed[None],
        grad_thoughts,
        flat(gain_one),
        flat(bias_one),
        grad_in,
        qv_b.reshape(2, -1),
        grad_proj,
        flat(proj_b),
        flat(gain_two),
        flat(bias_two),
        grad_up,
        flat(up_b),
        grad_down,
        flat(down_b),
    )


def vectors_of(params):
    return [params[k].reshape(1, -1) for k in (0, 1, 5, 6, 7, 11, 9)] + [params[3]]


def splice_side(place, x_rows, thoughts, thought_pos):
    shape = (4 * x_rows[0].shape[1], x_rows[0].shape[2])
    return call(splice_kernel, ((shape, LOW), (shape, F32)), place, *x_rows, thoughts, thought_pos)


def input_side(xhat, vecs, w_in, bias):
    length, width = xhat.shape
    kinds = (((length, width), LOW),) + (((length, w_in.shape[1] // 3), LOW),) * 3
    return call(input_kernel, kinds, xhat, vecs, w_in, bias)


def input_back(place, thought_pos, grad_queries, grad_keys, grad_values, w_in, xhat, grad_residual):
    length, width = xhat.shape
    count = thought_pos.shape[1]
    return call(
        input_back_kernel,
        (
            ((2, length // 4, width), F32),
            ((length // 4, width), LOW),
            ((length // 4, width), LOW),
            ((-(-(count + 2) // 8) * 8, width), F32),
            ((1, w_in.shape[1]), F32),
            ((-(-count // 8) * 8, width), F32),
        ),
        place,
        thought_pos[0],
        *grad_queries,
        grad_keys,
        grad_values,
        w_in,
        xhat,
        *grad_residual,
        scratch=(pltpu.VMEM((length, width), F32),),
    )


def output_side(place, keep, got, spliced, grad_residual, vecs, thought_pos, thoughts, small, picked, *pairs):
    rows, width = keep.shape
    embed, own, *more = call(
        output_kernel,
        (
            ((rows, width), F32),
            ((thoughts.shape[0], 1, width // 4), F32),
            *((p.shape[1:], F32) for p in pairs[::2]),
        ),
        place,
        keep,
        got,
        spliced,
        *grad_residual,
        vecs,
        thought_pos,
        thoughts,
        small,
        picked,
        *pairs,
    )
    return embed, jnp.moveaxis(own, 1, 0), *more


def result(place, keep, got, residual, vecs):
    return call(result_kernel, ((keep.shape, LOW),), place, keep, got, *residual, vecs)[0]


def down_part(hidden, w_down_t):
    shape = (2, hidden[0].shape[0] // 2, w_down_t.shape[0])
    return call(down_kernel, ((shape, F32), (shape, LOW)), *hidden, w_down_t)


def quick_block(place, starts, x_own, thoughts, thought_pos, params, cot_own):
    across = lambda a: swapped(a, "dp", 1)
    near = lambda a: swapped(a, "dp", 2)
    far = lambda a: swapped(a, "dp", 4)
    core = lambda a: swapped(a, "tensor", 1)
    over = lambda a: swapped(a, "tensor", 2)
    w_qkv, w_proj, w_up, w_down_own = params[2], params[4], params[8], params[10].T
    shard_rows, head_cols = w_qkv.shape[1:]
    width = x_own.shape[1]
    vectors = vectors_of(params)

    pack = first_pack(w_qkv, w_proj, *vectors)
    pack_across = across(pack)
    pack_far = far(pack)
    x_far = over(after(x_own, pack))
    pack_here, x_here = brought(pack, after(x_own, pack))
    both = stacked(after(w_up, pack), w_down_own)
    x_far, pack_far, pack_across, pack_here, x_here, both = together(
        x_far, pack_far, pack_across, pack_here, x_here, both
    )

    pack_near, pack_far_across = near(stacked(pack_here, pack_far)), across(pack_far)
    up_far = far(after(w_up, pack_far))
    both_across = across(both)
    cot_far = over(after(cot_own, x_far))
    pack_near, pack_far_across, up_far, both_across, cot_far = together(
        pack_near, pack_far_across, up_far, both_across, cot_far
    )

    pack_near_across = across(pack_near)
    up_near = near(stacked(w_up, up_far))
    down_far = far(after(w_down_own, up_far))
    x_both = pick(place, x_here, after(x_far, up_far))
    x_other = core(x_both)
    spliced, xhat = splice_side(place, (x_both, x_other), thoughts, thought_pos)
    pack_near_across, xhat = together(pack_near_across, xhat)
    up_far_across = across(after(up_far, pack_near_across))
    pieces = (pack_here[None], pack_across[None], pack_far[None], pack_near, pack_far_across[None], pack_near_across)
    w_in, w_proj_t, vecs, up_bias, all_bias = first_unpacked(place, pieces, vectors, 3 * head_cols, head_cols, width)
    normed, queries, keys, values = input_side(xhat, vecs, w_in, all_bias)
    att_zero, log_zero, keep_zero, send_zero = attend(0, place, starts, queries, keys, values, w_proj_t)
    send_zero, up_near, down_far, up_far_across = together(send_zero, up_near, down_far, up_far_across)
    near_and_far = stacked_three(up_near, down_far)

    mine_zero = add_low(keep_zero, core(send_zero))
    far_zero = over(mine_zero)
    down_near = near(stacked(w_down_own, down_far))
    three_across = across(near_and_far)
    att_one, log_one, keep_one, send_one = attend(1, after(place, mine_zero), starts, queries, keys, values, w_proj_t)
    send_one, far_zero, three_across, down_near = together(send_one, far_zero, three_across, down_near)
    down_near_across = across(down_near)

    mine_one = add_low(keep_one, core(send_one))
    far_one = over(mine_one)
    total_zero = add_low(mine_zero, far_zero)
    other_zero = core(total_zero)
    pieces = (w_up[None], both_across, up_far[None], up_near, up_far_across[None], three_across)
    w_up_all = unpacked(place, pieces, (0, 0, 0, 0, 0, 0))
    cot_both = pick(place, cot_own, cot_far)
    cot_other = core(cot_both)
    other_zero, cot_other, w_up_all, down_near_across = together(other_zero, cot_other, w_up_all, down_near_across)
    cots = (cot_both, cot_other)
    pieces = (w_down_own[None], both_across, down_far[None], down_near, three_across, down_near_across)
    probs_one = probs_of(1, after(place, mine_one), starts, queries, keys, log_one)
    probs_zero = probs_of(0, after(place, mine_one), starts, queries, keys, log_zero)
    probs_one, probs_zero, w_pieces = together(probs_one, probs_zero, pieces[0])
    pieces = (w_pieces, *pieces[1:])
    w_down_t = unpacked(place, pieces, (0, 1, 0, 0, 2, 0))

    weights = (vecs, up_bias, w_up_all, w_down_t)
    residual_zero, normed_zero, hidden_zero, grad_zero, up_sum_zero, keep_zero, send_zero = feed(
        0, spliced, total_zero, other_zero, cots, *weights
    )
    total_one = add_low(mine_one, far_one)
    other_one = core(total_one)
    mine_zero = add_low(keep_zero, core(send_zero))
    far_zero = over(mine_zero)
    residual_one, normed_one, hidden_one, grad_one, up_sum_one, keep_one, send_one = feed(
        1, after(spliced, mine_zero), total_one, other_one, cots, *weights
    )
    hidden_cols = hidden_one.shape[1]
    mine_one = add_low(keep_one, core(send_one))
    far_one = over(mine_one)
    b_keep, b_send = grad_blocks(
        grad_kernel, place, (hidden_cols,), normed_zero, normed_one, grad_zero, grad_one
    )
    b_got = across(b_send)
    c_keep, c_send = grad_blocks(
        cot_grad_kernel, after(place, b_send), (hidden_cols,), *cots, hidden_zero, hidden_one
    )
    mlp_keep, mlp_send = down_part((hidden_zero, after(hidden_one, b_send)), w_down_t)
    total_zero = add_low(after(mine_zero, c_send, mlp_send), far_zero, cost=0)
    other_zero = core(total_zero)
    residual = (residual_zero, residual_one)

    res_zero, branch_zero, gatt_zero, delta_zero, sums_zero = branch_back(
        0, total_zero, other_zero, residual_zero, cots, vecs, w_proj_t, att_zero
    )
    dq_zero, *early = back(0, place, queries, keys, values, probs_zero, gatt_zero, delta_zero, ())
    c_got = across(after(c_send, other_zero))
    total_one = add_low(after(mine_one, early[0], b_got), far_one)
    other_one = core(total_one)
    b_keep, b_send = fold(5, place, b_keep, after(b_got, total_one))
    b_got = near(b_send)
    mlp_got = core(after(mlp_send, other_zero))
    res_one, branch_one, gatt_one, delta_one, sums_one = branch_back(
        1, total_one, other_one, residual_one, cots, vecs, w_proj_t, att_one
    )
    dq_one, dk, dv = back(1, place, queries, keys, values, probs_one, gatt_one, delta_one, early)
    dk, b_got, c_got = together(dk, b_got, c_got)

    grad_residual = (res_zero, res_one)
    kinds = (((4, shard_rows, 2 * head_cols), F32), ((4, shard_rows, 2 * head_cols), LOW))
    scratch = (pltpu.VMEM((width, 2 * head_cols), F32),)
    d_keep, d_send = call(
        last_kernel_one, kinds, place, normed, dq_zero, dq_one, branch_zero, branch_one, att_zero, att_one, scratch=scratch
    )
    d_got = across(after(d_send, dk))
    c_keep, c_send = fold(5, place, c_keep, c_got)
    c_got = near(c_send)
    b_keep, b_send = fold(6, place, b_keep, b_got)
    b_got = far(b_send)
    keep, send_low, send_high, small, mixed_sums, picked = input_back(
        place, thought_pos, (dq_zero, dq_one), dk, dv, w_in, xhat, grad_residual
    )
    got_low, got_high = core(after(send_low, d_send)), core(after(send_high, d_send))
    small = add_full(small, core(small))
    small = add_full(small, over(small))
    shape = (4, shard_rows + 8, 2 * head_cols)
    e_keep, e_send = call(
        last_kernel_two,
        ((shape, F32), (shape, LOW)),
        place,
        normed,
        dk,
        dv,
        small,
        sums_zero,
        sums_one,
        up_sum_zero,
        up_sum_one,
        mixed_sums,
        scratch=(*scratch, pltpu.VMEM((8, 4 * head_cols), F32)),
    )
    e_got = across(e_send)
    keep, send, mlp_send = fold_rows(3, place, keep, got_low, got_high, mlp_keep, mlp_got)
    got = over(after(send, small))
    mlp_got = over(after(mlp_send, small))
    d_keep, d_send = fold(5, place, d_keep, after(d_got, c_got))
    d_got = near(d_send)
    c_keep, c_send = fold(6, place, c_keep, after(c_got, d_send))
    c_got = far(c_send)
    e_got, d_got, b_got = together(e_got, d_got, b_got)

    e_keep, e_send = fold(5, place, e_keep, e_got)
    e_got = near(e_send)
    d_keep, d_send = fold(6, place, d_keep, d_got)
    d_got = far(d_send)

    e_keep, e_send = fold(6, place, e_keep, e_got)
    e_got = far(e_send)
    embed_shape = (keep.shape[0], width)
    grad_embed, grad_thoughts, grad_up, grad_down, block_out = call(
        end_kernel,
        (
            (embed_shape, F32),
            ((thoughts.shape[0], 1, width // 4), F32),
            (b_keep.shape[1:], F32),
            (c_keep.shape[1:], F32),
            (embed_shape, LOW),
        ),
        place,
        keep,
        got,
        mlp_got,
        *residual,
        spliced,
        *grad_residual,
        vecs,
        thought_pos,
        thoughts,
        small,
        picked,
        b_keep,
        b_got,
        c_keep,
        c_got,
    )
    grad_thoughts = jnp.moveaxis(grad_thoughts, 1, 0)
    grad_embed, block_out, e_got, d_got = together(grad_embed, block_out, e_got, d_got)
    grad_in, grad_proj, *small = call(
        finish_kernel,
        (
            ((3, shard_rows, head_cols), F32),
            ((head_cols, shard_rows), F32),
            *((v.shape, F32) for v in vectors),
        ),
        d_keep,
        d_got,
        e_keep,
        e_got,
    )
    return block_out, grad_embed, grad_thoughts, grad_in, grad_proj, grad_up, grad_down.T, small


def plain_block(place, starts, x_own, thoughts, thought_pos, params, cot_own):
    dp = lax.axis_size("dp")
    w_qkv, w_proj, w_up, w_down_own = params[2], params[4], params[8], params[10].T
    shard_rows, head_cols = w_qkv.shape[1:]
    width = x_own.shape[1]
    x_rows, cots = rows_gather(x_own), rows_gather(cot_own)
    shard = jnp.concatenate([w_qkv[0], w_qkv[1], w_qkv[2], w_proj.T], axis=1)
    w_in, w_proj_t, vecs, up_bias, all_bias = plain_first(shard, vectors_of(params), 3 * head_cols, width)
    w_up_all = dp_gather(w_up).reshape(width, -1)
    w_down_t = dp_gather(w_down_own).reshape(width, -1)
    spliced, xhat = splice_side(place, x_rows, thoughts, thought_pos)
    normed, queries, keys, values = input_side(xhat, vecs, w_in, all_bias)

    def all_sum(keep, send):
        mine = add_low(keep, swapped(send, "tensor", 1))
        total = add_low(mine, swapped(mine, "tensor", 2))
        return total, swapped(total, "tensor", 1)

    def own_sum(keep, send):
        keep, send = fold(3, place, keep, swapped(send, "tensor", 1))
        return keep[0], swapped(send, "tensor", 2)[0]

    atts, logs, feds, grad_twos = [], [], [], []
    for chunk in range(2):
        att, log, *part = attend(chunk, place, starts, queries, keys, values, w_proj_t)
        feds.append(feed(chunk, spliced, *all_sum(*part), cots, vecs, up_bias, w_up_all, w_down_t))
        grad_twos.append(all_sum(*feds[-1][5:]))
        atts.append(att)
        logs.append(log)
    residual, normed_two, hidden, grad_hidden, up_sums = zip(feds[0][:5], feds[1][:5])
    block_out = result(place, *own_sum(*down_part(hidden, w_down_t)), residual, vecs)
    grad_up = plain_grad(shard_rows, *normed_two, *grad_hidden)
    grad_down = plain_grad(shard_rows, cots_rows(cots, 0), cots_rows(cots, 1), *hidden)
    branches, dqs, early = [], [], ()
    for chunk in range(2):
        branches.append(
            branch_back(chunk, *grad_twos[chunk], residual[chunk], cots, vecs, w_proj_t, atts[chunk])
        )
        probs = probs_of(chunk, place, starts, queries, keys, logs[chunk])
        dq, *early = back(
            chunk, place, queries, keys, values, probs, *branches[-1][2:4], early
        )
        dqs.append(dq)
    grad_residual, grad_branch = zip(branches[0][:2], branches[1][:2])
    keep, *send, small, mixed_sums, picked = input_back(
        place, thought_pos, dqs, *early, w_in, xhat, grad_residual
    )
    grad_mixed = jnp.concatenate([jnp.concatenate(dqs), *early], axis=1)
    small = small + swapped(small, "tensor", 1)
    small = small + swapped(small, "tensor", 2)
    grad_embed, grad_thoughts = output_side(
        place, *own_sum(keep, jnp.stack(send)), spliced, grad_residual, vecs, thought_pos, thoughts, small, picked
    )
    grad_in = plain_grad(shard_rows, normed, grad_mixed).reshape(shard_rows, 3, head_cols)
    grad_proj = plain_grad(shard_rows, *grad_branch, *atts)
    two = branches[0][4] + branches[1][4]
    count = small.shape[0] - 2
    vec = (small[count], small[count + 1], two[2], two[0], two[1], two[3], up_sums[0] + up_sums[1])
    vec += (mixed_sums[0, :head_cols], mixed_sums[0, 2 * head_cols :])
    vec = jnp.concatenate([v.reshape(dp, -1) for v in vec], axis=1)
    vec = dp_scatter_sum(vec[:, None, :])[0]
    small, first = [], 0
    for n in (params[k].size for k in (0, 1, 5, 6, 7, 11, 9, 3)):
        small.append(vec[first : first + n])
        first += n
    return (
        block_out,
        grad_embed,
        grad_thoughts,
        jnp.moveaxis(grad_in, 1, 0),
        grad_proj.T,
        grad_up,
        grad_down.T,
        small,
    )


def solution(mesh):
    in_specs = (
        P("dp", "tensor", None),
        P("dp", None, None),
        P("dp", None),
        P("dp", None),
        P("dp"),
        P("dp"),
        P(None, "dp", "tensor"),
        P(None, ("tensor", "dp")),
        P("tensor", "dp"),
        P("dp"),
        P("dp"),
        P("dp"),
        P("dp", "tensor"),
        P(("tensor", "dp")),
        P("tensor", "dp"),
        P("dp"),
        P("dp", "tensor", None),
    )
    out_specs = (
        P("dp", "tensor", None),
        P("dp", "tensor", None),
        P("dp", None, "tensor"),
        P("dp"),
        P("dp"),
        P(None, "dp", "tensor"),
        P(None, ("tensor", "dp")),
        P("tensor", "dp"),
        P("dp"),
        P("dp"),
        P("dp"),
        P("dp", "tensor"),
        P(("tensor", "dp")),
        P("tensor", "dp"),
        P("dp"),
    )
    return jax.shard_map(local, mesh=mesh, in_specs=in_specs, out_specs=out_specs, check_vma=False)
```

```python
import functools

import jax
import jax.numpy as jnp
from jax import lax
from jax.experimental import pallas as pl
from jax.experimental.pallas import tpu as pltpu
from jax.sharding import PartitionSpec as P

HD = 64
IMG = 256
EPSILON = 1e-05
F32 = jnp.float32
LOW = jnp.bfloat16
COST = 1000


def swapped(array, axis, mask):
    return lax.ppermute(array, axis, [(i, i ^ mask) for i in range(lax.axis_size(axis))])


def dp_masks():
    return [1 << b for b in reversed(range(lax.axis_size("dp").bit_length() - 1))]


def slot_owners(masks):
    owners = [0]
    for mask in masks:
        owners = owners + [o ^ mask for o in owners]
    return owners


def dp_gather(shard):
    masks, me = dp_masks(), lax.axis_index("dp")
    slots = shard[None]
    for mask in masks:
        other = swapped(slots, "dp", mask)
        first = (me & mask) == 0
        slots = jnp.where(
            first, jnp.concatenate([slots, other]), jnp.concatenate([other, slots])
        )
    owners = slot_owners(masks)
    return jnp.stack([slots[owners.index(s)] for s in range(len(owners))])


MASKS = ((0,), (1,), (4,), (2, 6), (5,), (3, 7))


def rows_pick(own, other):
    first = (lax.axis_index("tensor") >> 1) == 0
    return jnp.stack([jnp.where(first, own, other), jnp.where(first, other, own)])


def dp_scatter_sum(blocks):
    masks, me = dp_masks(), lax.axis_index("dp")
    slots = jnp.stack([blocks[s] for s in slot_owners(masks)])
    for mask in reversed(masks):
        half = slots.shape[0] // 2
        first = (me & mask) == 0
        keep = jnp.where(first, slots[:half], slots[half:])
        send = jnp.where(first, slots[half:], slots[:half])
        slots = keep.astype(F32) + swapped(send, "dp", mask).astype(F32)
    return slots[0]


def rows_gather(own):
    both = rows_pick(own, swapped(own, "tensor", 2))
    return both, swapped(both, "tensor", 1)


def after(value, *others):
    return lax.optimization_barrier((value, *others))[0]


def together(*values):
    return lax.optimization_barrier(values)


def dot(a, b, ca, cb, precision=None):
    return lax.dot_general(
        a, b, (((ca,), (cb,)), ((), ())), precision=precision, preferred_element_type=F32
    )


def normalised(values):
    centred = values - jnp.mean(values, axis=-1, keepdims=True)
    inverse = lax.rsqrt(jnp.mean(centred * centred, axis=-1, keepdims=True) + EPSILON)
    return centred * inverse, inverse


def norm_back(upstream, xhat, inverse, gain):
    scaled = upstream * gain
    return inverse * (
        scaled
        - jnp.mean(scaled, axis=-1, keepdims=True)
        - xhat * jnp.mean(scaled * xhat, axis=-1, keepdims=True)
    )


def gelu_pair(u):
    k, a = 0.7978845608028654, 0.044715
    square = u * u
    t = jnp.tanh(u * (k + (k * a) * square))
    rise = 0.5 * (1.0 + t)
    return u * rise, rise + (0.5 * u) * (1.0 - t * t) * (k + (3.0 * k * a) * square)


def cots_rows(cots, chunk):
    return jnp.concatenate([c[chunk] for c in cots])


def iota(shape, dim):
    return lax.broadcasted_iota(jnp.int32, shape, dim)


def call(kernel, outs, *args, scratch=(), mib=8, cost=0):
    spec = lambda a: pl.BlockSpec(
        memory_space=pltpu.SMEM if a.ndim == 1 and a.dtype == jnp.int32 else pltpu.VMEM
    )
    return pl.pallas_call(
        kernel,
        out_shape=tuple(jax.ShapeDtypeStruct(s, t) for s, t in outs),
        in_specs=[spec(a) for a in args],
        out_specs=tuple(pl.BlockSpec(memory_space=pltpu.VMEM) for _ in outs),
        scratch_shapes=scratch,
        compiler_params=pltpu.CompilerParams(vmem_limit_bytes=mib << 20),
        cost_estimate=pl.CostEstimate(flops=COST + cost, bytes_accessed=0, transcendentals=0),
    )(*args)


def splice_kernel(place, x_zero, x_one, thoughts, thought_pos, spliced_ref, xhat_ref):
    core = place[0]
    rows = x_zero.shape[1]
    for upper in range(2):
        for rel, ref in enumerate((x_zero, x_one)):
            first = upper * 2 * rows + (core ^ rel) * rows
            part = slice((2 * upper + rel) * rows, (2 * upper + rel + 1) * rows)
            match = (first + iota((rows, 1), 0)) == thought_pos[...]
            covered = jnp.sum(match.astype(F32), axis=1, keepdims=True) > 0.0
            picked = dot(match.astype(LOW), thoughts[...], 1, 0)
            spliced = jnp.where(covered, picked, ref[upper].astype(F32))
            spliced_ref[part, :] = spliced.astype(LOW)
            xhat_ref[part, :] = normalised(spliced)[0]


def input_kernel(xhat, vecs, w_in, bias, normed_ref, q_ref, k_ref, v_ref):
    rows = xhat.shape[0] // 4
    cols = q_ref.shape[1]
    for k in range(4):
        part = slice(k * rows, (k + 1) * rows)
        normed = (xhat[part, :] * vecs[0:1, :] + vecs[1:2, :]).astype(LOW)
        normed_ref[part, :] = normed
        mixed = (dot(normed, w_in[...], 1, 0) + bias[...]).astype(LOW)
        q_ref[part, :] = mixed[:, :cols]
        k_ref[part, :] = mixed[:, cols : 2 * cols]
        v_ref[part, :] = mixed[:, 2 * cols :]


def query_limits(place, starts, chunk, rows):
    core, start = place[0], starts[chunk]
    col = iota((1, 2 * rows), 1)
    query = 2 * rows * chunk + jnp.where(col < rows, col + core * rows, col - core * rows)
    inside = (query >= start) & (query < start + IMG)
    return jnp.where(inside, start + (IMG - 1), query)


def key_positions(place, block, rows):
    first = (block >> 1) * (2 * rows) + (place[0] ^ (block & 1)) * rows
    return first + iota((rows, 1), 0)


def attend_kernel(
    chunk, place, starts, q_ref, k_ref, v_ref, w_proj,
    att_ref, log_ref, keep_ref, send_ref, acc_ref, top_ref, sum_ref,
):
    half, cols = att_ref.shape
    rows = half // 2
    heads = cols // HD
    head_of = iota((1, cols), 1) // HD
    limits = query_limits(place, starts, chunk, rows)
    queries = q_ref[chunk * half : (chunk + 1) * half, :] * LOW(0.125)
    acc_ref[...] = jnp.zeros_like(acc_ref)
    top_ref[...] = jnp.full_like(top_ref, -1e30)
    sum_ref[...] = jnp.zeros_like(sum_ref)

    @pl.loop(0, 2 * chunk + 2)
    def _(block):
        span = pl.ds(pl.multiple_of(block * rows, rows), rows)
        keys = k_ref[span, :]
        values = v_ref[span, :].T
        allowed = key_positions(place, block, rows) <= limits
        for head in range(heads):
            scores = dot(jnp.where(head_of == head, keys, LOW(0)), queries, 1, 1)
            scores = jnp.where(allowed, scores, -1e30)
            top = top_ref[head : head + 1, :]
            new_top = jnp.maximum(top, jnp.max(scores, axis=0, keepdims=True))
            exps = jnp.exp(scores - new_top)
            fade = jnp.exp(top - new_top)
            top_ref[head : head + 1, :] = new_top
            sum_ref[head : head + 1, :] = sum_ref[head : head + 1, :] * fade + jnp.sum(
                exps, axis=0, keepdims=True
            )
            part = slice(head * HD, (head + 1) * HD)
            acc_ref[part, :] = acc_ref[part, :] * fade + dot(values[part, :], exps.astype(LOW), 1, 0)

    for head in range(heads):
        part = slice(head * HD, (head + 1) * HD)
        acc_ref[part, :] = acc_ref[part, :] / sum_ref[head : head + 1, :]
    log_ref[...] = top_ref[...] + jnp.log(jnp.maximum(sum_ref[...], 1e-30))
    attended = acc_ref[...].T.astype(LOW)
    att_ref[...] = attended
    branch = dot(attended, w_proj[...], 1, 1)
    keep_ref[...] = branch[:rows]
    send_ref[...] = branch[rows:].astype(LOW)


def attend(chunk, place, starts, queries, keys, values, w_proj):
    length, cols = queries.shape
    half, width = length // 2, w_proj.shape[0]
    return call(
        functools.partial(attend_kernel, chunk),
        (
            ((half, cols), LOW),
            ((8, half), F32),
            ((half // 2, width), F32),
            ((half // 2, width), LOW),
        ),
        place,
        starts,
        queries,
        keys,
        values,
        w_proj,
        scratch=(
            pltpu.VMEM((cols, half), F32),
            pltpu.VMEM((8, half), F32),
            pltpu.VMEM((8, half), F32),
        ),
    )


def feed_kernel(
    chunk, spliced, total, other, cot_zero, cot_one, vecs, up_bias, w_up, w_down,
    residual_ref, normed_ref, hidden_ref, grad_ref, sum_ref, keep_ref, send_ref,
):
    half, width = residual_ref.shape
    rows = half // 2
    for rel, ref in enumerate((total, other)):
        part = slice(rel * rows, (rel + 1) * rows)
        residual = (
            spliced[chunk * half + rel * rows : chunk * half + (rel + 1) * rows, :].astype(F32)
            + ref[...].astype(F32)
            + vecs[2:3, :]
        )
        residual_ref[part, :] = residual
        xhat, _ = normalised(residual)
        normed_ref[part, :] = (xhat * vecs[3:4, :] + vecs[4:5, :]).astype(LOW)
    hidden_cols = w_up.shape[1]
    step = 256 if hidden_cols % 256 == 0 else hidden_cols
    for first in range(0, hidden_cols, step):
        cols = slice(first, first + step)
        hidden, slope = gelu_pair(dot(normed_ref[...], w_up[:, cols], 1, 0) + up_bias[:, cols])
        hidden_ref[:, cols] = hidden.astype(LOW)
        back = jnp.concatenate(
            [dot(cot_zero[chunk], w_down[:, cols], 1, 0), dot(cot_one[chunk], w_down[:, cols], 1, 0)]
        )
        grad = (back * slope).astype(LOW)
        grad_ref[:, cols] = grad
        sum_ref[:, cols] = jnp.sum(grad.astype(F32), axis=0, keepdims=True)
    back = dot(grad_ref[...], w_up[...], 1, 1)
    keep_ref[...] = back[:rows]
    send_ref[...] = back[rows:].astype(LOW)


def feed(chunk, spliced, total, other, cots, vecs, up_bias, w_up, w_down):
    length, width = spliced.shape
    half, hidden = length // 2, w_up.shape[1]
    return call(
        functools.partial(feed_kernel, chunk),
        (
            ((half, width), F32),
            ((half, width), LOW),
            ((half, hidden), LOW),
            ((half, hidden), LOW),
            ((1, hidden), F32),
            ((half // 2, width), F32),
            ((half // 2, width), LOW),
        ),
        spliced,
        total,
        other,
        *cots,
        vecs,
        up_bias,
        w_up,
        w_down,
    )


def norm_back_kernel(
    chunk, total, other, residual, cot_zero, cot_one, vecs, w_proj, att,
    grad_res_ref, branch_ref, gatt_ref, delta_ref, sums_ref,
):
    half, width = residual.shape
    rows = half // 2
    gain = vecs[3:4, :]
    sums = [0.0, 0.0, 0.0, 0.0]
    for rel, (ref, cot) in enumerate(((total, cot_zero), (other, cot_one))):
        part = slice(rel * rows, (rel + 1) * rows)
        upstream = ref[...].astype(F32)
        xhat, inverse = normalised(residual[part, :])
        out_grad = cot[chunk].astype(F32)
        grad_res = out_grad + norm_back(upstream, xhat, inverse, gain)
        grad_res_ref[part, :] = grad_res
        branch_ref[part, :] = grad_res.astype(LOW)
        for k, term in enumerate((upstream * xhat, upstream, grad_res, out_grad)):
            sums[k] = sums[k] + jnp.sum(term, axis=0, keepdims=True)
    for k in range(4):
        sums_ref[k : k + 1, :] = sums[k]
    grad_att = dot(branch_ref[...], w_proj[...], 1, 0).astype(LOW)
    gatt_ref[...] = grad_att
    cols = att.shape[1]
    head_rows = (iota((8, cols), 0) == iota((8, cols), 1) // HD).astype(F32)
    delta_ref[...] = dot(
        head_rows, grad_att.astype(F32) * att[...].astype(F32), 1, 1, lax.Precision.HIGHEST
    )


def branch_back(chunk, total, other, residual, cots, vecs, w_proj, att):
    half, width = residual.shape
    cols = att.shape[1]
    return call(
        functools.partial(norm_back_kernel, chunk),
        (((half, width), F32), ((half, width), LOW), ((half, cols), LOW), ((8, half), F32), ((8, width), F32)),
        total,
        other,
        residual,
        *cots,
        vecs,
        w_proj,
        att,
    )


def probs_kernel(chunk, place, starts, q_ref, k_ref, log, out_ref):
    heads, _, half = out_ref.shape
    cols = q_ref.shape[1]
    rows = half // 2
    head_of = iota((1, cols), 1) // HD
    limits = query_limits(place, starts, chunk, rows)

    @pl.loop(0, 2 * chunk + 2)
    def _(block):
        span = pl.ds(pl.multiple_of(block * rows, rows), rows)
        keys = k_ref[span, :]
        queries = q_ref[chunk * half : (chunk + 1) * half, :] * LOW(0.125)
        allowed = key_positions(place, block, rows) <= limits
        for head in range(heads):
            scores = dot(jnp.where(head_of == head, keys, LOW(0)), queries, 1, 1)
            probs = jnp.exp(jnp.where(allowed, scores, -1e30) - log[head : head + 1, :])
            out_ref[head, span, :] = probs.astype(LOW)


def probs_of(chunk, place, starts, queries, keys, log):
    length, cols = queries.shape
    half = length // 2
    shape = (cols // HD, half * (chunk + 1), half)
    return call(functools.partial(probs_kernel, chunk), ((shape, LOW),), place, starts, queries, keys, log)[0]


def back_kernel(chunk, place, q_ref, k_ref, v_ref, probs_ref, gatt_ref, delta_ref, *rest):
    keys_in, rest = (rest[:2], rest[2:]) if chunk else ((), rest)
    dq_ref, dk_ref, dv_ref, dqt_ref = rest
    half, cols = gatt_ref.shape
    rows = half // 2
    heads = cols // HD
    head_of = iota((1, cols), 1) // HD
    dqt_ref[...] = jnp.zeros_like(dqt_ref)

    @pl.loop(0, 2 * chunk + 2)
    def _(block):
        span = pl.ds(pl.multiple_of(block * rows, rows), rows)
        values = v_ref[span, :]
        keys_t = k_ref[span, :].T
        queries = q_ref[chunk * half : (chunk + 1) * half, :] * LOW(0.125)
        grad_att = gatt_ref[...]
        dk = jnp.zeros((rows, cols), F32)
        dv = jnp.zeros((rows, cols), F32)
        for head in range(heads):
            mine = head_of == head
            probs = probs_ref[head, span, :]
            grad_probs = dot(jnp.where(mine, values, LOW(0)), grad_att, 1, 1)
            grad_scores = (probs.astype(F32) * (grad_probs - delta_ref[head : head + 1, :])).astype(LOW)
            dv = dv + dot(probs, jnp.where(mine, grad_att, LOW(0)), 1, 0)
            dk = dk + dot(grad_scores, jnp.where(mine, queries, LOW(0)), 1, 0)
            part = slice(head * HD, (head + 1) * HD)
            dqt_ref[part, :] = dqt_ref[part, :] + dot(keys_t[part, :], grad_scores, 1, 0)
        if chunk:
            seen = jnp.where(block < 2, 1.0, 0.0)
            early = pl.ds(pl.multiple_of((block & 1) * rows, rows), rows)
            dk = dk + keys_in[0][early, :] * seen
            dv = dv + keys_in[1][early, :] * seen
        dk_ref[span, :] = dk.astype(dk_ref.dtype)
        dv_ref[span, :] = dv.astype(dv_ref.dtype)

    dq_ref[...] = (dqt_ref[...] * 0.125).T.astype(LOW)


def back(chunk, place, queries, keys, values, probs, grad_att, delta, early):
    half, cols = grad_att.shape
    kind = (((half * (chunk + 1), cols), LOW if chunk else F32),) * 2
    return call(
        functools.partial(back_kernel, chunk),
        (((half, cols), LOW), *kind),
        place,
        queries,
        keys,
        values,
        probs,
        grad_att,
        delta,
        *early,
        scratch=(pltpu.VMEM((cols, half), F32),),
    )


def input_back_kernel(
    place, thought_pos, dq_zero, dq_one, dk, dv, w_in, xhat, res_zero, res_one,
    keep_ref, low_ref, high_ref, small_ref, colsum_ref, picked_ref, grad_ref,
):
    half, cols = dq_zero.shape
    rows = half // 2
    sums = [0.0, 0.0, 0.0]
    for upper, dq in enumerate((dq_zero, dq_one)):
        for rel in range(2):
            part = slice((2 * upper + rel) * rows, (2 * upper + rel + 1) * rows)
            mixed = jnp.concatenate(
                [dq[rel * rows : (rel + 1) * rows, :], dk[part, :], dv[part, :]], axis=1
            )
            grad = dot(mixed, w_in[...], 1, 1)
            grad_ref[part, :] = grad
            if rel:
                (low_ref, high_ref)[upper][...] = grad.astype(LOW)
            else:
                keep_ref[upper] = grad
            terms = (grad * xhat[part, :], grad, mixed.astype(F32))
            sums = [a + jnp.sum(b, axis=0, keepdims=True) for a, b in zip(sums, terms)]
    small_ref[...] = jnp.zeros_like(small_ref)
    picked_ref[...] = jnp.zeros_like(picked_ref)
    count = thought_pos.shape[0]
    for k in range(count):
        at = thought_pos[k]
        row = (at // half) * half + (((at // rows) & 1) ^ place[0]) * rows + at % rows
        small_ref[k : k + 1, :] = grad_ref[pl.ds(row, 1), :]
        low = res_zero[pl.ds(jnp.minimum(row, half - 1), 1), :]
        high = res_one[pl.ds(jnp.maximum(row - half, 0), 1), :]
        picked_ref[k : k + 1, :] = jnp.where(row < half, low, high)
    small_ref[count : count + 1, :] = sums[0]
    small_ref[count + 1 : count + 2, :] = sums[1]
    colsum_ref[...] = sums[2]


def output_kernel(place, keep, got, spliced, res_zero, res_one, vecs, thought_pos, thoughts, small, picked, *rest):
    pairs, (embed_ref, rows_ref, *more) = rest[: 2 * ((len(rest) - 2) // 3)], rest[2 * ((len(rest) - 2) // 3) :]
    rows = keep.shape[0]
    gain = vecs[0:1, :]
    own = pl.ds(pl.multiple_of(place[3] * (2 * rows), 2 * rows), rows)
    xhat, inverse = normalised(spliced[own, :].astype(F32))
    residual = jnp.where(place[3] == 0, res_zero[:rows, :], res_one[:rows, :])
    grad = norm_back(keep[...] + got[...].astype(F32), xhat, inverse, gain) + residual
    at = (2 * place[3] + place[0]) * rows + iota((rows, 1), 0)
    covered = jnp.sum((at == thought_pos[...]).astype(F32), axis=1, keepdims=True) > 0.0
    embed_ref[...] = jnp.where(covered, 0.0, grad)
    count = thoughts.shape[0]
    xhat, inverse = normalised(thoughts[...].astype(F32))
    grad = norm_back(small[:count, :], xhat, inverse, gain) + picked[:count, :]
    cols = rows_ref.shape[2]
    rank = 2 * place[3] + place[0]
    grad = sum(jnp.where(rank == k, 1.0, 0.0) * grad[:, k * cols : (k + 1) * cols] for k in range(4))
    for k in range(count):
        rows_ref[k] = grad[k : k + 1, :]
    for ref, keep, got in zip(more, pairs[::2], pairs[1::2]):
        ref[...] = keep[0] + got[0].astype(F32)


def end_kernel(place, keep, got, mlp_got, pre_zero, pre_one, *rest):
    *rest, result_ref = rest
    width = result_ref.shape[1]
    result_ref[...] = result_of(place, keep[:, width:], mlp_got, pre_zero, pre_one, rest[3])
    output_kernel(place, keep[:, :width], got, *rest)


def fold_kernel(bit, place, *refs):
    *parts, keep_ref, send_ref = refs
    half = keep_ref.shape[0]
    mine = place[bit] * half
    rest = half - mine
    first = 0
    for keep, got in zip(parts[::2], parts[1::2]):
        rows, cols = keep.shape[1:]
        below = rows < 16 and first > 0
        if below:
            at = (slice(keep_ref.shape[1] - rows, None), slice(0, cols))
        else:
            at = (slice(0, rows), slice(first, first + cols))
            first += cols
        for k in range(half):
            keep_ref[(k, *at)] = keep[mine + k] + got[mine + k].astype(F32)
            send_ref[(k, *at)] = (keep[rest + k] + got[rest + k].astype(F32)).astype(LOW)


def fold(bit, place, *parts):
    under = [p.shape[1] for p in parts[2::2] if p.shape[1] < 16]
    cols = sum(p.shape[2] for k, p in enumerate(parts[::2]) if k == 0 or p.shape[1] >= 16)
    shape = (parts[0].shape[0] // 2, parts[0].shape[1] + sum(under), cols)
    return call(functools.partial(fold_kernel, bit), ((shape, F32), (shape, LOW)), place, *parts)


def fold_rows_kernel(bit, place, keep, low, high, mlp_keep, mlp_got, keep_ref, send_ref, mlp_ref):
    first, cols = place[bit] == 0, low.shape[1]
    low, high = keep[0] + low[...].astype(F32), keep[1] + high[...].astype(F32)
    keep_ref[:, :cols] = jnp.where(first, low, high)
    send_ref[...] = jnp.where(first, high, low).astype(LOW)
    low, high = (mlp_keep[k] + mlp_got[k].astype(F32) for k in range(2))
    keep_ref[:, cols:] = jnp.where(first, low, high)
    mlp_ref[...] = jnp.where(first, high, low).astype(LOW)


def fold_rows(bit, place, keep, low, high, mlp_keep, mlp_got):
    shape = (low.shape[0], 2 * low.shape[1])
    args = (keep, low, high, mlp_keep, mlp_got)
    kinds = ((shape, F32), (low.shape, LOW), (low.shape, LOW))
    return call(functools.partial(fold_rows_kernel, bit), kinds, place, *args)


def add_kernel(a, b, out):
    out[...] = (a[...].astype(F32) + b[...].astype(F32)).astype(LOW)


def add_full_kernel(a, b, out):
    out[...] = a[...] + b[...]


def add_full(a, b):
    return call(add_full_kernel, ((a.shape, F32),), a, b)[0]


def add_low(a, b, cost=0):
    return call(add_kernel, ((a.shape, LOW),), a, b, cost=cost)[0]


def to_slots(place, sum_ref, first, keep_ref, send_ref, bit=0):
    rows, cols = sum_ref.shape[0] // 8, keep_ref.shape[2]
    here = place[(7, 5, 6)[bit]] << bit
    for slot, owner in enumerate(((0, 4, 2, 6), (0, 1, 4, 5))[bit]):
        mine = pl.ds(pl.multiple_of((owner ^ here) * rows, rows), rows)
        rest = pl.ds(pl.multiple_of((owner ^ here ^ (1 << bit)) * rows, rows), rows)
        keep_ref[slot, :rows, :] = sum_ref[mine, first : first + cols]
        send_ref[slot, :rows, :] = sum_ref[rest, first : first + cols].astype(LOW)


def all_slots(place, sum_ref, blocks):
    first = 0
    for keep_ref, send_ref in zip(blocks[::2], blocks[1::2]):
        to_slots(place, sum_ref, first, keep_ref, send_ref)
        first += keep_ref.shape[2]


def product(left, right):
    return sum(dot(a[...], b[...], 0, 0) for a, b in zip(left, right))


def grad_kernel(count, place, *refs):
    sides, blocks, sum_ref = refs[:count], refs[count:-1], refs[-1]
    half = count // 2
    sum_ref[...] = product(sides[:half], sides[half:])
    all_slots(place, sum_ref, blocks)


def cot_grad_kernel(count, place, cot_zero, cot_one, hidden_zero, hidden_one, *refs):
    blocks, sum_ref = refs[:-1], refs[-1]
    rows = cot_zero.shape[1]
    left = [c[upper] for upper in range(2) for c in (cot_zero, cot_one)]
    right = [h[k * rows : (k + 1) * rows, :] for h in (hidden_zero, hidden_one) for k in range(2)]
    sum_ref[...] = sum(dot(a, b, 0, 0) for a, b in zip(left, right))
    all_slots(place, sum_ref, blocks)


def last_kernel_one(place, normed, dq_zero, dq_one, branch_zero, branch_one, att_zero, att_one, *refs):
    *blocks, sum_ref = refs
    half, cols = att_zero.shape
    sum_ref[:, :cols] = product((branch_zero, branch_one), (att_zero, att_one))
    sum_ref[:, cols:] = dot(normed[:half, :], dq_zero[...], 0, 0) + dot(normed[half:, :], dq_one[...], 0, 0)
    all_slots(place, sum_ref, blocks)


def last_kernel_two(
    place, normed, dk, dv, small, back_zero, back_one, up_zero, up_one, mixed_sums, keep_ref, send_ref, sum_ref, flat_ref
):
    cols = dk.shape[1]
    sum_ref[:, :cols] = dot(normed[...], dk[...], 0, 0)
    sum_ref[:, cols:] = dot(normed[...], dv[...], 0, 0)
    to_slots(place, sum_ref, 0, keep_ref, send_ref)
    rows, wide_cols = keep_ref.shape[1] - 8, keep_ref.shape[2]
    count = small.shape[0] - 2
    back = back_zero[...] + back_one[...]
    wide = [small[count : count + 1, :], small[count + 1 :, :], back[2:3], back[0:1], back[1:2], back[3:4]]
    wide += [up_zero[...] + up_one[...], mixed_sums[:, :cols], mixed_sums[:, 2 * cols :]]
    for owner in range(8):
        parts = []
        for v in wide:
            n = v.shape[1] // 8
            parts.append(v[:, owner * n : (owner + 1) * n])
        parts.append(jnp.zeros((1, 2 * wide_cols - sum(p.shape[1] for p in parts)), F32))
        flat_ref[owner : owner + 1, :] = jnp.concatenate(parts, axis=1)
    first = iota((8, wide_cols), 0) == 0
    for slot, owner in enumerate((0, 4, 2, 6)):
        mine, other = (flat_ref[pl.ds(owner ^ k ^ place[7], 1), :] for k in range(2))
        keep_ref[slot, rows:, :] = jnp.where(first, mine[:, :wide_cols], mine[:, wide_cols:])
        send_ref[slot, rows:, :] = jnp.where(first, other[:, :wide_cols], other[:, wide_cols:]).astype(LOW)


def finish_kernel(
    d_keep, d_got, e_keep, e_got, in_ref, proj_ref, gain_one, bias_one, proj_b, gain_two, bias_two, down_b, up_b, qv_b
):
    rows, cols = in_ref.shape[1:]
    one = d_keep[0] + d_got[0].astype(F32)
    two = e_keep[0] + e_got[0].astype(F32)
    proj_ref[...] = one[:, :cols].T
    in_ref[0] = one[:, cols:]
    in_ref[1] = two[:rows, :cols]
    in_ref[2] = two[:rows, cols:]
    flat = jnp.concatenate([two[rows : rows + 1, :], two[rows + 1 : rows + 2, :]], axis=1)
    first = 0
    for ref in (gain_one, bias_one, proj_b, gain_two, bias_two, down_b, up_b):
        ref[...] = flat[:, first : first + ref.shape[1]]
        first += ref.shape[1]
    count = qv_b.shape[1]
    qv_b[...] = jnp.concatenate([flat[:, first : first + count], flat[:, first + count : first + 2 * count]])


def result_of(place, keep, got, res_zero, res_one, vecs):
    rows = keep.shape[0]
    residual = jnp.where(place[3] == 0, res_zero[:rows, :], res_one[:rows, :])
    return (residual + (keep[...] + got[...].astype(F32)) + vecs[5:6, :]).astype(LOW)


def result_kernel(place, keep, got, res_zero, res_one, vecs, out_ref):
    out_ref[...] = result_of(place, keep, got, res_zero, res_one, vecs)


def stack_three_kernel(pair, one, out_ref):
    out_ref[0] = pair[0]
    out_ref[1] = pair[1]
    out_ref[2] = one[...]


def stacked_three(pair, one):
    return call(stack_three_kernel, (((3, *one.shape), one.dtype),), pair, one)[0]


def pick_kernel(place, own, other, out_ref):
    out_ref[place[3]] = own[...]
    out_ref[1 - place[3]] = other[...]


def pick(place, own, other):
    return call(pick_kernel, (((2, *own.shape), own.dtype),), place, own, other)[0]


def copy_kernel(*refs):
    half = len(refs) // 2
    for a, b in zip(refs[:half], refs[half:]):
        b[...] = a[...]


def brought(*arrays, cost=0):
    return call(copy_kernel, tuple((a.shape, a.dtype) for a in arrays), *arrays, cost=cost)


def stack_kernel(a, b, out_ref):
    out_ref[0] = a[...]
    out_ref[1] = b[...]


def stacked(a, b):
    return call(stack_kernel, (((2, *a.shape), a.dtype),), a, b)[0]


def grad_blocks(kernel, place, splits, *sides):
    width, cols = sides[0].shape[-1], sides[-1].shape[1]
    shapes = []
    for n in splits:
        shapes += [((4, width // 8, n), F32), ((4, width // 8, n), LOW)]
    scratch = (pltpu.VMEM((width, cols), F32),)
    return call(functools.partial(kernel, len(sides)), shapes, place, *sides, scratch=scratch, mib=12)


def plain_grad(shard_rows, *sides):
    half = len(sides) // 2
    total = sum(dot(a, b, 0, 0) for a, b in zip(sides[:half], sides[half:])).astype(LOW)
    return dp_scatter_sum(total.reshape(-1, shard_rows, total.shape[1]))


def fast(shard_rows):
    return lax.axis_size("dp") == 8 and shard_rows % 16 == 0


def place_pieces(masks, place, pieces, write):
    for piece, owners in zip(pieces, masks):
        for k, mask in enumerate(owners):
            write(place[4] ^ mask, piece, k)


def first_kernel(masks, spans, hidden_cols, place, *refs):
    pieces, (w_in_ref, w_proj_ref, vecs_ref, up_ref, bias_ref, flat_ref) = refs[: len(masks)], refs[len(masks) :]
    width, qkv_cols = w_in_ref.shape
    shard_rows = width // 8

    def write(owner, piece, k):
        at = pl.ds(pl.multiple_of(owner * shard_rows, shard_rows), shard_rows)
        w_in_ref[at, :] = piece[k, :shard_rows, :qkv_cols]
        w_proj_ref[at, :] = piece[k, :shard_rows, qkv_cols:]
        flat_ref[pl.ds(owner, 1), :] = piece[k, shard_rows : shard_rows + 1, :].astype(F32)

    place_pieces(masks, place, pieces, write)
    flat = flat_ref[...]
    joined = [
        jnp.concatenate([flat[s : s + 1, a:b] for s in range(8)], axis=1) for a, b in zip(spans, spans[1:])
    ]
    for k in range(6):
        vecs_ref[k : k + 1, :] = joined[k]
    up_ref[...] = joined[6]
    bias_ref[...] = jnp.concatenate([joined[7], jnp.zeros_like(joined[7]), joined[8]], axis=1)


def plain_kernel(masks, firsts, place, *refs):
    *pieces, out_ref = refs
    rows = out_ref.shape[0] // 8
    for number, (piece, owners) in enumerate(zip(pieces, masks)):
        for k, mask in enumerate(owners):
            at = pl.ds(pl.multiple_of((place[4] ^ mask) * rows, rows), rows)
            out_ref[at, :] = piece[firsts[number] + k]


def pack_kernel(count, *refs):
    sources, out_ref, held, sems = refs[:count], refs[count], refs[count + 1 : -1], refs[-1]
    copies = [pltpu.make_async_copy(a, b, sems.at[k]) for k, (a, b) in enumerate(zip(sources, held))]
    for c in copies:
        c.start()
    for c in copies:
        c.wait()
    w_qkv, w_proj, *vectors = held
    rows = w_qkv.shape[1]
    out_ref[:rows, :] = jnp.concatenate([w_qkv[0], w_qkv[1], w_qkv[2], w_proj[...].T], axis=1)
    rows_of = [v[...].astype(F32) for v in vectors]
    rows_of = rows_of[:-1] + [rows_of[-1][0:1], rows_of[-1][1:2]]
    flat = jnp.concatenate(rows_of, axis=1)
    flat = jnp.concatenate([flat, jnp.zeros((1, out_ref.shape[1] - flat.shape[1]), F32)], axis=1)
    out_ref[rows:, :] = jnp.broadcast_to(flat, (8, flat.shape[1])).astype(LOW)


def first_pack(*args):
    w_qkv, w_proj = args[:2]
    return pl.pallas_call(
        functools.partial(pack_kernel, len(args)),
        out_shape=jax.ShapeDtypeStruct((w_qkv.shape[1] + 8, 3 * w_qkv.shape[2] + w_proj.shape[0]), LOW),
        in_specs=[pl.BlockSpec(memory_space=pl.ANY) for _ in args],
        out_specs=pl.BlockSpec(memory_space=pltpu.VMEM),
        scratch_shapes=[
            *(pltpu.VMEM(a.shape, a.dtype) for a in args),
            pltpu.SemaphoreType.DMA((len(args),)),
        ],
        compiler_params=pltpu.CompilerParams(vmem_limit_bytes=63 << 20),
        cost_estimate=pl.CostEstimate(flops=COST, bytes_accessed=0, transcendentals=0),
    )(*args)


def spans_of(vectors):
    spans = [0]
    for n in (*(v.shape[1] for v in vectors), vectors[-1].shape[1]):
        spans.append(spans[-1] + n)
    return spans


def first_unpacked(place, pieces, vectors, qkv_cols, head_cols, width):
    shapes = (
        ((width, qkv_cols), LOW),
        ((width, head_cols), LOW),
        ((6, width), F32),
        ((1, 8 * vectors[6].shape[1]), F32),
        ((1, qkv_cols), F32),
    )
    return call(
        functools.partial(first_kernel, MASKS, spans_of(vectors), 0),
        shapes,
        place,
        *pieces,
        scratch=(pltpu.VMEM((8, qkv_cols + head_cols), F32),),
    )


def unpacked(place, pieces, firsts):
    rows, cols = pieces[0].shape[1:]
    return call(functools.partial(plain_kernel, MASKS, firsts), (((8 * rows, cols), LOW),), place, *pieces)[0]


def plain_first(shard, vectors, qkv_cols, width):
    flat = dp_gather(jnp.concatenate([*vectors[:-1], vectors[-1][0:1], vectors[-1][1:2]], axis=1))[:, 0].astype(F32)
    whole = dp_gather(shard).reshape(width, -1)
    spans = spans_of(vectors)
    joined = [flat[:, a:b].reshape(1, -1) for a, b in zip(spans, spans[1:])]
    return (
        whole[:, :qkv_cols],
        whole[:, qkv_cols:],
        jnp.concatenate(joined[:6]),
        joined[6],
        jnp.concatenate([joined[7], jnp.zeros_like(joined[7]), joined[8]], axis=1),
    )


def down_kernel(hidden_zero, hidden_one, w_down, keep_ref, send_ref):
    rows = keep_ref.shape[1]
    for upper, hidden in enumerate((hidden_zero, hidden_one)):
        part = dot(hidden[...], w_down[...], 1, 1)
        keep_ref[upper] = part[:rows]
        send_ref[upper] = part[rows:].astype(LOW)


def local(x_embed, thoughts, thought_pos, img_start, *rest):
    *params, grad_out = rest
    dp = lax.axis_size("dp")
    table = []
    for d in range(dp):
        for t in range(4):
            table.append((t & 1, 0, 0, t >> 1, d, d >> 1 & 1, d >> 2 & 1, d & 1))
    place = jnp.asarray(table, jnp.int32)[lax.axis_index("dp") * 4 + lax.axis_index("tensor")]
    block = quick_block if fast(params[2].shape[1]) else plain_block
    block_out, grad_embed, grad_thoughts, grad_in, grad_proj, grad_up, grad_down, small = block(
        place, img_start[0], x_embed[0], thoughts[0], thought_pos, params, grad_out[0]
    )
    gain_one, bias_one, proj_b, gain_two, bias_two, down_b, up_b, qv_b = small
    flat = lambda a: a.reshape(-1)
    return (
        block_out[None],
        grad_embed[None],
        grad_thoughts,
        flat(gain_one),
        flat(bias_one),
        grad_in,
        qv_b.reshape(2, -1),
        grad_proj,
        flat(proj_b),
        flat(gain_two),
        flat(bias_two),
        grad_up,
        flat(up_b),
        grad_down,
        flat(down_b),
    )


def vectors_of(params):
    return [params[k].reshape(1, -1) for k in (0, 1, 5, 6, 7, 11, 9)] + [params[3]]


def splice_side(place, x_rows, thoughts, thought_pos):
    shape = (4 * x_rows[0].shape[1], x_rows[0].shape[2])
    return call(splice_kernel, ((shape, LOW), (shape, F32)), place, *x_rows, thoughts, thought_pos)


def input_side(xhat, vecs, w_in, bias):
    length, width = xhat.shape
    kinds = (((length, width), LOW),) + (((length, w_in.shape[1] // 3), LOW),) * 3
    return call(input_kernel, kinds, xhat, vecs, w_in, bias)


def input_back(place, thought_pos, grad_queries, grad_keys, grad_values, w_in, xhat, grad_residual):
    length, width = xhat.shape
    count = thought_pos.shape[1]
    return call(
        input_back_kernel,
        (
            ((2, length // 4, width), F32),
            ((length // 4, width), LOW),
            ((length // 4, width), LOW),
            ((-(-(count + 2) // 8) * 8, width), F32),
            ((1, w_in.shape[1]), F32),
            ((-(-count // 8) * 8, width), F32),
        ),
        place,
        thought_pos[0],
        *grad_queries,
        grad_keys,
        grad_values,
        w_in,
        xhat,
        *grad_residual,
        scratch=(pltpu.VMEM((length, width), F32),),
    )


def output_side(place, keep, got, spliced, grad_residual, vecs, thought_pos, thoughts, small, picked, *pairs):
    rows, width = keep.shape
    embed, own, *more = call(
        output_kernel,
        (
            ((rows, width), F32),
            ((thoughts.shape[0], 1, width // 4), F32),
            *((p.shape[1:], F32) for p in pairs[::2]),
        ),
        place,
        keep,
        got,
        spliced,
        *grad_residual,
        vecs,
        thought_pos,
        thoughts,
        small,
        picked,
        *pairs,
    )
    return embed, jnp.moveaxis(own, 1, 0), *more


def result(place, keep, got, residual, vecs):
    return call(result_kernel, ((keep.shape, LOW),), place, keep, got, *residual, vecs)[0]


def down_part(hidden, w_down_t):
    shape = (2, hidden[0].shape[0] // 2, w_down_t.shape[0])
    return call(down_kernel, ((shape, F32), (shape, LOW)), *hidden, w_down_t)


def quick_block(place, starts, x_own, thoughts, thought_pos, params, cot_own):
    across = lambda a: swapped(a, "dp", 1)
    near = lambda a: swapped(a, "dp", 2)
    far = lambda a: swapped(a, "dp", 4)
    core = lambda a: swapped(a, "tensor", 1)
    over = lambda a: swapped(a, "tensor", 2)
    w_qkv, w_proj, w_up, w_down_own = params[2], params[4], params[8], params[10].T
    shard_rows, head_cols = w_qkv.shape[1:]
    width = x_own.shape[1]
    vectors = vectors_of(params)

    pack = first_pack(w_qkv, w_proj, *vectors)
    pack_across = across(pack)
    pack_far = far(pack)
    x_far = over(after(x_own, pack))
    pack_here, x_here = brought(pack, after(x_own, pack))
    both = stacked(after(w_up, pack), w_down_own)
    x_far, pack_far, pack_across, pack_here, x_here, both = together(
        x_far, pack_far, pack_across, pack_here, x_here, both
    )

    pack_near, pack_far_across = near(stacked(pack_here, pack_far)), across(pack_far)
    up_far = far(after(w_up, pack_far))
    both_across = across(both)
    cot_far = over(after(cot_own, pack_far))
    pack_near, pack_far_across, up_far, both_across, cot_far = together(
        pack_near, pack_far_across, up_far, both_across, cot_far
    )

    pack_near_across = across(pack_near)
    up_near = near(stacked(w_up, up_far))
    down_far = far(after(w_down_own, up_far))
    x_both = pick(place, x_here, after(x_far, up_far))
    x_other = core(x_both)
    spliced, xhat = splice_side(place, (x_both, x_other), thoughts, thought_pos)
    pack_near_across, xhat = together(pack_near_across, xhat)
    up_far_across = across(after(up_far, pack_near_across))
    pieces = (pack_here[None], pack_across[None], pack_far[None], pack_near, pack_far_across[None], pack_near_across)
    w_in, w_proj_t, vecs, up_bias, all_bias = first_unpacked(place, pieces, vectors, 3 * head_cols, head_cols, width)
    normed, queries, keys, values = input_side(xhat, vecs, w_in, all_bias)
    att_zero, log_zero, keep_zero, send_zero = attend(0, place, starts, queries, keys, values, w_proj_t)
    send_zero, up_near, down_far, up_far_across = together(send_zero, up_near, down_far, up_far_across)
    near_and_far = stacked_three(up_near, down_far)

    mine_zero = add_low(keep_zero, core(send_zero))
    far_zero = over(mine_zero)
    down_near = near(stacked(w_down_own, down_far))
    three_across = across(near_and_far)
    att_one, log_one, keep_one, send_one = attend(1, after(place, mine_zero), starts, queries, keys, values, w_proj_t)
    send_one, far_zero, three_across, down_near = together(send_one, far_zero, three_across, down_near)
    down_near_across = across(down_near)

    mine_one = add_low(keep_one, core(send_one))
    far_one = over(mine_one)
    total_zero = add_low(mine_zero, far_zero)
    other_zero = core(total_zero)
    pieces = (w_up[None], both_across, up_far[None], up_near, up_far_across[None], three_across)
    w_up_all = unpacked(place, pieces, (0, 0, 0, 0, 0, 0))
    cot_both = pick(place, cot_own, cot_far)
    cot_other = core(cot_both)
    other_zero, cot_other, w_up_all, down_near_across = together(other_zero, cot_other, w_up_all, down_near_across)
    cots = (cot_both, cot_other)
    pieces = (w_down_own[None], both_across, down_far[None], down_near, three_across, down_near_across)
    probs_one = probs_of(1, after(place, mine_one), starts, queries, keys, log_one)
    probs_zero = probs_of(0, after(place, mine_one), starts, queries, keys, log_zero)
    probs_one, probs_zero, w_pieces = together(probs_one, probs_zero, pieces[0])
    pieces = (w_pieces, *pieces[1:])
    w_down_t = unpacked(place, pieces, (0, 1, 0, 0, 2, 0))

    weights = (vecs, up_bias, w_up_all, w_down_t)
    residual_zero, normed_zero, hidden_zero, grad_zero, up_sum_zero, keep_zero, send_zero = feed(
        0, spliced, total_zero, other_zero, cots, *weights
    )
    total_one = add_low(mine_one, far_one)
    other_one = core(total_one)
    mine_zero = add_low(keep_zero, core(send_zero))
    far_zero = over(mine_zero)
    residual_one, normed_one, hidden_one, grad_one, up_sum_one, keep_one, send_one = feed(
        1, after(spliced, mine_zero), total_one, other_one, cots, *weights
    )
    hidden_cols = hidden_one.shape[1]
    mine_one = add_low(keep_one, core(send_one))
    far_one = over(mine_one)
    b_keep, b_send = grad_blocks(
        grad_kernel, place, (hidden_cols,), normed_zero, normed_one, grad_zero, grad_one
    )
    b_got = across(b_send)
    c_keep, c_send = grad_blocks(
        cot_grad_kernel, after(place, b_send), (hidden_cols,), *cots, hidden_zero, hidden_one
    )
    mlp_keep, mlp_send = down_part((hidden_zero, after(hidden_one, b_send)), w_down_t)
    total_zero = add_low(after(mine_zero, b_send), far_zero, cost=0)
    other_zero = core(total_zero)
    residual = (residual_zero, residual_one)

    res_zero, branch_zero, gatt_zero, delta_zero, sums_zero = branch_back(
        0, total_zero, other_zero, residual_zero, cots, vecs, w_proj_t, att_zero
    )
    dq_zero, *early = back(0, place, queries, keys, values, probs_zero, gatt_zero, delta_zero, ())
    c_got = across(after(c_send, other_zero))
    total_one = add_low(after(mine_one, early[0], b_got), far_one)
    other_one = core(total_one)
    b_keep, b_send = fold(5, place, b_keep, after(b_got, total_one))
    b_got = near(b_send)
    mlp_got = core(after(mlp_send, other_zero))
    res_one, branch_one, gatt_one, delta_one, sums_one = branch_back(
        1, total_one, other_one, residual_one, cots, vecs, w_proj_t, att_one
    )
    dq_one, dk, dv = back(1, place, queries, keys, values, probs_one, gatt_one, delta_one, early)
    dk, b_got, c_got = together(dk, b_got, c_got)

    grad_residual = (res_zero, res_one)
    kinds = (((4, shard_rows, 2 * head_cols), F32), ((4, shard_rows, 2 * head_cols), LOW))
    scratch = (pltpu.VMEM((width, 2 * head_cols), F32),)
    d_keep, d_send = call(
        last_kernel_one, kinds, place, normed, dq_zero, dq_one, branch_zero, branch_one, att_zero, att_one, scratch=scratch
    )
    d_got = across(after(d_send, dk))
    c_keep, c_send = fold(5, place, c_keep, c_got)
    c_got = near(c_send)
    b_keep, b_send = fold(6, place, b_keep, after(b_got, c_send))
    b_got = far(b_send)
    keep, send_low, send_high, small, mixed_sums, picked = input_back(
        place, thought_pos, (dq_zero, dq_one), dk, dv, w_in, xhat, grad_residual
    )
    got_low, got_high = core(after(send_low, d_send)), core(after(send_high, d_send))
    small = add_full(small, core(small))
    small = add_full(small, over(small))
    shape = (4, shard_rows + 8, 2 * head_cols)
    e_keep, e_send = call(
        last_kernel_two,
        ((shape, F32), (shape, LOW)),
        place,
        normed,
        dk,
        dv,
        small,
        sums_zero,
        sums_one,
        up_sum_zero,
        up_sum_one,
        mixed_sums,
        scratch=(*scratch, pltpu.VMEM((8, 4 * head_cols), F32)),
    )
    e_got = across(e_send)
    keep, send, mlp_send = fold_rows(3, place, keep, got_low, got_high, mlp_keep, mlp_got)
    got = over(after(send, small))
    mlp_got = over(after(mlp_send, small))
    d_keep, d_send = fold(5, place, d_keep, after(d_got, c_got))
    d_got = near(d_send)
    c_keep, c_send = fold(6, place, c_keep, after(c_got, d_send))
    c_got = far(c_send)
    e_got, d_got, b_got = together(e_got, d_got, b_got)

    e_keep, e_send = fold(5, place, e_keep, e_got)
    e_got = near(e_send)
    d_keep, d_send = fold(6, place, d_keep, d_got)
    d_got = far(d_send)

    e_keep, e_send = fold(6, place, e_keep, e_got)
    e_got = far(e_send)
    embed_shape = (keep.shape[0], width)
    grad_embed, grad_thoughts, grad_up, grad_down, block_out = call(
        end_kernel,
        (
            (embed_shape, F32),
            ((thoughts.shape[0], 1, width // 4), F32),
            (b_keep.shape[1:], F32),
            (c_keep.shape[1:], F32),
            (embed_shape, LOW),
        ),
        place,
        keep,
        got,
        mlp_got,
        *residual,
        spliced,
        *grad_residual,
        vecs,
        thought_pos,
        thoughts,
        small,
        picked,
        b_keep,
        b_got,
        c_keep,
        c_got,
    )
    grad_thoughts = jnp.moveaxis(grad_thoughts, 1, 0)
    grad_embed, block_out, e_got, d_got = together(grad_embed, block_out, e_got, d_got)
    grad_in, grad_proj, *small = call(
        finish_kernel,
        (
            ((3, shard_rows, head_cols), F32),
            ((head_cols, shard_rows), F32),
            *((v.shape, F32) for v in vectors),
        ),
        d_keep,
        d_got,
        e_keep,
        e_got,
    )
    return block_out, grad_embed, grad_thoughts, grad_in, grad_proj, grad_up, grad_down.T, small


def plain_block(place, starts, x_own, thoughts, thought_pos, params, cot_own):
    dp = lax.axis_size("dp")
    w_qkv, w_proj, w_up, w_down_own = params[2], params[4], params[8], params[10].T
    shard_rows, head_cols = w_qkv.shape[1:]
    width = x_own.shape[1]
    x_rows, cots = rows_gather(x_own), rows_gather(cot_own)
    shard = jnp.concatenate([w_qkv[0], w_qkv[1], w_qkv[2], w_proj.T], axis=1)
    w_in, w_proj_t, vecs, up_bias, all_bias = plain_first(shard, vectors_of(params), 3 * head_cols, width)
    w_up_all = dp_gather(w_up).reshape(width, -1)
    w_down_t = dp_gather(w_down_own).reshape(width, -1)
    spliced, xhat = splice_side(place, x_rows, thoughts, thought_pos)
    normed, queries, keys, values = input_side(xhat, vecs, w_in, all_bias)

    def all_sum(keep, send):
        mine = add_low(keep, swapped(send, "tensor", 1))
        total = add_low(mine, swapped(mine, "tensor", 2))
        return total, swapped(total, "tensor", 1)

    def own_sum(keep, send):
        keep, send = fold(3, place, keep, swapped(send, "tensor", 1))
        return keep[0], swapped(send, "tensor", 2)[0]

    atts, logs, feds, grad_twos = [], [], [], []
    for chunk in range(2):
        att, log, *part = attend(chunk, place, starts, queries, keys, values, w_proj_t)
        feds.append(feed(chunk, spliced, *all_sum(*part), cots, vecs, up_bias, w_up_all, w_down_t))
        grad_twos.append(all_sum(*feds[-1][5:]))
        atts.append(att)
        logs.append(log)
    residual, normed_two, hidden, grad_hidden, up_sums = zip(feds[0][:5], feds[1][:5])
    block_out = result(place, *own_sum(*down_part(hidden, w_down_t)), residual, vecs)
    grad_up = plain_grad(shard_rows, *normed_two, *grad_hidden)
    grad_down = plain_grad(shard_rows, cots_rows(cots, 0), cots_rows(cots, 1), *hidden)
    branches, dqs, early = [], [], ()
    for chunk in range(2):
        branches.append(
            branch_back(chunk, *grad_twos[chunk], residual[chunk], cots, vecs, w_proj_t, atts[chunk])
        )
        probs = probs_of(chunk, place, starts, queries, keys, logs[chunk])
        dq, *early = back(
            chunk, place, queries, keys, values, probs, *branches[-1][2:4], early
        )
        dqs.append(dq)
    grad_residual, grad_branch = zip(branches[0][:2], branches[1][:2])
    keep, *send, small, mixed_sums, picked = input_back(
        place, thought_pos, dqs, *early, w_in, xhat, grad_residual
    )
    grad_mixed = jnp.concatenate([jnp.concatenate(dqs), *early], axis=1)
    small = small + swapped(small, "tensor", 1)
    small = small + swapped(small, "tensor", 2)
    grad_embed, grad_thoughts = output_side(
        place, *own_sum(keep, jnp.stack(send)), spliced, grad_residual, vecs, thought_pos, thoughts, small, picked
    )
    grad_in = plain_grad(shard_rows, normed, grad_mixed).reshape(shard_rows, 3, head_cols)
    grad_proj = plain_grad(shard_rows, *grad_branch, *atts)
    two = branches[0][4] + branches[1][4]
    count = small.shape[0] - 2
    vec = (small[count], small[count + 1], two[2], two[0], two[1], two[3], up_sums[0] + up_sums[1])
    vec += (mixed_sums[0, :head_cols], mixed_sums[0, 2 * head_cols :])
    vec = jnp.concatenate([v.reshape(dp, -1) for v in vec], axis=1)
    vec = dp_scatter_sum(vec[:, None, :])[0]
    small, first = [], 0
    for n in (params[k].size for k in (0, 1, 5, 6, 7, 11, 9, 3)):
        small.append(vec[first : first + n])
        first += n
    return (
        block_out,
        grad_embed,
        grad_thoughts,
        jnp.moveaxis(grad_in, 1, 0),
        grad_proj.T,
        grad_up,
        grad_down.T,
        small,
    )


def solution(mesh):
    in_specs = (
        P("dp", "tensor", None),
        P("dp", None, None),
        P("dp", None),
        P("dp", None),
        P("dp"),
        P("dp"),
        P(None, "dp", "tensor"),
        P(None, ("tensor", "dp")),
        P("tensor", "dp"),
        P("dp"),
        P("dp"),
        P("dp"),
        P("dp", "tensor"),
        P(("tensor", "dp")),
        P("tensor", "dp"),
        P("dp"),
        P("dp", "tensor", None),
    )
    out_specs = (
        P("dp", "tensor", None),
        P("dp", "tensor", None),
        P("dp", None, "tensor"),
        P("dp"),
        P("dp"),
        P(None, "dp", "tensor"),
        P(None, ("tensor", "dp")),
        P("tensor", "dp"),
        P("dp"),
        P("dp"),
        P("dp"),
        P("dp", "tensor"),
        P(("tensor", "dp")),
        P("tensor", "dp"),
        P("dp"),
    )
    return jax.shard_map(local, mesh=mesh, in_specs=in_specs, out_specs=out_specs, check_vma=False)
```
